32 devices in a mesh: fsdp: 4 (over y, x), ctx: 4 (over z), tp: 2 (over core).
Axes of the slice: x: 2, y: 2, z: 4, core: 2. Of those that a mesh axis runs over, the one named last changes fastest.
Arguments:
- tokens: bfloat16 [8, 1568, 1024], P('fsdp', 'ctx'), may hold values from -6 to 6
- clip_mask: int32 [8], P('fsdp'), may hold values 0 or 1
- cotangent: bfloat16 [8, 1568, 1024], P('fsdp', 'ctx'), may hold values from -6 to 6
- first_gain: float32 [1024], replicated, may hold values from 0.1 to 1.9
- first_shift: float32 [1024], replicated, may hold values from -1.75 to 1.75
- joint_weight: bfloat16 [1024, 3, 1024], P('fsdp', None, 'tp'), may hold values from -0.1875 to 0.1875
- joint_bias: float32 [2, 1024], P(None, 'tp'), may hold values from -0.625 to 0.625
- mixer_weight: bfloat16 [1024, 1024], P('fsdp', 'tp'), may hold values from -2 to 2
- mixer_bias: float32 [1024], replicated, may hold values from -1.75 to 1.75
- second_gain: float32 [1024], replicated, may hold values from 0.1 to 1.9
- second_shift: float32 [1024], replicated, may hold values from -1.75 to 1.75
- expand_weight: bfloat16 [1024, 4096], P('fsdp', 'tp'), may hold values from -0.1875 to 0.1875
- expand_bias: float32 [4096], P('tp'), may hold values from -1.75 to 1.75
- reduce_weight: bfloat16 [1024, 4096], P('fsdp', 'tp'), may hold values from -0.09375 to 0.09375
- reduce_bias: float32 [1024], replicated, may hold values from -1.75 to 1.75
Outputs:
- result: bfloat16 [8, 1568, 1024], P('fsdp', 'ctx')
- tokens_grad: float32 [8, 1568, 1024], P('fsdp', 'ctx')
- grad_first_gain: float32 [1024], P('fsdp')
- grad_first_shift: float32 [1024], P('fsdp')
- grad_joint_weight: float32 [1024, 3, 1024], P('fsdp', None, 'tp')
- grad_joint_bias: float32 [2, 1024], P(None, ('tp', 'fsdp'))
- grad_mixer_weight: float32 [1024, 1024], P('fsdp', 'tp')
- grad_mixer_bias: float32 [1024], P('fsdp')
- grad_second_gain: float32 [1024], P('fsdp')
- grad_second_shift: float32 [1024], P('fsdp')
- grad_expand_weight: float32 [1024, 4096], P('fsdp', 'tp')
- grad_expand_bias: float32 [4096], P(('tp', 'fsdp'))
- grad_reduce_weight: float32 [1024, 4096], P('fsdp', 'tp')
- grad_reduce_bias: float32 [1024], P('fsdp')
The draws below stay inside these ranges and needn't reach their ends.
Inputs may be any that keep to these rules, and one draw needn't show every extreme that they name: `clip_mask`: 1 marks a real clip, 0 a padding clip.
All inputs are finite; a program needn't handle non-finite values. No bound on the sum of `clip_mask` on one device may be relied on, other than what follows from the above.
Results may differ from the reference program's by a relative error of at most 0.02.
Values may be sent and summed in bfloat16 or wider, within the bound.
No kernel may reach another device: no remote copies, remote signals or barrier semaphores. Data moves between devices by JAX's collectives and lax.ppermute only.
A program may use at most 192 MiB of HBM per device.

```python
import jax
import jax.numpy as jnp
from jax import lax

D = 1024
HEADS = 16
HEAD_DIM = 64
FF = 4096
CLIP_LEN = 1568
CLIPS = 8
N_CTX = 4


def set_ends(array, key, smallest, largest):
    shape = array.shape
    index_at = [jax.random.randint(jax.random.fold_in(key, axis), (), 0, shape[axis]) for axis in range(len(shape))]
    array = array.at[tuple(index_at)].set(smallest)
    longest = shape.index(max(shape))
    index_at[longest] = (index_at[longest] + 1) % shape[longest]
    return array.at[tuple(index_at)].set(largest)


def level_of(stream_key, extent, pieces, least, largest):
    def one(dim, blocks):
        heights = jax.random.uniform(jax.random.fold_in(jax.random.fold_in(stream_key, 6), dim), (blocks,), jnp.float32, least / len(pieces), largest / len(pieces))
        return jnp.repeat(jnp.exp(heights), extent[dim] // blocks).reshape((-1,) + (1,) * (len(extent) - dim - 1))

    loudness = one(*pieces[0])
    for cut in pieces[1:]:
        loudness = loudness * one(*cut)
    return loudness


def noise(rng, dims, deviation, most, cuts=(), dtype=jnp.bfloat16):
    values = deviation * jax.random.normal(rng, dims, jnp.float32)
    if cuts:
        values = values * level_of(rng, dims, cuts, -0.22, 0.18)
    return jnp.clip(values, -most, most).astype(dtype)


def setup_inputs(seed: int = 0) -> dict:
    streams_of = jax.random.split(jax.random.key(seed), 16)
    tokens = noise(streams_of[0], (CLIPS, CLIP_LEN, D), 1.0, 6.0, ((0, 4), (1, 4)))
    clip_mask = set_ends((jax.random.randint(streams_of[1], (CLIPS,), 0, 4) < 3).astype(jnp.int32), jax.random.fold_in(streams_of[1], 1), 0, 1)
    cotangent = noise(streams_of[2], (CLIPS, CLIP_LEN, D), 1.0, 6.0, ((0, 4), (1, 4)))
    first_gain = jnp.clip(1.0 + 0.18 * jax.random.normal(streams_of[3], (D,), jnp.float32), 0.1, 1.9)
    first_shift = noise(streams_of[4], (D,), 0.3, 1.75, (), jnp.float32)
    joint_weight = noise(streams_of[5], (D, 3, D), D ** -0.5, 0.1875, ((0, 4), (2, 2)))
    joint_bias = noise(streams_of[6], (2, D), 0.1, 0.625, ((1, 2),), jnp.float32)
    mixer_weight = noise(streams_of[7], (D, D), 8 ** -0.5, 2.0, ((0, 4), (1, 2)))
    mixer_bias = noise(streams_of[8], (D,), 0.3, 1.75, (), jnp.float32)
    second_gain = jnp.clip(1.0 + 0.18 * jax.random.normal(streams_of[9], (D,), jnp.float32), 0.1, 1.9)
    second_shift = noise(streams_of[10], (D,), 0.3, 1.75, (), jnp.float32)
    expand_weight = noise(streams_of[11], (D, FF), D ** -0.5, 0.1875, ((0, 4), (1, 2)))
    expand_bias = noise(streams_of[12], (FF,), 0.3, 1.75, ((0, 2),), jnp.float32)
    reduce_weight = noise(streams_of[13], (D, FF), FF ** -0.5, 0.09375, ((0, 4), (1, 2)))
    reduce_bias = noise(streams_of[14], (D,), 0.3, 1.75, (), jnp.float32)
    return {"tokens": tokens, "clip_mask": clip_mask, "cotangent": cotangent, "first_gain": first_gain, "first_shift": first_shift, "joint_weight": joint_weight, "joint_bias": joint_bias, "mixer_weight": mixer_weight, "mixer_bias": mixer_bias, "second_gain": second_gain, "second_shift": second_shift, "expand_weight": expand_weight, "expand_bias": expand_bias, "reduce_weight": reduce_weight, "reduce_bias": reduce_bias}


EPSILON = 1e-06
TOP_PRECISION = lax.Precision.HIGHEST

@jax.custom_vjp
def reduced_cast(v):
    return lax.optimization_barrier(v.astype(jnp.bfloat16)).astype(jnp.float32)

@jax.custom_vjp
def reduced_cast_back(v):
    return v

def low_keep(v):
    return (reduced_cast(v), None)

def low_pass(kept, grad):
    return (grad,)

def back_keep(v):
    return (v, None)

def back_low(kept, grad):
    return (reduced_cast(grad),)
reduced_cast.defvjp(low_keep, low_pass)
reduced_cast_back.defvjp(back_keep, back_low)

def normalize(value_rows):
    center = value_rows - lax.optimization_barrier(jnp.mean(value_rows, axis=-1, keepdims=True))
    return center * lax.rsqrt(lax.optimization_barrier(jnp.mean(center * center, axis=-1, keepdims=True)) + EPSILON)

def attend(queries, key_rows, value_rows):
    score_scale = HEAD_DIM ** (-0.5)
    blocks = queries.reshape(N_CTX, -1, HEADS, HEAD_DIM)

    def one_block(encoder_block):
        attention_scores = reduced_cast_back(jnp.einsum('cts,rts->tcr', encoder_block, key_rows, precision=TOP_PRECISION) * score_scale)
        top = lax.optimization_barrier(jnp.max(attention_scores, axis=-1, keepdims=True))
        expo = jnp.exp(attention_scores - top)
        attention_probs = expo / lax.optimization_barrier(jnp.sum(expo, axis=-1, keepdims=True))
        return jnp.einsum('wqp,pwv->qwv', reduced_cast(attention_probs), value_rows, precision=TOP_PRECISION)
    return lax.map(jax.checkpoint(one_block), blocks).reshape(-1, HEADS * HEAD_DIM)

def clip_layer(params, clip_tokens, clip_valid):
    first_gain, first_shift, joint_weight, joint_bias, mixer_weight, mixer_bias, second_gain, second_shift, expand_weight, expand_bias, reduce_weight, reduce_bias = params
    first_normed = reduced_cast(normalize(clip_tokens) * first_gain + first_shift)
    joint_out = jnp.einsum('ld,dte->lte', first_normed, joint_weight, precision=TOP_PRECISION)
    queries = reduced_cast(reduced_cast_back(joint_out[:, 0] + joint_bias[0]))
    key_rows = reduced_cast(reduced_cast_back(joint_out[:, 1]))
    value_rows = reduced_cast(reduced_cast_back(joint_out[:, 2] + joint_bias[1]))
    shaped = (-1, HEADS, HEAD_DIM)
    attended = reduced_cast(reduced_cast_back(attend(queries.reshape(shaped), key_rows.reshape(shaped), value_rows.reshape(shaped))))
    mixer_out = reduced_cast_back(jnp.dot(attended, mixer_weight.T, precision=TOP_PRECISION) + mixer_bias)
    first_sum = clip_tokens + mixer_out
    second_normed = reduced_cast(normalize(first_sum) * second_gain + second_shift)
    expanded = reduced_cast_back(jnp.dot(second_normed, expand_weight, precision=TOP_PRECISION) + expand_bias)
    activated = reduced_cast(jax.nn.gelu(expanded, approximate=False))
    reduce_out = reduced_cast_back(jnp.dot(activated, reduce_weight.T, precision=TOP_PRECISION) + reduce_bias)
    return clip_tokens + clip_valid * (mixer_out + reduce_out)

def reference(tokens, clip_mask, cotangent, first_gain, first_shift, joint_weight, joint_bias, mixer_weight, mixer_bias, second_gain, second_shift, expand_weight, expand_bias, reduce_weight, reduce_bias):
    params = (first_gain.astype(jnp.float32), first_shift.astype(jnp.float32), joint_weight.astype(jnp.float32), joint_bias.astype(jnp.float32), mixer_weight.astype(jnp.float32), mixer_bias.astype(jnp.float32), second_gain.astype(jnp.float32), second_shift.astype(jnp.float32), expand_weight.astype(jnp.float32), expand_bias.astype(jnp.float32), reduce_weight.astype(jnp.float32), reduce_bias.astype(jnp.float32))
    inputs = tokens.astype(jnp.float32)
    valid = clip_mask.astype(jnp.float32)

    def forward(inputs, params):

        def one_clip(item):
            return clip_layer(params, item[0], item[1])
        return lax.map(jax.checkpoint(one_clip), (inputs, valid))
    result, pullback = jax.vjp(forward, inputs, params)
    tokens_grad, grads = pullback(cotangent.astype(jnp.float32))
    return (result.astype(jnp.bfloat16), tokens_grad, grads[0], grads[1], grads[2], grads[3], grads[4], grads[5], grads[6], grads[7], grads[8], grads[9], grads[10], grads[11])
```

```python
from functools import partial

import jax
import jax.numpy as jnp
from jax import lax
from jax.experimental import pallas as pl
from jax.experimental.pallas import tpu as pltpu
from jax.sharding import PartitionSpec as P

HEAD_DIM = 64
EPSILON = 1e-06
LOW = jnp.bfloat16
FULL = jnp.float32

ROW_BY_ROW = (((1,), (1,)), ((), ()))
PLAIN = (((1,), (0,)), ((), ()))
COLUMN_BY_COLUMN = (((0,), (0,)), ((), ()))


def product(left, right, dims):
    return lax.dot_general(left, right, dims, preferred_element_type=FULL)


def normalize(value_rows):
    center = value_rows - jnp.mean(value_rows, axis=-1, keepdims=True)
    inverse = lax.rsqrt(jnp.mean(center * center, axis=-1, keepdims=True) + EPSILON)
    return (center * inverse, inverse)


def norm_back(upstream, gain, scaled, inverse):
    weighted = upstream * gain
    return inverse * (
        weighted
        - jnp.mean(weighted, axis=-1, keepdims=True)
        - scaled * jnp.mean(weighted * scaled, axis=-1, keepdims=True)
    )


def attention_forward_kernel(q_ref, k_ref, v_ref, o_ref, lse_ref):
    rows, width = q_ref.shape
    scale = jnp.asarray(HEAD_DIM ** (-0.5), LOW)
    lane = lax.broadcasted_iota(jnp.int32, (rows, 128), 1)
    lse = jnp.zeros((rows, 128), FULL)
    for pair in range(width // 128):
        columns = slice(128 * pair, 128 * pair + 128)
        q = q_ref[:, columns] * scale
        k = k_ref[:, columns]
        v = v_ref[:, columns]
        out = None
        for side in range(2):
            mask = (lane // HEAD_DIM) == side
            scores = product(jnp.where(mask, q, jnp.zeros_like(q)), k, ROW_BY_ROW)
            top = jnp.max(scores, axis=-1, keepdims=True)
            weights = jnp.exp(scores - top)
            total = jnp.sum(weights, axis=-1, keepdims=True)
            part = product(weights.astype(LOW), v, PLAIN) / total
            out = part if side == 0 else jnp.where(mask, part, out)
            lse = jnp.where(lane == 2 * pair + side, top + jnp.log(total), lse)
        o_ref[:, columns] = out.astype(LOW)
    lse_ref[0] = lse.T[: lse_ref.shape[1]]


def row_chunk(count):
    for chunk in range(256, 0, -16):
        if count % chunk == 0:
            return chunk
    raise ValueError("rows")


def attention_forward(q, k, v):
    count, width = q.shape
    chunk = row_chunk(count)
    steps = count // chunk
    part = pl.BlockSpec((chunk, width), lambda i: (i, 0))
    whole = pl.BlockSpec((count, width), lambda i: (0, 0))
    out, lse = pl.pallas_call(
        attention_forward_kernel,
        grid=(steps,),
        in_specs=[part, whole, whole],
        out_specs=[part, pl.BlockSpec((1, 8, chunk), lambda i: (i, 0, 0))],
        out_shape=[
            jax.ShapeDtypeStruct((count, width), LOW),
            jax.ShapeDtypeStruct((steps, 8, chunk), FULL),
        ],
        compiler_params=pltpu.CompilerParams(vmem_limit_bytes=48 << 20),
        name="attention_forward",
    )(q, k, v)
    return out, lse.transpose(1, 0, 2).reshape(8, count)


def attention_backward_kernel(
    q_ref, k_ref, v_ref, da_ref, o_ref, lse_ref, dq_ref, dk_ref, dv_ref,
    q_heads, da_heads, delta_ref, dq_total,
):
    count, width = q_ref.shape
    chunk = k_ref.shape[0]
    step = pl.program_id(0)
    scale = jnp.asarray(HEAD_DIM ** (-0.5), LOW)

    @pl.when(step == 0)
    def _():
        lane = lax.broadcasted_iota(jnp.int32, (count, 128), 1)
        delta = jnp.zeros((count, 128), FULL)
        for pair in range(width // 128):
            columns = slice(128 * pair, 128 * pair + 128)
            q = q_ref[:, columns] * scale
            da = da_ref[:, columns]
            both = da.astype(FULL) * o_ref[:, columns].astype(FULL)
            for side in range(2):
                head = 2 * pair + side
                mask = (lane // HEAD_DIM) == side
                q_heads[head] = jnp.where(mask, q, jnp.zeros_like(q))
                da_heads[head] = jnp.where(mask, da, jnp.zeros_like(da))
                row = jnp.sum(jnp.where(mask, both, 0.0), axis=-1, keepdims=True)
                delta = jnp.where(lane == head, row, delta)
        delta_ref[...] = delta.T[:8]
        dq_total[...] = jnp.zeros_like(dq_total)

    lane = lax.broadcasted_iota(jnp.int32, (chunk, 128), 1)
    for pair in range(width // 128):
        columns = slice(128 * pair, 128 * pair + 128)
        k = k_ref[:, columns]
        v = v_ref[:, columns]
        scaled_k = k * scale
        dk = dv = None
        for side in range(2):
            head = 2 * pair + side
            q = q_heads[head]
            da = da_heads[head]
            probs = jnp.exp(product(k, q, ROW_BY_ROW) - lse_ref[head : head + 1, :])
            slope = probs * (product(v, da, ROW_BY_ROW) - delta_ref[head : head + 1, :])
            slope = slope.astype(LOW)
            dv_part = product(probs.astype(LOW), da, PLAIN)
            dk_part = product(slope, q, PLAIN)
            dv = dv_part if dv is None else dv + dv_part
            dk = dk_part if dk is None else dk + dk_part
            one_k = jnp.where((lane // HEAD_DIM) == side, scaled_k, jnp.zeros_like(k))
            dq_total[:, columns] += product(slope, one_k, COLUMN_BY_COLUMN)
        dk_ref[:, columns] = dk.astype(LOW)
        dv_ref[:, columns] = dv.astype(LOW)

    @pl.when(step == pl.num_programs(0) - 1)
    def _():
        dq_ref[...] = dq_total[...].astype(LOW)


def attention_backward(q, k, v, da, out, lse):
    count, width = q.shape
    chunk = row_chunk(count)
    heads = width // HEAD_DIM
    part = pl.BlockSpec((chunk, width), lambda i: (i, 0))
    whole = pl.BlockSpec((count, width), lambda i: (0, 0))
    grad = jax.ShapeDtypeStruct((count, width), LOW)
    return pl.pallas_call(
        attention_backward_kernel,
        grid=(count // chunk,),
        in_specs=[whole, part, part, whole, whole, pl.BlockSpec((8, count), lambda i: (0, 0))],
        out_specs=[whole, part, part],
        out_shape=[grad, grad, grad],
        scratch_shapes=[
            pltpu.VMEM((heads, count, 128), LOW),
            pltpu.VMEM((heads, count, 128), LOW),
            pltpu.VMEM((8, count), FULL),
            pltpu.VMEM((count, width), FULL),
        ],
        compiler_params=pltpu.CompilerParams(vmem_limit_bytes=56 << 20),
        name="attention_backward",
    )(q, k, v, da, out, lse)


def swap(value, axis, distance):
    size = lax.axis_size(axis)
    return lax.ppermute(value, axis, [(i, i ^ distance) for i in range(size)])


def gather_rows(rows_here):
    size = lax.axis_size("fsdp")
    if size != 4:
        return lax.all_gather(rows_here, "fsdp", axis=0, tiled=True)
    me = lax.axis_index("fsdp")
    count, width = rows_here.shape
    half = count // 2
    near = swap(rows_here, "fsdp", 1)
    side = swap(rows_here, "fsdp", 2)
    far_top = swap(side[:half], "fsdp", 1)
    far_low = swap(near[half:], "fsdp", 2)
    out = jnp.zeros((4 * count, width), rows_here.dtype)
    out = lax.dynamic_update_slice(out, rows_here, (me * count, 0))
    out = lax.dynamic_update_slice(out, near, ((me ^ 1) * count, 0))
    out = lax.dynamic_update_slice(out, side, ((me ^ 2) * count, 0))
    out = lax.dynamic_update_slice(out, far_top, ((me ^ 3) * count, 0))
    return lax.dynamic_update_slice(out, far_low, ((me ^ 3) * count + half, 0))


def sum_rows(left, right):
    size = lax.axis_size("fsdp")
    if size != 4:
        whole = product(left, right, COLUMN_BY_COLUMN).astype(LOW)
        return lax.psum_scatter(whole, "fsdp", scatter_dimension=0, tiled=True).astype(FULL)
    me = lax.axis_index("fsdp")
    count = left.shape[1] // 4
    half = count // 2

    def block(distance):
        piece = lax.dynamic_slice_in_dim(left, (me ^ distance) * count, count, 1)
        return product(piece, right, COLUMN_BY_COLUMN)

    far = block(3).astype(LOW)
    far_top = swap(far[:half], "fsdp", 1)
    far_low = swap(far[half:], "fsdp", 2)
    near = block(1)
    side = block(2)
    near_top = swap(near[:half].astype(LOW), "fsdp", 1)
    side_low = swap(side[half:].astype(LOW), "fsdp", 2)
    near_low = swap((near[half:] + far_low.astype(FULL)).astype(LOW), "fsdp", 1)
    side_top = swap((side[:half] + far_top.astype(FULL)).astype(LOW), "fsdp", 2)
    own = block(0)
    top = own[:half] + (near_top.astype(FULL) + side_top.astype(FULL))
    low = own[half:] + (near_low.astype(FULL) + side_low.astype(FULL))
    return jnp.concatenate([top, low], axis=0)


def in_order(bit, mine, other):
    return jnp.where(
        bit == 0,
        jnp.concatenate([mine, other], axis=0),
        jnp.concatenate([other, mine], axis=0),
    )


def sum_blocks(value):
    me = lax.axis_index("ctx")
    low_bit = me & 1
    high_bit = me >> 1
    half = value.shape[0] // 2
    keep = lax.dynamic_slice_in_dim(value, low_bit * half, half, 0)
    send = lax.dynamic_slice_in_dim(value, (1 - low_bit) * half, half, 0).astype(LOW)
    value = keep + swap(send, "ctx", 1).astype(FULL)
    half = half // 2
    keep = lax.dynamic_slice_in_dim(value, high_bit * half, half, 0)
    send = lax.dynamic_slice_in_dim(value, (1 - high_bit) * half, half, 0).astype(LOW)
    value = (keep + swap(send, "ctx", 2).astype(FULL)).astype(LOW)
    value = in_order(high_bit, value, swap(value, "ctx", 2))
    value = in_order(low_bit, value, swap(value, "ctx", 1))
    return value.astype(FULL)


def sum_pairwise(value, axis):
    near = value + swap(value, axis, 1)
    far = swap(value, axis, 2) + swap(value, axis, 3)
    return near + far


def sum_cores(part):
    part = part.astype(LOW)
    return part.astype(FULL) + swap(part, "tp", 1).astype(FULL)


def per_device(
    tokens,
    clip_mask,
    cotangent,
    first_gain,
    first_shift,
    joint_weight,
    joint_bias,
    mixer_weight,
    mixer_bias,
    second_gain,
    second_shift,
    expand_weight,
    expand_bias,
    reduce_weight,
    reduce_bias,
):
    clips_here, rows_here, width = tokens.shape
    if lax.axis_size("ctx") != 4 or lax.axis_size("tp") != 2 or clips_here != 2:
        raise ValueError("mesh")
    shard = lax.axis_index("fsdp")
    block = lax.axis_index("ctx")
    core = lax.axis_index("tp")
    clip_at = block >> 1
    part_at = block & 1
    width_half = width // 2
    features = joint_weight.shape[2]
    part_width = features // 2
    tokens_here = clips_here * rows_here

    inputs = tokens.astype(FULL)
    first_scaled, first_inverse = normalize(inputs)
    first_normed = (first_scaled * first_gain + first_shift).astype(LOW)
    mine = lax.dynamic_slice_in_dim(first_normed, core * width_half, width_half, 2)
    other_side = lax.dynamic_slice_in_dim(first_normed, (1 - core) * width_half, width_half, 2)
    own_clip = lax.dynamic_index_in_dim(mine, clip_at, 0, False)
    other_clip = lax.dynamic_index_in_dim(mine, 1 - clip_at, 0, False)
    near_rows = swap(own_clip, "ctx", 1)
    across_rows = swap(other_clip, "ctx", 2)
    far_rows = swap(other_clip, "ctx", 3)
    normed_mine = jnp.concatenate([own_clip, near_rows, across_rows, far_rows], axis=0)
    normed_other = jnp.concatenate(
        [
            lax.dynamic_index_in_dim(other_side, clip_at, 0, False),
            swap(near_rows, "tp", 1),
            swap(across_rows, "tp", 1),
            swap(far_rows, "tp", 1),
        ],
        axis=0,
    )
    normed_clip = jnp.concatenate([normed_mine, normed_other], axis=1)

    joint_part = lax.dynamic_slice_in_dim(joint_weight, part_at * part_width, part_width, 2)
    joint_part = jnp.concatenate([joint_part[:, kind] for kind in range(3)], axis=1)
    joint_rows = gather_rows(joint_part)
    joint_full = jnp.concatenate(
        [
            lax.dynamic_slice_in_dim(joint_rows, core * width_half, width_half, 0),
            lax.dynamic_slice_in_dim(joint_rows, (1 - core) * width_half, width_half, 0),
        ],
        axis=0,
    )
    mixer_full = gather_rows(mixer_weight)
    expand_full = gather_rows(expand_weight)
    reduce_full = gather_rows(reduce_weight)

    joint_out = product(normed_clip, joint_full, PLAIN)
    bias_part = lax.dynamic_slice_in_dim(joint_bias, part_at * part_width, part_width, 1)
    queries = (joint_out[:, :part_width] + bias_part[0]).astype(LOW)
    keys = joint_out[:, part_width : 2 * part_width].astype(LOW)
    values = (joint_out[:, 2 * part_width :] + bias_part[1]).astype(LOW)
    attended, log_total = attention_forward(queries, keys, values)

    attended_blocks = attended.reshape(4, rows_here, part_width)
    arrived = [attended_blocks[0]] + [swap(attended_blocks[d], "ctx", d) for d in (1, 2, 3)]

    def swapped_if(bit, pair):
        return [jnp.where(bit == 0, pair[0], pair[1]), jnp.where(bit == 0, pair[1], pair[0])]

    first_pair = swapped_if(part_at, arrived[:2])
    second_pair = swapped_if(part_at, arrived[2:])
    own_joined = jnp.concatenate(first_pair, axis=1)
    other_joined = jnp.concatenate(second_pair, axis=1)
    mixed_in = jnp.concatenate(swapped_if(clip_at, [own_joined, other_joined]), axis=0)

    flat_inputs = inputs.reshape(tokens_here, width)
    valid = jnp.broadcast_to(
        clip_mask.astype(FULL)[:, None, None], (clips_here, rows_here, 1)
    ).reshape(tokens_here, 1)
    mixer_out = sum_cores(product(mixed_in, mixer_full, ROW_BY_ROW)) + mixer_bias
    second_scaled, second_inverse = normalize(flat_inputs + mixer_out)
    second_normed = (second_scaled * second_gain + second_shift).astype(LOW)
    expanded = product(second_normed, expand_full, PLAIN) + expand_bias
    activated, gelu_back = jax.vjp(partial(jax.nn.gelu, approximate=False), expanded)
    activated_low = activated.astype(LOW)
    reduce_out = sum_cores(product(activated_low, reduce_full, ROW_BY_ROW)) + reduce_bias
    result = (flat_inputs + valid * (mixer_out + reduce_out)).astype(LOW)

    outer = cotangent.astype(FULL).reshape(tokens_here, width)
    branch_slope = outer * valid
    reduce_slope = branch_slope.astype(LOW)
    reduce_bias_grad = jnp.sum(reduce_slope.astype(FULL), axis=0)
    activated_slope = product(reduce_slope, reduce_full, PLAIN)
    expand_slope = gelu_back(activated_slope)[0].astype(LOW)
    expand_bias_grad = jnp.sum(expand_slope.astype(FULL), axis=0)
    second_slope = sum_cores(product(expand_slope, expand_full, ROW_BY_ROW))
    second_gain_grad = jnp.sum(second_slope * second_scaled, axis=0)
    second_shift_grad = jnp.sum(second_slope, axis=0)
    first_sum_back = norm_back(second_slope, second_gain, second_scaled, second_inverse)
    mixer_slope = (branch_slope + first_sum_back).astype(LOW)
    mixer_bias_grad = jnp.sum(mixer_slope.astype(FULL), axis=0)
    attended_slope = product(mixer_slope, mixer_full, PLAIN).astype(LOW)

    slope_clips = swapped_if(clip_at, [attended_slope[:rows_here], attended_slope[rows_here:]])
    leaving = []
    for piece in slope_clips:
        leaving += swapped_if(part_at, [piece[:, :part_width], piece[:, part_width:]])
    slope_clip = jnp.concatenate(
        [leaving[0]] + [swap(leaving[d], "ctx", d) for d in (1, 2, 3)], axis=0
    )

    reduce_grad = sum_blocks(sum_rows(reduce_slope, activated_low))
    expand_grad = sum_blocks(sum_rows(second_normed, expand_slope))
    mixer_grad = sum_blocks(sum_rows(mixer_slope, mixed_in))

    joint_slope = jnp.concatenate(
        attention_backward(queries, keys, values, slope_clip, attended, log_total), axis=1
    )
    slope_sums = jnp.sum(joint_slope.astype(FULL), axis=0)
    bias_sums = jnp.stack([slope_sums[:part_width], slope_sums[2 * part_width :]])
    joint_bias_grad = lax.dynamic_update_slice(
        jnp.zeros((2, features), FULL), bias_sums, (0, part_at * part_width)
    )

    first_part = product(joint_slope, joint_full, ROW_BY_ROW)
    first_half = first_part[:, :width_half].astype(LOW).astype(FULL) + swap(
        first_part[:, width_half:].astype(LOW), "tp", 1
    ).astype(FULL)
    pieces = first_half.astype(LOW).reshape(4, rows_here, width_half)
    own_half = pieces[0].astype(FULL) + swap(pieces[1], "ctx", 1).astype(FULL)
    other_half = swap(pieces[2], "ctx", 2).astype(FULL) + swap(pieces[3], "ctx", 3).astype(FULL)
    slope_half = jnp.concatenate(swapped_if(clip_at, [own_half, other_half]), axis=0).astype(LOW)
    slope_other = swap(slope_half, "tp", 1)
    first_slope = jnp.concatenate(swapped_if(core, [slope_half, slope_other]), axis=1).astype(FULL)

    flat_scaled = first_scaled.reshape(tokens_here, width)
    flat_inverse = first_inverse.reshape(tokens_here, 1)
    first_gain_grad = jnp.sum(first_slope * flat_scaled, axis=0)
    first_shift_grad = jnp.sum(first_slope, axis=0)
    tokens_grad = (
        outer + first_sum_back + norm_back(first_slope, first_gain, flat_scaled, flat_inverse)
    )

    normed_columns = jnp.concatenate(
        swapped_if(core, [normed_mine, normed_other]), axis=1
    )
    joint_sum = sum_rows(normed_columns, joint_slope).astype(LOW)
    joint_sum = (
        joint_sum.astype(FULL) + swap(joint_sum, "ctx", 2).astype(FULL)
    ).astype(LOW)
    joint_parts = swapped_if(part_at, [joint_sum, swap(joint_sum, "ctx", 1)])
    joint_grad = jnp.concatenate(
        [piece.reshape(-1, 3, part_width) for piece in joint_parts], axis=2
    ).astype(FULL)

    vectors = [
        first_gain_grad,
        first_shift_grad,
        joint_bias_grad[0],
        joint_bias_grad[1],
        mixer_bias_grad,
        second_gain_grad,
        second_shift_grad,
        expand_bias_grad,
        reduce_bias_grad,
    ]
    packed = sum_pairwise(jnp.concatenate(vectors).reshape(-1, 128), "ctx")
    if lax.axis_size("fsdp") == 4:
        packed = sum_pairwise(packed, "fsdp")
    else:
        packed = lax.psum(packed, "fsdp")
    packed = packed.reshape(-1)
    shares = []
    start = 0
    for vector in vectors:
        share = vector.shape[0] // lax.axis_size("fsdp")
        shares.append(lax.dynamic_slice_in_dim(packed, start + shard * share, share, 0))
        start += vector.shape[0]

    shape = (clips_here, rows_here, width)
    return (
        result.reshape(shape),
        tokens_grad.reshape(shape),
        shares[0],
        shares[1],
        joint_grad,
        jnp.stack([shares[2], shares[3]]),
        mixer_grad,
        shares[4],
        shares[5],
        shares[6],
        expand_grad,
        shares[7],
        reduce_grad,
        shares[8],
    )


def solution(mesh):
    return jax.shard_map(
        per_device,
        mesh=mesh,
        in_specs=(
            P("fsdp", "ctx", None),
            P("fsdp"),
            P("fsdp", "ctx", None),
            P(),
            P(),
            P("fsdp", None, "tp"),
            P(None, "tp"),
            P("fsdp", "tp"),
            P(),
            P(),
            P(),
            P("fsdp", "tp"),
            P("tp"),
            P("fsdp", "tp"),
            P(),
        ),
        out_specs=(
            P("fsdp", "ctx", None),
            P("fsdp", "ctx", None),
            P("fsdp"),
            P("fsdp"),
            P("fsdp", None, "tp"),
            P(None, ("tp", "fsdp")),
            P("fsdp", "tp"),
            P("fsdp"),
            P("fsdp"),
            P("fsdp"),
            P("fsdp", "tp"),
            P(("tp", "fsdp")),
            P("fsdp", "tp"),
            P("fsdp"),
        ),
        check_vma=False,
    )
```

```python
import jax
import jax.numpy as jnp
from jax import lax
from jax.experimental import pallas as pl
from jax.experimental.pallas import tpu as pltpu
from jax.sharding import PartitionSpec as P

HEAD_DIM = 64
EPSILON = 1e-06
LOW = jnp.bfloat16
FULL = jnp.float32

ROW_BY_ROW = (((1,), (1,)), ((), ()))
PLAIN = (((1,), (0,)), ((), ()))
COLUMN_BY_COLUMN = (((0,), (0,)), ((), ()))


def product(left, right, dims):
    return lax.dot_general(left, right, dims, preferred_element_type=FULL)


def normalize(value_rows):
    center = value_rows - jnp.mean(value_rows, axis=-1, keepdims=True)
    inverse = lax.rsqrt(jnp.mean(center * center, axis=-1, keepdims=True) + EPSILON)
    return (center * inverse, inverse)


def norm_back(upstream, gain, scaled, inverse):
    weighted = upstream * gain
    return inverse * (
        weighted
        - jnp.mean(weighted, axis=-1, keepdims=True)
        - scaled * jnp.mean(weighted * scaled, axis=-1, keepdims=True)
    )


def attention_forward_kernel(q_ref, k_ref, v_ref, o_ref, lse_ref):
    rows, width = q_ref.shape
    lane = lax.broadcasted_iota(jnp.int32, (rows, width), 1)
    lse = jnp.zeros((rows, width), FULL)
    q = q_ref[...] * jnp.asarray(HEAD_DIM ** (-0.5), LOW)
    k = k_ref[...]
    v = v_ref[...]
    out = None
    for head in range(width // HEAD_DIM):
        mask = (lane // HEAD_DIM) == head
        scores = product(jnp.where(mask, q, jnp.zeros_like(q)), k, ROW_BY_ROW)
        top = jnp.max(scores, axis=-1, keepdims=True)
        weights = jnp.exp(scores - top)
        total = jnp.sum(weights, axis=-1, keepdims=True)
        part = product(weights.astype(LOW), v, PLAIN) / total
        out = part if out is None else jnp.where(mask, part, out)
        lse = jnp.where(lane == head, top + jnp.log(total), lse)
    o_ref[...] = out.astype(LOW)
    lse_ref[0] = lse.T[: lse_ref.shape[1]]


def row_chunk(count):
    for chunk in range(256, 0, -16):
        if count % chunk == 0:
            return chunk
    raise ValueError("rows")


def attention_forward(joint, pair):
    count, columns = joint.shape
    width = 2 * HEAD_DIM
    chunk = row_chunk(count)
    steps = count // chunk
    kind = columns // (3 * width)
    whole_k = pl.BlockSpec((count, width), lambda i: (0, kind + pair))
    whole_v = pl.BlockSpec((count, width), lambda i: (0, 2 * kind + pair))
    out, lse = pl.pallas_call(
        attention_forward_kernel,
        grid=(steps,),
        in_specs=[pl.BlockSpec((chunk, width), lambda i: (i, pair)), whole_k, whole_v],
        out_specs=[
            pl.BlockSpec((chunk, width), lambda i: (i, 0)),
            pl.BlockSpec((1, 8, chunk), lambda i: (i, 0, 0)),
        ],
        out_shape=[
            jax.ShapeDtypeStruct((count, width), LOW),
            jax.ShapeDtypeStruct((steps, 8, chunk), FULL),
        ],
        compiler_params=pltpu.CompilerParams(vmem_limit_bytes=40 << 20),
        cost_estimate=pl.CostEstimate(
            flops=16 * count * count * width,
            transcendentals=2 * count * count,
            bytes_accessed=8 * count * width,
        ),
        name="attention_forward",
    )(joint, joint, joint)
    return out, lse.transpose(1, 0, 2).reshape(8, count)


def attention_backward_kernel(
    q_ref, k_ref, v_ref, da_ref, o_ref, lse_ref, dq_ref, dk_ref, dv_ref,
    q_heads, da_heads, delta_ref, dq_total,
):
    count, width = q_ref.shape
    chunk = k_ref.shape[0]
    step = pl.program_id(0)
    heads = width // HEAD_DIM
    scale = jnp.asarray(HEAD_DIM ** (-0.5), LOW)

    @pl.when(step == 0)
    def _():
        lane = lax.broadcasted_iota(jnp.int32, (count, width), 1)
        delta = jnp.zeros((count, width), FULL)
        q = q_ref[...] * scale
        da = da_ref[...]
        both = da.astype(FULL) * o_ref[...].astype(FULL)
        for head in range(heads):
            mask = (lane // HEAD_DIM) == head
            q_heads[head] = jnp.where(mask, q, jnp.zeros_like(q))
            da_heads[head] = jnp.where(mask, da, jnp.zeros_like(da))
            row = jnp.sum(jnp.where(mask, both, 0.0), axis=-1, keepdims=True)
            delta = jnp.where(lane == head, row, delta)
        delta_ref[...] = delta.T[:8]
        dq_total[...] = jnp.zeros_like(dq_total)

    lane = lax.broadcasted_iota(jnp.int32, (chunk, width), 1)
    k = k_ref[...]
    v = v_ref[...]
    scaled_k = k * scale
    dk = dv = None
    for head in range(heads):
        q = q_heads[head]
        da = da_heads[head]
        probs = jnp.exp(product(k, q, ROW_BY_ROW) - lse_ref[head : head + 1, :])
        slope = probs * (product(v, da, ROW_BY_ROW) - delta_ref[head : head + 1, :])
        slope = slope.astype(LOW)
        dv_part = product(probs.astype(LOW), da, PLAIN)
        dk_part = product(slope, q, PLAIN)
        dv = dv_part if dv is None else dv + dv_part
        dk = dk_part if dk is None else dk + dk_part
        one_k = jnp.where((lane // HEAD_DIM) == head, scaled_k, jnp.zeros_like(k))
        dq_total[...] += product(slope, one_k, COLUMN_BY_COLUMN)
    dk_ref[...] = dk.astype(LOW)
    dv_ref[...] = dv.astype(LOW)

    @pl.when(step == pl.num_programs(0) - 1)
    def _():
        dq_ref[...] = dq_total[...].astype(LOW)


def attention_backward(joint, da, out, lse, pair):
    count, columns = joint.shape
    width = 2 * HEAD_DIM
    chunk = row_chunk(count)
    kind = columns // (3 * width)
    part_k = pl.BlockSpec((chunk, width), lambda i: (i, kind + pair))
    part_v = pl.BlockSpec((chunk, width), lambda i: (i, 2 * kind + pair))
    whole = pl.BlockSpec((count, width), lambda i: (0, pair))
    alone = pl.BlockSpec((count, width), lambda i: (0, 0))
    part_out = pl.BlockSpec((chunk, width), lambda i: (i, 0))
    grad = jax.ShapeDtypeStruct((count, width), LOW)
    return pl.pallas_call(
        attention_backward_kernel,
        grid=(count // chunk,),
        in_specs=[whole, part_k, part_v, alone, alone, pl.BlockSpec((8, count), lambda i: (0, 0))],
        out_specs=[alone, part_out, part_out],
        out_shape=[grad, grad, grad],
        scratch_shapes=[
            pltpu.VMEM((2, count, width), LOW),
            pltpu.VMEM((2, count, width), LOW),
            pltpu.VMEM((8, count), FULL),
            pltpu.VMEM((count, width), FULL),
        ],
        compiler_params=pltpu.CompilerParams(vmem_limit_bytes=40 << 20),
        cost_estimate=pl.CostEstimate(
            flops=40 * count * count * width,
            transcendentals=2 * count * count,
            bytes_accessed=16 * count * width,
        ),
        name="attention_backward",
    )(joint, joint, joint, da, out, lse)


def feed_forward_kernel(
    normed_ref, slope_ref, expand_ref, bias_ref, reduce_ref,
    active_ref, expand_slope_ref, back_ref, bias_grad_ref, total,
):
    step = pl.program_id(0)
    count = normed_ref.shape[0]
    half = count // 2
    bias_grad = None
    for rows in (slice(0, half), slice(half, count)):
        hidden = product(normed_ref[rows], expand_ref[...], PLAIN) + bias_ref[...]
        upstream = product(slope_ref[rows], reduce_ref[...], PLAIN)
        share = 0.5 * (1.0 + lax.erf(hidden * (0.5**0.5)))
        active_ref[rows] = (hidden * share).astype(LOW)
        density = jnp.exp(-0.5 * hidden * hidden) * 0.3989422804014327
        slope = (upstream * (share + hidden * density)).astype(LOW)
        expand_slope_ref[rows] = slope
        part = jnp.sum(slope.astype(FULL), axis=0, keepdims=True)
        bias_grad = part if bias_grad is None else bias_grad + part
        back = product(slope, expand_ref[...], ROW_BY_ROW)

        @pl.when(step == 0)
        def _():
            total[rows] = back

        @pl.when(step > 0)
        def _():
            total[rows] += back

    bias_grad_ref[...] = bias_grad

    @pl.when(step == pl.num_programs(0) - 1)
    def _():
        back_ref[...] = total[...].astype(LOW)


def feed_forward(normed, slope, expand, bias, reduce):
    count, width = normed.shape
    hidden = expand.shape[1]
    block = 512 if hidden % 512 == 0 else hidden
    whole = pl.BlockSpec((count, width), lambda i: (0, 0))
    columns = pl.BlockSpec((width, block), lambda i: (0, i))
    out = pl.BlockSpec((count, block), lambda i: (0, i))
    row = pl.BlockSpec((1, block), lambda i: (0, i))
    return pl.pallas_call(
        feed_forward_kernel,
        grid=(hidden // block,),
        in_specs=[whole, whole, columns, row, columns],
        out_specs=[out, out, whole, row],
        out_shape=[
            jax.ShapeDtypeStruct((count, hidden), LOW),
            jax.ShapeDtypeStruct((count, hidden), LOW),
            jax.ShapeDtypeStruct((count, width), LOW),
            jax.ShapeDtypeStruct((1, hidden), FULL),
        ],
        scratch_shapes=[pltpu.VMEM((count, width), FULL)],
        compiler_params=pltpu.CompilerParams(vmem_limit_bytes=48 << 20),
        cost_estimate=pl.CostEstimate(
            flops=6 * count * width * hidden,
            transcendentals=2 * count * hidden,
            bytes_accessed=4 * (count * hidden + width * hidden) + 6 * count * width,
        ),
        name="feed_forward",
    )(normed, slope, expand, bias, reduce)


def swap(value, axis, distance):
    size = lax.axis_size(axis)
    return lax.ppermute(value, axis, [(i, i ^ distance) for i in range(size)])


def fence(*values):
    return lax.optimization_barrier(values)


def gather_near(rows_here):
    if lax.axis_size("fsdp") != 4:
        return (lax.all_gather(rows_here, "fsdp", axis=0, tiled=True),)
    return (rows_here, swap(rows_here, "fsdp", 1), swap(rows_here, "fsdp", 2))


def gather_far(held):
    if len(held) == 1:
        return held
    rows_here, near, side = held
    half = rows_here.shape[0] // 2
    return held + (swap(side[:half], "fsdp", 1), swap(near[half:], "fsdp", 2))


def place_near(held):
    if len(held) == 1:
        return held[0]
    rows_here, near, side = held[:3]
    me = lax.axis_index("fsdp")
    count, width = rows_here.shape
    out = jnp.zeros((4 * count, width), rows_here.dtype)
    out = lax.dynamic_update_slice(out, rows_here, (me * count, 0))
    out = lax.dynamic_update_slice(out, near, ((me ^ 1) * count, 0))
    return lax.dynamic_update_slice(out, side, ((me ^ 2) * count, 0))


def place_far(out, held):
    if len(held) == 1:
        return out
    far_top, far_low = held[3:]
    half = far_top.shape[0]
    start = (lax.axis_index("fsdp") ^ 3) * 2 * half
    out = lax.dynamic_update_slice(out, far_top, (start, 0))
    return lax.dynamic_update_slice(out, far_low, (start + half, 0))


def grad_block(left, right, distance):
    count = left.shape[1] // 4
    start = (lax.axis_index("fsdp") ^ distance) * count
    piece = lax.dynamic_slice_in_dim(left, start, count, 1)
    return product(piece, right, COLUMN_BY_COLUMN)


def sum_far(left, right):
    if lax.axis_size("fsdp") != 4:
        return ()
    far = grad_block(left, right, 3).astype(LOW)
    half = far.shape[0] // 2
    return (swap(far[:half], "fsdp", 1), swap(far[half:], "fsdp", 2))


def sum_near(left, right, far):
    if not far:
        whole = product(left, right, COLUMN_BY_COLUMN).astype(LOW)
        return (lax.psum_scatter(whole, "fsdp", scatter_dimension=0, tiled=True),)
    far_top, far_low = far
    half = far_top.shape[0]
    near = grad_block(left, right, 1)
    side = grad_block(left, right, 2)
    near = jnp.concatenate([near[:half], near[half:] + far_low.astype(FULL)], axis=0)
    side = jnp.concatenate([side[:half] + far_top.astype(FULL), side[half:]], axis=0)
    return (swap(near.astype(LOW), "fsdp", 1), swap(side.astype(LOW), "fsdp", 2))


def sum_own(left, right, near):
    if len(near) == 1:
        return near[0].astype(FULL)
    return grad_block(left, right, 0) + (near[0].astype(FULL) + near[1].astype(FULL))


def split_rows(value, bit, distance):
    half = value.shape[0] // 2
    keep = lax.dynamic_slice_in_dim(value, bit * half, half, 0)
    send = lax.dynamic_slice_in_dim(value, (1 - bit) * half, half, 0)
    return keep, swap(send.astype(LOW), "ctx", distance)


def both(pair):
    return pair[0].astype(FULL) + pair[1].astype(FULL)


def join_rows(value, bit, distance):
    other = swap(value, "ctx", distance)
    return jnp.where(
        bit == 0,
        jnp.concatenate([value, other], axis=0),
        jnp.concatenate([other, value], axis=0),
    )


def sum_pairwise(value, axis):
    near = value + swap(value, axis, 1)
    far = swap(value, axis, 2) + swap(value, axis, 3)
    return near + far


def swapped_if(bit, pair):
    return [jnp.where(bit == 0, pair[0], pair[1]), jnp.where(bit == 0, pair[1], pair[0])]


def per_device(
    tokens,
    clip_mask,
    cotangent,
    first_gain,
    first_shift,
    joint_weight,
    joint_bias,
    mixer_weight,
    mixer_bias,
    second_gain,
    second_shift,
    expand_weight,
    expand_bias,
    reduce_weight,
    reduce_bias,
):
    clips_here, rows_here, width = tokens.shape
    if lax.axis_size("ctx") != 4 or lax.axis_size("tp") != 2 or clips_here != 2:
        raise ValueError("mesh")
    shard = lax.axis_index("fsdp")
    block = lax.axis_index("ctx")
    core = lax.axis_index("tp")
    clip_at = block >> 1
    part_at = block & 1
    width_half = width // 2
    quarter = width_half // 2
    features = joint_weight.shape[2]
    part_width = features // 2
    pair_width = 2 * HEAD_DIM
    tokens_here = clips_here * rows_here

    expand_full = lax.all_gather(expand_weight, "fsdp", axis=0, tiled=True)
    inputs = tokens.astype(FULL)
    first_scaled, first_inverse = normalize(inputs)
    first_normed = (first_scaled * first_gain + first_shift).astype(LOW)
    mine = lax.dynamic_slice_in_dim(first_normed, core * width_half, width_half, 2)
    other_side = lax.dynamic_slice_in_dim(first_normed, (1 - core) * width_half, width_half, 2)
    own_clip = lax.dynamic_index_in_dim(mine, clip_at, 0, False)
    own_other = lax.dynamic_index_in_dim(other_side, clip_at, 0, False)
    other_clip = lax.dynamic_index_in_dim(mine, 1 - clip_at, 0, False)
    joint_part = lax.dynamic_slice_in_dim(joint_weight, part_at * part_width, part_width, 2)
    joint_part = jnp.concatenate([joint_part[:, kind] for kind in range(3)], axis=1)

    own_clip, left, right, joint_part = fence(
        own_clip, other_clip[:, :quarter], other_clip[:, quarter:], joint_part
    )
    near_rows = swap(own_clip, "ctx", 1)
    across_left = swap(left, "ctx", 2)
    far_right = swap(right, "ctx", 3)
    joint_held = gather_near(joint_part)

    near_rows, across_left, far_right, joint_held = fence(
        near_rows, across_left, far_right, joint_held
    )
    far_left = swap(across_left, "ctx", 1)
    across_right = swap(far_right, "ctx", 1)
    near_other = swap(near_rows, "tp", 1)
    joint_held = gather_far(joint_held)

    far_left, across_right, near_other, joint_held, mixer_weight = fence(
        far_left, across_right, near_other, joint_held, mixer_weight
    )
    cross_rows = jnp.concatenate(
        [
            jnp.concatenate([across_left, across_right], axis=1),
            jnp.concatenate([far_left, far_right], axis=1),
        ],
        axis=0,
    )
    cross_other = swap(cross_rows, "tp", 1)
    mixer_held = gather_near(mixer_weight)
    joint_rows = place_far(place_near(joint_held), joint_held)
    joint_full = jnp.concatenate(
        [
            lax.dynamic_slice_in_dim(joint_rows, core * width_half, width_half, 0),
            lax.dynamic_slice_in_dim(joint_rows, (1 - core) * width_half, width_half, 0),
        ],
        axis=0,
    )

    cross_other, mixer_held, joint_full, reduce_weight = fence(
        cross_other, mixer_held, joint_full, reduce_weight
    )
    mixer_held = gather_far(mixer_held)
    reduce_held = gather_near(reduce_weight)
    normed_mine = jnp.concatenate([own_clip, near_rows, cross_rows], axis=0)
    normed_other = jnp.concatenate([own_other, near_other, cross_other], axis=0)
    normed_clip = jnp.concatenate([normed_mine, normed_other], axis=1)
    bias_part = lax.dynamic_slice_in_dim(joint_bias, part_at * part_width, part_width, 1)
    bias_row = jnp.concatenate([bias_part[0], jnp.zeros_like(bias_part[0]), bias_part[1]])
    joint_out = (product(normed_clip, joint_full, PLAIN) + bias_row).astype(LOW)
    out_first, log_first = attention_forward(joint_out, 0)

    out_first, joint_out, mixer_held = fence(out_first, joint_out, mixer_held)
    first_blocks = out_first.reshape(4, rows_here, pair_width)
    arrived_first = [swap(first_blocks[d], "ctx", d) for d in (1, 2, 3)]
    out_second, log_second = attention_forward(joint_out, 1)

    out_second, arrived_first, reduce_held, expand_full = fence(
        out_second, arrived_first, reduce_held, expand_full
    )
    second_blocks = out_second.reshape(4, rows_here, pair_width)
    arrived_second = [swap(second_blocks[d], "ctx", d) for d in (1, 2, 3)]
    reduce_near = place_near(reduce_held)
    reduce_held = gather_far(reduce_held)
    mixer_full = place_far(place_near(mixer_held), mixer_held)

    arrived_second, reduce_held, reduce_near, mixer_full = fence(
        arrived_second, reduce_held, reduce_near, mixer_full
    )
    reduce_full = place_far(reduce_near, reduce_held)
    arrived = [jnp.concatenate([first_blocks[0], second_blocks[0]], axis=1)] + [
        jnp.concatenate([one, two], axis=1) for one, two in zip(arrived_first, arrived_second)
    ]
    own_joined = jnp.concatenate(swapped_if(part_at, arrived[:2]), axis=1)
    other_joined = jnp.concatenate(swapped_if(part_at, arrived[2:]), axis=1)
    mixed_in = jnp.concatenate(swapped_if(clip_at, [own_joined, other_joined]), axis=0)
    flat_inputs = inputs.reshape(tokens_here, width)
    valid = jnp.broadcast_to(
        clip_mask.astype(FULL)[:, None, None], (clips_here, rows_here, 1)
    ).reshape(tokens_here, 1)
    mixer_part = product(mixed_in, mixer_full, ROW_BY_ROW).astype(LOW)
    mixer_out = both((mixer_part, swap(mixer_part, "tp", 1))) + mixer_bias
    second_scaled, second_inverse = normalize(flat_inputs + mixer_out)
    second_normed = (second_scaled * second_gain + second_shift).astype(LOW)
    outer = cotangent.astype(FULL).reshape(tokens_here, width)
    branch_slope = outer * valid
    reduce_slope = branch_slope.astype(LOW)
    reduce_bias_grad = jnp.sum(reduce_slope.astype(FULL), axis=0)

    second_normed, reduce_slope, reduce_full = fence(second_normed, reduce_slope, reduce_full)
    activated, expand_slope, second_part, expand_bias_grad = feed_forward(
        second_normed, reduce_slope, expand_full, expand_bias[None], reduce_full
    )
    expand_bias_grad = expand_bias_grad[0]

    second_swapped = swap(second_part, "tp", 1)
    reduce_far = sum_far(reduce_slope, activated)
    second_slope = both((second_part, second_swapped))
    second_gain_grad = jnp.sum(second_slope * second_scaled, axis=0)
    second_shift_grad = jnp.sum(second_slope, axis=0)
    first_sum_back = norm_back(second_slope, second_gain, second_scaled, second_inverse)
    mixer_slope = (branch_slope + first_sum_back).astype(LOW)
    mixer_bias_grad = jnp.sum(mixer_slope.astype(FULL), axis=0)
    attended_slope = product(mixer_slope, mixer_full, PLAIN).astype(LOW)

    attended_slope, reduce_far, mixer_slope, expand_slope, mixed_in, activated = fence(
        attended_slope, reduce_far, mixer_slope, expand_slope, mixed_in, activated
    )
    leaving = []
    for piece in swapped_if(clip_at, [attended_slope[:rows_here], attended_slope[rows_here:]]):
        leaving += swapped_if(part_at, [piece[:, :part_width], piece[:, part_width:]])
    slope_first = [leaving[0][:, :pair_width]] + [
        swap(leaving[d][:, :pair_width], "ctx", d) for d in (1, 2, 3)
    ]
    reduce_near = sum_near(reduce_slope, activated, reduce_far)
    early_whole = jnp.concatenate(
        [
            product(second_normed, expand_slope, COLUMN_BY_COLUMN).astype(LOW),
            product(mixer_slope, mixed_in, COLUMN_BY_COLUMN).astype(LOW),
        ],
        axis=1,
    )

    slope_first, early_whole, leaving = fence(slope_first, early_whole, leaving)
    early_rows = lax.psum_scatter(early_whole, "fsdp", scatter_dimension=0, tiled=True)
    slope_second = [leaving[0][:, pair_width:]] + [
        swap(leaving[d][:, pair_width:], "ctx", d) for d in (1, 2, 3)
    ]
    grad_first = attention_backward(
        joint_out, jnp.concatenate(slope_first, axis=0), out_first, log_first, 0
    )

    grad_first, slope_second, reduce_near = fence(grad_first, slope_second, reduce_near)
    reduce_rows = split_rows(sum_own(reduce_slope, activated, reduce_near), part_at, 1)
    grad_second = attention_backward(
        joint_out, jnp.concatenate(slope_second, axis=0), out_second, log_second, 1
    )

    grad_second, reduce_rows = fence(grad_second, reduce_rows)
    reduce_rows = split_rows(both(reduce_rows), clip_at, 2)
    joint_slope = jnp.concatenate(
        [grad[kind] for kind in range(3) for grad in (grad_first, grad_second)], axis=1
    )
    first_there = product(joint_slope, joint_full[width_half:], ROW_BY_ROW).astype(LOW)
    first_here = product(joint_slope, joint_full[:width_half], ROW_BY_ROW).astype(LOW)
    first_half = both((first_here, swap(first_there, "tp", 1))).astype(LOW)

    first_half, reduce_rows, joint_slope, early_rows = fence(
        first_half, reduce_rows, joint_slope, early_rows
    )
    early_rows = lax.psum(early_rows, "ctx")
    pieces = first_half.reshape(4, rows_here, width_half)
    to_left = (pieces[2][:, :quarter], swap(pieces[3][:, :quarter], "ctx", 1))
    to_right = (pieces[3][:, quarter:], swap(pieces[2][:, quarter:], "ctx", 1))
    own_half = (pieces[0], swap(pieces[1], "ctx", 1))
    reduce_rows = both(reduce_rows).astype(LOW)
    normed_columns = jnp.concatenate(swapped_if(core, [normed_mine, normed_other]), axis=1)
    joint_far = sum_far(normed_columns, joint_slope)
    slope_sums = jnp.sum(joint_slope.astype(FULL), axis=0)
    bias_sums = jnp.stack([slope_sums[:part_width], slope_sums[2 * part_width :]])
    joint_bias_grad = lax.dynamic_update_slice(
        jnp.zeros((2, features), FULL), bias_sums, (0, part_at * part_width)
    )

    to_left, to_right, own_half, joint_far, activated = fence(
        to_left, to_right, own_half, joint_far, activated
    )
    other_half = jnp.concatenate(
        [
            swap(both(to_left).astype(LOW), "ctx", 2),
            swap(both(to_right).astype(LOW), "ctx", 3),
        ],
        axis=1,
    )
    joint_near = sum_near(normed_columns, joint_slope, joint_far)
    reduce_part = product(activated, reduce_full, ROW_BY_ROW).astype(LOW)
    reduce_swapped = swap(reduce_part, "tp", 1)

    other_half, joint_near, reduce_rows, reduce_part, reduce_swapped = fence(
        other_half, joint_near, reduce_rows, reduce_part, reduce_swapped
    )
    reduce_out = both((reduce_part, reduce_swapped)) + reduce_bias
    result = (flat_inputs + valid * (mixer_out + reduce_out)).astype(LOW)
    slope_half = jnp.concatenate(
        swapped_if(clip_at, [both(own_half).astype(LOW), other_half]), axis=0
    )
    slope_other = swap(slope_half, "tp", 1)
    first_slope = jnp.concatenate(swapped_if(core, [slope_half, slope_other]), axis=1)
    first_slope, early_rows = fence(first_slope, early_rows)
    first_slope = first_slope.astype(FULL)
    early_rows = early_rows.astype(FULL)
    expand_grad = early_rows[:, : expand_full.shape[1]]
    mixer_grad = early_rows[:, expand_full.shape[1] :]
    joint_sum = sum_own(normed_columns, joint_slope, joint_near).astype(LOW)
    joint_sum = both((joint_sum, swap(joint_sum, "ctx", 2))).astype(LOW)
    joint_parts = swapped_if(part_at, [joint_sum, swap(joint_sum, "ctx", 1)])
    joint_grad = jnp.concatenate(
        [piece.reshape(-1, 3, part_width) for piece in joint_parts], axis=2
    ).astype(FULL)
    reduce_grad = join_rows(join_rows(reduce_rows, clip_at, 2), part_at, 1).astype(FULL)

    flat_scaled = first_scaled.reshape(tokens_here, width)
    flat_inverse = first_inverse.reshape(tokens_here, 1)
    first_gain_grad = jnp.sum(first_slope * flat_scaled, axis=0)
    first_shift_grad = jnp.sum(first_slope, axis=0)
    tokens_grad = (
        outer + first_sum_back + norm_back(first_slope, first_gain, flat_scaled, flat_inverse)
    )

    vectors = [
        first_gain_grad,
        first_shift_grad,
        joint_bias_grad[0],
        joint_bias_grad[1],
        mixer_bias_grad,
        second_gain_grad,
        second_shift_grad,
        expand_bias_grad,
        reduce_bias_grad,
    ]
    packed = sum_pairwise(jnp.concatenate(vectors).reshape(-1, 128), "ctx")
    if lax.axis_size("fsdp") == 4:
        packed = sum_pairwise(packed, "fsdp")
    else:
        packed = lax.psum(packed, "fsdp")
    packed = packed.reshape(-1)
    shares = []
    start = 0
    for vector in vectors:
        share = vector.shape[0] // lax.axis_size("fsdp")
        shares.append(lax.dynamic_slice_in_dim(packed, start + shard * share, share, 0))
        start += vector.shape[0]

    shape = (clips_here, rows_here, width)
    return (
        result.reshape(shape),
        tokens_grad.reshape(shape),
        shares[0],
        shares[1],
        joint_grad,
        jnp.stack([shares[2], shares[3]]),
        mixer_grad,
        shares[4],
        shares[5],
        shares[6],
        expand_grad,
        shares[7],
        reduce_grad,
        shares[8],
    )


def solution(mesh):
    return jax.shard_map(
        per_device,
        mesh=mesh,
        in_specs=(
            P("fsdp", "ctx", None),
            P("fsdp"),
            P("fsdp", "ctx", None),
            P(),
            P(),
            P("fsdp", None, "tp"),
            P(None, "tp"),
            P("fsdp", "tp"),
            P(),
            P(),
            P(),
            P("fsdp", "tp"),
            P("tp"),
            P("fsdp", "tp"),
            P(),
        ),
        out_specs=(
            P("fsdp", "ctx", None),
            P("fsdp", "ctx", None),
            P("fsdp"),
            P("fsdp"),
            P("fsdp", None, "tp"),
            P(None, ("tp", "fsdp")),
            P("fsdp", "tp"),
            P("fsdp"),
            P("fsdp"),
            P("fsdp"),
            P("fsdp", "tp"),
            P(("tp", "fsdp")),
            P("fsdp", "tp"),
            P("fsdp"),
        ),
        check_vma=False,
    )
```

```python
import jax
import jax.numpy as jnp
from jax import lax
from jax.experimental import pallas as pl
from jax.experimental.pallas import tpu as pltpu
from jax.sharding import PartitionSpec as P

HEAD_DIM = 64
EPSILON = 1e-06
LOW = jnp.bfloat16
FULL = jnp.float32

ROW_BY_ROW = (((1,), (1,)), ((), ()))
PLAIN = (((1,), (0,)), ((), ()))
COLUMN_BY_COLUMN = (((0,), (0,)), ((), ()))


def product(left, right, dims):
    return lax.dot_general(left, right, dims, preferred_element_type=FULL)


def normalize(value_rows):
    center = value_rows - jnp.mean(value_rows, axis=-1, keepdims=True)
    inverse = lax.rsqrt(jnp.mean(center * center, axis=-1, keepdims=True) + EPSILON)
    return (center * inverse, inverse)


def norm_back(upstream, gain, scaled, inverse):
    weighted = upstream * gain
    return inverse * (
        weighted
        - jnp.mean(weighted, axis=-1, keepdims=True)
        - scaled * jnp.mean(weighted * scaled, axis=-1, keepdims=True)
    )


def row_chunk(count, most):
    for chunk in range(most, 0, -16):
        if count % chunk == 0:
            return chunk
    raise ValueError("rows")


def first_norm_kernel(tokens_ref, gain_ref, shift_ref, out_ref):
    scaled, _ = normalize(tokens_ref[...].astype(FULL))
    out_ref[...] = (scaled * gain_ref[...] + shift_ref[...]).astype(LOW)


def second_norm_kernel(tokens_ref, one_ref, two_ref, bias_ref, gain_ref, shift_ref, out_ref):
    mixed = one_ref[...].astype(FULL) + two_ref[...].astype(FULL) + bias_ref[...]
    scaled, _ = normalize(tokens_ref[...].astype(FULL) + mixed)
    out_ref[...] = (scaled * gain_ref[...] + shift_ref[...]).astype(LOW)


def add_sums(ref, rows):
    sums = jnp.concatenate([jnp.sum(row, axis=0, keepdims=True) for row in rows], axis=0)

    @pl.when(pl.program_id(0) == 0)
    def _():
        ref[: len(rows)] = sums

    @pl.when(pl.program_id(0) > 0)
    def _():
        ref[: len(rows)] += sums


def second_norm_back_kernel(
    tokens_ref, one_ref, two_ref, bias_ref, gain_ref, left_ref, right_ref, outer_ref,
    slope_ref, back_ref, sums_ref,
):
    mixed = one_ref[...].astype(FULL) + two_ref[...].astype(FULL) + bias_ref[...]
    scaled, inverse = normalize(tokens_ref[...].astype(FULL) + mixed)
    upstream = left_ref[...].astype(FULL) + right_ref[...].astype(FULL)
    back = norm_back(upstream, gain_ref[...], scaled, inverse)
    slope = (outer_ref[...].astype(FULL) + back).astype(LOW)
    slope_ref[...] = slope
    back_ref[...] = back
    add_sums(sums_ref, [upstream * scaled, upstream, slope.astype(FULL)])


def first_norm_back_kernel(
    tokens_ref, upstream_ref, gain_ref, outer_ref, back_ref, out_ref, sums_ref
):
    scaled, inverse = normalize(tokens_ref[...].astype(FULL))
    upstream = upstream_ref[...].astype(FULL)
    back = norm_back(upstream, gain_ref[...], scaled, inverse)
    out_ref[...] = outer_ref[...].astype(FULL) + back_ref[...] + back
    add_sums(sums_ref, [upstream * scaled, upstream])


def by_rows(kernel, name, out_types, sums, *values):
    count, width = values[0].shape
    chunk = row_chunk(count, 112)
    part = pl.BlockSpec((chunk, width), lambda i: (i, 0))
    in_specs = [
        part if value.shape[0] == count else pl.BlockSpec((1, width), lambda i: (0, 0))
        for value in values
    ]
    out_specs = [part for _ in out_types]
    out_shape = [jax.ShapeDtypeStruct((count, width), kind) for kind in out_types]
    if sums:
        out_specs.append(pl.BlockSpec((8, width), lambda i: (0, 0)))
        out_shape.append(jax.ShapeDtypeStruct((8, width), FULL))
    return pl.pallas_call(
        kernel,
        grid=(count // chunk,),
        in_specs=in_specs,
        out_specs=out_specs,
        out_shape=out_shape,
        compiler_params=pltpu.CompilerParams(vmem_limit_bytes=32 << 20),
        name=name,
    )(*values)


def joint_kernel(mine_ref, other_ref, weight_ref, bias_ref, out_ref):
    half = mine_ref.shape[1]
    out = product(mine_ref[...], weight_ref[:half], PLAIN)
    out += product(other_ref[...], weight_ref[half:], PLAIN)
    out_ref[...] = (out + bias_ref[...]).astype(LOW)


def joint_projection(mine, other, weight, bias):
    count, half = mine.shape
    columns = weight.shape[1]
    chunk = row_chunk(count, 784)
    part = pl.BlockSpec((chunk, half), lambda i: (i, 0))
    return pl.pallas_call(
        joint_kernel,
        grid=(count // chunk,),
        in_specs=[
            part,
            part,
            pl.BlockSpec(weight.shape, lambda i: (0, 0)),
            pl.BlockSpec((1, columns), lambda i: (0, 0)),
        ],
        out_specs=pl.BlockSpec((chunk, columns), lambda i: (i, 0)),
        out_shape=jax.ShapeDtypeStruct((count, columns), LOW),
        compiler_params=pltpu.CompilerParams(vmem_limit_bytes=40 << 20),
        name="joint_projection",
    )(mine, other, weight, bias)


def rows_kernel(left_ref, right_ref, out_ref):
    out_ref[...] = product(left_ref[...], right_ref[...], ROW_BY_ROW).astype(LOW)


def rows_product(left, right, name):
    count, depth = left.shape
    columns = right.shape[0]
    chunk = row_chunk(count, 400)
    return pl.pallas_call(
        rows_kernel,
        grid=(count // chunk,),
        in_specs=[
            pl.BlockSpec((chunk, depth), lambda i: (i, 0)),
            pl.BlockSpec((columns, depth), lambda i: (0, 0)),
        ],
        out_specs=pl.BlockSpec((chunk, columns), lambda i: (i, 0)),
        out_shape=jax.ShapeDtypeStruct((count, columns), LOW),
        compiler_params=pltpu.CompilerParams(vmem_limit_bytes=48 << 20),
        name=name,
    )(left, right)


def grad_kernel(distances, place_ref, *refs):
    lefts, (right_ref, out_ref, turned) = refs[:-3], refs[-3:]

    @pl.when(pl.program_id(1) == 0)
    def _():
        left = lefts[0][...]
        if len(lefts) == 2:
            slot = place_ref[0] ^ distance_at(distances, pl.program_id(0))
            left = jnp.where((slot >> 1) == 0, left, lefts[1][...])
        turned[...] = left.T

    out_ref[0] = product(turned[...], right_ref[...], PLAIN).astype(LOW)


def distance_at(distances, step):
    if len(distances) == 1:
        return distances[0]
    return distances[0] + step * (distances[1] - distances[0])


def grad_products(lefts, right, place, distances, name):
    tokens_here, columns = right.shape
    quarter = sum(left.shape[1] for left in lefts) // 4
    blocks = lefts[0].shape[1] // quarter
    width = 512 if columns % 512 == 0 else columns // 2 if columns % 256 == 0 else columns

    def left_at(i, j, place):
        return (0, (place[0] ^ distance_at(distances, i)) & (blocks - 1))

    return pl.pallas_call(
        lambda *refs: grad_kernel(distances, *refs),
        grid_spec=pltpu.PrefetchScalarGridSpec(
            num_scalar_prefetch=1,
            grid=(len(distances), columns // width),
            in_specs=[pl.BlockSpec((tokens_here, quarter), left_at) for _ in lefts]
            + [pl.BlockSpec((tokens_here, width), lambda i, j, place: (0, j))],
            out_specs=pl.BlockSpec((1, quarter, width), lambda i, j, place: (i, 0, j)),
            scratch_shapes=[pltpu.VMEM((quarter, tokens_here), LOW)],
        ),
        out_shape=jax.ShapeDtypeStruct((len(distances), quarter, columns), LOW),
        compiler_params=pltpu.CompilerParams(vmem_limit_bytes=48 << 20),
        name=name,
    )(place.astype(jnp.int32).reshape(1), *lefts, right)


def attention_forward_kernel(q_ref, k_ref, v_ref, o_ref, lse_ref):
    rows, width = q_ref.shape
    lane = lax.broadcasted_iota(jnp.int32, (rows, width), 1)
    lse = jnp.zeros((rows, width), FULL)
    q = q_ref[...] * jnp.asarray(HEAD_DIM ** (-0.5), LOW)
    k = k_ref[...]
    v = v_ref[...]
    out = None
    for head in range(width // HEAD_DIM):
        mask = (lane // HEAD_DIM) == head
        scores = product(jnp.where(mask, q, jnp.zeros_like(q)), k, ROW_BY_ROW)
        top = jnp.max(scores, axis=-1, keepdims=True)
        weights = jnp.exp(scores - top)
        total = jnp.sum(weights, axis=-1, keepdims=True)
        part = product(weights.astype(LOW), v, PLAIN) / total
        out = part if out is None else jnp.where(mask, part, out)
        lse = jnp.where(lane == head, top + jnp.log(total), lse)
    o_ref[...] = out.astype(LOW)
    lse_ref[0] = lse.T[: lse_ref.shape[1]]


def attention_forward(joint, pair):
    count, columns = joint.shape
    width = 2 * HEAD_DIM
    chunk = row_chunk(count, 256)
    steps = count // chunk
    kind = columns // (3 * width)
    whole_k = pl.BlockSpec((count, width), lambda i: (0, kind + pair))
    whole_v = pl.BlockSpec((count, width), lambda i: (0, 2 * kind + pair))
    out, lse = pl.pallas_call(
        attention_forward_kernel,
        grid=(steps,),
        in_specs=[pl.BlockSpec((chunk, width), lambda i: (i, pair)), whole_k, whole_v],
        out_specs=[
            pl.BlockSpec((chunk, width), lambda i: (i, 0)),
            pl.BlockSpec((1, 8, chunk), lambda i: (i, 0, 0)),
        ],
        out_shape=[
            jax.ShapeDtypeStruct((count, width), LOW),
            jax.ShapeDtypeStruct((steps, 8, chunk), FULL),
        ],
        compiler_params=pltpu.CompilerParams(vmem_limit_bytes=40 << 20),
        name="attention_forward",
    )(joint, joint, joint)
    return out, lse.transpose(1, 0, 2).reshape(8, count)


def attention_backward_kernel(
    q_ref, k_ref, v_ref, da_ref, o_ref, lse_ref, dq_ref, dk_ref, dv_ref,
    q_heads, da_heads, delta_ref, dq_total,
):
    count, width = q_ref.shape
    chunk = k_ref.shape[0]
    step = pl.program_id(0)
    heads = width // HEAD_DIM
    scale = jnp.asarray(HEAD_DIM ** (-0.5), LOW)

    @pl.when(step == 0)
    def _():
        lane = lax.broadcasted_iota(jnp.int32, (count, width), 1)
        delta = jnp.zeros((count, width), FULL)
        q = q_ref[...] * scale
        da = da_ref[...]
        both = da.astype(FULL) * o_ref[...].astype(FULL)
        for head in range(heads):
            mask = (lane // HEAD_DIM) == head
            q_heads[head] = jnp.where(mask, q, jnp.zeros_like(q))
            da_heads[head] = jnp.where(mask, da, jnp.zeros_like(da))
            row = jnp.sum(jnp.where(mask, both, 0.0), axis=-1, keepdims=True)
            delta = jnp.where(lane == head, row, delta)
        delta_ref[...] = delta.T[:8]
        dq_total[...] = jnp.zeros_like(dq_total)

    lane = lax.broadcasted_iota(jnp.int32, (chunk, width), 1)
    k = k_ref[...]
    v = v_ref[...]
    scaled_k = k * scale
    dk = dv = None
    for head in range(heads):
        q = q_heads[head]
        da = da_heads[head]
        probs = jnp.exp(product(k, q, ROW_BY_ROW) - lse_ref[head : head + 1, :])
        slope = probs * (product(v, da, ROW_BY_ROW) - delta_ref[head : head + 1, :])
        slope = slope.astype(LOW)
        dv_part = product(probs.astype(LOW), da, PLAIN)
        dk_part = product(slope, q, PLAIN)
        dv = dv_part if dv is None else dv + dv_part
        dk = dk_part if dk is None else dk + dk_part
        one_k = jnp.where((lane // HEAD_DIM) == head, scaled_k, jnp.zeros_like(k))
        dq_total[...] += product(slope, one_k, COLUMN_BY_COLUMN)
    dk_ref[...] = dk.astype(LOW)
    dv_ref[...] = dv.astype(LOW)

    @pl.when(step == pl.num_programs(0) - 1)
    def _():
        dq_ref[...] = dq_total[...].astype(LOW)


def attention_backward(joint, da, out, lse, pair):
    count, columns = joint.shape
    width = 2 * HEAD_DIM
    chunk = row_chunk(count, 256)
    kind = columns // (3 * width)
    part_k = pl.BlockSpec((chunk, width), lambda i: (i, kind + pair))
    part_v = pl.BlockSpec((chunk, width), lambda i: (i, 2 * kind + pair))
    whole = pl.BlockSpec((count, width), lambda i: (0, pair))
    alone = pl.BlockSpec((count, width), lambda i: (0, 0))
    part_out = pl.BlockSpec((chunk, width), lambda i: (i, 0))
    grad = jax.ShapeDtypeStruct((count, width), LOW)
    return pl.pallas_call(
        attention_backward_kernel,
        grid=(count // chunk,),
        in_specs=[whole, part_k, part_v, alone, alone, pl.BlockSpec((8, count), lambda i: (0, 0))],
        out_specs=[alone, part_out, part_out],
        out_shape=[grad, grad, grad],
        scratch_shapes=[
            pltpu.VMEM((2, count, width), LOW),
            pltpu.VMEM((2, count, width), LOW),
            pltpu.VMEM((8, count), FULL),
            pltpu.VMEM((count, width), FULL),
        ],
        compiler_params=pltpu.CompilerParams(vmem_limit_bytes=40 << 20),
        name="attention_backward",
    )(joint, joint, joint, da, out, lse)


def reduce_columns(place_ref, piece, rows):
    return pl.ds(pl.multiple_of(place_ref[piece], rows), rows)


def feed_forward_kernel(pieces, place_ref, normed_ref, slope_ref, expand_ref, bias_ref, *refs):
    reduce_refs = refs[:pieces]
    active_ref, expand_slope_ref, back_ref, bias_grad_ref, total = refs[pieces:]
    step = pl.program_id(0)
    count = normed_ref.shape[0]
    half = count // 2
    bias_grad = None
    for rows in (slice(0, half), slice(half, count)):
        hidden = product(normed_ref[rows], expand_ref[...], PLAIN) + bias_ref[...]
        upstream = None
        for piece, reduce_ref in enumerate(reduce_refs):
            columns = reduce_columns(place_ref, piece, reduce_ref.shape[0])
            part = product(slope_ref[rows, columns], reduce_ref[...], PLAIN)
            upstream = part if upstream is None else upstream + part
        share = 0.5 * (1.0 + lax.erf(hidden * (0.5**0.5)))
        active_ref[rows] = (hidden * share).astype(LOW)
        density = jnp.exp(-0.5 * hidden * hidden) * 0.3989422804014327
        slope = (upstream * (share + hidden * density)).astype(LOW)
        expand_slope_ref[rows] = slope
        part = jnp.sum(slope.astype(FULL), axis=0, keepdims=True)
        bias_grad = part if bias_grad is None else bias_grad + part
        back = product(slope, expand_ref[...], ROW_BY_ROW)

        @pl.when(step == 0)
        def _():
            total[rows] = back

        @pl.when(step > 0)
        def _():
            total[rows] += back

    bias_grad_ref[...] = bias_grad

    @pl.when(step == pl.num_programs(0) - 1)
    def _():
        back_ref[...] = total[...].astype(LOW)


def feed_forward(normed, slope, expand, bias, reduce, place):
    count, width = normed.shape
    hidden = expand.shape[1]
    block = 512 if hidden % 512 == 0 else hidden
    whole = pl.BlockSpec((count, width), lambda i, place: (0, 0))
    columns = pl.BlockSpec((width, block), lambda i, place: (0, i))
    out = pl.BlockSpec((count, block), lambda i, place: (0, i))
    row = pl.BlockSpec((1, block), lambda i, place: (0, i))
    return pl.pallas_call(
        lambda *refs: feed_forward_kernel(len(reduce), *refs),
        grid_spec=pltpu.PrefetchScalarGridSpec(
            num_scalar_prefetch=1,
            grid=(hidden // block,),
            in_specs=[whole, whole, columns, row]
            + [pl.BlockSpec((piece.shape[0], block), lambda i, place: (0, i)) for piece in reduce],
            out_specs=[out, out, whole, row],
            scratch_shapes=[pltpu.VMEM((count, width), FULL)],
        ),
        out_shape=[
            jax.ShapeDtypeStruct((count, hidden), LOW),
            jax.ShapeDtypeStruct((count, hidden), LOW),
            jax.ShapeDtypeStruct((count, width), LOW),
            jax.ShapeDtypeStruct((1, hidden), FULL),
        ],
        compiler_params=pltpu.CompilerParams(vmem_limit_bytes=48 << 20),
        name="feed_forward",
    )(place, normed, slope, expand, bias, *reduce)


def reduce_kernel(place_ref, active_ref, *refs):
    out_ref = refs[-1]
    for piece, reduce_ref in enumerate(refs[:-1]):
        columns = reduce_columns(place_ref, piece, reduce_ref.shape[0])
        out_ref[:, columns] = product(active_ref[...], reduce_ref[...], ROW_BY_ROW).astype(LOW)


def reduce_output(active, reduce, place):
    count, hidden = active.shape
    width = sum(piece.shape[0] for piece in reduce)
    chunk = row_chunk(count, 400)
    return pl.pallas_call(
        reduce_kernel,
        grid_spec=pltpu.PrefetchScalarGridSpec(
            num_scalar_prefetch=1,
            grid=(count // chunk,),
            in_specs=[pl.BlockSpec((chunk, hidden), lambda i, place: (i, 0))]
            + [pl.BlockSpec(piece.shape, lambda i, place: (0, 0)) for piece in reduce],
            out_specs=pl.BlockSpec((chunk, width), lambda i, place: (i, 0)),
        ),
        out_shape=jax.ShapeDtypeStruct((count, width), LOW),
        compiler_params=pltpu.CompilerParams(vmem_limit_bytes=48 << 20),
        name="reduce_output",
    )(place, active, *reduce)


def swap(value, axis, distance):
    size = lax.axis_size(axis)
    return lax.ppermute(value, axis, [(i, i ^ distance) for i in range(size)])


def fence(*values):
    return lax.optimization_barrier(values)


def gather_near(rows_here):
    if lax.axis_size("fsdp") != 4:
        return (lax.all_gather(rows_here, "fsdp", axis=0, tiled=True),)
    return (rows_here, swap(rows_here, "fsdp", 1), swap(rows_here, "fsdp", 2))


def gather_far(held):
    if len(held) == 1:
        return held
    rows_here, near, side = held
    half = rows_here.shape[0] // 2
    return held + (swap(side[:half], "fsdp", 1), swap(near[half:], "fsdp", 2))


def place_near(held):
    if len(held) == 1:
        return held[0]
    rows_here, near, side = held[:3]
    me = lax.axis_index("fsdp")
    count, width = rows_here.shape
    out = jnp.zeros((4 * count, width), rows_here.dtype)
    out = lax.dynamic_update_slice(out, rows_here, (me * count, 0))
    out = lax.dynamic_update_slice(out, near, ((me ^ 1) * count, 0))
    return lax.dynamic_update_slice(out, side, ((me ^ 2) * count, 0))


def place_far(out, held):
    if len(held) == 1:
        return out
    far_top, far_low = held[3:]
    half = far_top.shape[0]
    start = (lax.axis_index("fsdp") ^ 3) * 2 * half
    out = lax.dynamic_update_slice(out, far_top, (start, 0))
    return lax.dynamic_update_slice(out, far_low, (start + half, 0))


def far_halves(far):
    half = far.shape[0] // 2
    return (swap(far[:half], "fsdp", 1), swap(far[half:], "fsdp", 2))


def add_far(near, side, far):
    half = near.shape[0] // 2
    near = jnp.concatenate([near[:half], both((near[half:], far[1])).astype(LOW)], axis=0)
    side = jnp.concatenate([both((side[:half], far[0])).astype(LOW), side[half:]], axis=0)
    return (near, side)


def near_rows_out(pair):
    return (swap(pair[0], "fsdp", 1), swap(pair[1], "fsdp", 2))


def split_rows(value, bit, distance):
    half = value.shape[0] // 2
    keep = lax.dynamic_slice_in_dim(value, bit * half, half, 0)
    send = lax.dynamic_slice_in_dim(value, (1 - bit) * half, half, 0)
    return keep, swap(send.astype(LOW), "ctx", distance)


def both(pair):
    return pair[0].astype(FULL) + pair[1].astype(FULL)


def join_rows(value, bit, distance):
    other = swap(value, "ctx", distance)
    return jnp.where(
        bit == 0,
        jnp.concatenate([value, other], axis=0),
        jnp.concatenate([other, value], axis=0),
    )


def pairwise(pieces):
    return (pieces[0] + pieces[1]) + (pieces[2] + pieces[3])


def swapped_if(bit, pair):
    return [jnp.where(bit == 0, pair[0], pair[1]), jnp.where(bit == 0, pair[1], pair[0])]


def per_device(
    tokens,
    clip_mask,
    cotangent,
    first_gain,
    first_shift,
    joint_weight,
    joint_bias,
    mixer_weight,
    mixer_bias,
    second_gain,
    second_shift,
    expand_weight,
    expand_bias,
    reduce_weight,
    reduce_bias,
):
    clips_here, rows_here, width = tokens.shape
    if lax.axis_size("ctx") != 4 or lax.axis_size("tp") != 2 or clips_here != 2:
        raise ValueError("mesh")
    shard = lax.axis_index("fsdp")
    block = lax.axis_index("ctx")
    core = lax.axis_index("tp")
    clip_at = block >> 1
    part_at = block & 1
    width_half = width // 2
    quarter = width_half // 2
    features = joint_weight.shape[2]
    part_width = features // 2
    pair_width = 2 * HEAD_DIM
    tokens_here = clips_here * rows_here

    expand_full = lax.all_gather(expand_weight, "fsdp", axis=0, tiled=True)
    flat_tokens = tokens.reshape(tokens_here, width)
    (first_normed,) = by_rows(
        first_norm_kernel, "first_norm", [LOW], False,
        flat_tokens, first_gain[None], first_shift[None],
    )
    first_normed = first_normed.reshape(clips_here, rows_here, width)
    mine = lax.dynamic_slice_in_dim(first_normed, core * width_half, width_half, 2)
    other_side = lax.dynamic_slice_in_dim(first_normed, (1 - core) * width_half, width_half, 2)
    own_clip = lax.dynamic_index_in_dim(mine, clip_at, 0, False)
    own_other = lax.dynamic_index_in_dim(other_side, clip_at, 0, False)
    other_clip = lax.dynamic_index_in_dim(mine, 1 - clip_at, 0, False)
    joint_part = lax.dynamic_slice_in_dim(joint_weight, part_at * part_width, part_width, 2)
    both_parts = jnp.concatenate([joint_part[:, kind] for kind in range(3)] + [mixer_weight], axis=1)

    own_clip, left, right, both_parts = fence(
        own_clip, other_clip[:, :quarter], other_clip[:, quarter:], both_parts
    )
    near_rows = swap(own_clip, "ctx", 1)
    across_left = swap(left, "ctx", 2)
    far_right = swap(right, "ctx", 3)
    held = gather_near(both_parts)

    near_rows, across_left, far_right, held = fence(near_rows, across_left, far_right, held)
    passed = swap(jnp.concatenate([across_left, far_right], axis=1), "ctx", 1)
    near_other = swap(near_rows, "tp", 1)
    held = gather_far(held)

    passed, near_other, held = fence(passed, near_other, held)
    cross_rows = jnp.concatenate(
        [
            jnp.concatenate([across_left, passed[:, quarter:]], axis=1),
            jnp.concatenate([passed[:, :quarter], far_right], axis=1),
        ],
        axis=0,
    )
    cross_other = swap(cross_rows, "tp", 1)
    both_full = place_far(place_near(held), held)
    joint_columns = 3 * part_width
    joint_full = jnp.concatenate(
        [
            lax.dynamic_slice(both_full, (start * width_half, 0), (width_half, joint_columns))
            for start in (core, 1 - core)
        ],
        axis=0,
    )

    cross_other, joint_full, both_full, reduce_weight = fence(
        cross_other, joint_full, both_full, reduce_weight
    )
    mixer_full = both_full[:, joint_columns:]
    reduce_held = gather_near(reduce_weight)
    normed_mine = jnp.concatenate([own_clip, near_rows, cross_rows], axis=0)
    normed_other = jnp.concatenate([own_other, near_other, cross_other], axis=0)
    bias_part = lax.dynamic_slice_in_dim(joint_bias, part_at * part_width, part_width, 1)
    bias_row = jnp.concatenate([bias_part[0], jnp.zeros_like(bias_part[0]), bias_part[1]])
    joint_out = joint_projection(normed_mine, normed_other, joint_full, bias_row[None])
    out_first, log_first = attention_forward(joint_out, 0)

    out_first, joint_out, mixer_full = fence(out_first, joint_out, mixer_full)
    first_blocks = out_first.reshape(4, rows_here, pair_width)
    arrived_first = [swap(first_blocks[d], "ctx", d) for d in (1, 2, 3)]
    out_second, log_second = attention_forward(joint_out, 1)

    out_second, arrived_first, reduce_held, expand_full = fence(
        out_second, arrived_first, reduce_held, expand_full
    )
    second_blocks = out_second.reshape(4, rows_here, pair_width)
    arrived_second = [swap(second_blocks[d], "ctx", d) for d in (1, 2, 3)]
    reduce_held = gather_far(reduce_held)

    (arrived_second,) = fence(arrived_second)
    arrived = [jnp.concatenate([first_blocks[0], second_blocks[0]], axis=1)] + [
        jnp.concatenate([one, two], axis=1) for one, two in zip(arrived_first, arrived_second)
    ]
    own_joined = jnp.concatenate(swapped_if(part_at, arrived[:2]), axis=1)
    other_joined = jnp.concatenate(swapped_if(part_at, arrived[2:]), axis=1)
    mixed_in = jnp.concatenate(swapped_if(clip_at, [own_joined, other_joined]), axis=0)
    mixer_part = product(mixed_in, mixer_full, ROW_BY_ROW).astype(LOW)
    mixer_swapped = swap(mixer_part, "tp", 1)
    mixer_row = mixer_bias[None]
    (second_normed,) = by_rows(
        second_norm_kernel, "second_norm", [LOW], False,
        flat_tokens, mixer_part, mixer_swapped, mixer_row, second_gain[None], second_shift[None],
    )
    valid = clip_mask.astype(FULL)[:, None, None]
    reduce_slope = (cotangent.astype(FULL) * valid).astype(LOW).reshape(tokens_here, width)
    reduce_bias_grad = jnp.sum(reduce_slope.astype(FULL), axis=0)

    second_normed, reduce_slope, reduce_held = fence(second_normed, reduce_slope, reduce_held)
    four = lax.axis_size("fsdp") == 4
    start = jnp.zeros((), jnp.int32)
    if four:
        rows = width // 4
        reduce_at = jnp.stack([shard, shard ^ 1, shard ^ 2, shard ^ 3, shard ^ 3]) * rows
        reduce_at = (reduce_at + jnp.array([0, 0, 0, 0, rows // 2], jnp.int32)).astype(jnp.int32)
    else:
        reduce_at = start.reshape(1)
    activated, expand_slope, second_part, expand_bias_grad = feed_forward(
        second_normed, reduce_slope, expand_full, expand_bias[None], reduce_held, reduce_at
    )
    expand_bias_grad = expand_bias_grad[0]

    second_swapped = swap(second_part, "tp", 1)
    expand_whole = grad_products(
        [second_normed], expand_slope, start, (0, 1, 2, 3), "expand_grad"
    ).reshape(width, -1)
    expand_rows = lax.psum_scatter(expand_whole, "fsdp", scatter_dimension=0, tiled=True)
    mixer_slope, first_sum_back, second_sums = by_rows(
        second_norm_back_kernel, "second_norm_back", [LOW, FULL], True,
        flat_tokens, mixer_part, mixer_swapped, mixer_row, second_gain[None],
        second_part, second_swapped, reduce_slope,
    )
    attended_slope = product(mixer_slope, mixer_full, PLAIN).astype(LOW)

    attended_slope, mixer_slope, mixed_in, activated = fence(
        attended_slope, mixer_slope, mixed_in, activated
    )
    leaving = []
    for piece in swapped_if(clip_at, [attended_slope[:rows_here], attended_slope[rows_here:]]):
        leaving += swapped_if(part_at, [piece[:, :part_width], piece[:, part_width:]])
    slope_first = [leaving[0][:, :pair_width]] + [
        swap(leaving[d][:, :pair_width], "ctx", d) for d in (1, 2, 3)
    ]
    place, order = (shard, (3, 2, 1, 0)) if four else (start, (0, 1, 2, 3))
    reduce_parts = grad_products([reduce_slope], activated, place, order, "reduce_grad")
    mixer_parts = grad_products([mixer_slope], mixed_in, place, order, "mixer_grad")
    wide = jnp.concatenate([reduce_parts, mixer_parts], axis=2)

    slope_first, leaving, wide = fence(slope_first, leaving, wide)
    half = width // 8
    wide_far = far_halves(wide[0]) if four else ()
    slope_second = [leaving[0][:, pair_width:]] + [
        swap(leaving[d][:, pair_width:], "ctx", d) for d in (1, 2, 3)
    ]
    grad_first = attention_backward(
        joint_out, jnp.concatenate(slope_first, axis=0), out_first, log_first, 0
    )

    grad_first, slope_second, expand_rows, wide_far = fence(
        grad_first, slope_second, expand_rows, wide_far
    )
    wide_early, wide_late = (), ()
    if four:
        wide_late = (
            both((wide[2][half:], wide_far[1])).astype(LOW),
            both((wide[1][:half], wide_far[0])).astype(LOW),
        )
        wide_early = (wide[2][:half], wide[1][half:])
    expand_rows, slope_second, wide_early, wide_late = fence(
        expand_rows, slope_second, wide_early, wide_late
    )
    if four:
        wide_early = near_rows_out(wide_early)
    expand_rows = split_rows(expand_rows, part_at, 1)
    grad_second = attention_backward(
        joint_out, jnp.concatenate(slope_second, axis=0), out_second, log_second, 1
    )

    grad_second, expand_rows, wide_early, wide_late = fence(
        grad_second, expand_rows, wide_early, wide_late
    )
    expand_rows = split_rows(both(expand_rows), clip_at, 2)
    if four:
        wide_late = near_rows_out(wide_late)
    joint_slope = jnp.concatenate(
        [grad[kind] for kind in range(3) for grad in (grad_first, grad_second)], axis=1
    )
    first_there = product(joint_slope, joint_full[width_half:], ROW_BY_ROW).astype(LOW)
    first_here = rows_product(joint_slope, joint_full[:width_half], "first_slope")
    first_half = both((first_here, swap(first_there, "tp", 1))).astype(LOW)

    first_half, joint_slope, expand_rows, wide_late = fence(
        first_half, joint_slope, expand_rows, wide_late
    )
    expand_rows = both(expand_rows).astype(LOW)
    pieces = first_half.reshape(4, rows_here, width_half)
    passing = jnp.concatenate([pieces[1], pieces[3][:, :quarter], pieces[2][:, quarter:]], axis=1)
    passing = swap(passing, "ctx", 1)
    place = (shard if four else start) ^ (2 * core)
    joint_parts = grad_products([normed_mine, normed_other], joint_slope, place, order, "joint_grad")
    slope_sums = jnp.sum(joint_slope.astype(FULL), axis=0)
    bias_sums = jnp.stack([slope_sums[:part_width], slope_sums[2 * part_width :]])
    joint_bias_grad = lax.dynamic_update_slice(
        jnp.zeros((2, features), FULL), bias_sums, (0, part_at * part_width)
    )

    expand_rows = join_rows(expand_rows, clip_at, 2)

    passing, joint_parts, wide, expand_rows, activated = fence(
        passing, joint_parts, wide, expand_rows, activated
    )
    if four:
        wide_sum = jnp.concatenate(
            [both((wide_early[0], wide_late[1])), both((wide_late[0], wide_early[1]))], axis=0
        )
        wide_sum = wide[3].astype(FULL) + wide_sum
    else:
        wide_sum = lax.psum_scatter(
            wide.reshape(width, -1), "fsdp", scatter_dimension=0, tiled=True
        ).astype(FULL)
    wide_rows = split_rows(wide_sum, part_at, 1)
    joint_far = far_halves(joint_parts[0]) if four else ()
    own_half = both((pieces[0], passing[:, :width_half])).astype(LOW)
    to_left = both((pieces[2][:, :quarter], passing[:, width_half : width_half + quarter]))
    to_right = both((pieces[3][:, quarter:], passing[:, width_half + quarter :]))
    other_half = jnp.concatenate(
        [swap(to_left.astype(LOW), "ctx", 2), swap(to_right.astype(LOW), "ctx", 3)], axis=1
    )
    reduce_part = reduce_output(activated, reduce_held, reduce_at)

    other_half, joint_far, reduce_part, wide_rows = fence(
        other_half, joint_far, reduce_part, wide_rows
    )
    wide_rows = split_rows(both(wide_rows), clip_at, 2)
    slope_half = jnp.concatenate(
        swapped_if(clip_at, [own_half, other_half]), axis=0
    )
    slope_other = swap(slope_half, "tp", 1)
    first_slope = jnp.concatenate(swapped_if(core, [slope_half, slope_other]), axis=1)
    tokens_grad, first_sums = by_rows(
        first_norm_back_kernel, "first_norm_back", [FULL], True,
        flat_tokens, first_slope, first_gain[None],
        cotangent.reshape(tokens_here, width), first_sum_back,
    )
    reduce_swapped = swap(reduce_part, "tp", 1)
    if four:
        joint_near = near_rows_out(add_far(joint_parts[2], joint_parts[1], joint_far))
    else:
        joint_near = lax.psum_scatter(
            joint_parts.reshape(width, -1), "fsdp", scatter_dimension=0, tiled=True
        )

    first_sums, tokens_grad, joint_near, wide_rows, reduce_swapped = fence(
        first_sums, tokens_grad, joint_near, wide_rows, reduce_swapped
    )
    vectors = [
        first_sums[0],
        first_sums[1],
        joint_bias_grad[0],
        joint_bias_grad[1],
        second_sums[2],
        second_sums[0],
        second_sums[1],
        expand_bias_grad,
        reduce_bias_grad,
    ]
    packed = jnp.concatenate(vectors).reshape(-1, 128)
    packed_pieces = [packed] + [swap(packed, "ctx", d) for d in (1, 2, 3)]
    joint_sum = joint_parts[3].astype(FULL) + both(joint_near) if four else joint_near
    joint_sum = joint_sum.astype(LOW)
    joint_sum = (joint_sum, swap(joint_sum, "ctx", 2))
    wide_rows = join_rows(both(wide_rows).astype(LOW), clip_at, 2)
    reduce_out = both((reduce_part, reduce_swapped)) + reduce_bias
    mixer_out = both((mixer_part, mixer_swapped)) + mixer_bias
    branches = (mixer_out + reduce_out).reshape(clips_here, rows_here, width)
    result = (tokens.astype(FULL) + valid * branches).astype(LOW)

    packed_pieces, joint_sum, wide_rows, result = fence(
        packed_pieces, joint_sum, wide_rows, result
    )
    packed = pairwise(packed_pieces)
    if four:
        packed = pairwise([packed] + [swap(packed, "fsdp", d) for d in (1, 2, 3)])
    else:
        packed = lax.psum(packed, "fsdp")
    joint_sum = both(joint_sum).astype(LOW)
    joint_parts = swapped_if(part_at, [joint_sum, swap(joint_sum, "ctx", 1)])
    joint_grad = jnp.concatenate(
        [piece.reshape(-1, 3, part_width) for piece in joint_parts], axis=2
    ).astype(FULL)
    wide_rows = join_rows(wide_rows, part_at, 1).astype(FULL)
    reduce_grad = wide_rows[:, : activated.shape[1]]
    mixer_grad = wide_rows[:, activated.shape[1] :]
    expand_grad = join_rows(expand_rows, part_at, 1).astype(FULL)
    packed = packed.reshape(-1)
    shares = []
    start = 0
    for vector in vectors:
        share = vector.shape[0] // lax.axis_size("fsdp")
        shares.append(lax.dynamic_slice_in_dim(packed, start + shard * share, share, 0))
        start += vector.shape[0]

    shape = (clips_here, rows_here, width)
    return (
        result,
        tokens_grad.reshape(shape),
        shares[0],
        shares[1],
        joint_grad,
        jnp.stack([shares[2], shares[3]]),
        mixer_grad,
        shares[4],
        shares[5],
        shares[6],
        expand_grad,
        shares[7],
        reduce_grad,
        shares[8],
    )


def solution(mesh):
    return jax.shard_map(
        per_device,
        mesh=mesh,
        in_specs=(
            P("fsdp", "ctx", None),
            P("fsdp"),
            P("fsdp", "ctx", None),
            P(),
            P(),
            P("fsdp", None, "tp"),
            P(None, "tp"),
            P("fsdp", "tp"),
            P(),
            P(),
            P(),
            P("fsdp", "tp"),
            P("tp"),
            P("fsdp", "tp"),
            P(),
        ),
        out_specs=(
            P("fsdp", "ctx", None),
            P("fsdp", "ctx", None),
            P("fsdp"),
            P("fsdp"),
            P("fsdp", None, "tp"),
            P(None, ("tp", "fsdp")),
            P("fsdp", "tp"),
            P("fsdp"),
            P("fsdp"),
            P("fsdp"),
            P("fsdp", "tp"),
            P(("tp", "fsdp")),
            P("fsdp", "tp"),
            P("fsdp"),
        ),
        check_vma=False,
    )
```

```python
import jax
import jax.numpy as jnp
from jax import lax
from jax.experimental import pallas as pl
from jax.experimental.pallas import tpu as pltpu
from jax.sharding import PartitionSpec as P

HEAD_DIM = 64
EPSILON = 1e-06
LOW = jnp.bfloat16
FULL = jnp.float32

ROW_BY_ROW = (((1,), (1,)), ((), ()))
PLAIN = (((1,), (0,)), ((), ()))
COLUMN_BY_COLUMN = (((0,), (0,)), ((), ()))


def product(left, right, dims):
    return lax.dot_general(left, right, dims, preferred_element_type=FULL)


def normalize(value_rows):
    center = value_rows - jnp.mean(value_rows, axis=-1, keepdims=True)
    inverse = lax.rsqrt(jnp.mean(center * center, axis=-1, keepdims=True) + EPSILON)
    return (center * inverse, inverse)


def norm_back(upstream, gain, scaled, inverse):
    weighted = upstream * gain
    return inverse * (
        weighted
        - jnp.mean(weighted, axis=-1, keepdims=True)
        - scaled * jnp.mean(weighted * scaled, axis=-1, keepdims=True)
    )


def row_chunk(count, most):
    for chunk in range(most, 0, -16):
        if count % chunk == 0:
            return chunk
    raise ValueError("rows")


def first_norm_kernel(tokens_ref, gain_ref, shift_ref, out_ref):
    scaled, _ = normalize(tokens_ref[...].astype(FULL))
    out_ref[...] = (scaled * gain_ref[...] + shift_ref[...]).astype(LOW)


def second_norm_kernel(tokens_ref, one_ref, two_ref, bias_ref, gain_ref, shift_ref, out_ref):
    mixed = one_ref[...].astype(FULL) + two_ref[...].astype(FULL) + bias_ref[...]
    scaled, _ = normalize(tokens_ref[...].astype(FULL) + mixed)
    out_ref[...] = (scaled * gain_ref[...] + shift_ref[...]).astype(LOW)


def add_sums(ref, rows):
    sums = jnp.concatenate([jnp.sum(row, axis=0, keepdims=True) for row in rows], axis=0)

    @pl.when(pl.program_id(0) == 0)
    def _():
        ref[: len(rows)] = sums

    @pl.when(pl.program_id(0) > 0)
    def _():
        ref[: len(rows)] += sums


def second_norm_back_kernel(
    tokens_ref, one_ref, two_ref, bias_ref, gain_ref, left_ref, right_ref, outer_ref,
    slope_ref, back_ref, sums_ref,
):
    mixed = one_ref[...].astype(FULL) + two_ref[...].astype(FULL) + bias_ref[...]
    scaled, inverse = normalize(tokens_ref[...].astype(FULL) + mixed)
    upstream = left_ref[...].astype(FULL) + right_ref[...].astype(FULL)
    back = norm_back(upstream, gain_ref[...], scaled, inverse)
    slope = (outer_ref[...].astype(FULL) + back).astype(LOW)
    slope_ref[...] = slope
    back_ref[...] = back
    add_sums(sums_ref, [upstream * scaled, upstream, slope.astype(FULL)])


def first_norm_back_kernel(
    tokens_ref, upstream_ref, gain_ref, outer_ref, back_ref, out_ref, sums_ref
):
    scaled, inverse = normalize(tokens_ref[...].astype(FULL))
    upstream = upstream_ref[...].astype(FULL)
    back = norm_back(upstream, gain_ref[...], scaled, inverse)
    out_ref[...] = outer_ref[...].astype(FULL) + back_ref[...] + back
    add_sums(sums_ref, [upstream * scaled, upstream])


def by_rows(kernel, name, out_types, sums, *values):
    count, width = values[0].shape
    chunk = row_chunk(count, 112)
    part = pl.BlockSpec((chunk, width), lambda i: (i, 0))
    in_specs = [
        part if value.shape[0] == count else pl.BlockSpec((1, width), lambda i: (0, 0))
        for value in values
    ]
    out_specs = [part for _ in out_types]
    out_shape = [jax.ShapeDtypeStruct((count, width), kind) for kind in out_types]
    if sums:
        out_specs.append(pl.BlockSpec((8, width), lambda i: (0, 0)))
        out_shape.append(jax.ShapeDtypeStruct((8, width), FULL))
    return pl.pallas_call(
        kernel,
        grid=(count // chunk,),
        in_specs=in_specs,
        out_specs=out_specs,
        out_shape=out_shape,
        compiler_params=pltpu.CompilerParams(vmem_limit_bytes=16 << 20),
        name=name,
    )(*values)


def joint_kernel(mine_ref, other_ref, weight_ref, bias_ref, out_ref):
    half = mine_ref.shape[1]
    out = product(mine_ref[...], weight_ref[:half], PLAIN)
    out += product(other_ref[...], weight_ref[half:], PLAIN)
    out_ref[...] = (out + bias_ref[...]).astype(LOW)


def joint_projection(mine, other, weight, bias):
    count, half = mine.shape
    columns = weight.shape[1]
    chunk = row_chunk(count, 784)
    part = pl.BlockSpec((chunk, half), lambda i: (i, 0))
    return pl.pallas_call(
        joint_kernel,
        grid=(count // chunk,),
        in_specs=[
            part,
            part,
            pl.BlockSpec(weight.shape, lambda i: (0, 0)),
            pl.BlockSpec((1, columns), lambda i: (0, 0)),
        ],
        out_specs=pl.BlockSpec((chunk, columns), lambda i: (i, 0)),
        out_shape=jax.ShapeDtypeStruct((count, columns), LOW),
        compiler_params=pltpu.CompilerParams(vmem_limit_bytes=40 << 20),
        name="joint_projection",
    )(mine, other, weight, bias)


def rows_kernel(left_ref, right_ref, out_ref):
    out_ref[...] = product(left_ref[...], right_ref[...], ROW_BY_ROW).astype(LOW)


def rows_product(left, right, name):
    count, depth = left.shape
    columns = right.shape[0]
    chunk = row_chunk(count, 400)
    return pl.pallas_call(
        rows_kernel,
        grid=(count // chunk,),
        in_specs=[
            pl.BlockSpec((chunk, depth), lambda i: (i, 0)),
            pl.BlockSpec((columns, depth), lambda i: (0, 0)),
        ],
        out_specs=pl.BlockSpec((chunk, columns), lambda i: (i, 0)),
        out_shape=jax.ShapeDtypeStruct((count, columns), LOW),
        compiler_params=pltpu.CompilerParams(vmem_limit_bytes=48 << 20),
        name=name,
    )(left, right)


def grad_kernel(distances, place_ref, *refs):
    lefts, (right_ref, out_ref) = refs[:-2], refs[-2:]
    left = lefts[0][...]
    if len(lefts) == 2:
        slot = place_ref[0] ^ distance_at(distances, pl.program_id(0))
        left = jnp.where((slot >> 1) == 0, left, lefts[1][...])
    out_ref[0] = product(left, right_ref[...], COLUMN_BY_COLUMN).astype(LOW)


def distance_at(distances, step):
    if len(distances) == 1:
        return distances[0]
    return distances[0] + step * (distances[1] - distances[0])


def grad_products(lefts, right, place, distances, name):
    tokens_here, columns = right.shape
    quarter = sum(left.shape[1] for left in lefts) // 4
    blocks = lefts[0].shape[1] // quarter

    def left_at(i, place):
        return (0, (place[0] ^ distance_at(distances, i)) & (blocks - 1))

    return pl.pallas_call(
        lambda *refs: grad_kernel(distances, *refs),
        grid_spec=pltpu.PrefetchScalarGridSpec(
            num_scalar_prefetch=1,
            grid=(len(distances),),
            in_specs=[pl.BlockSpec((tokens_here, quarter), left_at) for _ in lefts]
            + [pl.BlockSpec((tokens_here, columns), lambda i, place: (0, 0))],
            out_specs=pl.BlockSpec((1, quarter, columns), lambda i, place: (i, 0, 0)),
        ),
        out_shape=jax.ShapeDtypeStruct((len(distances), quarter, columns), LOW),
        compiler_params=pltpu.CompilerParams(vmem_limit_bytes=48 << 20),
        name=name,
    )(place.astype(jnp.int32).reshape(1), *lefts, right)


def attention_forward_kernel(q_ref, k_ref, v_ref, o_ref, lse_ref):
    rows, width = q_ref.shape
    lane = lax.broadcasted_iota(jnp.int32, (rows, width), 1)
    lse = jnp.zeros((rows, width), FULL)
    q = q_ref[...] * jnp.asarray(HEAD_DIM ** (-0.5), LOW)
    k = k_ref[...]
    v = v_ref[...]
    out = None
    for head in range(width // HEAD_DIM):
        mask = (lane // HEAD_DIM) == head
        scores = product(jnp.where(mask, q, jnp.zeros_like(q)), k, ROW_BY_ROW)
        top = jnp.max(scores, axis=-1, keepdims=True)
        weights = jnp.exp(scores - top)
        total = jnp.sum(weights, axis=-1, keepdims=True)
        part = product(weights.astype(LOW), v, PLAIN) / total
        out = part if out is None else jnp.where(mask, part, out)
        lse = jnp.where(lane == head, top + jnp.log(total), lse)
    o_ref[...] = out.astype(LOW)
    lse_ref[0] = lse.T[: lse_ref.shape[1]]


def attention_forward(joint, pair):
    count, columns = joint.shape
    width = 2 * HEAD_DIM
    chunk = row_chunk(count, 256)
    steps = count // chunk
    kind = columns // (3 * width)
    whole_k = pl.BlockSpec((count, width), lambda i: (0, kind + pair))
    whole_v = pl.BlockSpec((count, width), lambda i: (0, 2 * kind + pair))
    out, lse = pl.pallas_call(
        attention_forward_kernel,
        grid=(steps,),
        in_specs=[pl.BlockSpec((chunk, width), lambda i: (i, pair)), whole_k, whole_v],
        out_specs=[
            pl.BlockSpec((chunk, width), lambda i: (i, 0)),
            pl.BlockSpec((1, 8, chunk), lambda i: (i, 0, 0)),
        ],
        out_shape=[
            jax.ShapeDtypeStruct((count, width), LOW),
            jax.ShapeDtypeStruct((steps, 8, chunk), FULL),
        ],
        compiler_params=pltpu.CompilerParams(vmem_limit_bytes=40 << 20),
        name="attention_forward",
    )(joint, joint, joint)
    return out, lse.transpose(1, 0, 2).reshape(8, count)


def attention_backward_kernel(
    q_ref, k_ref, v_ref, da_ref, o_ref, lse_ref, dq_ref, dk_ref, dv_ref,
    q_heads, da_heads, delta_ref, dq_total,
):
    count, width = q_ref.shape
    chunk = k_ref.shape[0]
    step = pl.program_id(0)
    heads = width // HEAD_DIM
    scale = jnp.asarray(HEAD_DIM ** (-0.5), LOW)

    @pl.when(step == 0)
    def _():
        lane = lax.broadcasted_iota(jnp.int32, (count, width), 1)
        delta = jnp.zeros((count, width), FULL)
        q = q_ref[...] * scale
        da = da_ref[...]
        both = da.astype(FULL) * o_ref[...].astype(FULL)
        for head in range(heads):
            mask = (lane // HEAD_DIM) == head
            q_heads[head] = jnp.where(mask, q, jnp.zeros_like(q))
            da_heads[head] = jnp.where(mask, da, jnp.zeros_like(da))
            row = jnp.sum(jnp.where(mask, both, 0.0), axis=-1, keepdims=True)
            delta = jnp.where(lane == head, row, delta)
        delta_ref[...] = delta.T[:8]
        dq_total[...] = jnp.zeros_like(dq_total)

    lane = lax.broadcasted_iota(jnp.int32, (chunk, width), 1)
    k = k_ref[...]
    v = v_ref[...]
    scaled_k = k * scale
    dk = dv = None
    for head in range(heads):
        q = q_heads[head]
        da = da_heads[head]
        probs = jnp.exp(product(k, q, ROW_BY_ROW) - lse_ref[head : head + 1, :])
        slope = probs * (product(v, da, ROW_BY_ROW) - delta_ref[head : head + 1, :])
        slope = slope.astype(LOW)
        dv_part = product(probs.astype(LOW), da, PLAIN)
        dk_part = product(slope, q, PLAIN)
        dv = dv_part if dv is None else dv + dv_part
        dk = dk_part if dk is None else dk + dk_part
        one_k = jnp.where((lane // HEAD_DIM) == head, scaled_k, jnp.zeros_like(k))
        dq_total[...] += product(slope, one_k, COLUMN_BY_COLUMN)
    dk_ref[...] = dk.astype(LOW)
    dv_ref[...] = dv.astype(LOW)

    @pl.when(step == pl.num_programs(0) - 1)
    def _():
        dq_ref[...] = dq_total[...].astype(LOW)


def attention_backward(joint, da, out, lse, pair):
    count, columns = joint.shape
    width = 2 * HEAD_DIM
    chunk = row_chunk(count, 256)
    kind = columns // (3 * width)
    part_k = pl.BlockSpec((chunk, width), lambda i: (i, kind + pair))
    part_v = pl.BlockSpec((chunk, width), lambda i: (i, 2 * kind + pair))
    whole = pl.BlockSpec((count, width), lambda i: (0, pair))
    alone = pl.BlockSpec((count, width), lambda i: (0, 0))
    part_out = pl.BlockSpec((chunk, width), lambda i: (i, 0))
    grad = jax.ShapeDtypeStruct((count, width), LOW)
    return pl.pallas_call(
        attention_backward_kernel,
        grid=(count // chunk,),
        in_specs=[whole, part_k, part_v, alone, alone, pl.BlockSpec((8, count), lambda i: (0, 0))],
        out_specs=[alone, part_out, part_out],
        out_shape=[grad, grad, grad],
        scratch_shapes=[
            pltpu.VMEM((2, count, width), LOW),
            pltpu.VMEM((2, count, width), LOW),
            pltpu.VMEM((8, count), FULL),
            pltpu.VMEM((count, width), FULL),
        ],
        compiler_params=pltpu.CompilerParams(vmem_limit_bytes=40 << 20),
        name="attention_backward",
    )(joint, joint, joint, da, out, lse)


def columns_of(place_ref, piece, rows):
    return pl.ds(pl.multiple_of(place_ref[piece], rows), rows)


def feed_forward_kernel(pieces, place_ref, normed_ref, slope_ref, bias_ref, *refs):
    expand_refs, reduce_refs = refs[:pieces], refs[pieces : 2 * pieces]
    active_ref, expand_slope_ref, back_ref, bias_grad_ref, total = refs[2 * pieces :]
    step = pl.program_id(0)
    count = normed_ref.shape[0]
    half = count // 2
    bias_grad = None
    for rows in (slice(0, half), slice(half, count)):
        hidden = bias_ref[...]
        upstream = None
        for piece in range(pieces):
            columns = columns_of(place_ref, piece, expand_refs[piece].shape[0])
            hidden = hidden + product(normed_ref[rows, columns], expand_refs[piece][...], PLAIN)
            part = product(slope_ref[rows, columns], reduce_refs[piece][...], PLAIN)
            upstream = part if upstream is None else upstream + part
        share = 0.5 * (1.0 + lax.erf(hidden * (0.5**0.5)))
        active_ref[rows] = (hidden * share).astype(LOW)
        density = jnp.exp(-0.5 * hidden * hidden) * 0.3989422804014327
        slope = (upstream * (share + hidden * density)).astype(LOW)
        expand_slope_ref[rows] = slope
        part = jnp.sum(slope.astype(FULL), axis=0, keepdims=True)
        bias_grad = part if bias_grad is None else bias_grad + part
        start = 0
        for piece in range(pieces):
            columns = slice(start, start + expand_refs[piece].shape[0])
            start = columns.stop
            back = product(slope, expand_refs[piece][...], ROW_BY_ROW)

            @pl.when(step == 0)
            def _():
                total[rows, columns] = back

            @pl.when(step > 0)
            def _():
                total[rows, columns] += back

    bias_grad_ref[...] = bias_grad

    @pl.when(step == pl.num_programs(0) - 1)
    def _():
        start = 0
        for piece in range(pieces):
            size = expand_refs[piece].shape[0]
            part = total[:, start : start + size].astype(LOW)
            back_ref[:, columns_of(place_ref, piece, size)] = part
            start += size


def feed_forward(normed, slope, bias, expand, reduce, place):
    count, width = normed.shape
    hidden = bias.shape[1]
    block = 512 if hidden % 512 == 0 else hidden
    whole = pl.BlockSpec((count, width), lambda i, place: (0, 0))
    out = pl.BlockSpec((count, block), lambda i, place: (0, i))
    row = pl.BlockSpec((1, block), lambda i, place: (0, i))
    return pl.pallas_call(
        lambda *refs: feed_forward_kernel(len(reduce), *refs),
        grid_spec=pltpu.PrefetchScalarGridSpec(
            num_scalar_prefetch=1,
            grid=(hidden // block,),
            in_specs=[whole, whole, row]
            + [
                pl.BlockSpec((piece.shape[0], block), lambda i, place: (0, i))
                for piece in [*expand, *reduce]
            ],
            out_specs=[out, out, whole, row],
            scratch_shapes=[pltpu.VMEM((count, width), FULL)],
        ),
        out_shape=[
            jax.ShapeDtypeStruct((count, hidden), LOW),
            jax.ShapeDtypeStruct((count, hidden), LOW),
            jax.ShapeDtypeStruct((count, width), LOW),
            jax.ShapeDtypeStruct((1, hidden), FULL),
        ],
        compiler_params=pltpu.CompilerParams(vmem_limit_bytes=40 << 20),
        name="feed_forward",
    )(place, normed, slope, bias, *expand, *reduce)


def reduce_kernel(place_ref, active_ref, *refs):
    reduce_refs, (out_ref, total) = refs[:-2], refs[-2:]
    start = 0
    for reduce_ref in reduce_refs:
        columns = slice(start, start + reduce_ref.shape[0])
        start = columns.stop
        part = product(active_ref[...], reduce_ref[...], ROW_BY_ROW)

        @pl.when(pl.program_id(0) == 0)
        def _():
            total[:, columns] = part

        @pl.when(pl.program_id(0) > 0)
        def _():
            total[:, columns] += part

    @pl.when(pl.program_id(0) == pl.num_programs(0) - 1)
    def _():
        start = 0
        for piece, reduce_ref in enumerate(reduce_refs):
            size = reduce_ref.shape[0]
            part = total[:, start : start + size].astype(LOW)
            out_ref[:, columns_of(place_ref, piece, size)] = part
            start += size


def reduce_output(active, reduce, place):
    count, hidden = active.shape
    width = sum(piece.shape[0] for piece in reduce)
    block = 512 if hidden % 512 == 0 else hidden
    return pl.pallas_call(
        reduce_kernel,
        grid_spec=pltpu.PrefetchScalarGridSpec(
            num_scalar_prefetch=1,
            grid=(hidden // block,),
            in_specs=[pl.BlockSpec((count, block), lambda i, place: (0, i))]
            + [
                pl.BlockSpec((piece.shape[0], block), lambda i, place: (0, i)) for piece in reduce
            ],
            out_specs=pl.BlockSpec((count, width), lambda i, place: (0, 0)),
            scratch_shapes=[pltpu.VMEM((count, width), FULL)],
        ),
        out_shape=jax.ShapeDtypeStruct((count, width), LOW),
        compiler_params=pltpu.CompilerParams(vmem_limit_bytes=32 << 20),
        name="reduce_output",
    )(place, active, *reduce)


def swap(value, axis, distance):
    size = lax.axis_size(axis)
    return lax.ppermute(value, axis, [(i, i ^ distance) for i in range(size)])


def fence(*values):
    return lax.optimization_barrier(values)


def gather_near(rows_here):
    if lax.axis_size("fsdp") != 4:
        return (lax.all_gather(rows_here, "fsdp", axis=0, tiled=True),)
    return (rows_here, swap(rows_here, "fsdp", 1), swap(rows_here, "fsdp", 2))


def gather_far(held):
    if len(held) == 1:
        return held
    rows_here, near, side = held
    half = rows_here.shape[0] // 2
    return held + (swap(side[:half], "fsdp", 1), swap(near[half:], "fsdp", 2))


def with_far(held):
    return held if len(held) == 1 else held[:3] + (jnp.concatenate(held[3:], axis=0),)


def place_near(held):
    if len(held) == 1:
        return held[0]
    rows_here, near, side = held[:3]
    me = lax.axis_index("fsdp")
    count, width = rows_here.shape
    out = jnp.zeros((4 * count, width), rows_here.dtype)
    out = lax.dynamic_update_slice(out, rows_here, (me * count, 0))
    out = lax.dynamic_update_slice(out, near, ((me ^ 1) * count, 0))
    return lax.dynamic_update_slice(out, side, ((me ^ 2) * count, 0))


def place_far(out, held):
    if len(held) == 1:
        return out
    far_top, far_low = held[3:]
    half = far_top.shape[0]
    start = (lax.axis_index("fsdp") ^ 3) * 2 * half
    out = lax.dynamic_update_slice(out, far_top, (start, 0))
    return lax.dynamic_update_slice(out, far_low, (start + half, 0))


def far_halves(far):
    half = far.shape[0] // 2
    return (swap(far[:half], "fsdp", 1), swap(far[half:], "fsdp", 2))


def add_far(near, side, far):
    half = near.shape[0] // 2
    near = jnp.concatenate([near[:half], both((near[half:], far[1])).astype(LOW)], axis=0)
    side = jnp.concatenate([both((side[:half], far[0])).astype(LOW), side[half:]], axis=0)
    return (near, side)


def near_rows_out(pair):
    return (swap(pair[0], "fsdp", 1), swap(pair[1], "fsdp", 2))


def halves(value, bit):
    half = value.shape[0] // 2
    keep = lax.dynamic_slice_in_dim(value, bit * half, half, 0)
    send = lax.dynamic_slice_in_dim(value, (1 - bit) * half, half, 0)
    return keep, send.astype(LOW)


def split_rows(value, bit, distance):
    keep, send = halves(value, bit)
    return keep, swap(send, "ctx", distance)


def both(pair):
    return pair[0].astype(FULL) + pair[1].astype(FULL)


def join_rows(value, bit, distance):
    other = swap(value, "ctx", distance)
    return jnp.where(
        bit == 0,
        jnp.concatenate([value, other], axis=0),
        jnp.concatenate([other, value], axis=0),
    )


def pairwise(pieces):
    return (pieces[0] + pieces[1]) + (pieces[2] + pieces[3])


def swapped_if(bit, pair):
    return [jnp.where(bit == 0, pair[0], pair[1]), jnp.where(bit == 0, pair[1], pair[0])]


def per_device(
    tokens,
    clip_mask,
    cotangent,
    first_gain,
    first_shift,
    joint_weight,
    joint_bias,
    mixer_weight,
    mixer_bias,
    second_gain,
    second_shift,
    expand_weight,
    expand_bias,
    reduce_weight,
    reduce_bias,
):
    clips_here, rows_here, width = tokens.shape
    if lax.axis_size("ctx") != 4 or lax.axis_size("tp") != 2 or clips_here != 2:
        raise ValueError("mesh")
    shard = lax.axis_index("fsdp")
    block = lax.axis_index("ctx")
    core = lax.axis_index("tp")
    clip_at = block >> 1
    part_at = block & 1
    width_half = width // 2
    quarter = width_half // 2
    features = joint_weight.shape[2]
    part_width = features // 2
    pair_width = 2 * HEAD_DIM
    tokens_here = clips_here * rows_here

    flat_tokens = tokens.reshape(tokens_here, width)
    (first_normed,) = by_rows(
        first_norm_kernel, "first_norm", [LOW], False,
        flat_tokens, first_gain[None], first_shift[None],
    )
    first_normed = first_normed.reshape(clips_here, rows_here, width)
    mine = lax.dynamic_slice_in_dim(first_normed, core * width_half, width_half, 2)
    other_side = lax.dynamic_slice_in_dim(first_normed, (1 - core) * width_half, width_half, 2)
    own_clip = lax.dynamic_index_in_dim(mine, clip_at, 0, False)
    own_other = lax.dynamic_index_in_dim(other_side, clip_at, 0, False)
    other_clip = lax.dynamic_index_in_dim(mine, 1 - clip_at, 0, False)
    joint_part = lax.dynamic_slice_in_dim(joint_weight, part_at * part_width, part_width, 2)
    both_parts = jnp.concatenate([joint_part[:, kind] for kind in range(3)] + [mixer_weight], axis=1)

    own_clip, left, right, both_parts = fence(
        own_clip, other_clip[:, :quarter], other_clip[:, quarter:], both_parts
    )
    near_rows = swap(own_clip, "ctx", 1)
    across_left = swap(left, "ctx", 2)
    far_right = swap(right, "ctx", 3)
    held = gather_near(both_parts)

    near_rows, across_left, far_right, held, expand_weight = fence(
        near_rows, across_left, far_right, held, expand_weight
    )
    passed = swap(jnp.concatenate([across_left, far_right], axis=1), "ctx", 1)
    held = gather_far(held)
    expand_held = gather_near(expand_weight)

    passed, held = fence(passed, held)
    cross_rows = jnp.concatenate(
        [
            near_rows,
            jnp.concatenate([across_left, passed[:, quarter:]], axis=1),
            jnp.concatenate([passed[:, :quarter], far_right], axis=1),
        ],
        axis=0,
    )
    cross_other = swap(cross_rows, "tp", 1)
    both_full = place_far(place_near(held), held)
    joint_columns = 3 * part_width
    joint_full = jnp.concatenate(
        [
            lax.dynamic_slice(both_full, (start * width_half, 0), (width_half, joint_columns))
            for start in (core, 1 - core)
        ],
        axis=0,
    )

    cross_other, joint_full, both_full, reduce_weight = fence(
        cross_other, joint_full, both_full, reduce_weight
    )
    mixer_full = both_full[:, joint_columns:]
    reduce_held = gather_near(reduce_weight)
    normed_mine = jnp.concatenate([own_clip, cross_rows], axis=0)
    normed_other = jnp.concatenate([own_other, cross_other], axis=0)
    bias_part = lax.dynamic_slice_in_dim(joint_bias, part_at * part_width, part_width, 1)
    bias_row = jnp.concatenate([bias_part[0], jnp.zeros_like(bias_part[0]), bias_part[1]])
    joint_out = joint_projection(normed_mine, normed_other, joint_full, bias_row[None])
    out_first, log_first = attention_forward(joint_out, 0)

    out_first, joint_out, mixer_full, expand_held = fence(
        out_first, joint_out, mixer_full, expand_held
    )
    first_blocks = out_first.reshape(4, rows_here, pair_width)
    arrived_first = [swap(first_blocks[d], "ctx", d) for d in (1, 2, 3)]
    out_second, log_second = attention_forward(joint_out, 1)

    out_second, arrived_first, reduce_held, expand_held = fence(
        out_second, arrived_first, reduce_held, expand_held
    )
    second_blocks = out_second.reshape(4, rows_here, pair_width)
    arrived_second = [swap(second_blocks[d], "ctx", d) for d in (1, 2, 3)]
    expand_held = gather_far(expand_held)

    arrived_second, expand_held, reduce_held = fence(arrived_second, expand_held, reduce_held)
    expand_held = with_far(expand_held)
    reduce_held = gather_far(reduce_held)
    arrived = [jnp.concatenate([first_blocks[0], second_blocks[0]], axis=1)] + [
        jnp.concatenate([one, two], axis=1) for one, two in zip(arrived_first, arrived_second)
    ]
    own_joined = jnp.concatenate(swapped_if(part_at, arrived[:2]), axis=1)
    other_joined = jnp.concatenate(swapped_if(part_at, arrived[2:]), axis=1)
    mixed_in = jnp.concatenate(swapped_if(clip_at, [own_joined, other_joined]), axis=0)
    mixer_part = product(mixed_in, mixer_full, ROW_BY_ROW).astype(LOW)
    mixer_swapped = swap(mixer_part, "tp", 1)
    mixer_row = mixer_bias[None]
    (second_normed,) = by_rows(
        second_norm_kernel, "second_norm", [LOW], False,
        flat_tokens, mixer_part, mixer_swapped, mixer_row, second_gain[None], second_shift[None],
    )
    valid = clip_mask.astype(FULL)[:, None, None]
    reduce_slope = (cotangent.astype(FULL) * valid).astype(LOW).reshape(tokens_here, width)
    reduce_bias_grad = jnp.sum(reduce_slope.astype(FULL), axis=0)

    second_normed, reduce_slope, reduce_held = fence(second_normed, reduce_slope, reduce_held)
    four = lax.axis_size("fsdp") == 4
    start = jnp.zeros((), jnp.int32)
    reduce_held = with_far(reduce_held)
    if four:
        pieces_at = jnp.stack([shard, shard ^ 1, shard ^ 2, shard ^ 3]).astype(jnp.int32)
        pieces_at = pieces_at * (width // 4)
    else:
        pieces_at = start.reshape(1)
    activated, expand_slope, second_part, expand_bias_grad = feed_forward(
        second_normed, reduce_slope, expand_bias[None], expand_held, reduce_held, pieces_at
    )
    expand_bias_grad = expand_bias_grad[0]

    second_swapped = swap(second_part, "tp", 1)
    place, order = (shard, (3, 2, 1, 0)) if four else (start, (0, 1, 2, 3))
    expand_parts = grad_products([second_normed], expand_slope, place, order, "expand_grad")
    second_swapped, expand_parts = fence(second_swapped, expand_parts)
    expand_far = far_halves(expand_parts[0]) if four else ()
    mixer_slope, first_sum_back, second_sums = by_rows(
        second_norm_back_kernel, "second_norm_back", [LOW, FULL], True,
        flat_tokens, mixer_part, mixer_swapped, mixer_row, second_gain[None],
        second_part, second_swapped, reduce_slope,
    )
    attended_slope = product(mixer_slope, mixer_full, PLAIN).astype(LOW)

    leaving = []
    for pair in range(2):
        for distance in range(4):
            to = block ^ distance
            corner = ((to >> 1) * rows_here, (to & 1) * part_width + pair * pair_width)
            leaving.append(lax.dynamic_slice(attended_slope, corner, (rows_here, pair_width)))
    leaving, mixer_slope, mixed_in, activated, expand_far = fence(
        leaving, mixer_slope, mixed_in, activated, expand_far
    )
    slope_first = [leaving[0]] + [swap(leaving[d], "ctx", d) for d in (1, 2, 3)]
    expand_near = add_far(expand_parts[2], expand_parts[1], expand_far) if four else ()
    reduce_parts = grad_products([reduce_slope], activated, place, order, "reduce_grad")
    mixer_parts = grad_products([mixer_slope], mixed_in, place, order, "mixer_grad")
    wide = jnp.concatenate([reduce_parts, mixer_parts], axis=2)

    slope_first, leaving, wide, expand_near = fence(slope_first, leaving, wide, expand_near)
    half = width // 8
    slope_second = [leaving[4]] + [swap(leaving[4 + d], "ctx", d) for d in (1, 2, 3)]
    if four:
        expand_near = near_rows_out(expand_near)
    grad_first = attention_backward(
        joint_out, jnp.concatenate(slope_first, axis=0), out_first, log_first, 0
    )

    grad_first, slope_second, expand_near, wide = fence(
        grad_first, slope_second, expand_near, wide
    )
    if four:
        expand_sum = expand_parts[3].astype(FULL) + both(expand_near)
    else:
        expand_sum = lax.psum_scatter(
            expand_parts.reshape(width, -1), "fsdp", scatter_dimension=0, tiled=True
        ).astype(FULL)
    expand_keep, expand_send = halves(expand_sum, part_at)
    expand_send, slope_second = fence(expand_send, slope_second)
    expand_rows = (expand_keep, swap(expand_send, "ctx", 1))
    wide_far = far_halves(wide[0]) if four else ()
    grad_second = attention_backward(
        joint_out, jnp.concatenate(slope_second, axis=0), out_second, log_second, 1
    )

    grad_second, expand_rows, wide_far = fence(grad_second, expand_rows, wide_far)
    expand_rows = split_rows(both(expand_rows), clip_at, 2)
    if four:
        wide_near = near_rows_out(add_far(wide[2], wide[1], wide_far))
    joint_slope = jnp.concatenate(
        [grad[kind] for kind in range(3) for grad in (grad_first, grad_second)], axis=1
    )
    first_there = product(joint_slope, joint_full[width_half:], ROW_BY_ROW).astype(LOW)
    first_here = rows_product(joint_slope, joint_full[:width_half], "first_slope")
    first_half = both((first_here, swap(first_there, "tp", 1))).astype(LOW)

    first_half, joint_slope, expand_rows = fence(first_half, joint_slope, expand_rows)
    expand_rows = both(expand_rows).astype(LOW)
    pieces = first_half.reshape(4, rows_here, width_half)
    passing = jnp.concatenate([pieces[1], pieces[3][:, :quarter], pieces[2][:, quarter:]], axis=1)
    passing = swap(passing, "ctx", 1)
    place = (shard if four else start) ^ (2 * core)
    joint_parts = grad_products([normed_mine, normed_other], joint_slope, place, order, "joint_grad")
    slope_sums = jnp.sum(joint_slope.astype(FULL), axis=0)
    bias_sums = jnp.stack([slope_sums[:part_width], slope_sums[2 * part_width :]])
    joint_bias_grad = lax.dynamic_update_slice(
        jnp.zeros((2, features), FULL), bias_sums, (0, part_at * part_width)
    )

    expand_rows = join_rows(expand_rows, clip_at, 2)

    if not four:
        wide_near = lax.psum_scatter(
            wide.reshape(width, -1), "fsdp", scatter_dimension=0, tiled=True
        )
    passing, joint_parts, wide_near, expand_rows = fence(
        passing, joint_parts, wide_near, expand_rows
    )
    wide_sum = wide[3].astype(FULL) + both(wide_near) if four else wide_near.astype(FULL)
    wide_keep, wide_send = halves(wide_sum, part_at)
    own_half = both((pieces[0], passing[:, :width_half])).astype(LOW)
    to_left = both((pieces[2][:, :quarter], passing[:, width_half : width_half + quarter]))
    to_right = both((pieces[3][:, quarter:], passing[:, width_half + quarter :]))
    to_left, to_right, own_half, wide_send, joint_parts, activated = fence(
        to_left.astype(LOW), to_right.astype(LOW), own_half, wide_send, joint_parts, activated
    )
    other_half = jnp.concatenate(
        [swap(to_left, "ctx", 2), swap(to_right, "ctx", 3)], axis=1
    )
    joint_far = far_halves(joint_parts[0]) if four else ()
    wide_rows = (wide_keep, swap(wide_send, "ctx", 1))
    reduce_part = reduce_output(activated, reduce_held, pieces_at)

    other_half, joint_far, wide_rows, reduce_part, expand_rows = fence(
        other_half, joint_far, wide_rows, reduce_part, expand_rows
    )
    reduce_swapped = swap(reduce_part, "tp", 1)
    wide_rows = split_rows(both(wide_rows), clip_at, 2)
    slope_half = jnp.concatenate(
        swapped_if(clip_at, [own_half, other_half]), axis=0
    )
    slope_other = swap(slope_half, "tp", 1)
    first_slope = jnp.concatenate(swapped_if(core, [slope_half, slope_other]), axis=1)
    tokens_grad, first_sums = by_rows(
        first_norm_back_kernel, "first_norm_back", [FULL], True,
        flat_tokens, first_slope, first_gain[None],
        cotangent.reshape(tokens_here, width), first_sum_back,
    )
    if four:
        joint_near = near_rows_out(add_far(joint_parts[2], joint_parts[1], joint_far))
    else:
        joint_near = lax.psum_scatter(
            joint_parts.reshape(width, -1), "fsdp", scatter_dimension=0, tiled=True
        )

    first_sums, tokens_grad, joint_near, wide_rows, reduce_swapped = fence(
        first_sums, tokens_grad, joint_near, wide_rows, reduce_swapped
    )
    vectors = [
        first_sums[0],
        first_sums[1],
        joint_bias_grad[0],
        joint_bias_grad[1],
        second_sums[2],
        second_sums[0],
        second_sums[1],
        expand_bias_grad,
        reduce_bias_grad,
    ]
    packed = jnp.concatenate(vectors).reshape(-1, 128)
    packed_pieces = [packed] + [swap(packed, "ctx", d) for d in (1, 2, 3)]
    joint_sum = joint_parts[3].astype(FULL) + both(joint_near) if four else joint_near
    joint_sum = joint_sum.astype(LOW)
    joint_sum = (joint_sum, swap(joint_sum, "ctx", 2))
    wide_rows = join_rows(both(wide_rows).astype(LOW), clip_at, 2)
    reduce_out = both((reduce_part, reduce_swapped)) + reduce_bias
    mixer_out = both((mixer_part, mixer_swapped)) + mixer_bias
    branches = (mixer_out + reduce_out).reshape(clips_here, rows_here, width)
    result = (tokens.astype(FULL) + valid * branches).astype(LOW)

    packed_pieces, joint_sum, wide_rows, result = fence(
        packed_pieces, joint_sum, wide_rows, result
    )
    packed = pairwise(packed_pieces)
    if four:
        packed = pairwise([packed] + [swap(packed, "fsdp", d) for d in (1, 2, 3)])
    else:
        packed = lax.psum(packed, "fsdp")
    joint_sum = both(joint_sum).astype(LOW)
    joint_parts = swapped_if(part_at, [joint_sum, swap(joint_sum, "ctx", 1)])
    joint_grad = jnp.concatenate(
        [piece.reshape(-1, 3, part_width) for piece in joint_parts], axis=2
    ).astype(FULL)
    wide_rows = join_rows(wide_rows, part_at, 1).astype(FULL)
    reduce_grad = wide_rows[:, : activated.shape[1]]
    mixer_grad = wide_rows[:, activated.shape[1] :]
    expand_grad = join_rows(expand_rows, part_at, 1).astype(FULL)
    packed = packed.reshape(-1)
    shares = []
    start = 0
    for vector in vectors:
        share = vector.shape[0] // lax.axis_size("fsdp")
        shares.append(lax.dynamic_slice_in_dim(packed, start + shard * share, share, 0))
        start += vector.shape[0]

    shape = (clips_here, rows_here, width)
    return (
        result,
        tokens_grad.reshape(shape),
        shares[0],
        shares[1],
        joint_grad,
        jnp.stack([shares[2], shares[3]]),
        mixer_grad,
        shares[4],
        shares[5],
        shares[6],
        expand_grad,
        shares[7],
        reduce_grad,
        shares[8],
    )


def solution(mesh):
    return jax.shard_map(
        per_device,
        mesh=mesh,
        in_specs=(
            P("fsdp", "ctx", None),
            P("fsdp"),
            P("fsdp", "ctx", None),
            P(),
            P(),
            P("fsdp", None, "tp"),
            P(None, "tp"),
            P("fsdp", "tp"),
            P(),
            P(),
            P(),
            P("fsdp", "tp"),
            P("tp"),
            P("fsdp", "tp"),
            P(),
        ),
        out_specs=(
            P("fsdp", "ctx", None),
            P("fsdp", "ctx", None),
            P("fsdp"),
            P("fsdp"),
            P("fsdp", None, "tp"),
            P(None, ("tp", "fsdp")),
            P("fsdp", "tp"),
            P("fsdp"),
            P("fsdp"),
            P("fsdp"),
            P("fsdp", "tp"),
            P(("tp", "fsdp")),
            P("fsdp", "tp"),
            P("fsdp"),
        ),
        check_vma=False,
    )
```

```python
import jax
import jax.numpy as jnp
from jax import lax
from jax.experimental import pallas as pl
from jax.experimental.pallas import tpu as pltpu
from jax.sharding import PartitionSpec as P

HEAD_DIM = 64
EPSILON = 1e-06
LOW = jnp.bfloat16
FULL = jnp.float32

ROW_BY_ROW = (((1,), (1,)), ((), ()))
PLAIN = (((1,), (0,)), ((), ()))
COLUMN_BY_COLUMN = (((0,), (0,)), ((), ()))


def product(left, right, dims):
    return lax.dot_general(left, right, dims, preferred_element_type=FULL)


def normalize(value_rows):
    center = value_rows - jnp.mean(value_rows, axis=-1, keepdims=True)
    inverse = lax.rsqrt(jnp.mean(center * center, axis=-1, keepdims=True) + EPSILON)
    return (center * inverse, inverse)


def norm_back(upstream, gain, scaled, inverse):
    weighted = upstream * gain
    return inverse * (
        weighted
        - jnp.mean(weighted, axis=-1, keepdims=True)
        - scaled * jnp.mean(weighted * scaled, axis=-1, keepdims=True)
    )


def row_chunk(count, most):
    for chunk in range(most, 0, -16):
        if count % chunk == 0:
            return chunk
    raise ValueError("rows")


def first_norm_kernel(tokens_ref, gain_ref, shift_ref, out_ref):
    scaled, _ = normalize(tokens_ref[...].astype(FULL))
    out_ref[...] = (scaled * gain_ref[...] + shift_ref[...]).astype(LOW)


def second_norm_kernel(tokens_ref, one_ref, two_ref, bias_ref, gain_ref, shift_ref, out_ref):
    mixed = one_ref[...].astype(FULL) + two_ref[...].astype(FULL) + bias_ref[...]
    scaled, _ = normalize(tokens_ref[...].astype(FULL) + mixed)
    out_ref[...] = (scaled * gain_ref[...] + shift_ref[...]).astype(LOW)


def add_sums(ref, rows):
    sums = jnp.concatenate([jnp.sum(row, axis=0, keepdims=True) for row in rows], axis=0)

    @pl.when(pl.program_id(0) == 0)
    def _():
        ref[: len(rows)] = sums

    @pl.when(pl.program_id(0) > 0)
    def _():
        ref[: len(rows)] += sums


def second_norm_back_kernel(
    tokens_ref, one_ref, two_ref, bias_ref, gain_ref, left_ref, right_ref, outer_ref,
    slope_ref, back_ref, sums_ref,
):
    mixed = one_ref[...].astype(FULL) + two_ref[...].astype(FULL) + bias_ref[...]
    scaled, inverse = normalize(tokens_ref[...].astype(FULL) + mixed)
    upstream = left_ref[...].astype(FULL) + right_ref[...].astype(FULL)
    back = norm_back(upstream, gain_ref[...], scaled, inverse)
    slope = (outer_ref[...].astype(FULL) + back).astype(LOW)
    slope_ref[...] = slope
    back_ref[...] = back
    add_sums(sums_ref, [upstream * scaled, upstream, slope.astype(FULL)])


def first_norm_back_kernel(
    tokens_ref, upstream_ref, gain_ref, outer_ref, back_ref, out_ref, sums_ref
):
    scaled, inverse = normalize(tokens_ref[...].astype(FULL))
    upstream = upstream_ref[...].astype(FULL)
    back = norm_back(upstream, gain_ref[...], scaled, inverse)
    out_ref[...] = outer_ref[...].astype(FULL) + back_ref[...] + back
    add_sums(sums_ref, [upstream * scaled, upstream])


def by_rows(kernel, name, out_types, sums, *values):
    count, width = values[0].shape
    chunk = row_chunk(count, 112)
    part = pl.BlockSpec((chunk, width), lambda i: (i, 0))
    in_specs = [
        part if value.shape[0] == count else pl.BlockSpec((1, width), lambda i: (0, 0))
        for value in values
    ]
    out_specs = [part for _ in out_types]
    out_shape = [jax.ShapeDtypeStruct((count, width), kind) for kind in out_types]
    if sums:
        out_specs.append(pl.BlockSpec((8, width), lambda i: (0, 0)))
        out_shape.append(jax.ShapeDtypeStruct((8, width), FULL))
    return pl.pallas_call(
        kernel,
        grid=(count // chunk,),
        in_specs=in_specs,
        out_specs=out_specs,
        out_shape=out_shape,
        compiler_params=pltpu.CompilerParams(vmem_limit_bytes=16 << 20),
        name=name,
    )(*values)


def joint_kernel(mine_ref, other_ref, weight_ref, bias_ref, out_ref):
    half = mine_ref.shape[1]
    out = product(mine_ref[...], weight_ref[:half], PLAIN)
    out += product(other_ref[...], weight_ref[half:], PLAIN)
    out_ref[...] = (out + bias_ref[...]).astype(LOW)


def joint_projection(mine, other, weight, bias):
    count, half = mine.shape
    columns = weight.shape[1]
    chunk = row_chunk(count, 784)
    part = pl.BlockSpec((chunk, half), lambda i: (i, 0))
    return pl.pallas_call(
        joint_kernel,
        grid=(count // chunk,),
        in_specs=[
            part,
            part,
            pl.BlockSpec(weight.shape, lambda i: (0, 0)),
            pl.BlockSpec((1, columns), lambda i: (0, 0)),
        ],
        out_specs=pl.BlockSpec((chunk, columns), lambda i: (i, 0)),
        out_shape=jax.ShapeDtypeStruct((count, columns), LOW),
        compiler_params=pltpu.CompilerParams(vmem_limit_bytes=40 << 20),
        name="joint_projection",
    )(mine, other, weight, bias)


def rows_kernel(left_ref, right_ref, out_ref):
    out_ref[...] = product(left_ref[...], right_ref[...], ROW_BY_ROW).astype(LOW)


def rows_product(left, right, name):
    count, depth = left.shape
    columns = right.shape[0]
    chunk = row_chunk(count, 400)
    return pl.pallas_call(
        rows_kernel,
        grid=(count // chunk,),
        in_specs=[
            pl.BlockSpec((chunk, depth), lambda i: (i, 0)),
            pl.BlockSpec((columns, depth), lambda i: (0, 0)),
        ],
        out_specs=pl.BlockSpec((chunk, columns), lambda i: (i, 0)),
        out_shape=jax.ShapeDtypeStruct((count, columns), LOW),
        compiler_params=pltpu.CompilerParams(vmem_limit_bytes=48 << 20),
        name=name,
    )(left, right)


def grad_kernel(distances, place_ref, *refs):
    lefts, (right_ref, out_ref) = refs[:-2], refs[-2:]
    left = lefts[0][...]
    if len(lefts) == 2:
        slot = place_ref[0] ^ distance_at(distances, pl.program_id(0))
        left = jnp.where((slot >> 1) == 0, left, lefts[1][...])
    out_ref[0] = product(left, right_ref[...], COLUMN_BY_COLUMN).astype(LOW)


def distance_at(distances, step):
    if len(distances) == 1:
        return distances[0]
    return distances[0] + step * (distances[1] - distances[0])


def grad_products(lefts, right, place, distances, name):
    tokens_here, columns = right.shape
    quarter = sum(left.shape[1] for left in lefts) // 4
    blocks = lefts[0].shape[1] // quarter

    def left_at(i, place):
        return (0, (place[0] ^ distance_at(distances, i)) & (blocks - 1))

    return pl.pallas_call(
        lambda *refs: grad_kernel(distances, *refs),
        grid_spec=pltpu.PrefetchScalarGridSpec(
            num_scalar_prefetch=1,
            grid=(len(distances),),
            in_specs=[pl.BlockSpec((tokens_here, quarter), left_at) for _ in lefts]
            + [pl.BlockSpec((tokens_here, columns), lambda i, place: (0, 0))],
            out_specs=pl.BlockSpec((1, quarter, columns), lambda i, place: (i, 0, 0)),
        ),
        out_shape=jax.ShapeDtypeStruct((len(distances), quarter, columns), LOW),
        compiler_params=pltpu.CompilerParams(vmem_limit_bytes=48 << 20),
        name=name,
    )(place.astype(jnp.int32).reshape(1), *lefts, right)


def attention_forward_kernel(q_ref, k_ref, v_ref, o_ref, lse_ref):
    count, width = q_ref.shape
    rows = row_chunk(count, 256)
    lane = lax.broadcasted_iota(jnp.int32, (rows, width), 1)
    k = k_ref[...]
    v = v_ref[...]
    units = [(start, head) for start in range(0, count, rows) for head in range(width // HEAD_DIM)]

    def scores_of(unit):
        start, head = unit
        q = q_ref[start : start + rows] * jnp.asarray(HEAD_DIM ** (-0.5), LOW)
        return product(jnp.where((lane // HEAD_DIM) == head, q, jnp.zeros_like(q)), k, ROW_BY_ROW)

    logs = []
    ahead = scores_of(units[0])
    for step, (start, head) in enumerate(units):
        scores = ahead
        if step + 1 < len(units):
            ahead = scores_of(units[step + 1])
        top = jnp.max(scores, axis=-1, keepdims=True)
        weights = jnp.exp(scores - top)
        total = jnp.sum(weights, axis=-1, keepdims=True)
        part = product(weights.astype(LOW), v, PLAIN) / total
        if head == 0:
            out = part
            logs.append(jnp.zeros((rows, width), FULL))
        else:
            out = jnp.where((lane // HEAD_DIM) == head, part, out)
            o_ref[start : start + rows] = out.astype(LOW)
        logs[-1] = jnp.where(lane == head, top + jnp.log(total), logs[-1])
    lse_ref[...] = jnp.concatenate(logs, axis=0).T[: lse_ref.shape[0]]


def attention_forward(joint, pair):
    count, columns = joint.shape
    width = 2 * HEAD_DIM
    kind = columns // (3 * width)
    return pl.pallas_call(
        attention_forward_kernel,
        grid=(1,),
        in_specs=[
            pl.BlockSpec((count, width), lambda i: (0, pair)),
            pl.BlockSpec((count, width), lambda i: (0, kind + pair)),
            pl.BlockSpec((count, width), lambda i: (0, 2 * kind + pair)),
        ],
        out_specs=[
            pl.BlockSpec((count, width), lambda i: (0, 0)),
            pl.BlockSpec((8, count), lambda i: (0, 0)),
        ],
        out_shape=[
            jax.ShapeDtypeStruct((count, width), LOW),
            jax.ShapeDtypeStruct((8, count), FULL),
        ],
        compiler_params=pltpu.CompilerParams(vmem_limit_bytes=48 << 20),
        name="attention_forward",
    )(joint, joint, joint)


def attention_backward_kernel(
    q_ref, k_ref, v_ref, da_ref, o_ref, lse_ref, dq_ref, dk_ref, dv_ref,
    q_heads, da_heads, delta_ref, dq_total,
):
    count, width = q_ref.shape
    rows = row_chunk(count, 256)
    heads = width // HEAD_DIM
    scale = jnp.asarray(HEAD_DIM ** (-0.5), LOW)

    lane = lax.broadcasted_iota(jnp.int32, (count, width), 1)
    delta = jnp.zeros((count, width), FULL)
    q = q_ref[...] * scale
    da = da_ref[...]
    both_rows = da.astype(FULL) * o_ref[...].astype(FULL)
    for head in range(heads):
        mask = (lane // HEAD_DIM) == head
        q_heads[head] = jnp.where(mask, q, jnp.zeros_like(q))
        da_heads[head] = jnp.where(mask, da, jnp.zeros_like(da))
        row = jnp.sum(jnp.where(mask, both_rows, 0.0), axis=-1, keepdims=True)
        delta = jnp.where(lane == head, row, delta)
    delta_ref[...] = delta.T[:8]
    dq_total[...] = jnp.zeros_like(dq_total)

    lane = lax.broadcasted_iota(jnp.int32, (rows, width), 1)
    for start in range(0, count, rows):
        k = k_ref[start : start + rows]
        v = v_ref[start : start + rows]
        scaled_k = k * scale
        dk = dv = None
        for head in range(heads):
            q = q_heads[head]
            da = da_heads[head]
            probs = jnp.exp(product(k, q, ROW_BY_ROW) - lse_ref[head : head + 1, :])
            slope = probs * (product(v, da, ROW_BY_ROW) - delta_ref[head : head + 1, :])
            slope = slope.astype(LOW)
            dv_part = product(probs.astype(LOW), da, PLAIN)
            dk_part = product(slope, q, PLAIN)
            dv = dv_part if dv is None else dv + dv_part
            dk = dk_part if dk is None else dk + dk_part
            one_k = jnp.where((lane // HEAD_DIM) == head, scaled_k, jnp.zeros_like(k))
            dq_total[...] += product(slope, one_k, COLUMN_BY_COLUMN)
        dk_ref[start : start + rows] = dk.astype(LOW)
        dv_ref[start : start + rows] = dv.astype(LOW)
    dq_ref[...] = dq_total[...].astype(LOW)


def attention_backward(joint, da, out, lse, pair):
    count, columns = joint.shape
    width = 2 * HEAD_DIM
    kind = columns // (3 * width)
    alone = pl.BlockSpec((count, width), lambda i: (0, 0))
    grad = jax.ShapeDtypeStruct((count, width), LOW)
    return pl.pallas_call(
        attention_backward_kernel,
        grid=(1,),
        in_specs=[
            pl.BlockSpec((count, width), lambda i: (0, pair)),
            pl.BlockSpec((count, width), lambda i: (0, kind + pair)),
            pl.BlockSpec((count, width), lambda i: (0, 2 * kind + pair)),
            alone,
            alone,
            pl.BlockSpec((8, count), lambda i: (0, 0)),
        ],
        out_specs=[alone, alone, alone],
        out_shape=[grad, grad, grad],
        scratch_shapes=[
            pltpu.VMEM((2, count, width), LOW),
            pltpu.VMEM((2, count, width), LOW),
            pltpu.VMEM((8, count), FULL),
            pltpu.VMEM((count, width), FULL),
        ],
        compiler_params=pltpu.CompilerParams(vmem_limit_bytes=48 << 20),
        name="attention_backward",
    )(joint, joint, joint, da, out, lse)


def put_together(place_ref, whole_ref, piece_refs):
    for piece, piece_ref in enumerate(piece_refs):
        rows = piece_ref.shape[0]
        start = pl.multiple_of(place_ref[piece], rows)
        whole_ref[pl.ds(start, rows), :] = piece_ref[...]


def feed_forward_kernel(pieces, place_ref, normed_ref, slope_ref, bias_ref, *refs):
    active_ref, expand_slope_ref, back_ref, bias_grad_ref = refs[2 * pieces : 2 * pieces + 4]
    total, expand_ref, reduce_ref = refs[2 * pieces + 4 :]
    put_together(place_ref, expand_ref, refs[:pieces])
    put_together(place_ref, reduce_ref, refs[pieces : 2 * pieces])
    step = pl.program_id(0)
    count = normed_ref.shape[0]
    half = count // 2
    bias_grad = None
    for rows in (slice(0, half), slice(half, count)):
        hidden = product(normed_ref[rows], expand_ref[...], PLAIN) + bias_ref[...]
        upstream = product(slope_ref[rows], reduce_ref[...], PLAIN)
        share = 0.5 * (1.0 + lax.erf(hidden * (0.5**0.5)))
        active_ref[rows] = (hidden * share).astype(LOW)
        density = jnp.exp(-0.5 * hidden * hidden) * 0.3989422804014327
        slope = (upstream * (share + hidden * density)).astype(LOW)
        expand_slope_ref[rows] = slope
        part = jnp.sum(slope.astype(FULL), axis=0, keepdims=True)
        bias_grad = part if bias_grad is None else bias_grad + part
        back = product(slope, expand_ref[...], ROW_BY_ROW)

        @pl.when(step == 0)
        def _():
            total[rows] = back

        @pl.when(step > 0)
        def _():
            total[rows] += back

    bias_grad_ref[...] = bias_grad

    @pl.when(step == pl.num_programs(0) - 1)
    def _():
        back_ref[...] = total[...].astype(LOW)


def feed_forward(normed, slope, bias, expand, reduce, place):
    count, width = normed.shape
    hidden = bias.shape[1]
    block = 512 if hidden % 512 == 0 else hidden
    whole = pl.BlockSpec((count, width), lambda i, place: (0, 0))
    out = pl.BlockSpec((count, block), lambda i, place: (0, i))
    row = pl.BlockSpec((1, block), lambda i, place: (0, i))
    return pl.pallas_call(
        lambda *refs: feed_forward_kernel(len(reduce), *refs),
        grid_spec=pltpu.PrefetchScalarGridSpec(
            num_scalar_prefetch=1,
            grid=(hidden // block,),
            in_specs=[whole, whole, row]
            + [
                pl.BlockSpec((piece.shape[0], block), lambda i, place: (0, i))
                for piece in [*expand, *reduce]
            ],
            out_specs=[out, out, whole, row],
            scratch_shapes=[
                pltpu.VMEM((count, width), FULL),
                pltpu.VMEM((width, block), LOW),
                pltpu.VMEM((width, block), LOW),
            ],
        ),
        out_shape=[
            jax.ShapeDtypeStruct((count, hidden), LOW),
            jax.ShapeDtypeStruct((count, hidden), LOW),
            jax.ShapeDtypeStruct((count, width), LOW),
            jax.ShapeDtypeStruct((1, hidden), FULL),
        ],
        compiler_params=pltpu.CompilerParams(vmem_limit_bytes=44 << 20),
        name="feed_forward",
    )(place, normed, slope, bias, *expand, *reduce)


def reduce_kernel(place_ref, active_ref, *refs):
    out_ref, total, reduce_ref = refs[-3:]
    put_together(place_ref, reduce_ref, refs[:-3])
    part = product(active_ref[...], reduce_ref[...], ROW_BY_ROW)

    @pl.when(pl.program_id(0) == 0)
    def _():
        total[...] = part

    @pl.when(pl.program_id(0) > 0)
    def _():
        total[...] += part

    @pl.when(pl.program_id(0) == pl.num_programs(0) - 1)
    def _():
        out_ref[...] = total[...].astype(LOW)


def reduce_output(active, reduce, place):
    count, hidden = active.shape
    width = sum(piece.shape[0] for piece in reduce)
    block = 512 if hidden % 512 == 0 else hidden
    return pl.pallas_call(
        reduce_kernel,
        grid_spec=pltpu.PrefetchScalarGridSpec(
            num_scalar_prefetch=1,
            grid=(hidden // block,),
            in_specs=[pl.BlockSpec((count, block), lambda i, place: (0, i))]
            + [
                pl.BlockSpec((piece.shape[0], block), lambda i, place: (0, i)) for piece in reduce
            ],
            out_specs=pl.BlockSpec((count, width), lambda i, place: (0, 0)),
            scratch_shapes=[pltpu.VMEM((count, width), FULL), pltpu.VMEM((width, block), LOW)],
        ),
        out_shape=jax.ShapeDtypeStruct((count, width), LOW),
        compiler_params=pltpu.CompilerParams(vmem_limit_bytes=32 << 20),
        name="reduce_output",
    )(place, active, *reduce)


def swap(value, axis, distance):
    size = lax.axis_size(axis)
    return lax.ppermute(value, axis, [(i, i ^ distance) for i in range(size)])


def fence(*values):
    return lax.optimization_barrier(values)


def gather_near(rows_here):
    if lax.axis_size("fsdp") != 4:
        return (lax.all_gather(rows_here, "fsdp", axis=0, tiled=True),)
    return (rows_here, swap(rows_here, "fsdp", 1), swap(rows_here, "fsdp", 2))


def gather_far(held):
    if len(held) == 1:
        return held
    rows_here, near, side = held
    half = rows_here.shape[0] // 2
    return held + (swap(side[:half], "fsdp", 1), swap(near[half:], "fsdp", 2))


def place_near(held):
    if len(held) == 1:
        return held[0]
    rows_here, near, side = held[:3]
    me = lax.axis_index("fsdp")
    count, width = rows_here.shape
    out = jnp.zeros((4 * count, width), rows_here.dtype)
    out = lax.dynamic_update_slice(out, rows_here, (me * count, 0))
    out = lax.dynamic_update_slice(out, near, ((me ^ 1) * count, 0))
    return lax.dynamic_update_slice(out, side, ((me ^ 2) * count, 0))


def place_far(out, held):
    if len(held) == 1:
        return out
    far_top, far_low = held[3:]
    half = far_top.shape[0]
    start = (lax.axis_index("fsdp") ^ 3) * 2 * half
    out = lax.dynamic_update_slice(out, far_top, (start, 0))
    return lax.dynamic_update_slice(out, far_low, (start + half, 0))


def far_halves(far):
    half = far.shape[0] // 2
    return (swap(far[:half], "fsdp", 1), swap(far[half:], "fsdp", 2))


def add_far(near, side, far):
    half = near.shape[0] // 2
    near = jnp.concatenate([near[:half], both((near[half:], far[1])).astype(LOW)], axis=0)
    side = jnp.concatenate([both((side[:half], far[0])).astype(LOW), side[half:]], axis=0)
    return (near, side)


def near_rows_out(pair):
    return (swap(pair[0], "fsdp", 1), swap(pair[1], "fsdp", 2))


def halves(value, bit):
    half = value.shape[0] // 2
    keep = lax.dynamic_slice_in_dim(value, bit * half, half, 0)
    send = lax.dynamic_slice_in_dim(value, (1 - bit) * half, half, 0)
    return keep, send.astype(LOW)


def split_rows(value, bit, distance):
    keep, send = halves(value, bit)
    return keep, swap(send, "ctx", distance)


def both(pair):
    return pair[0].astype(FULL) + pair[1].astype(FULL)


def join_rows(value, bit, distance):
    other = swap(value, "ctx", distance)
    return jnp.where(
        bit == 0,
        jnp.concatenate([value, other], axis=0),
        jnp.concatenate([other, value], axis=0),
    )


def pairwise(pieces):
    return (pieces[0] + pieces[1]) + (pieces[2] + pieces[3])


def swapped_if(bit, pair):
    return [jnp.where(bit == 0, pair[0], pair[1]), jnp.where(bit == 0, pair[1], pair[0])]


def per_device(
    tokens,
    clip_mask,
    cotangent,
    first_gain,
    first_shift,
    joint_weight,
    joint_bias,
    mixer_weight,
    mixer_bias,
    second_gain,
    second_shift,
    expand_weight,
    expand_bias,
    reduce_weight,
    reduce_bias,
):
    clips_here, rows_here, width = tokens.shape
    if lax.axis_size("ctx") != 4 or lax.axis_size("tp") != 2 or clips_here != 2:
        raise ValueError("mesh")
    shard = lax.axis_index("fsdp")
    block = lax.axis_index("ctx")
    core = lax.axis_index("tp")
    clip_at = block >> 1
    part_at = block & 1
    width_half = width // 2
    quarter = width_half // 2
    features = joint_weight.shape[2]
    part_width = features // 2
    pair_width = 2 * HEAD_DIM
    tokens_here = clips_here * rows_here

    flat_tokens = tokens.reshape(tokens_here, width)
    (first_normed,) = by_rows(
        first_norm_kernel, "first_norm", [LOW], False,
        flat_tokens, first_gain[None], first_shift[None],
    )
    first_normed = first_normed.reshape(clips_here, rows_here, width)
    mine = lax.dynamic_slice_in_dim(first_normed, core * width_half, width_half, 2)
    other_side = lax.dynamic_slice_in_dim(first_normed, (1 - core) * width_half, width_half, 2)
    own_clip = lax.dynamic_index_in_dim(mine, clip_at, 0, False)
    own_other = lax.dynamic_index_in_dim(other_side, clip_at, 0, False)
    other_clip = lax.dynamic_index_in_dim(mine, 1 - clip_at, 0, False)
    joint_part = lax.dynamic_slice_in_dim(joint_weight, part_at * part_width, part_width, 2)
    both_parts = jnp.concatenate([joint_part[:, kind] for kind in range(3)] + [mixer_weight], axis=1)

    own_clip, left, right, both_parts = fence(
        own_clip, other_clip[:, :quarter], other_clip[:, quarter:], both_parts
    )
    near_rows = swap(own_clip, "ctx", 1)
    across_left = swap(left, "ctx", 2)
    far_right = swap(right, "ctx", 3)
    held = gather_near(both_parts)

    near_rows, across_left, far_right, held, expand_weight = fence(
        near_rows, across_left, far_right, held, expand_weight
    )
    passed = swap(jnp.concatenate([across_left, far_right], axis=1), "ctx", 1)
    held = gather_far(held)
    expand_held = gather_near(expand_weight)

    passed, held = fence(passed, held)
    cross_rows = jnp.concatenate(
        [
            near_rows,
            jnp.concatenate([across_left, passed[:, quarter:]], axis=1),
            jnp.concatenate([passed[:, :quarter], far_right], axis=1),
        ],
        axis=0,
    )
    cross_other = swap(cross_rows, "tp", 1)
    both_full = place_far(place_near(held), held)
    joint_columns = 3 * part_width
    joint_full = jnp.concatenate(
        [
            lax.dynamic_slice(both_full, (start * width_half, 0), (width_half, joint_columns))
            for start in (core, 1 - core)
        ],
        axis=0,
    )

    cross_other, joint_full, both_full, reduce_weight = fence(
        cross_other, joint_full, both_full, reduce_weight
    )
    mixer_full = both_full[:, joint_columns:]
    reduce_held = gather_near(reduce_weight)
    normed_mine = jnp.concatenate([own_clip, cross_rows], axis=0)
    normed_other = jnp.concatenate([own_other, cross_other], axis=0)
    bias_part = lax.dynamic_slice_in_dim(joint_bias, part_at * part_width, part_width, 1)
    bias_row = jnp.concatenate([bias_part[0], jnp.zeros_like(bias_part[0]), bias_part[1]])
    joint_out = joint_projection(normed_mine, normed_other, joint_full, bias_row[None])
    out_first, log_first = attention_forward(joint_out, 0)

    out_first, joint_out, mixer_full, expand_held = fence(
        out_first, joint_out, mixer_full, expand_held
    )
    first_blocks = out_first.reshape(4, rows_here, pair_width)
    arrived_first = [swap(first_blocks[d], "ctx", d) for d in (1, 2, 3)]
    out_second, log_second = attention_forward(joint_out, 1)

    out_second, arrived_first, reduce_held, expand_held = fence(
        out_second, arrived_first, reduce_held, expand_held
    )
    second_blocks = out_second.reshape(4, rows_here, pair_width)
    arrived_second = [swap(second_blocks[d], "ctx", d) for d in (1, 2, 3)]
    expand_held = gather_far(expand_held)

    arrived_second, expand_held, reduce_held, log_first, log_second = fence(
        arrived_second, expand_held, reduce_held, log_first, log_second
    )
    reduce_held = gather_far(reduce_held)
    arrived = [jnp.concatenate([first_blocks[0], second_blocks[0]], axis=1)] + [
        jnp.concatenate([one, two], axis=1) for one, two in zip(arrived_first, arrived_second)
    ]
    own_joined = jnp.concatenate(swapped_if(part_at, arrived[:2]), axis=1)
    other_joined = jnp.concatenate(swapped_if(part_at, arrived[2:]), axis=1)
    mixed_in = jnp.concatenate(swapped_if(clip_at, [own_joined, other_joined]), axis=0)
    mixer_part = product(mixed_in, mixer_full, ROW_BY_ROW).astype(LOW)
    mixer_swapped = swap(mixer_part, "tp", 1)
    mixer_row = mixer_bias[None]
    (second_normed,) = by_rows(
        second_norm_kernel, "second_norm", [LOW], False,
        flat_tokens, mixer_part, mixer_swapped, mixer_row, second_gain[None], second_shift[None],
    )
    valid = clip_mask.astype(FULL)[:, None, None]
    reduce_slope = (cotangent.astype(FULL) * valid).astype(LOW).reshape(tokens_here, width)
    reduce_bias_grad = jnp.sum(reduce_slope.astype(FULL), axis=0)

    second_normed, reduce_slope, reduce_held = fence(second_normed, reduce_slope, reduce_held)
    four = lax.axis_size("fsdp") == 4
    start = jnp.zeros((), jnp.int32)
    if four:
        rows = width // 4
        pieces_at = jnp.stack([shard, shard ^ 1, shard ^ 2, shard ^ 3, shard ^ 3]) * rows
        pieces_at = pieces_at.astype(jnp.int32) + jnp.array([0, 0, 0, 0, rows // 2], jnp.int32)
    else:
        pieces_at = start.reshape(1)
    activated, expand_slope, second_part, expand_bias_grad = feed_forward(
        second_normed, reduce_slope, expand_bias[None], expand_held, reduce_held, pieces_at
    )
    expand_bias_grad = expand_bias_grad[0]

    second_swapped = swap(second_part, "tp", 1)
    place, order = (shard, (3, 2, 1, 0)) if four else (start, (0, 1, 2, 3))
    expand_parts = grad_products([second_normed], expand_slope, place, order, "expand_grad")
    second_swapped, expand_parts = fence(second_swapped, expand_parts)
    expand_far = far_halves(expand_parts[0]) if four else ()
    mixer_slope, first_sum_back, second_sums = by_rows(
        second_norm_back_kernel, "second_norm_back", [LOW, FULL], True,
        flat_tokens, mixer_part, mixer_swapped, mixer_row, second_gain[None],
        second_part, second_swapped, reduce_slope,
    )
    attended_slope = product(mixer_slope, mixer_full, PLAIN).astype(LOW)

    leaving = []
    for pair in range(2):
        for distance in range(4):
            to = block ^ distance
            corner = ((to >> 1) * rows_here, (to & 1) * part_width + pair * pair_width)
            leaving.append(lax.dynamic_slice(attended_slope, corner, (rows_here, pair_width)))
    leaving, mixer_slope, mixed_in, activated, expand_far = fence(
        leaving, mixer_slope, mixed_in, activated, expand_far
    )
    slope_first = [leaving[0]] + [swap(leaving[d], "ctx", d) for d in (1, 2, 3)]
    expand_near = add_far(expand_parts[2], expand_parts[1], expand_far) if four else ()
    reduce_parts = grad_products([reduce_slope], activated, place, order, "reduce_grad")
    mixer_parts = grad_products([mixer_slope], mixed_in, place, order, "mixer_grad")
    wide = jnp.concatenate([reduce_parts, mixer_parts], axis=2)

    slope_first, leaving, wide, expand_near = fence(slope_first, leaving, wide, expand_near)
    half = width // 8
    slope_second = [leaving[4]] + [swap(leaving[4 + d], "ctx", d) for d in (1, 2, 3)]
    if four:
        expand_near = near_rows_out(expand_near)
    grad_first = attention_backward(
        joint_out, jnp.concatenate(slope_first, axis=0), out_first, log_first, 0
    )

    grad_first, slope_second, expand_near, wide = fence(
        grad_first, slope_second, expand_near, wide
    )
    if four:
        expand_sum = expand_parts[3].astype(FULL) + both(expand_near)
    else:
        expand_sum = lax.psum_scatter(
            expand_parts.reshape(width, -1), "fsdp", scatter_dimension=0, tiled=True
        ).astype(FULL)
    expand_keep, expand_send = halves(expand_sum, part_at)
    expand_send, slope_second = fence(expand_send, slope_second)
    expand_rows = (expand_keep, swap(expand_send, "ctx", 1))
    wide_far = far_halves(wide[0]) if four else ()
    grad_second = attention_backward(
        joint_out, jnp.concatenate(slope_second, axis=0), out_second, log_second, 1
    )

    grad_second, expand_rows, wide_far = fence(grad_second, expand_rows, wide_far)
    expand_rows = split_rows(both(expand_rows), clip_at, 2)
    if four:
        wide_near = near_rows_out(add_far(wide[2], wide[1], wide_far))
    joint_slope = jnp.concatenate(
        [grad[kind] for kind in range(3) for grad in (grad_first, grad_second)], axis=1
    )
    first_there = product(joint_slope, joint_full[width_half:], ROW_BY_ROW).astype(LOW)
    first_here = rows_product(joint_slope, joint_full[:width_half], "first_slope")
    first_half = both((first_here, swap(first_there, "tp", 1))).astype(LOW)

    first_half, joint_slope, expand_rows = fence(first_half, joint_slope, expand_rows)
    expand_rows = both(expand_rows).astype(LOW)
    pieces = first_half.reshape(4, rows_here, width_half)
    passing = jnp.concatenate([pieces[1], pieces[3][:, :quarter], pieces[2][:, quarter:]], axis=1)
    passing = swap(passing, "ctx", 1)
    place = (shard if four else start) ^ (2 * core)
    joint_parts = grad_products([normed_mine, normed_other], joint_slope, place, order, "joint_grad")
    slope_sums = jnp.sum(joint_slope.astype(FULL), axis=0)
    bias_sums = jnp.stack([slope_sums[:part_width], slope_sums[2 * part_width :]])
    joint_bias_grad = lax.dynamic_update_slice(
        jnp.zeros((2, features), FULL), bias_sums, (0, part_at * part_width)
    )

    expand_rows = join_rows(expand_rows, clip_at, 2)

    if not four:
        wide_near = lax.psum_scatter(
            wide.reshape(width, -1), "fsdp", scatter_dimension=0, tiled=True
        )
    passing, joint_parts, expand_rows = fence(passing, joint_parts, expand_rows)
    own_half = both((pieces[0], passing[:, :width_half])).astype(LOW)
    to_left = both((pieces[2][:, :quarter], passing[:, width_half : width_half + quarter]))
    to_right = both((pieces[3][:, quarter:], passing[:, width_half + quarter :]))
    to_left, to_right, own_half, joint_parts, activated = fence(
        to_left.astype(LOW), to_right.astype(LOW), own_half, joint_parts, activated
    )
    other_half = jnp.concatenate(
        [swap(to_left, "ctx", 2), swap(to_right, "ctx", 3)], axis=1
    )
    joint_leaves, wide_near = fence(joint_parts[0], wide_near)
    joint_far = far_halves(joint_leaves) if four else ()
    reduce_part = reduce_output(activated, reduce_held, pieces_at)

    other_half, joint_far, wide_near, reduce_part, expand_rows = fence(
        other_half, joint_far, wide_near, reduce_part, expand_rows
    )
    reduce_swapped = swap(reduce_part, "tp", 1)
    wide_sum = wide[3].astype(FULL) + both(wide_near) if four else wide_near.astype(FULL)
    wide_rows = split_rows(wide_sum, part_at, 1)
    slope_half = jnp.concatenate(
        swapped_if(clip_at, [own_half, other_half]), axis=0
    )
    slope_other = swap(slope_half, "tp", 1)
    first_slope = jnp.concatenate(swapped_if(core, [slope_half, slope_other]), axis=1)
    tokens_grad, first_sums = by_rows(
        first_norm_back_kernel, "first_norm_back", [FULL], True,
        flat_tokens, first_slope, first_gain[None],
        cotangent.reshape(tokens_here, width), first_sum_back,
    )
    if four:
        joint_near = near_rows_out(add_far(joint_parts[2], joint_parts[1], joint_far))
    else:
        joint_near = lax.psum_scatter(
            joint_parts.reshape(width, -1), "fsdp", scatter_dimension=0, tiled=True
        )

    first_sums, tokens_grad, joint_near, wide_rows, reduce_swapped = fence(
        first_sums, tokens_grad, joint_near, wide_rows, reduce_swapped
    )
    vectors = [
        first_sums[0],
        first_sums[1],
        joint_bias_grad[0],
        joint_bias_grad[1],
        second_sums[2],
        second_sums[0],
        second_sums[1],
        expand_bias_grad,
        reduce_bias_grad,
    ]
    packed = jnp.concatenate(vectors).reshape(-1, 128)
    packed_pieces = [packed] + [swap(packed, "ctx", d) for d in (1, 2, 3)]
    joint_sum = joint_parts[3].astype(FULL) + both(joint_near) if four else joint_near
    joint_sum = joint_sum.astype(LOW)
    joint_sum = (joint_sum, swap(joint_sum, "ctx", 2))
    wide_rows = split_rows(both(wide_rows), clip_at, 2)
    reduce_out = both((reduce_part, reduce_swapped)) + reduce_bias
    mixer_out = both((mixer_part, mixer_swapped)) + mixer_bias
    branches = (mixer_out + reduce_out).reshape(clips_here, rows_here, width)
    result = (tokens.astype(FULL) + valid * branches).astype(LOW)

    packed_pieces, joint_sum, wide_rows, result = fence(
        packed_pieces, joint_sum, wide_rows, result
    )
    packed = pairwise(packed_pieces)
    if four:
        packed = pairwise([packed] + [swap(packed, "fsdp", d) for d in (1, 2, 3)])
    else:
        packed = lax.psum(packed, "fsdp")
    joint_sum = both(joint_sum).astype(LOW)
    joint_parts = swapped_if(part_at, [joint_sum, swap(joint_sum, "ctx", 1)])
    joint_grad = jnp.concatenate(
        [piece.reshape(-1, 3, part_width) for piece in joint_parts], axis=2
    ).astype(FULL)
    wide_rows = join_rows(both(wide_rows).astype(LOW), clip_at, 2)
    wide_rows = join_rows(wide_rows, part_at, 1).astype(FULL)
    reduce_grad = wide_rows[:, : activated.shape[1]]
    mixer_grad = wide_rows[:, activated.shape[1] :]
    expand_grad = join_rows(expand_rows, part_at, 1).astype(FULL)
    packed = packed.reshape(-1)
    shares = []
    start = 0
    for vector in vectors:
        share = vector.shape[0] // lax.axis_size("fsdp")
        shares.append(lax.dynamic_slice_in_dim(packed, start + shard * share, share, 0))
        start += vector.shape[0]

    shape = (clips_here, rows_here, width)
    return (
        result,
        tokens_grad.reshape(shape),
        shares[0],
        shares[1],
        joint_grad,
        jnp.stack([shares[2], shares[3]]),
        mixer_grad,
        shares[4],
        shares[5],
        shares[6],
        expand_grad,
        shares[7],
        reduce_grad,
        shares[8],
    )


def solution(mesh):
    return jax.shard_map(
        per_device,
        mesh=mesh,
        in_specs=(
            P("fsdp", "ctx", None),
            P("fsdp"),
            P("fsdp", "ctx", None),
            P(),
            P(),
            P("fsdp", None, "tp"),
            P(None, "tp"),
            P("fsdp", "tp"),
            P(),
            P(),
            P(),
            P("fsdp", "tp"),
            P("tp"),
            P("fsdp", "tp"),
            P(),
        ),
        out_specs=(
            P("fsdp", "ctx", None),
            P("fsdp", "ctx", None),
            P("fsdp"),
            P("fsdp"),
            P("fsdp", None, "tp"),
            P(None, ("tp", "fsdp")),
            P("fsdp", "tp"),
            P("fsdp"),
            P("fsdp"),
            P("fsdp"),
            P("fsdp", "tp"),
            P(("tp", "fsdp")),
            P("fsdp", "tp"),
            P("fsdp"),
        ),
        check_vma=False,
    )
```

```python
import jax
import jax.numpy as jnp
from jax import lax
from jax.experimental import pallas as pl
from jax.experimental.pallas import tpu as pltpu
from jax.sharding import PartitionSpec as P

HEAD_DIM = 64
EPSILON = 1e-06
LOW = jnp.bfloat16
FULL = jnp.float32

ROW_BY_ROW = (((1,), (1,)), ((), ()))
PLAIN = (((1,), (0,)), ((), ()))
COLUMN_BY_COLUMN = (((0,), (0,)), ((), ()))


def product(left, right, dims):
    return lax.dot_general(left, right, dims, preferred_element_type=FULL)


def normalize(value_rows):
    center = value_rows - jnp.mean(value_rows, axis=-1, keepdims=True)
    inverse = lax.rsqrt(jnp.mean(center * center, axis=-1, keepdims=True) + EPSILON)
    return (center * inverse, inverse)


def norm_back(upstream, gain, scaled, inverse):
    weighted = upstream * gain
    return inverse * (
        weighted
        - jnp.mean(weighted, axis=-1, keepdims=True)
        - scaled * jnp.mean(weighted * scaled, axis=-1, keepdims=True)
    )


def row_chunk(count, most):
    for chunk in range(most, 0, -16):
        if count % chunk == 0:
            return chunk
    raise ValueError("rows")


def first_norm_kernel(tokens_ref, gain_ref, shift_ref, out_ref):
    scaled, _ = normalize(tokens_ref[...].astype(FULL))
    out_ref[...] = (scaled * gain_ref[...] + shift_ref[...]).astype(LOW)


def second_norm_kernel(tokens_ref, one_ref, two_ref, bias_ref, gain_ref, shift_ref, out_ref):
    mixed = one_ref[...].astype(FULL) + two_ref[...].astype(FULL) + bias_ref[...]
    scaled, _ = normalize(tokens_ref[...].astype(FULL) + mixed)
    out_ref[...] = (scaled * gain_ref[...] + shift_ref[...]).astype(LOW)


def add_sums(ref, rows):
    sums = jnp.concatenate([jnp.sum(row, axis=0, keepdims=True) for row in rows], axis=0)

    @pl.when(pl.program_id(0) == 0)
    def _():
        ref[: len(rows)] = sums

    @pl.when(pl.program_id(0) > 0)
    def _():
        ref[: len(rows)] += sums


def second_norm_back_kernel(
    tokens_ref, one_ref, two_ref, bias_ref, gain_ref, left_ref, right_ref, outer_ref,
    slope_ref, back_ref, sums_ref,
):
    mixed = one_ref[...].astype(FULL) + two_ref[...].astype(FULL) + bias_ref[...]
    scaled, inverse = normalize(tokens_ref[...].astype(FULL) + mixed)
    upstream = left_ref[...].astype(FULL) + right_ref[...].astype(FULL)
    back = norm_back(upstream, gain_ref[...], scaled, inverse)
    slope = (outer_ref[...].astype(FULL) + back).astype(LOW)
    slope_ref[...] = slope
    back_ref[...] = back
    add_sums(sums_ref, [upstream * scaled, upstream, slope.astype(FULL)])


def first_norm_back_kernel(
    tokens_ref, upstream_ref, gain_ref, outer_ref, back_ref, out_ref, sums_ref
):
    scaled, inverse = normalize(tokens_ref[...].astype(FULL))
    upstream = upstream_ref[...].astype(FULL)
    back = norm_back(upstream, gain_ref[...], scaled, inverse)
    out_ref[...] = outer_ref[...].astype(FULL) + back_ref[...] + back
    add_sums(sums_ref, [upstream * scaled, upstream])


def by_rows(kernel, name, out_types, sums, *values):
    count, width = values[0].shape
    chunk = row_chunk(count, 112)
    part = pl.BlockSpec((chunk, width), lambda i: (i, 0))
    in_specs = [
        part if value.shape[0] == count else pl.BlockSpec((1, width), lambda i: (0, 0))
        for value in values
    ]
    out_specs = [part for _ in out_types]
    out_shape = [jax.ShapeDtypeStruct((count, width), kind) for kind in out_types]
    if sums:
        out_specs.append(pl.BlockSpec((8, width), lambda i: (0, 0)))
        out_shape.append(jax.ShapeDtypeStruct((8, width), FULL))
    return pl.pallas_call(
        kernel,
        grid=(count // chunk,),
        in_specs=in_specs,
        out_specs=out_specs,
        out_shape=out_shape,
        compiler_params=pltpu.CompilerParams(vmem_limit_bytes=16 << 20),
        name=name,
    )(*values)


def joint_kernel(mine_ref, other_ref, weight_ref, bias_ref, out_ref):
    half = mine_ref.shape[1]
    out = product(mine_ref[...], weight_ref[:half], PLAIN)
    out += product(other_ref[...], weight_ref[half:], PLAIN)
    out_ref[...] = (out + bias_ref[...]).astype(LOW)


def joint_projection(mine, other, weight, bias):
    count, half = mine.shape
    columns = weight.shape[1]
    chunk = row_chunk(count, 784)
    part = pl.BlockSpec((chunk, half), lambda i: (i, 0))
    return pl.pallas_call(
        joint_kernel,
        grid=(count // chunk,),
        in_specs=[
            part,
            part,
            pl.BlockSpec(weight.shape, lambda i: (0, 0)),
            pl.BlockSpec((1, columns), lambda i: (0, 0)),
        ],
        out_specs=pl.BlockSpec((chunk, columns), lambda i: (i, 0)),
        out_shape=jax.ShapeDtypeStruct((count, columns), LOW),
        compiler_params=pltpu.CompilerParams(vmem_limit_bytes=40 << 20),
        name="joint_projection",
    )(mine, other, weight, bias)


def rows_kernel(left_ref, right_ref, out_ref):
    out_ref[...] = product(left_ref[...], right_ref[...], ROW_BY_ROW).astype(LOW)


def rows_product(left, right, name):
    count, depth = left.shape
    columns = right.shape[0]
    chunk = row_chunk(count, 400)
    return pl.pallas_call(
        rows_kernel,
        grid=(count // chunk,),
        in_specs=[
            pl.BlockSpec((chunk, depth), lambda i: (i, 0)),
            pl.BlockSpec((columns, depth), lambda i: (0, 0)),
        ],
        out_specs=pl.BlockSpec((chunk, columns), lambda i: (i, 0)),
        out_shape=jax.ShapeDtypeStruct((count, columns), LOW),
        compiler_params=pltpu.CompilerParams(vmem_limit_bytes=48 << 20),
        name=name,
    )(left, right)


def grad_kernel(distances, place_ref, *refs):
    lefts, (right_ref, out_ref) = refs[:-2], refs[-2:]
    left = lefts[0][...]
    if len(lefts) == 2:
        slot = place_ref[0] ^ distance_at(distances, pl.program_id(0))
        left = jnp.where((slot >> 1) == 0, left, lefts[1][...])
    out_ref[0] = product(left, right_ref[...], COLUMN_BY_COLUMN).astype(LOW)


def distance_at(distances, step):
    if len(distances) == 1:
        return distances[0]
    return distances[0] + step * (distances[1] - distances[0])


def grad_products(lefts, right, place, distances, name):
    tokens_here, columns = right.shape
    quarter = sum(left.shape[1] for left in lefts) // 4
    blocks = lefts[0].shape[1] // quarter

    def left_at(i, place):
        return (0, (place[0] ^ distance_at(distances, i)) & (blocks - 1))

    return pl.pallas_call(
        lambda *refs: grad_kernel(distances, *refs),
        grid_spec=pltpu.PrefetchScalarGridSpec(
            num_scalar_prefetch=1,
            grid=(len(distances),),
            in_specs=[pl.BlockSpec((tokens_here, quarter), left_at) for _ in lefts]
            + [pl.BlockSpec((tokens_here, columns), lambda i, place: (0, 0))],
            out_specs=pl.BlockSpec((1, quarter, columns), lambda i, place: (i, 0, 0)),
        ),
        out_shape=jax.ShapeDtypeStruct((len(distances), quarter, columns), LOW),
        compiler_params=pltpu.CompilerParams(vmem_limit_bytes=48 << 20),
        name=name,
    )(place.astype(jnp.int32).reshape(1), *lefts, right)


def attention_forward_kernel(q_ref, k_ref, v_ref, o_ref, lse_ref):
    count, width = q_ref.shape
    rows = row_chunk(count, 256)
    lane = lax.broadcasted_iota(jnp.int32, (rows, width), 1)
    k = k_ref[...]
    v = v_ref[...]
    units = [(start, head) for start in range(0, count, rows) for head in range(width // HEAD_DIM)]

    def scores_of(unit):
        start, head = unit
        q = q_ref[start : start + rows] * jnp.asarray(HEAD_DIM ** (-0.5), LOW)
        return product(jnp.where((lane // HEAD_DIM) == head, q, jnp.zeros_like(q)), k, ROW_BY_ROW)

    logs = []
    ahead = scores_of(units[0])
    for step, (start, head) in enumerate(units):
        scores = ahead
        if step + 1 < len(units):
            ahead = scores_of(units[step + 1])
        top = jnp.max(scores, axis=-1, keepdims=True)
        weights = jnp.exp(scores - top)
        total = jnp.sum(weights, axis=-1, keepdims=True)
        part = product(weights.astype(LOW), v, PLAIN) / total
        if head == 0:
            out = part
            logs.append(jnp.zeros((rows, width), FULL))
        else:
            out = jnp.where((lane // HEAD_DIM) == head, part, out)
            o_ref[start : start + rows] = out.astype(LOW)
        logs[-1] = jnp.where(lane == head, top + jnp.log(total), logs[-1])
    lse_ref[...] = jnp.concatenate(logs, axis=0).T[: lse_ref.shape[0]]


def attention_forward(joint, pair):
    count, columns = joint.shape
    width = 2 * HEAD_DIM
    kind = columns // (3 * width)
    return pl.pallas_call(
        attention_forward_kernel,
        grid=(1,),
        in_specs=[
            pl.BlockSpec((count, width), lambda i: (0, pair)),
            pl.BlockSpec((count, width), lambda i: (0, kind + pair)),
            pl.BlockSpec((count, width), lambda i: (0, 2 * kind + pair)),
        ],
        out_specs=[
            pl.BlockSpec((count, width), lambda i: (0, 0)),
            pl.BlockSpec((8, count), lambda i: (0, 0)),
        ],
        out_shape=[
            jax.ShapeDtypeStruct((count, width), LOW),
            jax.ShapeDtypeStruct((8, count), FULL),
        ],
        compiler_params=pltpu.CompilerParams(vmem_limit_bytes=48 << 20),
        name="attention_forward",
    )(joint, joint, joint)


def attention_backward_kernel(
    q_ref, k_ref, v_ref, da_ref, o_ref, lse_ref, dq_ref, dk_ref, dv_ref,
    q_heads, da_heads, delta_ref, dq_total,
):
    count, width = q_ref.shape
    rows = row_chunk(count, 256)
    heads = width // HEAD_DIM
    scale = jnp.asarray(HEAD_DIM ** (-0.5), LOW)

    lane = lax.broadcasted_iota(jnp.int32, (count, width), 1)
    delta = jnp.zeros((count, width), FULL)
    q = q_ref[...] * scale
    da = da_ref[...]
    both_rows = da.astype(FULL) * o_ref[...].astype(FULL)
    for head in range(heads):
        mask = (lane // HEAD_DIM) == head
        q_heads[head] = jnp.where(mask, q, jnp.zeros_like(q))
        da_heads[head] = jnp.where(mask, da, jnp.zeros_like(da))
        row = jnp.sum(jnp.where(mask, both_rows, 0.0), axis=-1, keepdims=True)
        delta = jnp.where(lane == head, row, delta)
    delta_ref[...] = delta.T[:8]
    dq_total[...] = jnp.zeros_like(dq_total)

    lane = lax.broadcasted_iota(jnp.int32, (rows, width), 1)
    for start in range(0, count, rows):
        k = k_ref[start : start + rows]
        v = v_ref[start : start + rows]
        scaled_k = k * scale
        dk = dv = None
        for head in range(heads):
            q = q_heads[head]
            da = da_heads[head]
            probs = jnp.exp(product(k, q, ROW_BY_ROW) - lse_ref[head : head + 1, :])
            slope = probs * (product(v, da, ROW_BY_ROW) - delta_ref[head : head + 1, :])
            slope = slope.astype(LOW)
            dv_part = product(probs.astype(LOW), da, PLAIN)
            dk_part = product(slope, q, PLAIN)
            dv = dv_part if dv is None else dv + dv_part
            dk = dk_part if dk is None else dk + dk_part
            one_k = jnp.where((lane // HEAD_DIM) == head, scaled_k, jnp.zeros_like(k))
            dq_total[...] += product(slope, one_k, COLUMN_BY_COLUMN)
        dk_ref[start : start + rows] = dk.astype(LOW)
        dv_ref[start : start + rows] = dv.astype(LOW)
    dq_ref[...] = dq_total[...].astype(LOW)


def attention_backward(joint, da, out, lse, pair):
    count, columns = joint.shape
    width = 2 * HEAD_DIM
    kind = columns // (3 * width)
    alone = pl.BlockSpec((count, width), lambda i: (0, 0))
    grad = jax.ShapeDtypeStruct((count, width), LOW)
    return pl.pallas_call(
        attention_backward_kernel,
        grid=(1,),
        in_specs=[
            pl.BlockSpec((count, width), lambda i: (0, pair)),
            pl.BlockSpec((count, width), lambda i: (0, kind + pair)),
            pl.BlockSpec((count, width), lambda i: (0, 2 * kind + pair)),
            alone,
            alone,
            pl.BlockSpec((8, count), lambda i: (0, 0)),
        ],
        out_specs=[alone, alone, alone],
        out_shape=[grad, grad, grad],
        scratch_shapes=[
            pltpu.VMEM((2, count, width), LOW),
            pltpu.VMEM((2, count, width), LOW),
            pltpu.VMEM((8, count), FULL),
            pltpu.VMEM((count, width), FULL),
        ],
        compiler_params=pltpu.CompilerParams(vmem_limit_bytes=48 << 20),
        name="attention_backward",
    )(joint, joint, joint, da, out, lse)


def put_together(place_ref, whole_ref, piece_refs):
    for piece, piece_ref in enumerate(piece_refs):
        rows = piece_ref.shape[0]
        start = pl.multiple_of(place_ref[piece], rows)
        whole_ref[pl.ds(start, rows), :] = piece_ref[...]


def feed_forward_kernel(pieces, place_ref, normed_ref, slope_ref, bias_ref, *refs):
    active_ref, expand_slope_ref, back_ref, bias_grad_ref = refs[2 * pieces : 2 * pieces + 4]
    total, expand_ref, reduce_ref = refs[2 * pieces + 4 :]
    put_together(place_ref, expand_ref, refs[:pieces])
    put_together(place_ref, reduce_ref, refs[pieces : 2 * pieces])
    step = pl.program_id(0)
    count = normed_ref.shape[0]
    half = count // 2
    bias_grad = None
    for rows in (slice(0, half), slice(half, count)):
        hidden = product(normed_ref[rows], expand_ref[...], PLAIN) + bias_ref[...]
        upstream = product(slope_ref[rows], reduce_ref[...], PLAIN)
        share = 0.5 * (1.0 + lax.erf(hidden * (0.5**0.5)))
        active_ref[rows] = (hidden * share).astype(LOW)
        density = jnp.exp(-0.5 * hidden * hidden) * 0.3989422804014327
        slope = (upstream * (share + hidden * density)).astype(LOW)
        expand_slope_ref[rows] = slope
        part = jnp.sum(slope.astype(FULL), axis=0, keepdims=True)
        bias_grad = part if bias_grad is None else bias_grad + part
        back = product(slope, expand_ref[...], ROW_BY_ROW)

        @pl.when(step == 0)
        def _():
            total[rows] = back

        @pl.when(step > 0)
        def _():
            total[rows] += back

    bias_grad_ref[...] = bias_grad

    @pl.when(step == pl.num_programs(0) - 1)
    def _():
        back_ref[...] = total[...].astype(LOW)


def feed_forward(normed, slope, bias, expand, reduce, place):
    count, width = normed.shape
    hidden = bias.shape[1]
    block = 512 if hidden % 512 == 0 else hidden
    whole = pl.BlockSpec((count, width), lambda i, place: (0, 0))
    out = pl.BlockSpec((count, block), lambda i, place: (0, i))
    row = pl.BlockSpec((1, block), lambda i, place: (0, i))
    return pl.pallas_call(
        lambda *refs: feed_forward_kernel(len(reduce), *refs),
        grid_spec=pltpu.PrefetchScalarGridSpec(
            num_scalar_prefetch=1,
            grid=(hidden // block,),
            in_specs=[whole, whole, row]
            + [
                pl.BlockSpec((piece.shape[0], block), lambda i, place: (0, i))
                for piece in [*expand, *reduce]
            ],
            out_specs=[out, out, whole, row],
            scratch_shapes=[
                pltpu.VMEM((count, width), FULL),
                pltpu.VMEM((width, block), LOW),
                pltpu.VMEM((width, block), LOW),
            ],
        ),
        out_shape=[
            jax.ShapeDtypeStruct((count, hidden), LOW),
            jax.ShapeDtypeStruct((count, hidden), LOW),
            jax.ShapeDtypeStruct((count, width), LOW),
            jax.ShapeDtypeStruct((1, hidden), FULL),
        ],
        compiler_params=pltpu.CompilerParams(vmem_limit_bytes=44 << 20),
        name="feed_forward",
    )(place, normed, slope, bias, *expand, *reduce)


def reduce_kernel(place_ref, active_ref, *refs):
    out_ref, total, reduce_ref = refs[-3:]
    put_together(place_ref, reduce_ref, refs[:-3])
    part = product(active_ref[...], reduce_ref[...], ROW_BY_ROW)

    @pl.when(pl.program_id(0) == 0)
    def _():
        total[...] = part

    @pl.when(pl.program_id(0) > 0)
    def _():
        total[...] += part

    @pl.when(pl.program_id(0) == pl.num_programs(0) - 1)
    def _():
        out_ref[...] = total[...].astype(LOW)


def reduce_output(active, reduce, place):
    count, hidden = active.shape
    width = sum(piece.shape[0] for piece in reduce)
    block = 512 if hidden % 512 == 0 else hidden
    return pl.pallas_call(
        reduce_kernel,
        grid_spec=pltpu.PrefetchScalarGridSpec(
            num_scalar_prefetch=1,
            grid=(hidden // block,),
            in_specs=[pl.BlockSpec((count, block), lambda i, place: (0, i))]
            + [
                pl.BlockSpec((piece.shape[0], block), lambda i, place: (0, i)) for piece in reduce
            ],
            out_specs=pl.BlockSpec((count, width), lambda i, place: (0, 0)),
            scratch_shapes=[pltpu.VMEM((count, width), FULL), pltpu.VMEM((width, block), LOW)],
        ),
        out_shape=jax.ShapeDtypeStruct((count, width), LOW),
        compiler_params=pltpu.CompilerParams(vmem_limit_bytes=32 << 20),
        name="reduce_output",
    )(place, active, *reduce)


def swap(value, axis, distance):
    size = lax.axis_size(axis)
    return lax.ppermute(value, axis, [(i, i ^ distance) for i in range(size)])


def fence(*values):
    return lax.optimization_barrier(values)


def gather_near(rows_here):
    if lax.axis_size("fsdp") != 4:
        return (lax.all_gather(rows_here, "fsdp", axis=0, tiled=True),)
    return (rows_here, swap(rows_here, "fsdp", 1), swap(rows_here, "fsdp", 2))


def far_of(held):
    if len(held) == 1:
        return ()
    half = held[0].shape[0] // 2
    return (held[2][:half], held[1][half:])


def send_far(leaves):
    return (swap(leaves[0], "fsdp", 1), swap(leaves[1], "fsdp", 2)) if leaves else ()


def gather_far(held):
    return held + send_far(far_of(held))


def place_near(held):
    if len(held) == 1:
        return held[0]
    rows_here, near, side = held[:3]
    me = lax.axis_index("fsdp")
    count, width = rows_here.shape
    out = jnp.zeros((4 * count, width), rows_here.dtype)
    out = lax.dynamic_update_slice(out, rows_here, (me * count, 0))
    out = lax.dynamic_update_slice(out, near, ((me ^ 1) * count, 0))
    return lax.dynamic_update_slice(out, side, ((me ^ 2) * count, 0))


def place_far(out, held):
    if len(held) == 1:
        return out
    far_top, far_low = held[3:]
    half = far_top.shape[0]
    start = (lax.axis_index("fsdp") ^ 3) * 2 * half
    out = lax.dynamic_update_slice(out, far_top, (start, 0))
    return lax.dynamic_update_slice(out, far_low, (start + half, 0))


def far_halves(far):
    half = far.shape[0] // 2
    return (swap(far[:half], "fsdp", 1), swap(far[half:], "fsdp", 2))


def add_far(near, side, far):
    half = near.shape[0] // 2
    near = jnp.concatenate([near[:half], both((near[half:], far[1])).astype(LOW)], axis=0)
    side = jnp.concatenate([both((side[:half], far[0])).astype(LOW), side[half:]], axis=0)
    return (near, side)


def near_rows_out(pair):
    return (swap(pair[0], "fsdp", 1), swap(pair[1], "fsdp", 2))


def halves(value, bit):
    half = value.shape[0] // 2
    keep = lax.dynamic_slice_in_dim(value, bit * half, half, 0)
    send = lax.dynamic_slice_in_dim(value, (1 - bit) * half, half, 0)
    return keep, send.astype(LOW)


def split_rows(value, bit, distance):
    keep, send = halves(value, bit)
    return keep, swap(send, "ctx", distance)


def both(pair):
    return pair[0].astype(FULL) + pair[1].astype(FULL)


def join_rows(value, bit, distance):
    other = swap(value, "ctx", distance)
    return jnp.where(
        bit == 0,
        jnp.concatenate([value, other], axis=0),
        jnp.concatenate([other, value], axis=0),
    )


def pairwise(pieces):
    return (pieces[0] + pieces[1]) + (pieces[2] + pieces[3])


def swapped_if(bit, pair):
    return [jnp.where(bit == 0, pair[0], pair[1]), jnp.where(bit == 0, pair[1], pair[0])]


def per_device(
    tokens,
    clip_mask,
    cotangent,
    first_gain,
    first_shift,
    joint_weight,
    joint_bias,
    mixer_weight,
    mixer_bias,
    second_gain,
    second_shift,
    expand_weight,
    expand_bias,
    reduce_weight,
    reduce_bias,
):
    clips_here, rows_here, width = tokens.shape
    if lax.axis_size("ctx") != 4 or lax.axis_size("tp") != 2 or clips_here != 2:
        raise ValueError("mesh")
    shard = lax.axis_index("fsdp")
    block = lax.axis_index("ctx")
    core = lax.axis_index("tp")
    clip_at = block >> 1
    part_at = block & 1
    width_half = width // 2
    quarter = width_half // 2
    features = joint_weight.shape[2]
    part_width = features // 2
    pair_width = 2 * HEAD_DIM
    tokens_here = clips_here * rows_here

    flat_tokens = tokens.reshape(tokens_here, width)
    (first_normed,) = by_rows(
        first_norm_kernel, "first_norm", [LOW], False,
        flat_tokens, first_gain[None], first_shift[None],
    )
    first_normed = first_normed.reshape(clips_here, rows_here, width)
    mine = lax.dynamic_slice_in_dim(first_normed, core * width_half, width_half, 2)
    other_side = lax.dynamic_slice_in_dim(first_normed, (1 - core) * width_half, width_half, 2)
    own_clip = lax.dynamic_index_in_dim(mine, clip_at, 0, False)
    own_other = lax.dynamic_index_in_dim(other_side, clip_at, 0, False)
    other_clip = lax.dynamic_index_in_dim(mine, 1 - clip_at, 0, False)
    joint_part = lax.dynamic_slice_in_dim(joint_weight, part_at * part_width, part_width, 2)
    both_parts = jnp.concatenate([joint_part[:, kind] for kind in range(3)] + [mixer_weight], axis=1)

    own_clip, left, right, both_parts = fence(
        own_clip, other_clip[:, :quarter], other_clip[:, quarter:], both_parts
    )
    near_rows = swap(own_clip, "ctx", 1)
    across_left = swap(left, "ctx", 2)
    far_right = swap(right, "ctx", 3)
    held = gather_near(both_parts)

    near_rows, across_left, far_right, held, expand_weight = fence(
        near_rows, across_left, far_right, held, expand_weight
    )
    passed = swap(jnp.concatenate([across_left, far_right], axis=1), "ctx", 1)
    held = gather_far(held)
    expand_held = gather_near(expand_weight)

    passed, held = fence(passed, held)
    cross_rows = jnp.concatenate(
        [
            near_rows,
            jnp.concatenate([across_left, passed[:, quarter:]], axis=1),
            jnp.concatenate([passed[:, :quarter], far_right], axis=1),
        ],
        axis=0,
    )
    cross_other = swap(cross_rows, "tp", 1)
    both_full = place_far(place_near(held), held)
    joint_columns = 3 * part_width
    joint_full = jnp.concatenate(
        [
            lax.dynamic_slice(both_full, (start * width_half, 0), (width_half, joint_columns))
            for start in (core, 1 - core)
        ],
        axis=0,
    )

    cross_other, joint_full, both_full, reduce_weight = fence(
        cross_other, joint_full, both_full, reduce_weight
    )
    mixer_full = both_full[:, joint_columns:]
    reduce_held = gather_near(reduce_weight)
    normed_mine = jnp.concatenate([own_clip, cross_rows], axis=0)
    normed_other = jnp.concatenate([own_other, cross_other], axis=0)
    bias_part = lax.dynamic_slice_in_dim(joint_bias, part_at * part_width, part_width, 1)
    bias_row = jnp.concatenate([bias_part[0], jnp.zeros_like(bias_part[0]), bias_part[1]])
    joint_out = joint_projection(normed_mine, normed_other, joint_full, bias_row[None])
    out_first, log_first = attention_forward(joint_out, 0)

    out_first, joint_out, mixer_full, expand_held = fence(
        out_first, joint_out, mixer_full, expand_held
    )
    first_blocks = out_first.reshape(4, rows_here, pair_width)
    arrived_first = [swap(first_blocks[d], "ctx", d) for d in (1, 2, 3)]
    out_second, log_second = attention_forward(joint_out, 1)

    out_second, arrived_first, reduce_held, expand_held = fence(
        out_second, arrived_first, reduce_held, expand_held
    )
    second_blocks = out_second.reshape(4, rows_here, pair_width)
    arrived_second = [swap(second_blocks[d], "ctx", d) for d in (1, 2, 3)]
    expand_held = gather_far(expand_held)

    arrived_second, expand_held, reduce_held, log_first, log_second = fence(
        arrived_second, expand_held, reduce_held, log_first, log_second
    )
    reduce_held = gather_far(reduce_held)
    arrived = [jnp.concatenate([first_blocks[0], second_blocks[0]], axis=1)] + [
        jnp.concatenate([one, two], axis=1) for one, two in zip(arrived_first, arrived_second)
    ]
    own_joined = jnp.concatenate(swapped_if(part_at, arrived[:2]), axis=1)
    other_joined = jnp.concatenate(swapped_if(part_at, arrived[2:]), axis=1)
    mixed_in = jnp.concatenate(swapped_if(clip_at, [own_joined, other_joined]), axis=0)
    mixer_part = product(mixed_in, mixer_full, ROW_BY_ROW).astype(LOW)
    mixer_swapped = swap(mixer_part, "tp", 1)
    mixer_row = mixer_bias[None]
    (second_normed,) = by_rows(
        second_norm_kernel, "second_norm", [LOW], False,
        flat_tokens, mixer_part, mixer_swapped, mixer_row, second_gain[None], second_shift[None],
    )
    valid = clip_mask.astype(FULL)[:, None, None]
    reduce_slope = (cotangent.astype(FULL) * valid).astype(LOW).reshape(tokens_here, width)
    reduce_bias_grad = jnp.sum(reduce_slope.astype(FULL), axis=0)

    second_normed, reduce_slope, reduce_held = fence(second_normed, reduce_slope, reduce_held)
    four = lax.axis_size("fsdp") == 4
    start = jnp.zeros((), jnp.int32)
    if four:
        rows = width // 4
        pieces_at = jnp.stack([shard, shard ^ 1, shard ^ 2, shard ^ 3, shard ^ 3]) * rows
        pieces_at = pieces_at.astype(jnp.int32) + jnp.array([0, 0, 0, 0, rows // 2], jnp.int32)
    else:
        pieces_at = start.reshape(1)
    activated, expand_slope, second_part, expand_bias_grad = feed_forward(
        second_normed, reduce_slope, expand_bias[None], expand_held, reduce_held, pieces_at
    )
    expand_bias_grad = expand_bias_grad[0]

    second_swapped = swap(second_part, "tp", 1)
    place, order = (shard, (3, 2, 1, 0)) if four else (start, (0, 1, 2, 3))
    expand_parts = grad_products([second_normed], expand_slope, place, order, "expand_grad")
    second_swapped, expand_parts = fence(second_swapped, expand_parts)
    expand_far = far_halves(expand_parts[0]) if four else ()
    mixer_slope, first_sum_back, second_sums = by_rows(
        second_norm_back_kernel, "second_norm_back", [LOW, FULL], True,
        flat_tokens, mixer_part, mixer_swapped, mixer_row, second_gain[None],
        second_part, second_swapped, reduce_slope,
    )
    attended_slope = product(mixer_slope, mixer_full, PLAIN).astype(LOW)

    leaving = []
    for pair in range(2):
        for distance in range(4):
            to = block ^ distance
            corner = ((to >> 1) * rows_here, (to & 1) * part_width + pair * pair_width)
            leaving.append(lax.dynamic_slice(attended_slope, corner, (rows_here, pair_width)))
    expand_near = add_far(expand_parts[2], expand_parts[1], expand_far) if four else ()
    leaving, mixer_slope, mixed_in, activated, expand_near = fence(
        leaving, mixer_slope, mixed_in, activated, expand_near
    )
    slope_first = [leaving[0]] + [swap(leaving[d], "ctx", d) for d in (1, 2, 3)]
    if four:
        expand_near = near_rows_out(expand_near)
    reduce_parts = grad_products([reduce_slope], activated, place, order, "reduce_grad")
    mixer_parts = grad_products([mixer_slope], mixed_in, place, order, "mixer_grad")
    wide = jnp.concatenate([reduce_parts, mixer_parts], axis=2)
    if four:
        half = width // 8
        far_top, far_low = wide[0][:half], wide[0][half:]
        wide_early = (wide[2][:half], wide[1][half:])
    else:
        far_top, far_low, wide_early = (), (), ()

    slope_first, leaving, expand_near, far_top, far_low = fence(
        slope_first, leaving, expand_near, far_top, far_low
    )
    slope_second = [leaving[4]] + [swap(leaving[4 + d], "ctx", d) for d in (1, 2, 3)]
    wide_far = (swap(far_top, "fsdp", 1), swap(far_low, "fsdp", 2)) if four else ()
    grad_first = attention_backward(
        joint_out, jnp.concatenate(slope_first, axis=0), out_first, log_first, 0
    )

    grad_first, slope_second, wide_far = fence(grad_first, slope_second, wide_far)
    if four:
        expand_sum = expand_parts[3].astype(FULL) + both(expand_near)
        wide_late = (
            both((wide[2][half:], wide_far[1])).astype(LOW),
            both((wide[1][:half], wide_far[0])).astype(LOW),
        )
    else:
        wide_late = ()
        expand_sum = lax.psum_scatter(
            expand_parts.reshape(width, -1), "fsdp", scatter_dimension=0, tiled=True
        ).astype(FULL)
    expand_keep, expand_send = halves(expand_sum, part_at)
    slope_second = jnp.concatenate(slope_second, axis=0)
    expand_send, slope_second, wide_early, wide_late = fence(
        expand_send, slope_second, wide_early, wide_late
    )
    if four:
        wide_early = near_rows_out(wide_early)
    expand_rows = (expand_keep, swap(expand_send, "ctx", 1))
    grad_second = attention_backward(joint_out, slope_second, out_second, log_second, 1)

    grad_second, expand_rows, wide_early, wide_late = fence(
        grad_second, expand_rows, wide_early, wide_late
    )
    if four:
        wide_late = near_rows_out(wide_late)
    expand_rows = split_rows(both(expand_rows), clip_at, 2)
    joint_slope = jnp.concatenate(
        [grad[kind] for kind in range(3) for grad in (grad_first, grad_second)], axis=1
    )
    first_there = product(joint_slope, joint_full[width_half:], ROW_BY_ROW).astype(LOW)
    first_here = rows_product(joint_slope, joint_full[:width_half], "first_slope")
    first_half = both((first_here, swap(first_there, "tp", 1))).astype(LOW)

    if not four:
        wide_near = lax.psum_scatter(
            wide.reshape(width, -1), "fsdp", scatter_dimension=0, tiled=True
        )
    first_half, joint_slope, expand_rows, wide_late = fence(
        first_half, joint_slope, expand_rows, wide_late
    )
    expand_rows = join_rows(both(expand_rows).astype(LOW), clip_at, 2)
    pieces = first_half.reshape(4, rows_here, width_half)
    passing = jnp.concatenate([pieces[1], pieces[3][:, :quarter], pieces[2][:, quarter:]], axis=1)
    passing = swap(passing, "ctx", 1)
    place = (shard if four else start) ^ (2 * core)
    joint_parts = grad_products([normed_mine, normed_other], joint_slope, place, order, "joint_grad")
    if four:
        near_sum = [both((wide_early[0], wide_late[1])), both((wide_late[0], wide_early[1]))]
        wide_sum = wide[3].astype(FULL) + jnp.concatenate(near_sum, axis=0)
    else:
        wide_sum = wide_near.astype(FULL)
    wide_keep, wide_send = halves(wide_sum, part_at)
    joint_parts, wide_send = fence(joint_parts, wide_send)
    joint_far = far_halves(joint_parts[0]) if four else ()
    slope_sums = jnp.sum(joint_slope.astype(FULL), axis=0)
    bias_sums = jnp.stack([slope_sums[:part_width], slope_sums[2 * part_width :]])
    joint_bias_grad = lax.dynamic_update_slice(
        jnp.zeros((2, features), FULL), bias_sums, (0, part_at * part_width)
    )

    passing, joint_far = fence(passing, joint_far)
    own_half = both((pieces[0], passing[:, :width_half])).astype(LOW)
    to_left = both((pieces[2][:, :quarter], passing[:, width_half : width_half + quarter]))
    to_right = both((pieces[3][:, quarter:], passing[:, width_half + quarter :]))
    joint_near = add_far(joint_parts[2], joint_parts[1], joint_far) if four else ()
    to_left, to_right, own_half, wide_send, joint_near, activated = fence(
        to_left.astype(LOW), to_right.astype(LOW), own_half, wide_send, joint_near, activated
    )
    other_half = jnp.concatenate([swap(to_left, "ctx", 2), swap(to_right, "ctx", 3)], axis=1)
    wide_rows = (wide_keep, swap(wide_send, "ctx", 1))
    if four:
        joint_near = near_rows_out(joint_near)
    else:
        joint_near = lax.psum_scatter(
            joint_parts.reshape(width, -1), "fsdp", scatter_dimension=0, tiled=True
        )
    reduce_part = reduce_output(activated, reduce_held, pieces_at)

    other_half, joint_near, wide_rows, reduce_part, expand_rows = fence(
        other_half, joint_near, wide_rows, reduce_part, expand_rows
    )
    slope_half = jnp.concatenate(swapped_if(clip_at, [own_half, other_half]), axis=0)
    slope_other = swap(slope_half, "tp", 1)
    first_slope = jnp.concatenate(swapped_if(core, [slope_half, slope_other]), axis=1)
    wide_rows = split_rows(both(wide_rows), clip_at, 2)
    reduce_swapped = swap(reduce_part, "tp", 1)
    joint_sum = joint_parts[3].astype(FULL) + both(joint_near) if four else joint_near
    joint_sum = joint_sum.astype(LOW)
    joint_sum = (joint_sum, swap(joint_sum, "ctx", 2))
    tokens_grad, first_sums = by_rows(
        first_norm_back_kernel, "first_norm_back", [FULL], True,
        flat_tokens, first_slope, first_gain[None],
        cotangent.reshape(tokens_here, width), first_sum_back,
    )
    first_sums, tokens_grad, reduce_swapped = fence(first_sums, tokens_grad, reduce_swapped)
    vectors = [
        first_sums[0],
        first_sums[1],
        joint_bias_grad[0],
        joint_bias_grad[1],
        second_sums[2],
        second_sums[0],
        second_sums[1],
        expand_bias_grad,
        reduce_bias_grad,
    ]
    packed = jnp.concatenate(vectors).reshape(-1, 128)
    packed_pieces = [packed] + [swap(packed, "ctx", d) for d in (1, 2, 3)]
    reduce_out = both((reduce_part, reduce_swapped)) + reduce_bias
    mixer_out = both((mixer_part, mixer_swapped)) + mixer_bias
    branches = (mixer_out + reduce_out).reshape(clips_here, rows_here, width)
    result = (tokens.astype(FULL) + valid * branches).astype(LOW)

    packed_pieces, joint_sum, wide_rows, result = fence(
        packed_pieces, joint_sum, wide_rows, result
    )
    packed = pairwise(packed_pieces)
    if four:
        packed = pairwise([packed] + [swap(packed, "fsdp", d) for d in (1, 2, 3)])
    else:
        packed = lax.psum(packed, "fsdp")
    joint_sum = both(joint_sum).astype(LOW)
    joint_parts = swapped_if(part_at, [joint_sum, swap(joint_sum, "ctx", 1)])
    joint_grad = jnp.concatenate(
        [piece.reshape(-1, 3, part_width) for piece in joint_parts], axis=2
    ).astype(FULL)
    wide_rows = join_rows(both(wide_rows).astype(LOW), clip_at, 2)
    wide_rows = join_rows(wide_rows, part_at, 1).astype(FULL)
    reduce_grad = wide_rows[:, : activated.shape[1]]
    mixer_grad = wide_rows[:, activated.shape[1] :]
    expand_grad = join_rows(expand_rows, part_at, 1).astype(FULL)
    packed = packed.reshape(-1)
    shares = []
    start = 0
    for vector in vectors:
        share = vector.shape[0] // lax.axis_size("fsdp")
        shares.append(lax.dynamic_slice_in_dim(packed, start + shard * share, share, 0))
        start += vector.shape[0]

    shape = (clips_here, rows_here, width)
    return (
        result,
        tokens_grad.reshape(shape),
        shares[0],
        shares[1],
        joint_grad,
        jnp.stack([shares[2], shares[3]]),
        mixer_grad,
        shares[4],
        shares[5],
        shares[6],
        expand_grad,
        shares[7],
        reduce_grad,
        shares[8],
    )


def solution(mesh):
    return jax.shard_map(
        per_device,
        mesh=mesh,
        in_specs=(
            P("fsdp", "ctx", None),
            P("fsdp"),
            P("fsdp", "ctx", None),
            P(),
            P(),
            P("fsdp", None, "tp"),
            P(None, "tp"),
            P("fsdp", "tp"),
            P(),
            P(),
            P(),
            P("fsdp", "tp"),
            P("tp"),
            P("fsdp", "tp"),
            P(),
        ),
        out_specs=(
            P("fsdp", "ctx", None),
            P("fsdp", "ctx", None),
            P("fsdp"),
            P("fsdp"),
            P("fsdp", None, "tp"),
            P(None, ("tp", "fsdp")),
            P("fsdp", "tp"),
            P("fsdp"),
            P("fsdp"),
            P("fsdp"),
            P("fsdp", "tp"),
            P(("tp", "fsdp")),
            P("fsdp", "tp"),
            P("fsdp"),
        ),
        check_vma=False,
    )
```

```python
import jax
import jax.numpy as jnp
from jax import lax
from jax.experimental import pallas as pl
from jax.experimental.pallas import tpu as pltpu
from jax.sharding import PartitionSpec as P

HEAD_DIM = 64
EPSILON = 1e-06
LOW = jnp.bfloat16
FULL = jnp.float32

ROW_BY_ROW = (((1,), (1,)), ((), ()))
PLAIN = (((1,), (0,)), ((), ()))
COLUMN_BY_COLUMN = (((0,), (0,)), ((), ()))


def product(left, right, dims):
    return lax.dot_general(left, right, dims, preferred_element_type=FULL)


def normalize(value_rows):
    center = value_rows - jnp.mean(value_rows, axis=-1, keepdims=True)
    inverse = lax.rsqrt(jnp.mean(center * center, axis=-1, keepdims=True) + EPSILON)
    return (center * inverse, inverse)


def norm_back(upstream, gain, scaled, inverse):
    weighted = upstream * gain
    return inverse * (
        weighted
        - jnp.mean(weighted, axis=-1, keepdims=True)
        - scaled * jnp.mean(weighted * scaled, axis=-1, keepdims=True)
    )


def row_chunk(count, most):
    for chunk in range(most, 0, -16):
        if count % chunk == 0:
            return chunk
    raise ValueError("rows")


def first_norm_kernel(tokens_ref, gain_ref, shift_ref, out_ref):
    scaled, _ = normalize(tokens_ref[...].astype(FULL))
    out_ref[...] = (scaled * gain_ref[...] + shift_ref[...]).astype(LOW)


def second_norm_kernel(tokens_ref, one_ref, two_ref, bias_ref, gain_ref, shift_ref, out_ref):
    mixed = one_ref[...].astype(FULL) + two_ref[...].astype(FULL) + bias_ref[...]
    scaled, _ = normalize(tokens_ref[...].astype(FULL) + mixed)
    out_ref[...] = (scaled * gain_ref[...] + shift_ref[...]).astype(LOW)


def add_sums(ref, rows):
    sums = jnp.concatenate([jnp.sum(row, axis=0, keepdims=True) for row in rows], axis=0)

    @pl.when(pl.program_id(0) == 0)
    def _():
        ref[: len(rows)] = sums

    @pl.when(pl.program_id(0) > 0)
    def _():
        ref[: len(rows)] += sums


def second_norm_back_kernel(
    tokens_ref, one_ref, two_ref, bias_ref, gain_ref, left_ref, right_ref, outer_ref,
    slope_ref, back_ref, sums_ref,
):
    mixed = one_ref[...].astype(FULL) + two_ref[...].astype(FULL) + bias_ref[...]
    scaled, inverse = normalize(tokens_ref[...].astype(FULL) + mixed)
    upstream = left_ref[...].astype(FULL) + right_ref[...].astype(FULL)
    back = norm_back(upstream, gain_ref[...], scaled, inverse)
    slope = (outer_ref[...].astype(FULL) + back).astype(LOW)
    slope_ref[...] = slope
    back_ref[...] = back
    add_sums(sums_ref, [upstream * scaled, upstream, slope.astype(FULL)])


def first_norm_back_kernel(
    tokens_ref, upstream_ref, gain_ref, outer_ref, back_ref, out_ref, sums_ref
):
    scaled, inverse = normalize(tokens_ref[...].astype(FULL))
    upstream = upstream_ref[...].astype(FULL)
    back = norm_back(upstream, gain_ref[...], scaled, inverse)
    out_ref[...] = outer_ref[...].astype(FULL) + back_ref[...] + back
    add_sums(sums_ref, [upstream * scaled, upstream])


def by_rows(kernel, name, out_types, sums, *values):
    count, width = values[0].shape
    chunk = row_chunk(count, 112)
    part = pl.BlockSpec((chunk, width), lambda i: (i, 0))
    in_specs = [
        part if value.shape[0] == count else pl.BlockSpec((1, width), lambda i: (0, 0))
        for value in values
    ]
    out_specs = [part for _ in out_types]
    out_shape = [jax.ShapeDtypeStruct((count, width), kind) for kind in out_types]
    if sums:
        out_specs.append(pl.BlockSpec((8, width), lambda i: (0, 0)))
        out_shape.append(jax.ShapeDtypeStruct((8, width), FULL))
    return pl.pallas_call(
        kernel,
        grid=(count // chunk,),
        in_specs=in_specs,
        out_specs=out_specs,
        out_shape=out_shape,
        compiler_params=pltpu.CompilerParams(vmem_limit_bytes=16 << 20),
        name=name,
    )(*values)


def joint_kernel(mine_ref, other_ref, weight_ref, bias_ref, out_ref):
    half = mine_ref.shape[1]
    out = product(mine_ref[...], weight_ref[:half], PLAIN)
    out += product(other_ref[...], weight_ref[half:], PLAIN)
    out_ref[...] = (out + bias_ref[...]).astype(LOW)


def joint_projection(mine, other, weight, bias):
    count, half = mine.shape
    columns = weight.shape[1]
    chunk = row_chunk(count, 784)
    part = pl.BlockSpec((chunk, half), lambda i: (i, 0))
    return pl.pallas_call(
        joint_kernel,
        grid=(count // chunk,),
        in_specs=[
            part,
            part,
            pl.BlockSpec(weight.shape, lambda i: (0, 0)),
            pl.BlockSpec((1, columns), lambda i: (0, 0)),
        ],
        out_specs=pl.BlockSpec((chunk, columns), lambda i: (i, 0)),
        out_shape=jax.ShapeDtypeStruct((count, columns), LOW),
        compiler_params=pltpu.CompilerParams(vmem_limit_bytes=40 << 20),
        name="joint_projection",
    )(mine, other, weight, bias)


def rows_kernel(left_ref, right_ref, out_ref):
    out_ref[...] = product(left_ref[...], right_ref[...], ROW_BY_ROW).astype(LOW)


def rows_product(left, right, name):
    count, depth = left.shape
    columns = right.shape[0]
    chunk = row_chunk(count, 400)
    return pl.pallas_call(
        rows_kernel,
        grid=(count // chunk,),
        in_specs=[
            pl.BlockSpec((chunk, depth), lambda i: (i, 0)),
            pl.BlockSpec((columns, depth), lambda i: (0, 0)),
        ],
        out_specs=pl.BlockSpec((chunk, columns), lambda i: (i, 0)),
        out_shape=jax.ShapeDtypeStruct((count, columns), LOW),
        compiler_params=pltpu.CompilerParams(vmem_limit_bytes=48 << 20),
        name=name,
    )(left, right)


def grad_kernel(distances, place_ref, *refs):
    lefts, (right_ref, out_ref) = refs[:-2], refs[-2:]
    left = lefts[0][...]
    if len(lefts) == 2:
        slot = place_ref[0] ^ distance_at(distances, pl.program_id(0))
        left = jnp.where((slot >> 1) == 0, left, lefts[1][...])
    out_ref[0] = product(left, right_ref[...], COLUMN_BY_COLUMN).astype(LOW)


def distance_at(distances, step):
    if len(distances) == 1:
        return distances[0]
    return distances[0] + step * (distances[1] - distances[0])


def grad_products(lefts, right, place, distances, name):
    tokens_here, columns = right.shape
    quarter = sum(left.shape[1] for left in lefts) // 4
    blocks = lefts[0].shape[1] // quarter

    def left_at(i, place):
        return (0, (place[0] ^ distance_at(distances, i)) & (blocks - 1))

    return pl.pallas_call(
        lambda *refs: grad_kernel(distances, *refs),
        grid_spec=pltpu.PrefetchScalarGridSpec(
            num_scalar_prefetch=1,
            grid=(len(distances),),
            in_specs=[pl.BlockSpec((tokens_here, quarter), left_at) for _ in lefts]
            + [pl.BlockSpec((tokens_here, columns), lambda i, place: (0, 0))],
            out_specs=pl.BlockSpec((1, quarter, columns), lambda i, place: (i, 0, 0)),
        ),
        out_shape=jax.ShapeDtypeStruct((len(distances), quarter, columns), LOW),
        compiler_params=pltpu.CompilerParams(vmem_limit_bytes=48 << 20),
        name=name,
    )(place.astype(jnp.int32).reshape(1), *lefts, right)


def attention_forward_kernel(q_ref, k_ref, v_ref, o_ref, lse_ref):
    count, width = q_ref.shape
    rows = row_chunk(count, 256)
    lane = lax.broadcasted_iota(jnp.int32, (rows, width), 1)
    k = k_ref[...]
    v = v_ref[...]
    units = [(start, head) for start in range(0, count, rows) for head in range(width // HEAD_DIM)]

    def scores_of(unit):
        start, head = unit
        q = q_ref[start : start + rows] * jnp.asarray(HEAD_DIM ** (-0.5), LOW)
        return product(jnp.where((lane // HEAD_DIM) == head, q, jnp.zeros_like(q)), k, ROW_BY_ROW)

    logs = []
    ahead = scores_of(units[0])
    for step, (start, head) in enumerate(units):
        scores = ahead
        if step + 1 < len(units):
            ahead = scores_of(units[step + 1])
        top = jnp.max(scores, axis=-1, keepdims=True)
        weights = jnp.exp(scores - top)
        total = jnp.sum(weights, axis=-1, keepdims=True)
        part = product(weights.astype(LOW), v, PLAIN) / total
        if head == 0:
            out = part
            logs.append(jnp.zeros((rows, width), FULL))
        else:
            out = jnp.where((lane // HEAD_DIM) == head, part, out)
            o_ref[start : start + rows] = out.astype(LOW)
        logs[-1] = jnp.where(lane == head, top + jnp.log(total), logs[-1])
    lse_ref[...] = jnp.concatenate(logs, axis=0).T[: lse_ref.shape[0]]


def attention_forward(joint, pair):
    count, columns = joint.shape
    width = 2 * HEAD_DIM
    kind = columns // (3 * width)
    return pl.pallas_call(
        attention_forward_kernel,
        grid=(1,),
        in_specs=[
            pl.BlockSpec((count, width), lambda i: (0, pair)),
            pl.BlockSpec((count, width), lambda i: (0, kind + pair)),
            pl.BlockSpec((count, width), lambda i: (0, 2 * kind + pair)),
        ],
        out_specs=[
            pl.BlockSpec((count, width), lambda i: (0, 0)),
            pl.BlockSpec((8, count), lambda i: (0, 0)),
        ],
        out_shape=[
            jax.ShapeDtypeStruct((count, width), LOW),
            jax.ShapeDtypeStruct((8, count), FULL),
        ],
        compiler_params=pltpu.CompilerParams(vmem_limit_bytes=48 << 20),
        name="attention_forward",
    )(joint, joint, joint)


def attention_backward_kernel(
    q_ref, k_ref, v_ref, da_ref, o_ref, lse_ref, dq_ref, dk_ref, dv_ref,
    q_heads, da_heads, delta_ref, dq_total,
):
    count, width = q_ref.shape
    rows = row_chunk(count, 256)
    heads = width // HEAD_DIM
    scale = jnp.asarray(HEAD_DIM ** (-0.5), LOW)

    lane = lax.broadcasted_iota(jnp.int32, (count, width), 1)
    delta = jnp.zeros((count, width), FULL)
    q = q_ref[...] * scale
    da = da_ref[...]
    both_rows = da.astype(FULL) * o_ref[...].astype(FULL)
    for head in range(heads):
        mask = (lane // HEAD_DIM) == head
        q_heads[head] = jnp.where(mask, q, jnp.zeros_like(q))
        da_heads[head] = jnp.where(mask, da, jnp.zeros_like(da))
        row = jnp.sum(jnp.where(mask, both_rows, 0.0), axis=-1, keepdims=True)
        delta = jnp.where(lane == head, row, delta)
    delta_ref[...] = delta.T[:8]
    dq_total[...] = jnp.zeros_like(dq_total)

    lane = lax.broadcasted_iota(jnp.int32, (rows, width), 1)
    for start in range(0, count, rows):
        k = k_ref[start : start + rows]
        v = v_ref[start : start + rows]
        scaled_k = k * scale
        dk = dv = None
        for head in range(heads):
            q = q_heads[head]
            da = da_heads[head]
            probs = jnp.exp(product(k, q, ROW_BY_ROW) - lse_ref[head : head + 1, :])
            slope = probs * (product(v, da, ROW_BY_ROW) - delta_ref[head : head + 1, :])
            slope = slope.astype(LOW)
            dv_part = product(probs.astype(LOW), da, PLAIN)
            dk_part = product(slope, q, PLAIN)
            dv = dv_part if dv is None else dv + dv_part
            dk = dk_part if dk is None else dk + dk_part
            one_k = jnp.where((lane // HEAD_DIM) == head, scaled_k, jnp.zeros_like(k))
            dq_total[...] += product(slope, one_k, COLUMN_BY_COLUMN)
        dk_ref[start : start + rows] = dk.astype(LOW)
        dv_ref[start : start + rows] = dv.astype(LOW)
    dq_ref[...] = dq_total[...].astype(LOW)


def attention_backward(joint, da, out, lse, pair):
    count, columns = joint.shape
    width = 2 * HEAD_DIM
    kind = columns // (3 * width)
    alone = pl.BlockSpec((count, width), lambda i: (0, 0))
    grad = jax.ShapeDtypeStruct((count, width), LOW)
    return pl.pallas_call(
        attention_backward_kernel,
        grid=(1,),
        in_specs=[
            pl.BlockSpec((count, width), lambda i: (0, pair)),
            pl.BlockSpec((count, width), lambda i: (0, kind + pair)),
            pl.BlockSpec((count, width), lambda i: (0, 2 * kind + pair)),
            alone,
            alone,
            pl.BlockSpec((8, count), lambda i: (0, 0)),
        ],
        out_specs=[alone, alone, alone],
        out_shape=[grad, grad, grad],
        scratch_shapes=[
            pltpu.VMEM((2, count, width), LOW),
            pltpu.VMEM((2, count, width), LOW),
            pltpu.VMEM((8, count), FULL),
            pltpu.VMEM((count, width), FULL),
        ],
        compiler_params=pltpu.CompilerParams(vmem_limit_bytes=48 << 20),
        name="attention_backward",
    )(joint, joint, joint, da, out, lse)


def put_together(place_ref, whole_ref, piece_refs):
    for piece, piece_ref in enumerate(piece_refs):
        rows = piece_ref.shape[0]
        start = pl.multiple_of(place_ref[piece], rows)
        whole_ref[pl.ds(start, rows), :] = piece_ref[...]


def feed_forward_kernel(pieces, place_ref, normed_ref, slope_ref, bias_ref, *refs):
    active_ref, expand_slope_ref, back_ref, bias_grad_ref = refs[2 * pieces : 2 * pieces + 4]
    total, expand_ref, reduce_ref = refs[2 * pieces + 4 :]
    put_together(place_ref, expand_ref, refs[:pieces])
    put_together(place_ref, reduce_ref, refs[pieces : 2 * pieces])
    step = pl.program_id(0)
    count = normed_ref.shape[0]
    half = count // 2
    bias_grad = None
    for rows in (slice(0, half), slice(half, count)):
        hidden = product(normed_ref[rows], expand_ref[...], PLAIN) + bias_ref[...]
        upstream = product(slope_ref[rows], reduce_ref[...], PLAIN)
        share = 0.5 * (1.0 + lax.erf(hidden * (0.5**0.5)))
        active_ref[rows] = (hidden * share).astype(LOW)
        density = jnp.exp(-0.5 * hidden * hidden) * 0.3989422804014327
        slope = (upstream * (share + hidden * density)).astype(LOW)
        expand_slope_ref[rows] = slope
        part = jnp.sum(slope.astype(FULL), axis=0, keepdims=True)
        bias_grad = part if bias_grad is None else bias_grad + part
        back = product(slope, expand_ref[...], ROW_BY_ROW)

        @pl.when(step == 0)
        def _():
            total[rows] = back

        @pl.when(step > 0)
        def _():
            total[rows] += back

    bias_grad_ref[...] = bias_grad

    @pl.when(step == pl.num_programs(0) - 1)
    def _():
        back_ref[...] = total[...].astype(LOW)


def feed_forward(normed, slope, bias, expand, reduce, place):
    count, width = normed.shape
    hidden = bias.shape[1]
    block = 512 if hidden % 512 == 0 else hidden
    whole = pl.BlockSpec((count, width), lambda i, place: (0, 0))
    out = pl.BlockSpec((count, block), lambda i, place: (0, i))
    row = pl.BlockSpec((1, block), lambda i, place: (0, i))
    return pl.pallas_call(
        lambda *refs: feed_forward_kernel(len(reduce), *refs),
        grid_spec=pltpu.PrefetchScalarGridSpec(
            num_scalar_prefetch=1,
            grid=(hidden // block,),
            in_specs=[whole, whole, row]
            + [
                pl.BlockSpec((piece.shape[0], block), lambda i, place: (0, i))
                for piece in [*expand, *reduce]
            ],
            out_specs=[out, out, whole, row],
            scratch_shapes=[
                pltpu.VMEM((count, width), FULL),
                pltpu.VMEM((width, block), LOW),
                pltpu.VMEM((width, block), LOW),
            ],
        ),
        out_shape=[
            jax.ShapeDtypeStruct((count, hidden), LOW),
            jax.ShapeDtypeStruct((count, hidden), LOW),
            jax.ShapeDtypeStruct((count, width), LOW),
            jax.ShapeDtypeStruct((1, hidden), FULL),
        ],
        compiler_params=pltpu.CompilerParams(vmem_limit_bytes=44 << 20),
        name="feed_forward",
    )(place, normed, slope, bias, *expand, *reduce)


def reduce_kernel(place_ref, active_ref, *refs):
    out_ref, total, reduce_ref = refs[-3:]
    put_together(place_ref, reduce_ref, refs[:-3])
    part = product(active_ref[...], reduce_ref[...], ROW_BY_ROW)

    @pl.when(pl.program_id(0) == 0)
    def _():
        total[...] = part

    @pl.when(pl.program_id(0) > 0)
    def _():
        total[...] += part

    @pl.when(pl.program_id(0) == pl.num_programs(0) - 1)
    def _():
        out_ref[...] = total[...].astype(LOW)


def reduce_output(active, reduce, place):
    count, hidden = active.shape
    width = sum(piece.shape[0] for piece in reduce)
    block = 512 if hidden % 512 == 0 else hidden
    return pl.pallas_call(
        reduce_kernel,
        grid_spec=pltpu.PrefetchScalarGridSpec(
            num_scalar_prefetch=1,
            grid=(hidden // block,),
            in_specs=[pl.BlockSpec((count, block), lambda i, place: (0, i))]
            + [
                pl.BlockSpec((piece.shape[0], block), lambda i, place: (0, i)) for piece in reduce
            ],
            out_specs=pl.BlockSpec((count, width), lambda i, place: (0, 0)),
            scratch_shapes=[pltpu.VMEM((count, width), FULL), pltpu.VMEM((width, block), LOW)],
        ),
        out_shape=jax.ShapeDtypeStruct((count, width), LOW),
        compiler_params=pltpu.CompilerParams(vmem_limit_bytes=32 << 20),
        name="reduce_output",
    )(place, active, *reduce)


def swap(value, axis, distance):
    size = lax.axis_size(axis)
    return lax.ppermute(value, axis, [(i, i ^ distance) for i in range(size)])


def fence(*values):
    return lax.optimization_barrier(values)


def gather_near(rows_here):
    if lax.axis_size("fsdp") != 4:
        return (lax.all_gather(rows_here, "fsdp", axis=0, tiled=True),)
    return (rows_here, swap(rows_here, "fsdp", 1), swap(rows_here, "fsdp", 2))


def far_of(held):
    if len(held) == 1:
        return ()
    half = held[0].shape[0] // 2
    return (held[2][:half], held[1][half:])


def send_far(leaves):
    return (swap(leaves[0], "fsdp", 1), swap(leaves[1], "fsdp", 2)) if leaves else ()


def gather_far(held):
    return held + send_far(far_of(held))


def place_near(held):
    if len(held) == 1:
        return held[0]
    rows_here, near, side = held[:3]
    me = lax.axis_index("fsdp")
    count, width = rows_here.shape
    out = jnp.zeros((4 * count, width), rows_here.dtype)
    out = lax.dynamic_update_slice(out, rows_here, (me * count, 0))
    out = lax.dynamic_update_slice(out, near, ((me ^ 1) * count, 0))
    return lax.dynamic_update_slice(out, side, ((me ^ 2) * count, 0))


def place_far(out, held):
    if len(held) == 1:
        return out
    far_top, far_low = held[3:]
    half = far_top.shape[0]
    start = (lax.axis_index("fsdp") ^ 3) * 2 * half
    out = lax.dynamic_update_slice(out, far_top, (start, 0))
    return lax.dynamic_update_slice(out, far_low, (start + half, 0))


def rows_at(matrices, distance):
    parts = []
    for matrix in matrices:
        count = matrix.shape[0] // 4
        start = (lax.axis_index("fsdp") ^ distance) * count
        parts.append(lax.dynamic_slice_in_dim(matrix, start, count, 0))
    return parts[0] if len(parts) == 1 else jnp.concatenate(parts, axis=1)


def far_halves(far):
    half = far.shape[0] // 2
    return (swap(far[:half], "fsdp", 1), swap(far[half:], "fsdp", 2))


def add_far(near, side, far):
    half = near.shape[0] // 2
    near = jnp.concatenate([near[:half], both((near[half:], far[1])).astype(LOW)], axis=0)
    side = jnp.concatenate([both((side[:half], far[0])).astype(LOW), side[half:]], axis=0)
    return (near, side)


def near_rows_out(pair):
    return (swap(pair[0], "fsdp", 1), swap(pair[1], "fsdp", 2))


def halves(value, bit):
    half = value.shape[0] // 2
    keep = lax.dynamic_slice_in_dim(value, bit * half, half, 0)
    send = lax.dynamic_slice_in_dim(value, (1 - bit) * half, half, 0)
    return keep, send.astype(LOW)


def split_rows(value, bit, distance):
    keep, send = halves(value, bit)
    return keep, swap(send, "ctx", distance)


def both(pair):
    return pair[0].astype(FULL) + pair[1].astype(FULL)


def join_rows(value, bit, distance):
    other = swap(value, "ctx", distance)
    return jnp.where(
        bit == 0,
        jnp.concatenate([value, other], axis=0),
        jnp.concatenate([other, value], axis=0),
    )


def pairwise(pieces):
    return (pieces[0] + pieces[1]) + (pieces[2] + pieces[3])


def swapped_if(bit, pair):
    return [jnp.where(bit == 0, pair[0], pair[1]), jnp.where(bit == 0, pair[1], pair[0])]


def per_device(
    tokens,
    clip_mask,
    cotangent,
    first_gain,
    first_shift,
    joint_weight,
    joint_bias,
    mixer_weight,
    mixer_bias,
    second_gain,
    second_shift,
    expand_weight,
    expand_bias,
    reduce_weight,
    reduce_bias,
):
    clips_here, rows_here, width = tokens.shape
    if lax.axis_size("ctx") != 4 or lax.axis_size("tp") != 2 or clips_here != 2:
        raise ValueError("mesh")
    shard = lax.axis_index("fsdp")
    block = lax.axis_index("ctx")
    core = lax.axis_index("tp")
    clip_at = block >> 1
    part_at = block & 1
    width_half = width // 2
    quarter = width_half // 2
    features = joint_weight.shape[2]
    part_width = features // 2
    pair_width = 2 * HEAD_DIM
    tokens_here = clips_here * rows_here

    flat_tokens = tokens.reshape(tokens_here, width)
    (first_normed,) = by_rows(
        first_norm_kernel, "first_norm", [LOW], False,
        flat_tokens, first_gain[None], first_shift[None],
    )
    first_normed = first_normed.reshape(clips_here, rows_here, width)
    mine = lax.dynamic_slice_in_dim(first_normed, core * width_half, width_half, 2)
    other_side = lax.dynamic_slice_in_dim(first_normed, (1 - core) * width_half, width_half, 2)
    own_clip = lax.dynamic_index_in_dim(mine, clip_at, 0, False)
    own_other = lax.dynamic_index_in_dim(other_side, clip_at, 0, False)
    other_clip = lax.dynamic_index_in_dim(mine, 1 - clip_at, 0, False)
    joint_part = lax.dynamic_slice_in_dim(joint_weight, part_at * part_width, part_width, 2)
    both_parts = jnp.concatenate([joint_part[:, kind] for kind in range(3)] + [mixer_weight], axis=1)

    own_clip, left, right, both_parts = fence(
        own_clip, other_clip[:, :quarter], other_clip[:, quarter:], both_parts
    )
    near_rows = swap(own_clip, "ctx", 1)
    across_left = swap(left, "ctx", 2)
    far_right = swap(right, "ctx", 3)
    held = gather_near(both_parts)

    near_rows, across_left, far_right, held, expand_weight = fence(
        near_rows, across_left, far_right, held, expand_weight
    )
    passed = swap(jnp.concatenate([across_left, far_right], axis=1), "ctx", 1)
    held = gather_far(held)
    expand_held = gather_near(expand_weight)

    passed, held = fence(passed, held)
    cross_rows = jnp.concatenate(
        [
            near_rows,
            jnp.concatenate([across_left, passed[:, quarter:]], axis=1),
            jnp.concatenate([passed[:, :quarter], far_right], axis=1),
        ],
        axis=0,
    )
    cross_other = swap(cross_rows, "tp", 1)
    both_full = place_far(place_near(held), held)
    joint_columns = 3 * part_width
    joint_full = jnp.concatenate(
        [
            lax.dynamic_slice(both_full, (start * width_half, 0), (width_half, joint_columns))
            for start in (core, 1 - core)
        ],
        axis=0,
    )

    cross_other, joint_full, both_full, reduce_weight = fence(
        cross_other, joint_full, both_full, reduce_weight
    )
    mixer_full = both_full[:, joint_columns:]
    reduce_held = gather_near(reduce_weight)
    normed_mine = jnp.concatenate([own_clip, cross_rows], axis=0)
    normed_other = jnp.concatenate([own_other, cross_other], axis=0)
    bias_part = lax.dynamic_slice_in_dim(joint_bias, part_at * part_width, part_width, 1)
    bias_row = jnp.concatenate([bias_part[0], jnp.zeros_like(bias_part[0]), bias_part[1]])
    joint_out = joint_projection(normed_mine, normed_other, joint_full, bias_row[None])
    out_first, log_first = attention_forward(joint_out, 0)

    out_first, joint_out, mixer_full, expand_held = fence(
        out_first, joint_out, mixer_full, expand_held
    )
    first_blocks = out_first.reshape(4, rows_here, pair_width)
    arrived_first = [swap(first_blocks[d], "ctx", d) for d in (1, 2, 3)]
    out_second, log_second = attention_forward(joint_out, 1)

    out_second, arrived_first, reduce_held, expand_held = fence(
        out_second, arrived_first, reduce_held, expand_held
    )
    second_blocks = out_second.reshape(4, rows_here, pair_width)
    arrived_second = [swap(second_blocks[d], "ctx", d) for d in (1, 2, 3)]
    expand_held = gather_far(expand_held)

    arrived_second, expand_held, reduce_held, log_first, log_second = fence(
        arrived_second, expand_held, reduce_held, log_first, log_second
    )
    reduce_held = gather_far(reduce_held)
    arrived = [jnp.concatenate([first_blocks[0], second_blocks[0]], axis=1)] + [
        jnp.concatenate([one, two], axis=1) for one, two in zip(arrived_first, arrived_second)
    ]
    own_joined = jnp.concatenate(swapped_if(part_at, arrived[:2]), axis=1)
    other_joined = jnp.concatenate(swapped_if(part_at, arrived[2:]), axis=1)
    mixed_in = jnp.concatenate(swapped_if(clip_at, [own_joined, other_joined]), axis=0)
    mixer_part = product(mixed_in, mixer_full, ROW_BY_ROW).astype(LOW)
    mixer_swapped = swap(mixer_part, "tp", 1)
    mixer_row = mixer_bias[None]
    (second_normed,) = by_rows(
        second_norm_kernel, "second_norm", [LOW], False,
        flat_tokens, mixer_part, mixer_swapped, mixer_row, second_gain[None], second_shift[None],
    )
    valid = clip_mask.astype(FULL)[:, None, None]
    reduce_slope = (cotangent.astype(FULL) * valid).astype(LOW).reshape(tokens_here, width)
    reduce_bias_grad = jnp.sum(reduce_slope.astype(FULL), axis=0)

    second_normed, reduce_slope, reduce_held = fence(second_normed, reduce_slope, reduce_held)
    four = lax.axis_size("fsdp") == 4
    start = jnp.zeros((), jnp.int32)
    if four:
        rows = width // 4
        pieces_at = jnp.stack([shard, shard ^ 1, shard ^ 2, shard ^ 3, shard ^ 3]) * rows
        pieces_at = pieces_at.astype(jnp.int32) + jnp.array([0, 0, 0, 0, rows // 2], jnp.int32)
    else:
        pieces_at = start.reshape(1)
    activated, expand_slope, second_part, expand_bias_grad = feed_forward(
        second_normed, reduce_slope, expand_bias[None], expand_held, reduce_held, pieces_at
    )
    expand_bias_grad = expand_bias_grad[0]

    second_swapped = swap(second_part, "tp", 1)
    place, order = (shard, (3, 2, 1, 0)) if four else (start, (0, 1, 2, 3))
    expand_whole = product(second_normed, expand_slope, COLUMN_BY_COLUMN).astype(LOW)
    second_swapped, expand_whole = fence(second_swapped, expand_whole)
    expand_far = far_halves(rows_at((expand_whole,), 3)) if four else ()
    mixer_slope, first_sum_back, second_sums = by_rows(
        second_norm_back_kernel, "second_norm_back", [LOW, FULL], True,
        flat_tokens, mixer_part, mixer_swapped, mixer_row, second_gain[None],
        second_part, second_swapped, reduce_slope,
    )
    attended_slope = product(mixer_slope, mixer_full, PLAIN).astype(LOW)

    leaving = []
    for pair in range(2):
        for distance in range(4):
            to = block ^ distance
            corner = ((to >> 1) * rows_here, (to & 1) * part_width + pair * pair_width)
            leaving.append(lax.dynamic_slice(attended_slope, corner, (rows_here, pair_width)))
    if four:
        expand_near = add_far(
            rows_at((expand_whole,), 1), rows_at((expand_whole,), 2), expand_far
        )
    else:
        expand_near = ()
    leaving, mixer_slope, mixed_in, activated, expand_near = fence(
        leaving, mixer_slope, mixed_in, activated, expand_near
    )
    slope_first = [leaving[0]] + [swap(leaving[d], "ctx", d) for d in (1, 2, 3)]
    if four:
        expand_near = near_rows_out(expand_near)
    wide = (
        product(reduce_slope, activated, COLUMN_BY_COLUMN).astype(LOW),
        product(mixer_slope, mixed_in, COLUMN_BY_COLUMN).astype(LOW),
    )
    if four:
        half = width // 8
        wide_far, wide_side, wide_next = (rows_at(wide, distance) for distance in (3, 2, 1))
        far_top, far_low = wide_far[:half], wide_far[half:]
        wide_early = (wide_next[:half], wide_side[half:])
    else:
        far_top, far_low, wide_early = (), (), ()

    slope_first, leaving, expand_near, far_top, far_low = fence(
        slope_first, leaving, expand_near, far_top, far_low
    )
    slope_second = [leaving[4]] + [swap(leaving[4 + d], "ctx", d) for d in (1, 2, 3)]
    wide_far = (swap(far_top, "fsdp", 1), swap(far_low, "fsdp", 2)) if four else ()
    grad_first = attention_backward(
        joint_out, jnp.concatenate(slope_first, axis=0), out_first, log_first, 0
    )

    grad_first, slope_second, wide_far = fence(grad_first, slope_second, wide_far)
    if four:
        expand_sum = rows_at((expand_whole,), 0).astype(FULL) + both(expand_near)
        wide_late = (
            both((wide_next[half:], wide_far[1])).astype(LOW),
            both((wide_side[:half], wide_far[0])).astype(LOW),
        )
    else:
        wide_late = ()
        expand_sum = lax.psum_scatter(
            expand_whole, "fsdp", scatter_dimension=0, tiled=True
        ).astype(FULL)
    expand_keep, expand_send = halves(expand_sum, part_at)
    slope_second = jnp.concatenate(slope_second, axis=0)
    expand_send, slope_second, wide_early, wide_late = fence(
        expand_send, slope_second, wide_early, wide_late
    )
    if four:
        wide_early = near_rows_out(wide_early)
    expand_rows = (expand_keep, swap(expand_send, "ctx", 1))
    grad_second = attention_backward(joint_out, slope_second, out_second, log_second, 1)

    grad_second, expand_rows, wide_early, wide_late = fence(
        grad_second, expand_rows, wide_early, wide_late
    )
    if four:
        wide_late = near_rows_out(wide_late)
    joint_slope = jnp.concatenate(
        [grad[kind] for kind in range(3) for grad in (grad_first, grad_second)], axis=1
    )
    expand_keep, expand_send = halves(both(expand_rows), clip_at)
    joint_slope, expand_send = fence(joint_slope, expand_send)
    expand_rows = (expand_keep, swap(expand_send, "ctx", 2))
    first_there = product(joint_slope, joint_full[width_half:], ROW_BY_ROW).astype(LOW)
    first_here = rows_product(joint_slope, joint_full[:width_half], "first_slope")
    first_half = both((first_here, swap(first_there, "tp", 1))).astype(LOW)

    if not four:
        wide_near = lax.psum_scatter(
            jnp.concatenate(wide, axis=1), "fsdp", scatter_dimension=0, tiled=True
        )
    first_half, joint_slope, expand_rows = fence(first_half, joint_slope, expand_rows)
    expand_rows = join_rows(both(expand_rows).astype(LOW), clip_at, 2)
    pieces = first_half.reshape(4, rows_here, width_half)
    passing = jnp.concatenate([pieces[1], pieces[3][:, :quarter], pieces[2][:, quarter:]], axis=1)
    passing = swap(passing, "ctx", 1)
    place = (shard if four else start) ^ (2 * core)
    joint_parts = grad_products([normed_mine, normed_other], joint_slope, place, order, "joint_grad")
    slope_sums = jnp.sum(joint_slope.astype(FULL), axis=0)
    bias_sums = jnp.stack([slope_sums[:part_width], slope_sums[2 * part_width :]])
    joint_bias_grad = lax.dynamic_update_slice(
        jnp.zeros((2, features), FULL), bias_sums, (0, part_at * part_width)
    )

    passing, joint_parts, wide_late, expand_rows = fence(
        passing, joint_parts, wide_late, expand_rows
    )
    if four:
        near_sum = [both((wide_early[0], wide_late[1])), both((wide_late[0], wide_early[1]))]
        wide_sum = rows_at(wide, 0).astype(FULL) + jnp.concatenate(near_sum, axis=0)
    else:
        wide_sum = wide_near.astype(FULL)
    wide_keep, wide_send = halves(wide_sum, part_at)
    own_half = both((pieces[0], passing[:, :width_half])).astype(LOW)
    to_left = both((pieces[2][:, :quarter], passing[:, width_half : width_half + quarter]))
    to_right = both((pieces[3][:, quarter:], passing[:, width_half + quarter :]))
    to_left, to_right, own_half, wide_send, joint_parts, activated = fence(
        to_left.astype(LOW), to_right.astype(LOW), own_half, wide_send, joint_parts, activated
    )
    other_half = jnp.concatenate([swap(to_left, "ctx", 2), swap(to_right, "ctx", 3)], axis=1)
    wide_rows = (wide_keep, swap(wide_send, "ctx", 1))
    joint_far = far_halves(joint_parts[0]) if four else ()
    reduce_part = reduce_output(activated, reduce_held, pieces_at)

    other_half, joint_far, wide_rows, reduce_part = fence(
        other_half, joint_far, wide_rows, reduce_part
    )
    slope_half = jnp.concatenate(swapped_if(clip_at, [own_half, other_half]), axis=0)
    slope_other = swap(slope_half, "tp", 1)
    slope_other, expand_rows = fence(slope_other, expand_rows)
    expand_grad = join_rows(expand_rows, part_at, 1).astype(FULL)
    first_slope = jnp.concatenate(swapped_if(core, [slope_half, slope_other]), axis=1)
    wide_rows = split_rows(both(wide_rows), clip_at, 2)
    reduce_swapped = swap(reduce_part, "tp", 1)
    if four:
        joint_near = near_rows_out(add_far(joint_parts[2], joint_parts[1], joint_far))
    else:
        joint_near = lax.psum_scatter(
            joint_parts.reshape(width, -1), "fsdp", scatter_dimension=0, tiled=True
        )
    tokens_grad, first_sums = by_rows(
        first_norm_back_kernel, "first_norm_back", [FULL], True,
        flat_tokens, first_slope, first_gain[None],
        cotangent.reshape(tokens_here, width), first_sum_back,
    )
    first_sums, tokens_grad, reduce_swapped, joint_near, wide_rows = fence(
        first_sums, tokens_grad, reduce_swapped, joint_near, wide_rows
    )
    joint_sum = joint_parts[3].astype(FULL) + both(joint_near) if four else joint_near
    joint_sum = joint_sum.astype(LOW)
    joint_sum = (joint_sum, swap(joint_sum, "ctx", 2))
    wide_rows = join_rows(both(wide_rows).astype(LOW), clip_at, 2)
    vectors = [
        first_sums[0],
        first_sums[1],
        joint_bias_grad[0],
        joint_bias_grad[1],
        second_sums[2],
        second_sums[0],
        second_sums[1],
        expand_bias_grad,
        reduce_bias_grad,
    ]
    packed = jnp.concatenate(vectors).reshape(-1, 128)
    packed_pieces = [packed] + [swap(packed, "ctx", d) for d in (1, 2, 3)]
    reduce_out = both((reduce_part, reduce_swapped)) + reduce_bias
    mixer_out = both((mixer_part, mixer_swapped)) + mixer_bias
    branches = (mixer_out + reduce_out).reshape(clips_here, rows_here, width)
    result = (tokens.astype(FULL) + valid * branches).astype(LOW)

    packed_pieces, joint_sum, wide_rows, result = fence(
        packed_pieces, joint_sum, wide_rows, result
    )
    packed = pairwise(packed_pieces)
    if four:
        packed = pairwise([packed] + [swap(packed, "fsdp", d) for d in (1, 2, 3)])
    else:
        packed = lax.psum(packed, "fsdp")
    joint_sum = both(joint_sum).astype(LOW)
    joint_parts = swapped_if(part_at, [joint_sum, swap(joint_sum, "ctx", 1)])
    joint_grad = jnp.concatenate(
        [piece.reshape(-1, 3, part_width) for piece in joint_parts], axis=2
    ).astype(FULL)
    wide_rows = join_rows(wide_rows, part_at, 1).astype(FULL)
    reduce_grad = wide_rows[:, : activated.shape[1]]
    mixer_grad = wide_rows[:, activated.shape[1] :]
    packed = packed.reshape(-1)
    shares = []
    start = 0
    for vector in vectors:
        share = vector.shape[0] // lax.axis_size("fsdp")
        shares.append(lax.dynamic_slice_in_dim(packed, start + shard * share, share, 0))
        start += vector.shape[0]

    shape = (clips_here, rows_here, width)
    return (
        result,
        tokens_grad.reshape(shape),
        shares[0],
        shares[1],
        joint_grad,
        jnp.stack([shares[2], shares[3]]),
        mixer_grad,
        shares[4],
        shares[5],
        shares[6],
        expand_grad,
        shares[7],
        reduce_grad,
        shares[8],
    )


def solution(mesh):
    return jax.shard_map(
        per_device,
        mesh=mesh,
        in_specs=(
            P("fsdp", "ctx", None),
            P("fsdp"),
            P("fsdp", "ctx", None),
            P(),
            P(),
            P("fsdp", None, "tp"),
            P(None, "tp"),
            P("fsdp", "tp"),
            P(),
            P(),
            P(),
            P("fsdp", "tp"),
            P("tp"),
            P("fsdp", "tp"),
            P(),
        ),
        out_specs=(
            P("fsdp", "ctx", None),
            P("fsdp", "ctx", None),
            P("fsdp"),
            P("fsdp"),
            P("fsdp", None, "tp"),
            P(None, ("tp", "fsdp")),
            P("fsdp", "tp"),
            P("fsdp"),
            P("fsdp"),
            P("fsdp"),
            P("fsdp", "tp"),
            P(("tp", "fsdp")),
            P("fsdp", "tp"),
            P("fsdp"),
        ),
        check_vma=False,
    )
```

```python
import jax
import jax.numpy as jnp
from jax import lax
from jax.experimental import pallas as pl
from jax.experimental.pallas import tpu as pltpu
from jax.sharding import PartitionSpec as P

HEAD_DIM = 64
EPSILON = 1e-06
LOW = jnp.bfloat16
FULL = jnp.float32

ROW_BY_ROW = (((1,), (1,)), ((), ()))
PLAIN = (((1,), (0,)), ((), ()))
COLUMN_BY_COLUMN = (((0,), (0,)), ((), ()))


def product(left, right, dims):
    return lax.dot_general(left, right, dims, preferred_element_type=FULL)


def normalize(value_rows):
    center = value_rows - jnp.mean(value_rows, axis=-1, keepdims=True)
    inverse = lax.rsqrt(jnp.mean(center * center, axis=-1, keepdims=True) + EPSILON)
    return (center * inverse, inverse)


def norm_back(upstream, gain, scaled, inverse):
    weighted = upstream * gain
    return inverse * (
        weighted
        - jnp.mean(weighted, axis=-1, keepdims=True)
        - scaled * jnp.mean(weighted * scaled, axis=-1, keepdims=True)
    )


def row_chunk(count, most):
    for chunk in range(most, 0, -16):
        if count % chunk == 0:
            return chunk
    raise ValueError("rows")


def first_norm_kernel(tokens_ref, gain_ref, shift_ref, out_ref):
    scaled, _ = normalize(tokens_ref[...].astype(FULL))
    out_ref[...] = (scaled * gain_ref[...] + shift_ref[...]).astype(LOW)


def second_norm_kernel(tokens_ref, one_ref, two_ref, bias_ref, gain_ref, shift_ref, out_ref):
    mixed = one_ref[...].astype(FULL) + two_ref[...].astype(FULL) + bias_ref[...]
    scaled, _ = normalize(tokens_ref[...].astype(FULL) + mixed)
    out_ref[...] = (scaled * gain_ref[...] + shift_ref[...]).astype(LOW)


def add_sums(ref, rows):
    sums = jnp.concatenate([jnp.sum(row, axis=0, keepdims=True) for row in rows], axis=0)

    @pl.when(pl.program_id(0) == 0)
    def _():
        ref[: len(rows)] = sums

    @pl.when(pl.program_id(0) > 0)
    def _():
        ref[: len(rows)] += sums


def second_norm_back_kernel(
    tokens_ref, one_ref, two_ref, bias_ref, gain_ref, left_ref, right_ref, outer_ref,
    slope_ref, back_ref, sums_ref,
):
    mixed = one_ref[...].astype(FULL) + two_ref[...].astype(FULL) + bias_ref[...]
    scaled, inverse = normalize(tokens_ref[...].astype(FULL) + mixed)
    upstream = left_ref[...].astype(FULL) + right_ref[...].astype(FULL)
    back = norm_back(upstream, gain_ref[...], scaled, inverse)
    slope = (outer_ref[...].astype(FULL) + back).astype(LOW)
    slope_ref[...] = slope
    back_ref[...] = back
    add_sums(sums_ref, [upstream * scaled, upstream, slope.astype(FULL)])


def first_norm_back_kernel(
    tokens_ref, upstream_ref, gain_ref, outer_ref, back_ref, out_ref, sums_ref
):
    scaled, inverse = normalize(tokens_ref[...].astype(FULL))
    upstream = upstream_ref[...].astype(FULL)
    back = norm_back(upstream, gain_ref[...], scaled, inverse)
    out_ref[...] = outer_ref[...].astype(FULL) + back_ref[...] + back
    add_sums(sums_ref, [upstream * scaled, upstream])


def by_rows(kernel, name, out_types, sums, *values):
    count, width = values[0].shape
    chunk = row_chunk(count, 112)
    part = pl.BlockSpec((chunk, width), lambda i: (i, 0))
    in_specs = [
        part if value.shape[0] == count else pl.BlockSpec((1, width), lambda i: (0, 0))
        for value in values
    ]
    out_specs = [part for _ in out_types]
    out_shape = [jax.ShapeDtypeStruct((count, width), kind) for kind in out_types]
    if sums:
        out_specs.append(pl.BlockSpec((8, width), lambda i: (0, 0)))
        out_shape.append(jax.ShapeDtypeStruct((8, width), FULL))
    return pl.pallas_call(
        kernel,
        grid=(count // chunk,),
        in_specs=in_specs,
        out_specs=out_specs,
        out_shape=out_shape,
        compiler_params=pltpu.CompilerParams(vmem_limit_bytes=16 << 20),
        name=name,
    )(*values)


def joint_kernel(mine_ref, other_ref, weight_ref, bias_ref, out_ref):
    half = mine_ref.shape[1]
    out = product(mine_ref[...], weight_ref[:half], PLAIN)
    out += product(other_ref[...], weight_ref[half:], PLAIN)
    out_ref[...] = (out + bias_ref[...]).astype(LOW)


def joint_projection(mine, other, weight, bias):
    count, half = mine.shape
    columns = weight.shape[1]
    chunk = row_chunk(count, 784)
    part = pl.BlockSpec((chunk, half), lambda i: (i, 0))
    return pl.pallas_call(
        joint_kernel,
        grid=(count // chunk,),
        in_specs=[
            part,
            part,
            pl.BlockSpec(weight.shape, lambda i: (0, 0)),
            pl.BlockSpec((1, columns), lambda i: (0, 0)),
        ],
        out_specs=pl.BlockSpec((chunk, columns), lambda i: (i, 0)),
        out_shape=jax.ShapeDtypeStruct((count, columns), LOW),
        compiler_params=pltpu.CompilerParams(vmem_limit_bytes=40 << 20),
        name="joint_projection",
    )(mine, other, weight, bias)


def rows_kernel(left_ref, right_ref, out_ref):
    out_ref[...] = product(left_ref[...], right_ref[...], ROW_BY_ROW).astype(LOW)


def rows_product(left, right, name):
    count, depth = left.shape
    columns = right.shape[0]
    chunk = row_chunk(count, 400)
    return pl.pallas_call(
        rows_kernel,
        grid=(count // chunk,),
        in_specs=[
            pl.BlockSpec((chunk, depth), lambda i: (i, 0)),
            pl.BlockSpec((columns, depth), lambda i: (0, 0)),
        ],
        out_specs=pl.BlockSpec((chunk, columns), lambda i: (i, 0)),
        out_shape=jax.ShapeDtypeStruct((count, columns), LOW),
        compiler_params=pltpu.CompilerParams(vmem_limit_bytes=48 << 20),
        name=name,
    )(left, right)


def grad_kernel(distances, place_ref, *refs):
    lefts, (right_ref, out_ref) = refs[:-2], refs[-2:]
    left = lefts[0][...]
    if len(lefts) == 2:
        slot = place_ref[0] ^ distance_at(distances, pl.program_id(0))
        left = jnp.where((slot >> 1) == 0, left, lefts[1][...])
    out_ref[0] = product(left, right_ref[...], COLUMN_BY_COLUMN).astype(LOW)


def distance_at(distances, step):
    if len(distances) == 1:
        return distances[0]
    return distances[0] + step * (distances[1] - distances[0])


def grad_products(lefts, right, place, distances, name):
    tokens_here, columns = right.shape
    quarter = sum(left.shape[1] for left in lefts) // 4
    blocks = lefts[0].shape[1] // quarter

    def left_at(i, place):
        return (0, (place[0] ^ distance_at(distances, i)) & (blocks - 1))

    return pl.pallas_call(
        lambda *refs: grad_kernel(distances, *refs),
        grid_spec=pltpu.PrefetchScalarGridSpec(
            num_scalar_prefetch=1,
            grid=(len(distances),),
            in_specs=[pl.BlockSpec((tokens_here, quarter), left_at) for _ in lefts]
            + [pl.BlockSpec((tokens_here, columns), lambda i, place: (0, 0))],
            out_specs=pl.BlockSpec((1, quarter, columns), lambda i, place: (i, 0, 0)),
        ),
        out_shape=jax.ShapeDtypeStruct((len(distances), quarter, columns), LOW),
        compiler_params=pltpu.CompilerParams(vmem_limit_bytes=48 << 20),
        name=name,
    )(place.astype(jnp.int32).reshape(1), *lefts, right)


def attention_forward_kernel(q_ref, k_ref, v_ref, o_ref, lse_ref):
    count, width = q_ref.shape
    rows = row_chunk(count, 256)
    lane = lax.broadcasted_iota(jnp.int32, (rows, width), 1)
    k = k_ref[...]
    v = v_ref[...]
    units = [(start, head) for start in range(0, count, rows) for head in range(width // HEAD_DIM)]

    def scores_of(unit):
        start, head = unit
        q = q_ref[start : start + rows] * jnp.asarray(HEAD_DIM ** (-0.5), LOW)
        return product(jnp.where((lane // HEAD_DIM) == head, q, jnp.zeros_like(q)), k, ROW_BY_ROW)

    logs = []
    ahead = scores_of(units[0])
    for step, (start, head) in enumerate(units):
        scores = ahead
        if step + 1 < len(units):
            ahead = scores_of(units[step + 1])
        top = jnp.max(scores, axis=-1, keepdims=True)
        weights = jnp.exp(scores - top)
        total = jnp.sum(weights, axis=-1, keepdims=True)
        part = product(weights.astype(LOW), v, PLAIN) / total
        if head == 0:
            out = part
            logs.append(jnp.zeros((rows, width), FULL))
        else:
            out = jnp.where((lane // HEAD_DIM) == head, part, out)
            o_ref[start : start + rows] = out.astype(LOW)
        logs[-1] = jnp.where(lane == head, top + jnp.log(total), logs[-1])
    lse_ref[...] = jnp.concatenate(logs, axis=0).T[: lse_ref.shape[0]]


def attention_forward(joint, pair):
    count, columns = joint.shape
    width = 2 * HEAD_DIM
    kind = columns // (3 * width)
    return pl.pallas_call(
        attention_forward_kernel,
        grid=(1,),
        in_specs=[
            pl.BlockSpec((count, width), lambda i: (0, pair)),
            pl.BlockSpec((count, width), lambda i: (0, kind + pair)),
            pl.BlockSpec((count, width), lambda i: (0, 2 * kind + pair)),
        ],
        out_specs=[
            pl.BlockSpec((count, width), lambda i: (0, 0)),
            pl.BlockSpec((8, count), lambda i: (0, 0)),
        ],
        out_shape=[
            jax.ShapeDtypeStruct((count, width), LOW),
            jax.ShapeDtypeStruct((8, count), FULL),
        ],
        compiler_params=pltpu.CompilerParams(vmem_limit_bytes=48 << 20),
        name="attention_forward",
    )(joint, joint, joint)


def attention_backward_kernel(
    q_ref, k_ref, v_ref, da_ref, o_ref, lse_ref, dq_ref, dk_ref, dv_ref,
    q_heads, da_heads, delta_ref, dq_total,
):
    count, width = q_ref.shape
    rows = row_chunk(count, 256)
    heads = width // HEAD_DIM
    scale = jnp.asarray(HEAD_DIM ** (-0.5), LOW)

    lane = lax.broadcasted_iota(jnp.int32, (count, width), 1)
    delta = jnp.zeros((count, width), FULL)
    q = q_ref[...] * scale
    da = da_ref[...]
    both_rows = da.astype(FULL) * o_ref[...].astype(FULL)
    for head in range(heads):
        mask = (lane // HEAD_DIM) == head
        q_heads[head] = jnp.where(mask, q, jnp.zeros_like(q))
        da_heads[head] = jnp.where(mask, da, jnp.zeros_like(da))
        row = jnp.sum(jnp.where(mask, both_rows, 0.0), axis=-1, keepdims=True)
        delta = jnp.where(lane == head, row, delta)
    delta_ref[...] = delta.T[:8]
    dq_total[...] = jnp.zeros_like(dq_total)

    lane = lax.broadcasted_iota(jnp.int32, (rows, width), 1)
    for start in range(0, count, rows):
        k = k_ref[start : start + rows]
        v = v_ref[start : start + rows]
        scaled_k = k * scale
        dk = dv = None
        for head in range(heads):
            q = q_heads[head]
            da = da_heads[head]
            probs = jnp.exp(product(k, q, ROW_BY_ROW) - lse_ref[head : head + 1, :])
            slope = probs * (product(v, da, ROW_BY_ROW) - delta_ref[head : head + 1, :])
            slope = slope.astype(LOW)
            dv_part = product(probs.astype(LOW), da, PLAIN)
            dk_part = product(slope, q, PLAIN)
            dv = dv_part if dv is None else dv + dv_part
            dk = dk_part if dk is None else dk + dk_part
            one_k = jnp.where((lane // HEAD_DIM) == head, scaled_k, jnp.zeros_like(k))
            dq_total[...] += product(slope, one_k, COLUMN_BY_COLUMN)
        dk_ref[start : start + rows] = dk.astype(LOW)
        dv_ref[start : start + rows] = dv.astype(LOW)
    dq_ref[...] = dq_total[...].astype(LOW)


def attention_backward(joint, da, out, lse, pair):
    count, columns = joint.shape
    width = 2 * HEAD_DIM
    kind = columns // (3 * width)
    alone = pl.BlockSpec((count, width), lambda i: (0, 0))
    grad = jax.ShapeDtypeStruct((count, width), LOW)
    return pl.pallas_call(
        attention_backward_kernel,
        grid=(1,),
        in_specs=[
            pl.BlockSpec((count, width), lambda i: (0, pair)),
            pl.BlockSpec((count, width), lambda i: (0, kind + pair)),
            pl.BlockSpec((count, width), lambda i: (0, 2 * kind + pair)),
            pl.BlockSpec((count, width), lambda i: (0, pair)),
            alone,
            pl.BlockSpec((8, count), lambda i: (0, 0)),
        ],
        out_specs=[alone, alone, alone],
        out_shape=[grad, grad, grad],
        scratch_shapes=[
            pltpu.VMEM((2, count, width), LOW),
            pltpu.VMEM((2, count, width), LOW),
            pltpu.VMEM((8, count), FULL),
            pltpu.VMEM((count, width), FULL),
        ],
        compiler_params=pltpu.CompilerParams(vmem_limit_bytes=48 << 20),
        name="attention_backward",
    )(joint, joint, joint, da, out, lse)


def put_together(place_ref, whole_ref, piece_refs):
    for piece, piece_ref in enumerate(piece_refs):
        rows = piece_ref.shape[0]
        start = pl.multiple_of(place_ref[piece], rows)
        whole_ref[pl.ds(start, rows), :] = piece_ref[...]


def feed_forward_kernel(pieces, place_ref, normed_ref, slope_ref, bias_ref, *refs):
    active_ref, expand_slope_ref, back_ref, bias_grad_ref = refs[2 * pieces : 2 * pieces + 4]
    total, expand_ref, reduce_ref = refs[2 * pieces + 4 :]
    put_together(place_ref, expand_ref, refs[:pieces])
    put_together(place_ref, reduce_ref, refs[pieces : 2 * pieces])
    step = pl.program_id(0)
    count = normed_ref.shape[0]
    half = count // 2
    bias_grad = None
    for rows in (slice(0, half), slice(half, count)):
        hidden = product(normed_ref[rows], expand_ref[...], PLAIN) + bias_ref[...]
        upstream = product(slope_ref[rows], reduce_ref[...], PLAIN)
        share = 0.5 * (1.0 + lax.erf(hidden * (0.5**0.5)))
        active_ref[rows] = (hidden * share).astype(LOW)
        density = jnp.exp(-0.5 * hidden * hidden) * 0.3989422804014327
        slope = (upstream * (share + hidden * density)).astype(LOW)
        expand_slope_ref[rows] = slope
        part = jnp.sum(slope.astype(FULL), axis=0, keepdims=True)
        bias_grad = part if bias_grad is None else bias_grad + part
        back = product(slope, expand_ref[...], ROW_BY_ROW)

        @pl.when(step == 0)
        def _():
            total[rows] = back

        @pl.when(step > 0)
        def _():
            total[rows] += back

    bias_grad_ref[...] = bias_grad

    @pl.when(step == pl.num_programs(0) - 1)
    def _():
        back_ref[...] = total[...].astype(LOW)


def feed_forward(normed, slope, bias, expand, reduce, place):
    count, width = normed.shape
    hidden = bias.shape[1]
    block = 512 if hidden % 512 == 0 else hidden
    whole = pl.BlockSpec((count, width), lambda i, place: (0, 0))
    out = pl.BlockSpec((count, block), lambda i, place: (0, i))
    row = pl.BlockSpec((1, block), lambda i, place: (0, i))
    return pl.pallas_call(
        lambda *refs: feed_forward_kernel(len(reduce), *refs),
        grid_spec=pltpu.PrefetchScalarGridSpec(
            num_scalar_prefetch=1,
            grid=(hidden // block,),
            in_specs=[whole, whole, row]
            + [
                pl.BlockSpec((piece.shape[0], block), lambda i, place: (0, i))
                for piece in [*expand, *reduce]
            ],
            out_specs=[out, out, whole, row],
            scratch_shapes=[
                pltpu.VMEM((count, width), FULL),
                pltpu.VMEM((width, block), LOW),
                pltpu.VMEM((width, block), LOW),
            ],
        ),
        out_shape=[
            jax.ShapeDtypeStruct((count, hidden), LOW),
            jax.ShapeDtypeStruct((count, hidden), LOW),
            jax.ShapeDtypeStruct((count, width), LOW),
            jax.ShapeDtypeStruct((1, hidden), FULL),
        ],
        compiler_params=pltpu.CompilerParams(vmem_limit_bytes=44 << 20),
        name="feed_forward",
    )(place, normed, slope, bias, *expand, *reduce)


def reduce_kernel(place_ref, active_ref, *refs):
    out_ref, total, reduce_ref = refs[-3:]
    put_together(place_ref, reduce_ref, refs[:-3])
    part = product(active_ref[...], reduce_ref[...], ROW_BY_ROW)

    @pl.when(pl.program_id(0) == 0)
    def _():
        total[...] = part

    @pl.when(pl.program_id(0) > 0)
    def _():
        total[...] += part

    @pl.when(pl.program_id(0) == pl.num_programs(0) - 1)
    def _():
        out_ref[...] = total[...].astype(LOW)


def reduce_output(active, reduce, place):
    count, hidden = active.shape
    width = sum(piece.shape[0] for piece in reduce)
    block = 512 if hidden % 512 == 0 else hidden
    return pl.pallas_call(
        reduce_kernel,
        grid_spec=pltpu.PrefetchScalarGridSpec(
            num_scalar_prefetch=1,
            grid=(hidden // block,),
            in_specs=[pl.BlockSpec((count, block), lambda i, place: (0, i))]
            + [
                pl.BlockSpec((piece.shape[0], block), lambda i, place: (0, i)) for piece in reduce
            ],
            out_specs=pl.BlockSpec((count, width), lambda i, place: (0, 0)),
            scratch_shapes=[pltpu.VMEM((count, width), FULL), pltpu.VMEM((width, block), LOW)],
        ),
        out_shape=jax.ShapeDtypeStruct((count, width), LOW),
        compiler_params=pltpu.CompilerParams(vmem_limit_bytes=32 << 20),
        name="reduce_output",
    )(place, active, *reduce)


def swap(value, axis, distance):
    size = lax.axis_size(axis)
    return lax.ppermute(value, axis, [(i, i ^ distance) for i in range(size)])


def fence(*values):
    return lax.optimization_barrier(values)


def gather_near(rows_here):
    if lax.axis_size("fsdp") != 4:
        return (lax.all_gather(rows_here, "fsdp", axis=0, tiled=True),)
    return (rows_here, swap(rows_here, "fsdp", 1), swap(rows_here, "fsdp", 2))


def far_of(held):
    if len(held) == 1:
        return ()
    half = held[0].shape[0] // 2
    return (held[2][:half], held[1][half:])


def send_far(leaves):
    return (swap(leaves[0], "fsdp", 1), swap(leaves[1], "fsdp", 2)) if leaves else ()


def gather_far(held):
    return held + send_far(far_of(held))


def place_near(held):
    if len(held) == 1:
        return held[0]
    rows_here, near, side = held[:3]
    me = lax.axis_index("fsdp")
    count, width = rows_here.shape
    out = jnp.zeros((4 * count, width), rows_here.dtype)
    out = lax.dynamic_update_slice(out, rows_here, (me * count, 0))
    out = lax.dynamic_update_slice(out, near, ((me ^ 1) * count, 0))
    return lax.dynamic_update_slice(out, side, ((me ^ 2) * count, 0))


def place_far(out, held):
    if len(held) == 1:
        return out
    far_top, far_low = held[3:]
    half = far_top.shape[0]
    start = (lax.axis_index("fsdp") ^ 3) * 2 * half
    out = lax.dynamic_update_slice(out, far_top, (start, 0))
    return lax.dynamic_update_slice(out, far_low, (start + half, 0))


def rows_at(matrices, distance):
    parts = []
    for matrix in matrices:
        count = matrix.shape[0] // 4
        start = (lax.axis_index("fsdp") ^ distance) * count
        parts.append(lax.dynamic_slice_in_dim(matrix, start, count, 0))
    return parts[0] if len(parts) == 1 else jnp.concatenate(parts, axis=1)


def far_halves(far):
    half = far.shape[0] // 2
    return (swap(far[:half], "fsdp", 1), swap(far[half:], "fsdp", 2))


def add_far(near, side, far):
    half = near.shape[0] // 2
    near = jnp.concatenate([near[:half], both((near[half:], far[1])).astype(LOW)], axis=0)
    side = jnp.concatenate([both((side[:half], far[0])).astype(LOW), side[half:]], axis=0)
    return (near, side)


def near_rows_out(pair):
    return (swap(pair[0], "fsdp", 1), swap(pair[1], "fsdp", 2))


def halves(value, bit):
    half = value.shape[0] // 2
    keep = lax.dynamic_slice_in_dim(value, bit * half, half, 0)
    send = lax.dynamic_slice_in_dim(value, (1 - bit) * half, half, 0)
    return keep, send.astype(LOW)


def split_rows(value, bit, distance):
    keep, send = halves(value, bit)
    return keep, swap(send, "ctx", distance)


def both(pair):
    return pair[0].astype(FULL) + pair[1].astype(FULL)


def join_rows(value, bit, distance):
    other = swap(value, "ctx", distance)
    return jnp.where(
        bit == 0,
        jnp.concatenate([value, other], axis=0),
        jnp.concatenate([other, value], axis=0),
    )


def pairwise(pieces):
    return (pieces[0] + pieces[1]) + (pieces[2] + pieces[3])


def swapped_if(bit, pair):
    return [jnp.where(bit == 0, pair[0], pair[1]), jnp.where(bit == 0, pair[1], pair[0])]


def per_device(
    tokens,
    clip_mask,
    cotangent,
    first_gain,
    first_shift,
    joint_weight,
    joint_bias,
    mixer_weight,
    mixer_bias,
    second_gain,
    second_shift,
    expand_weight,
    expand_bias,
    reduce_weight,
    reduce_bias,
):
    clips_here, rows_here, width = tokens.shape
    if lax.axis_size("ctx") != 4 or lax.axis_size("tp") != 2 or clips_here != 2:
        raise ValueError("mesh")
    shard = lax.axis_index("fsdp")
    block = lax.axis_index("ctx")
    core = lax.axis_index("tp")
    clip_at = block >> 1
    part_at = block & 1
    width_half = width // 2
    quarter = width_half // 2
    features = joint_weight.shape[2]
    part_width = features // 2
    pair_width = 2 * HEAD_DIM
    tokens_here = clips_here * rows_here

    flat_tokens = tokens.reshape(tokens_here, width)
    (first_normed,) = by_rows(
        first_norm_kernel, "first_norm", [LOW], False,
        flat_tokens, first_gain[None], first_shift[None],
    )
    first_normed = first_normed.reshape(clips_here, rows_here, width)
    mine = lax.dynamic_slice_in_dim(first_normed, core * width_half, width_half, 2)
    other_side = lax.dynamic_slice_in_dim(first_normed, (1 - core) * width_half, width_half, 2)
    own_clip = lax.dynamic_index_in_dim(mine, clip_at, 0, False)
    own_other = lax.dynamic_index_in_dim(other_side, clip_at, 0, False)
    other_clip = lax.dynamic_index_in_dim(mine, 1 - clip_at, 0, False)
    joint_part = lax.dynamic_slice_in_dim(joint_weight, part_at * part_width, part_width, 2)
    both_parts = jnp.concatenate([joint_part[:, kind] for kind in range(3)] + [mixer_weight], axis=1)

    own_clip, left, right, both_parts = fence(
        own_clip, other_clip[:, :quarter], other_clip[:, quarter:], both_parts
    )
    near_rows = swap(own_clip, "ctx", 1)
    across_left = swap(left, "ctx", 2)
    far_right = swap(right, "ctx", 3)
    held = gather_near(both_parts)

    near_rows, across_left, far_right, held, expand_weight = fence(
        near_rows, across_left, far_right, held, expand_weight
    )
    passed = swap(jnp.concatenate([across_left, far_right], axis=1), "ctx", 1)
    held = gather_far(held)
    expand_held = gather_near(expand_weight)

    passed, held = fence(passed, held)
    cross_rows = jnp.concatenate(
        [
            near_rows,
            jnp.concatenate([across_left, passed[:, quarter:]], axis=1),
            jnp.concatenate([passed[:, :quarter], far_right], axis=1),
        ],
        axis=0,
    )
    cross_other = swap(cross_rows, "tp", 1)
    both_full = place_far(place_near(held), held)
    joint_columns = 3 * part_width
    joint_full = jnp.concatenate(
        [
            lax.dynamic_slice(both_full, (start * width_half, 0), (width_half, joint_columns))
            for start in (core, 1 - core)
        ],
        axis=0,
    )

    cross_other, joint_full, both_full, reduce_weight = fence(
        cross_other, joint_full, both_full, reduce_weight
    )
    mixer_full = both_full[:, joint_columns:]
    reduce_held = gather_near(reduce_weight)
    normed_mine = jnp.concatenate([own_clip, cross_rows], axis=0)
    normed_other = jnp.concatenate([own_other, cross_other], axis=0)
    bias_part = lax.dynamic_slice_in_dim(joint_bias, part_at * part_width, part_width, 1)
    bias_row = jnp.concatenate([bias_part[0], jnp.zeros_like(bias_part[0]), bias_part[1]])
    joint_out = joint_projection(normed_mine, normed_other, joint_full, bias_row[None])
    out_first, log_first = attention_forward(joint_out, 0)

    out_first, joint_out, mixer_full, expand_held = fence(
        out_first, joint_out, mixer_full, expand_held
    )
    first_blocks = out_first.reshape(4, rows_here, pair_width)
    arrived_first = [swap(first_blocks[d], "ctx", d) for d in (1, 2, 3)]
    out_second, log_second = attention_forward(joint_out, 1)

    out_second, arrived_first, reduce_held, expand_held = fence(
        out_second, arrived_first, reduce_held, expand_held
    )
    second_blocks = out_second.reshape(4, rows_here, pair_width)
    arrived_second = [swap(second_blocks[d], "ctx", d) for d in (1, 2, 3)]
    expand_held = gather_far(expand_held)

    arrived_second, expand_held, reduce_held, log_first, log_second = fence(
        arrived_second, expand_held, reduce_held, log_first, log_second
    )
    reduce_held = gather_far(reduce_held)
    arrived = [jnp.concatenate([first_blocks[0], second_blocks[0]], axis=1)] + [
        jnp.concatenate([one, two], axis=1) for one, two in zip(arrived_first, arrived_second)
    ]
    own_joined = jnp.concatenate(swapped_if(part_at, arrived[:2]), axis=1)
    other_joined = jnp.concatenate(swapped_if(part_at, arrived[2:]), axis=1)
    mixed_in = jnp.concatenate(swapped_if(clip_at, [own_joined, other_joined]), axis=0)
    mixer_part = product(mixed_in, mixer_full, ROW_BY_ROW).astype(LOW)
    mixer_swapped = swap(mixer_part, "tp", 1)
    mixer_row = mixer_bias[None]
    (second_normed,) = by_rows(
        second_norm_kernel, "second_norm", [LOW], False,
        flat_tokens, mixer_part, mixer_swapped, mixer_row, second_gain[None], second_shift[None],
    )
    valid = clip_mask.astype(FULL)[:, None, None]
    reduce_slope = (cotangent.astype(FULL) * valid).astype(LOW).reshape(tokens_here, width)
    reduce_bias_grad = jnp.sum(reduce_slope.astype(FULL), axis=0)

    second_normed, reduce_slope, reduce_held = fence(second_normed, reduce_slope, reduce_held)
    four = lax.axis_size("fsdp") == 4
    start = jnp.zeros((), jnp.int32)
    if four:
        rows = width // 4
        pieces_at = jnp.stack([shard, shard ^ 1, shard ^ 2, shard ^ 3, shard ^ 3]) * rows
        pieces_at = pieces_at.astype(jnp.int32) + jnp.array([0, 0, 0, 0, rows // 2], jnp.int32)
    else:
        pieces_at = start.reshape(1)
    activated, expand_slope, second_part, expand_bias_grad = feed_forward(
        second_normed, reduce_slope, expand_bias[None], expand_held, reduce_held, pieces_at
    )
    expand_bias_grad = expand_bias_grad[0]

    second_swapped = swap(second_part, "tp", 1)
    place, order = (shard, (3, 2, 1, 0)) if four else (start, (0, 1, 2, 3))
    expand_whole = product(second_normed, expand_slope, COLUMN_BY_COLUMN).astype(LOW)
    second_swapped, expand_whole = fence(second_swapped, expand_whole)
    expand_far = far_halves(rows_at((expand_whole,), 3)) if four else ()
    mixer_slope, first_sum_back, second_sums = by_rows(
        second_norm_back_kernel, "second_norm_back", [LOW, FULL], True,
        flat_tokens, mixer_part, mixer_swapped, mixer_row, second_gain[None],
        second_part, second_swapped, reduce_slope,
    )
    attended_slope = product(mixer_slope, mixer_full, PLAIN).astype(LOW)

    leaving = []
    for distance in range(4):
        to = block ^ distance
        corner = ((to >> 1) * rows_here, (to & 1) * part_width)
        leaving.append(lax.dynamic_slice(attended_slope, corner, (rows_here, part_width)))
    if four:
        expand_near = add_far(
            rows_at((expand_whole,), 1), rows_at((expand_whole,), 2), expand_far
        )
    else:
        expand_near = ()
    leaving, mixer_slope, mixed_in, activated, expand_near = fence(
        leaving, mixer_slope, mixed_in, activated, expand_near
    )
    slope_blocks = [leaving[0]] + [swap(leaving[d], "ctx", d) for d in (1, 2, 3)]
    if four:
        expand_near = near_rows_out(expand_near)
    wide = (
        product(reduce_slope, activated, COLUMN_BY_COLUMN).astype(LOW),
        product(mixer_slope, mixed_in, COLUMN_BY_COLUMN).astype(LOW),
    )
    if four:
        half = width // 8
        wide_far, wide_side, wide_next = (rows_at(wide, distance) for distance in (3, 2, 1))
        far_top, far_low = wide_far[:half], wide_far[half:]
        wide_early = (wide_next[:half], wide_side[half:])
    else:
        far_top, far_low, wide_early = (), (), ()

    slope_blocks, expand_near, far_top, far_low = fence(
        slope_blocks, expand_near, far_top, far_low
    )
    if four:
        expand_sum = rows_at((expand_whole,), 0).astype(FULL) + both(expand_near)
    else:
        expand_sum = lax.psum_scatter(
            expand_whole, "fsdp", scatter_dimension=0, tiled=True
        ).astype(FULL)
    expand_keep, expand_send = halves(expand_sum, part_at)
    slope_clip = jnp.concatenate(slope_blocks, axis=0)
    expand_send, slope_clip, far_top, far_low = fence(expand_send, slope_clip, far_top, far_low)
    wide_far = (swap(far_top, "fsdp", 1), swap(far_low, "fsdp", 2)) if four else ()
    expand_rows = (expand_keep, swap(expand_send, "ctx", 1))
    grad_first = attention_backward(joint_out, slope_clip, out_first, log_first, 0)

    grad_first, slope_clip, wide_far, expand_rows = fence(
        grad_first, slope_clip, wide_far, expand_rows
    )
    if four:
        wide_late = (
            both((wide_next[half:], wide_far[1])).astype(LOW),
            both((wide_side[:half], wide_far[0])).astype(LOW),
        )
    else:
        wide_late = ()
    expand_keep, expand_send = halves(both(expand_rows), clip_at)
    expand_send, slope_clip, wide_early, wide_late = fence(
        expand_send, slope_clip, wide_early, wide_late
    )
    if four:
        wide_early = near_rows_out(wide_early)
    expand_rows = (expand_keep, swap(expand_send, "ctx", 2))
    grad_second = attention_backward(joint_out, slope_clip, out_second, log_second, 1)

    grad_second, expand_rows, wide_early, wide_late = fence(
        grad_second, expand_rows, wide_early, wide_late
    )
    if four:
        wide_late = near_rows_out(wide_late)
    expand_rows = join_rows(both(expand_rows).astype(LOW), clip_at, 2)
    joint_slope = jnp.concatenate(
        [grad[kind] for kind in range(3) for grad in (grad_first, grad_second)], axis=1
    )
    first_there = product(joint_slope, joint_full[width_half:], ROW_BY_ROW).astype(LOW)
    first_here = rows_product(joint_slope, joint_full[:width_half], "first_slope")
    first_half = both((first_here, swap(first_there, "tp", 1))).astype(LOW)

    if not four:
        wide_near = lax.psum_scatter(
            jnp.concatenate(wide, axis=1), "fsdp", scatter_dimension=0, tiled=True
        )
    first_half, joint_slope = fence(first_half, joint_slope)
    pieces = first_half.reshape(4, rows_here, width_half)
    passing = jnp.concatenate([pieces[1], pieces[3][:, :quarter], pieces[2][:, quarter:]], axis=1)
    passing = swap(passing, "ctx", 1)
    place = (shard if four else start) ^ (2 * core)
    joint_parts = grad_products([normed_mine, normed_other], joint_slope, place, order, "joint_grad")
    slope_sums = jnp.sum(joint_slope.astype(FULL), axis=0)
    bias_sums = jnp.stack([slope_sums[:part_width], slope_sums[2 * part_width :]])
    joint_bias_grad = lax.dynamic_update_slice(
        jnp.zeros((2, features), FULL), bias_sums, (0, part_at * part_width)
    )

    joint_far = far_halves(joint_parts[0]) if four else ()
    passing, joint_far, wide_late, expand_rows = fence(
        passing, joint_far, wide_late, expand_rows
    )
    if four:
        near_sum = [both((wide_early[0], wide_late[1])), both((wide_late[0], wide_early[1]))]
        wide_sum = rows_at(wide, 0).astype(FULL) + jnp.concatenate(near_sum, axis=0)
    else:
        wide_sum = wide_near.astype(FULL)
    wide_keep, wide_send = halves(wide_sum, part_at)
    own_half = both((pieces[0], passing[:, :width_half])).astype(LOW)
    to_left = both((pieces[2][:, :quarter], passing[:, width_half : width_half + quarter]))
    to_right = both((pieces[3][:, quarter:], passing[:, width_half + quarter :]))
    joint_near = add_far(joint_parts[2], joint_parts[1], joint_far) if four else ()
    to_left, to_right, own_half, wide_send, joint_near, activated = fence(
        to_left.astype(LOW), to_right.astype(LOW), own_half, wide_send, joint_near, activated
    )
    other_half = jnp.concatenate([swap(to_left, "ctx", 2), swap(to_right, "ctx", 3)], axis=1)
    wide_rows = (wide_keep, swap(wide_send, "ctx", 1))
    if four:
        joint_near = near_rows_out(joint_near)
    else:
        joint_near = lax.psum_scatter(
            joint_parts.reshape(width, -1), "fsdp", scatter_dimension=0, tiled=True
        )
    reduce_part = reduce_output(activated, reduce_held, pieces_at)

    other_half, joint_near, wide_rows, reduce_part = fence(
        other_half, joint_near, wide_rows, reduce_part
    )
    slope_half = jnp.concatenate(swapped_if(clip_at, [own_half, other_half]), axis=0)
    slope_other = swap(slope_half, "tp", 1)
    slope_other, expand_rows = fence(slope_other, expand_rows)
    expand_grad = join_rows(expand_rows, part_at, 1).astype(FULL)
    first_slope = jnp.concatenate(swapped_if(core, [slope_half, slope_other]), axis=1)
    wide_rows = split_rows(both(wide_rows), clip_at, 2)
    reduce_swapped = swap(reduce_part, "tp", 1)
    joint_sum = joint_parts[3].astype(FULL) + both(joint_near) if four else joint_near
    joint_sum = joint_sum.astype(LOW)
    joint_sum = (joint_sum, swap(joint_sum, "ctx", 2))
    tokens_grad, first_sums = by_rows(
        first_norm_back_kernel, "first_norm_back", [FULL], True,
        flat_tokens, first_slope, first_gain[None],
        cotangent.reshape(tokens_here, width), first_sum_back,
    )
    first_sums, tokens_grad, reduce_swapped = fence(first_sums, tokens_grad, reduce_swapped)
    vectors = [
        first_sums[0],
        first_sums[1],
        joint_bias_grad[0],
        joint_bias_grad[1],
        second_sums[2],
        second_sums[0],
        second_sums[1],
        expand_bias_grad,
        reduce_bias_grad,
    ]
    packed = jnp.concatenate(vectors).reshape(-1, 128)
    packed_pieces = [packed] + [swap(packed, "ctx", d) for d in (1, 2, 3)]
    reduce_out = both((reduce_part, reduce_swapped)) + reduce_bias
    mixer_out = both((mixer_part, mixer_swapped)) + mixer_bias
    branches = (mixer_out + reduce_out).reshape(clips_here, rows_here, width)
    result = (tokens.astype(FULL) + valid * branches).astype(LOW)

    packed_pieces, joint_sum, wide_rows, result = fence(
        packed_pieces, joint_sum, wide_rows, result
    )
    packed = pairwise(packed_pieces)
    if four:
        packed = pairwise([packed] + [swap(packed, "fsdp", d) for d in (1, 2, 3)])
    else:
        packed = lax.psum(packed, "fsdp")
    joint_sum = both(joint_sum).astype(LOW)
    joint_parts = swapped_if(part_at, [joint_sum, swap(joint_sum, "ctx", 1)])
    joint_grad = jnp.concatenate(
        [piece.reshape(-1, 3, part_width) for piece in joint_parts], axis=2
    ).astype(FULL)
    wide_rows = join_rows(both(wide_rows).astype(LOW), clip_at, 2)
    wide_rows = join_rows(wide_rows, part_at, 1).astype(FULL)
    reduce_grad = wide_rows[:, : activated.shape[1]]
    mixer_grad = wide_rows[:, activated.shape[1] :]
    packed = packed.reshape(-1)
    shares = []
    start = 0
    for vector in vectors:
        share = vector.shape[0] // lax.axis_size("fsdp")
        shares.append(lax.dynamic_slice_in_dim(packed, start + shard * share, share, 0))
        start += vector.shape[0]

    shape = (clips_here, rows_here, width)
    return (
        result,
        tokens_grad.reshape(shape),
        shares[0],
        shares[1],
        joint_grad,
        jnp.stack([shares[2], shares[3]]),
        mixer_grad,
        shares[4],
        shares[5],
        shares[6],
        expand_grad,
        shares[7],
        reduce_grad,
        shares[8],
    )


def solution(mesh):
    return jax.shard_map(
        per_device,
        mesh=mesh,
        in_specs=(
            P("fsdp", "ctx", None),
            P("fsdp"),
            P("fsdp", "ctx", None),
            P(),
            P(),
            P("fsdp", None, "tp"),
            P(None, "tp"),
            P("fsdp", "tp"),
            P(),
            P(),
            P(),
            P("fsdp", "tp"),
            P("tp"),
            P("fsdp", "tp"),
            P(),
        ),
        out_specs=(
            P("fsdp", "ctx", None),
            P("fsdp", "ctx", None),
            P("fsdp"),
            P("fsdp"),
            P("fsdp", None, "tp"),
            P(None, ("tp", "fsdp")),
            P("fsdp", "tp"),
            P("fsdp"),
            P("fsdp"),
            P("fsdp"),
            P("fsdp", "tp"),
            P(("tp", "fsdp")),
            P("fsdp", "tp"),
            P("fsdp"),
        ),
        check_vma=False,
    )
```

```python
import jax
import jax.numpy as jnp
from jax import lax
from jax.experimental import pallas as pl
from jax.experimental.pallas import tpu as pltpu
from jax.sharding import PartitionSpec as P

HEAD_DIM = 64
EPSILON = 1e-06
LOW = jnp.bfloat16
FULL = jnp.float32

ROW_BY_ROW = (((1,), (1,)), ((), ()))
PLAIN = (((1,), (0,)), ((), ()))
COLUMN_BY_COLUMN = (((0,), (0,)), ((), ()))


def product(left, right, dims):
    return lax.dot_general(left, right, dims, preferred_element_type=FULL)


def normalize(value_rows):
    center = value_rows - jnp.mean(value_rows, axis=-1, keepdims=True)
    inverse = lax.rsqrt(jnp.mean(center * center, axis=-1, keepdims=True) + EPSILON)
    return (center * inverse, inverse)


def norm_back(upstream, gain, scaled, inverse):
    weighted = upstream * gain
    return inverse * (
        weighted
        - jnp.mean(weighted, axis=-1, keepdims=True)
        - scaled * jnp.mean(weighted * scaled, axis=-1, keepdims=True)
    )


def row_chunk(count, most):
    for chunk in range(most, 0, -16):
        if count % chunk == 0:
            return chunk
    raise ValueError("rows")


def first_norm_kernel(tokens_ref, gain_ref, shift_ref, out_ref):
    scaled, _ = normalize(tokens_ref[...].astype(FULL))
    out_ref[...] = (scaled * gain_ref[...] + shift_ref[...]).astype(LOW)


def second_norm_kernel(tokens_ref, one_ref, two_ref, bias_ref, gain_ref, shift_ref, out_ref):
    mixed = one_ref[...].astype(FULL) + two_ref[...].astype(FULL) + bias_ref[...]
    scaled, _ = normalize(tokens_ref[...].astype(FULL) + mixed)
    out_ref[...] = (scaled * gain_ref[...] + shift_ref[...]).astype(LOW)


def add_sums(ref, rows):
    sums = jnp.concatenate([jnp.sum(row, axis=0, keepdims=True) for row in rows], axis=0)

    @pl.when(pl.program_id(0) == 0)
    def _():
        ref[: len(rows)] = sums

    @pl.when(pl.program_id(0) > 0)
    def _():
        ref[: len(rows)] += sums


def second_norm_back_kernel(
    tokens_ref, one_ref, two_ref, bias_ref, gain_ref, left_ref, right_ref, outer_ref,
    slope_ref, back_ref, sums_ref,
):
    mixed = one_ref[...].astype(FULL) + two_ref[...].astype(FULL) + bias_ref[...]
    scaled, inverse = normalize(tokens_ref[...].astype(FULL) + mixed)
    upstream = left_ref[...].astype(FULL) + right_ref[...].astype(FULL)
    back = norm_back(upstream, gain_ref[...], scaled, inverse)
    slope = (outer_ref[...].astype(FULL) + back).astype(LOW)
    slope_ref[...] = slope
    back_ref[...] = back
    add_sums(sums_ref, [upstream * scaled, upstream, slope.astype(FULL)])


def first_norm_back_kernel(
    tokens_ref, upstream_ref, gain_ref, outer_ref, back_ref, out_ref, sums_ref
):
    scaled, inverse = normalize(tokens_ref[...].astype(FULL))
    upstream = upstream_ref[...].astype(FULL)
    back = norm_back(upstream, gain_ref[...], scaled, inverse)
    out_ref[...] = outer_ref[...].astype(FULL) + back_ref[...] + back
    add_sums(sums_ref, [upstream * scaled, upstream])


def by_rows(kernel, name, out_types, sums, *values):
    count, width = values[0].shape
    chunk = row_chunk(count, 112)
    part = pl.BlockSpec((chunk, width), lambda i: (i, 0))
    in_specs = [
        part if value.shape[0] == count else pl.BlockSpec((1, width), lambda i: (0, 0))
        for value in values
    ]
    out_specs = [part for _ in out_types]
    out_shape = [jax.ShapeDtypeStruct((count, width), kind) for kind in out_types]
    if sums:
        out_specs.append(pl.BlockSpec((8, width), lambda i: (0, 0)))
        out_shape.append(jax.ShapeDtypeStruct((8, width), FULL))
    return pl.pallas_call(
        kernel,
        grid=(count // chunk,),
        in_specs=in_specs,
        out_specs=out_specs,
        out_shape=out_shape,
        compiler_params=pltpu.CompilerParams(vmem_limit_bytes=16 << 20),
        name=name,
    )(*values)


def joint_kernel(mine_ref, other_ref, weight_ref, bias_ref, out_ref):
    half = mine_ref.shape[1]
    out = product(mine_ref[...], weight_ref[:half], PLAIN)
    out += product(other_ref[...], weight_ref[half:], PLAIN)
    out_ref[...] = (out + bias_ref[...]).astype(LOW)


def joint_projection(mine, other, weight, bias):
    count, half = mine.shape
    columns = weight.shape[1]
    chunk = row_chunk(count, 784)
    part = pl.BlockSpec((chunk, half), lambda i: (i, 0))
    return pl.pallas_call(
        joint_kernel,
        grid=(count // chunk,),
        in_specs=[
            part,
            part,
            pl.BlockSpec(weight.shape, lambda i: (0, 0)),
            pl.BlockSpec((1, columns), lambda i: (0, 0)),
        ],
        out_specs=pl.BlockSpec((chunk, columns), lambda i: (i, 0)),
        out_shape=jax.ShapeDtypeStruct((count, columns), LOW),
        compiler_params=pltpu.CompilerParams(vmem_limit_bytes=40 << 20),
        name="joint_projection",
    )(mine, other, weight, bias)


def rows_kernel(left_ref, right_ref, out_ref):
    out_ref[...] = product(left_ref[...], right_ref[...], ROW_BY_ROW).astype(LOW)


def rows_product(left, right, name):
    count, depth = left.shape
    columns = right.shape[0]
    chunk = row_chunk(count, 400)
    return pl.pallas_call(
        rows_kernel,
        grid=(count // chunk,),
        in_specs=[
            pl.BlockSpec((chunk, depth), lambda i: (i, 0)),
            pl.BlockSpec((columns, depth), lambda i: (0, 0)),
        ],
        out_specs=pl.BlockSpec((chunk, columns), lambda i: (i, 0)),
        out_shape=jax.ShapeDtypeStruct((count, columns), LOW),
        compiler_params=pltpu.CompilerParams(vmem_limit_bytes=48 << 20),
        name=name,
    )(left, right)


def grad_kernel(distances, place_ref, *refs):
    lefts, (right_ref, out_ref) = refs[:-2], refs[-2:]
    left = lefts[0][...]
    if len(lefts) == 2:
        slot = place_ref[0] ^ distance_at(distances, pl.program_id(0))
        left = jnp.where((slot >> 1) == 0, left, lefts[1][...])
    out_ref[0] = product(left, right_ref[...], COLUMN_BY_COLUMN).astype(LOW)


def distance_at(distances, step):
    if len(distances) == 1:
        return distances[0]
    return distances[0] + step * (distances[1] - distances[0])


def grad_products(lefts, right, place, distances, name):
    tokens_here, columns = right.shape
    quarter = sum(left.shape[1] for left in lefts) // 4
    blocks = lefts[0].shape[1] // quarter

    def left_at(i, place):
        return (0, (place[0] ^ distance_at(distances, i)) & (blocks - 1))

    return pl.pallas_call(
        lambda *refs: grad_kernel(distances, *refs),
        grid_spec=pltpu.PrefetchScalarGridSpec(
            num_scalar_prefetch=1,
            grid=(len(distances),),
            in_specs=[pl.BlockSpec((tokens_here, quarter), left_at) for _ in lefts]
            + [pl.BlockSpec((tokens_here, columns), lambda i, place: (0, 0))],
            out_specs=pl.BlockSpec((1, quarter, columns), lambda i, place: (i, 0, 0)),
        ),
        out_shape=jax.ShapeDtypeStruct((len(distances), quarter, columns), LOW),
        compiler_params=pltpu.CompilerParams(vmem_limit_bytes=48 << 20),
        name=name,
    )(place.astype(jnp.int32).reshape(1), *lefts, right)


def attention_forward_kernel(q_ref, k_ref, v_ref, o_ref, lse_ref):
    count, width = q_ref.shape
    rows = row_chunk(count, 256)
    lane = lax.broadcasted_iota(jnp.int32, (rows, width), 1)
    k = k_ref[...]
    v = v_ref[...]
    units = [(start, head) for start in range(0, count, rows) for head in range(width // HEAD_DIM)]

    def scores_of(unit):
        start, head = unit
        q = q_ref[start : start + rows] * jnp.asarray(HEAD_DIM ** (-0.5), LOW)
        return product(jnp.where((lane // HEAD_DIM) == head, q, jnp.zeros_like(q)), k, ROW_BY_ROW)

    logs = []
    ahead = scores_of(units[0])
    for step, (start, head) in enumerate(units):
        scores = ahead
        if step + 1 < len(units):
            ahead = scores_of(units[step + 1])
        top = jnp.max(scores, axis=-1, keepdims=True)
        weights = jnp.exp(scores - top)
        total = jnp.sum(weights, axis=-1, keepdims=True)
        part = product(weights.astype(LOW), v, PLAIN) / total
        if head == 0:
            out = part
            logs.append(jnp.zeros((rows, width), FULL))
        else:
            out = jnp.where((lane // HEAD_DIM) == head, part, out)
            o_ref[start : start + rows] = out.astype(LOW)
        logs[-1] = jnp.where(lane == head, top + jnp.log(total), logs[-1])
    lse_ref[...] = jnp.concatenate(logs, axis=0).T[: lse_ref.shape[0]]


def attention_forward(joint, pair):
    count, columns = joint.shape
    width = 2 * HEAD_DIM
    kind = columns // (3 * width)
    return pl.pallas_call(
        attention_forward_kernel,
        grid=(1,),
        in_specs=[
            pl.BlockSpec((count, width), lambda i: (0, pair)),
            pl.BlockSpec((count, width), lambda i: (0, kind + pair)),
            pl.BlockSpec((count, width), lambda i: (0, 2 * kind + pair)),
        ],
        out_specs=[
            pl.BlockSpec((count, width), lambda i: (0, 0)),
            pl.BlockSpec((8, count), lambda i: (0, 0)),
        ],
        out_shape=[
            jax.ShapeDtypeStruct((count, width), LOW),
            jax.ShapeDtypeStruct((8, count), FULL),
        ],
        compiler_params=pltpu.CompilerParams(vmem_limit_bytes=48 << 20),
        name="attention_forward",
    )(joint, joint, joint)


def attention_backward_kernel(
    q_ref, k_ref, v_ref, da_ref, o_ref, lse_ref, dq_ref, dk_ref, dv_ref,
    q_heads, da_heads, delta_ref, dq_total,
):
    count, width = q_ref.shape
    rows = row_chunk(count, 256)
    heads = width // HEAD_DIM
    scale = jnp.asarray(HEAD_DIM ** (-0.5), LOW)

    lane = lax.broadcasted_iota(jnp.int32, (count, width), 1)
    delta = jnp.zeros((count, width), FULL)
    q = q_ref[...] * scale
    da = da_ref[...]
    both_rows = da.astype(FULL) * o_ref[...].astype(FULL)
    for head in range(heads):
        mask = (lane // HEAD_DIM) == head
        q_heads[head] = jnp.where(mask, q, jnp.zeros_like(q))
        da_heads[head] = jnp.where(mask, da, jnp.zeros_like(da))
        row = jnp.sum(jnp.where(mask, both_rows, 0.0), axis=-1, keepdims=True)
        delta = jnp.where(lane == head, row, delta)
    delta_ref[...] = delta.T[:8]
    dq_total[...] = jnp.zeros_like(dq_total)

    lane = lax.broadcasted_iota(jnp.int32, (rows, width), 1)
    for start in range(0, count, rows):
        k = k_ref[start : start + rows]
        v = v_ref[start : start + rows]
        scaled_k = k * scale
        dk = dv = None
        for head in range(heads):
            q = q_heads[head]
            da = da_heads[head]
            probs = jnp.exp(product(k, q, ROW_BY_ROW) - lse_ref[head : head + 1, :])
            slope = probs * (product(v, da, ROW_BY_ROW) - delta_ref[head : head + 1, :])
            slope = slope.astype(LOW)
            dv_part = product(probs.astype(LOW), da, PLAIN)
            dk_part = product(slope, q, PLAIN)
            dv = dv_part if dv is None else dv + dv_part
            dk = dk_part if dk is None else dk + dk_part
            one_k = jnp.where((lane // HEAD_DIM) == head, scaled_k, jnp.zeros_like(k))
            dq_total[...] += product(slope, one_k, COLUMN_BY_COLUMN)
        dk_ref[start : start + rows] = dk.astype(LOW)
        dv_ref[start : start + rows] = dv.astype(LOW)
    dq_ref[...] = dq_total[...].astype(LOW)


def attention_backward(joint, da, out, lse, pair):
    count, columns = joint.shape
    width = 2 * HEAD_DIM
    kind = columns // (3 * width)
    alone = pl.BlockSpec((count, width), lambda i: (0, 0))
    grad = jax.ShapeDtypeStruct((count, width), LOW)
    return pl.pallas_call(
        attention_backward_kernel,
        grid=(1,),
        in_specs=[
            pl.BlockSpec((count, width), lambda i: (0, pair)),
            pl.BlockSpec((count, width), lambda i: (0, kind + pair)),
            pl.BlockSpec((count, width), lambda i: (0, 2 * kind + pair)),
            pl.BlockSpec((count, width), lambda i: (0, pair)),
            alone,
            pl.BlockSpec((8, count), lambda i: (0, 0)),
        ],
        out_specs=[alone, alone, alone],
        out_shape=[grad, grad, grad],
        scratch_shapes=[
            pltpu.VMEM((2, count, width), LOW),
            pltpu.VMEM((2, count, width), LOW),
            pltpu.VMEM((8, count), FULL),
            pltpu.VMEM((count, width), FULL),
        ],
        compiler_params=pltpu.CompilerParams(vmem_limit_bytes=48 << 20),
        name="attention_backward",
    )(joint, joint, joint, da, out, lse)


def put_together(place_ref, whole_ref, pieces, edge=0):
    for piece, refs in enumerate(pieces):
        rows = refs[0].shape[0]
        place = pl.ds(pl.multiple_of(place_ref[piece], rows), rows)
        if len(refs) == 1:
            whole_ref[place, :] = refs[0][...]
            continue

        @pl.when(pl.program_id(0) < edge)
        def _():
            whole_ref[place, :] = refs[0][...]

        @pl.when(pl.program_id(0) >= edge)
        def _():
            whole_ref[place, :] = refs[1][...]


def nested(refs, like):
    refs = iter(refs)
    return [tuple(next(refs) for _ in piece) for piece in like]


def feed_forward_kernel(
    expand, reduce, edge, place_ref, normed_ref, slope_ref, bias_ref, *refs
):
    active_ref, expand_slope_ref, back_ref, bias_grad_ref, total, expand_ref, reduce_ref = refs[-7:]
    arrays = sum(len(piece) for piece in expand)
    put_together(place_ref, expand_ref, nested(refs[:arrays], expand), edge)
    put_together(place_ref, reduce_ref, nested(refs[arrays:-7], reduce))
    step = pl.program_id(0)
    count = normed_ref.shape[0]
    half = count // 2
    bias_grad = None
    for rows in (slice(0, half), slice(half, count)):
        hidden = product(normed_ref[rows], expand_ref[...], PLAIN) + bias_ref[...]
        upstream = product(slope_ref[rows], reduce_ref[...], PLAIN)
        share = 0.5 * (1.0 + lax.erf(hidden * (0.5**0.5)))
        active_ref[rows] = (hidden * share).astype(LOW)
        density = jnp.exp(-0.5 * hidden * hidden) * 0.3989422804014327
        slope = (upstream * (share + hidden * density)).astype(LOW)
        expand_slope_ref[rows] = slope
        part = jnp.sum(slope.astype(FULL), axis=0, keepdims=True)
        bias_grad = part if bias_grad is None else bias_grad + part
        back = product(slope, expand_ref[...], ROW_BY_ROW)

        @pl.when(step == 0)
        def _():
            total[rows] = back

        @pl.when(step > 0)
        def _():
            total[rows] += back

    bias_grad_ref[...] = bias_grad

    @pl.when(step == pl.num_programs(0) - 1)
    def _():
        back_ref[...] = total[...].astype(LOW)


def feed_forward(normed, slope, bias, expand, early, reduce, place):
    count, width = normed.shape
    hidden = bias.shape[1]
    block = 512
    edge = early // block
    whole = pl.BlockSpec((count, width), lambda i, place: (0, 0))
    out = pl.BlockSpec((count, block), lambda i, place: (0, i))
    row = pl.BlockSpec((1, block), lambda i, place: (0, i))
    specs = []
    arrays = []
    for piece in [*expand, *reduce]:
        shape = (piece[0].shape[0], block)
        arrays += piece
        if len(piece) == 1:
            specs.append(pl.BlockSpec(shape, lambda i, place: (0, i)))
        else:
            specs.append(pl.BlockSpec(shape, lambda i, place: (0, jnp.minimum(i, edge - 1))))
            specs.append(pl.BlockSpec(shape, lambda i, place: (0, jnp.maximum(i - edge, 0))))
    return pl.pallas_call(
        lambda *refs: feed_forward_kernel(expand, reduce, edge, *refs),
        grid_spec=pltpu.PrefetchScalarGridSpec(
            num_scalar_prefetch=1,
            grid=(hidden // block,),
            in_specs=[whole, whole, row] + specs,
            out_specs=[out, out, whole, row],
            scratch_shapes=[
                pltpu.VMEM((count, width), FULL),
                pltpu.VMEM((width, block), LOW),
                pltpu.VMEM((width, block), LOW),
            ],
        ),
        out_shape=[
            jax.ShapeDtypeStruct((count, hidden), LOW),
            jax.ShapeDtypeStruct((count, hidden), LOW),
            jax.ShapeDtypeStruct((count, width), LOW),
            jax.ShapeDtypeStruct((1, hidden), FULL),
        ],
        compiler_params=pltpu.CompilerParams(vmem_limit_bytes=44 << 20),
        name="feed_forward",
    )(place, normed, slope, bias, *arrays)


def reduce_kernel(place_ref, active_ref, *refs):
    out_ref, total, reduce_ref = refs[-3:]
    put_together(place_ref, reduce_ref, [(ref,) for ref in refs[:-3]])
    part = product(active_ref[...], reduce_ref[...], ROW_BY_ROW)

    @pl.when(pl.program_id(0) == 0)
    def _():
        total[...] = part

    @pl.when(pl.program_id(0) > 0)
    def _():
        total[...] += part

    @pl.when(pl.program_id(0) == pl.num_programs(0) - 1)
    def _():
        out_ref[...] = total[...].astype(LOW)


def reduce_output(active, reduce, place):
    count, hidden = active.shape
    width = sum(piece.shape[0] for piece in reduce)
    block = 512 if hidden % 512 == 0 else hidden
    return pl.pallas_call(
        reduce_kernel,
        grid_spec=pltpu.PrefetchScalarGridSpec(
            num_scalar_prefetch=1,
            grid=(hidden // block,),
            in_specs=[pl.BlockSpec((count, block), lambda i, place: (0, i))]
            + [
                pl.BlockSpec((piece.shape[0], block), lambda i, place: (0, i)) for piece in reduce
            ],
            out_specs=pl.BlockSpec((count, width), lambda i, place: (0, 0)),
            scratch_shapes=[pltpu.VMEM((count, width), FULL), pltpu.VMEM((width, block), LOW)],
        ),
        out_shape=jax.ShapeDtypeStruct((count, width), LOW),
        compiler_params=pltpu.CompilerParams(vmem_limit_bytes=32 << 20),
        name="reduce_output",
    )(place, active, *reduce)


def swap(value, axis, distance):
    size = lax.axis_size(axis)
    return lax.ppermute(value, axis, [(i, i ^ distance) for i in range(size)])


def fence(*values):
    return lax.optimization_barrier(values)


def gather_near(rows_here):
    if lax.axis_size("fsdp") != 4:
        return (lax.all_gather(rows_here, "fsdp", axis=0, tiled=True),)
    return (rows_here, swap(rows_here, "fsdp", 1), swap(rows_here, "fsdp", 2))


def far_of(held):
    if len(held) == 1:
        return ()
    half = held[0].shape[0] // 2
    return (held[2][:half], held[1][half:])


def send_far(leaves):
    return (swap(leaves[0], "fsdp", 1), swap(leaves[1], "fsdp", 2)) if leaves else ()


def far_of(held):
    if len(held) == 1:
        return ()
    half = held[0].shape[0] // 2
    return (held[2][:half], held[1][half:])


def send_far(leaves):
    return (swap(leaves[0], "fsdp", 1), swap(leaves[1], "fsdp", 2)) if leaves else ()


def gather_far(held):
    return held + send_far(far_of(held))


def place_near(held):
    if len(held) == 1:
        return held[0]
    rows_here, near, side = held[:3]
    me = lax.axis_index("fsdp")
    count, width = rows_here.shape
    out = jnp.zeros((4 * count, width), rows_here.dtype)
    out = lax.dynamic_update_slice(out, rows_here, (me * count, 0))
    out = lax.dynamic_update_slice(out, near, ((me ^ 1) * count, 0))
    return lax.dynamic_update_slice(out, side, ((me ^ 2) * count, 0))


def place_far(out, held):
    if len(held) == 1:
        return out
    far_top, far_low = held[3:]
    half = far_top.shape[0]
    start = (lax.axis_index("fsdp") ^ 3) * 2 * half
    out = lax.dynamic_update_slice(out, far_top, (start, 0))
    return lax.dynamic_update_slice(out, far_low, (start + half, 0))


def grad_rows(left, right, distance):
    count = left.shape[1] // 4
    start = (lax.axis_index("fsdp") ^ distance) * count
    piece = lax.dynamic_slice_in_dim(left, start, count, 1)
    return product(piece, right, COLUMN_BY_COLUMN).astype(LOW)


def rows_at(matrices, distance):
    parts = []
    for matrix in matrices:
        count = matrix.shape[0] // 4
        start = (lax.axis_index("fsdp") ^ distance) * count
        parts.append(lax.dynamic_slice_in_dim(matrix, start, count, 0))
    return parts[0] if len(parts) == 1 else jnp.concatenate(parts, axis=1)


def far_halves(far):
    half = far.shape[0] // 2
    return (swap(far[:half], "fsdp", 1), swap(far[half:], "fsdp", 2))


def add_far(near, side, far):
    half = near.shape[0] // 2
    near = jnp.concatenate([near[:half], both((near[half:], far[1])).astype(LOW)], axis=0)
    side = jnp.concatenate([both((side[:half], far[0])).astype(LOW), side[half:]], axis=0)
    return (near, side)


def near_rows_out(pair):
    return (swap(pair[0], "fsdp", 1), swap(pair[1], "fsdp", 2))


def halves(value, bit):
    half = value.shape[0] // 2
    keep = lax.dynamic_slice_in_dim(value, bit * half, half, 0)
    send = lax.dynamic_slice_in_dim(value, (1 - bit) * half, half, 0)
    return keep, send.astype(LOW)


def split_rows(value, bit, distance):
    keep, send = halves(value, bit)
    return keep, swap(send, "ctx", distance)


def both(pair):
    return pair[0].astype(FULL) + pair[1].astype(FULL)


def join_rows(value, bit, distance):
    other = swap(value, "ctx", distance)
    return jnp.where(
        bit == 0,
        jnp.concatenate([value, other], axis=0),
        jnp.concatenate([other, value], axis=0),
    )


def pairwise(pieces):
    return (pieces[0] + pieces[1]) + (pieces[2] + pieces[3])


def swapped_if(bit, pair):
    return [jnp.where(bit == 0, pair[0], pair[1]), jnp.where(bit == 0, pair[1], pair[0])]


def per_device(
    tokens,
    clip_mask,
    cotangent,
    first_gain,
    first_shift,
    joint_weight,
    joint_bias,
    mixer_weight,
    mixer_bias,
    second_gain,
    second_shift,
    expand_weight,
    expand_bias,
    reduce_weight,
    reduce_bias,
):
    clips_here, rows_here, width = tokens.shape
    if lax.axis_size("ctx") != 4 or lax.axis_size("tp") != 2 or clips_here != 2:
        raise ValueError("mesh")
    shard = lax.axis_index("fsdp")
    block = lax.axis_index("ctx")
    core = lax.axis_index("tp")
    clip_at = block >> 1
    part_at = block & 1
    width_half = width // 2
    quarter = width_half // 2
    features = joint_weight.shape[2]
    part_width = features // 2
    pair_width = 2 * HEAD_DIM
    tokens_here = clips_here * rows_here

    flat_tokens = tokens.reshape(tokens_here, width)
    (first_normed,) = by_rows(
        first_norm_kernel, "first_norm", [LOW], False,
        flat_tokens, first_gain[None], first_shift[None],
    )
    first_normed = first_normed.reshape(clips_here, rows_here, width)
    mine = lax.dynamic_slice_in_dim(first_normed, core * width_half, width_half, 2)
    other_side = lax.dynamic_slice_in_dim(first_normed, (1 - core) * width_half, width_half, 2)
    own_clip = lax.dynamic_index_in_dim(mine, clip_at, 0, False)
    own_other = lax.dynamic_index_in_dim(other_side, clip_at, 0, False)
    other_clip = lax.dynamic_index_in_dim(mine, 1 - clip_at, 0, False)
    joint_part = lax.dynamic_slice_in_dim(joint_weight, part_at * part_width, part_width, 2)
    early = expand_weight.shape[1] // 2
    wide_part = jnp.concatenate(
        [expand_weight[:, :early]] + [joint_part[:, kind] for kind in range(3)] + [mixer_weight],
        axis=1,
    )

    own_clip, left, right, wide_part = fence(
        own_clip, other_clip[:, :quarter], other_clip[:, quarter:], wide_part
    )
    near_rows = swap(own_clip, "ctx", 1)
    across_left = swap(left, "ctx", 2)
    far_right = swap(right, "ctx", 3)
    wide_held = gather_near(wide_part)

    near_rows, across_left, far_right, wide_held, expand_rest = fence(
        near_rows, across_left, far_right, wide_held, expand_weight[:, early:]
    )
    passed = swap(jnp.concatenate([across_left, far_right], axis=1), "ctx", 1)
    held = gather_far(tuple(piece[:, early:] for piece in wide_held))
    rest_held = gather_near(expand_rest)

    passed, held = fence(passed, held)
    cross_rows = jnp.concatenate(
        [
            near_rows,
            jnp.concatenate([across_left, passed[:, quarter:]], axis=1),
            jnp.concatenate([passed[:, :quarter], far_right], axis=1),
        ],
        axis=0,
    )
    cross_other = swap(cross_rows, "tp", 1)
    both_full = place_far(place_near(held), held)
    joint_columns = 3 * part_width
    joint_full = jnp.concatenate(
        [
            lax.dynamic_slice(both_full, (start * width_half, 0), (width_half, joint_columns))
            for start in (core, 1 - core)
        ],
        axis=0,
    )

    cross_other, joint_full, both_full, reduce_weight = fence(
        cross_other, joint_full, both_full, reduce_weight
    )
    mixer_full = both_full[:, joint_columns:]
    reduce_held = gather_near(reduce_weight)
    normed_mine = jnp.concatenate([own_clip, cross_rows], axis=0)
    normed_other = jnp.concatenate([own_other, cross_other], axis=0)
    bias_part = lax.dynamic_slice_in_dim(joint_bias, part_at * part_width, part_width, 1)
    bias_row = jnp.concatenate([bias_part[0], jnp.zeros_like(bias_part[0]), bias_part[1]])
    joint_out = joint_projection(normed_mine, normed_other, joint_full, bias_row[None])
    out_first, log_first = attention_forward(joint_out, 0)

    out_first, joint_out, mixer_full, rest_held = fence(
        out_first, joint_out, mixer_full, rest_held
    )
    first_blocks = out_first.reshape(4, rows_here, pair_width)
    arrived_first = [swap(first_blocks[d], "ctx", d) for d in (1, 2, 3)]
    out_second, log_second = attention_forward(joint_out, 1)

    far_leaves = far_of(
        tuple(
            jnp.concatenate([one[:, :early], two], axis=1)
            for one, two in zip(wide_held, rest_held)
        )
    )
    out_second, arrived_first, reduce_held, far_leaves = fence(
        out_second, arrived_first, reduce_held, far_leaves
    )
    second_blocks = out_second.reshape(4, rows_here, pair_width)
    arrived_second = [swap(second_blocks[d], "ctx", d) for d in (1, 2, 3)]
    expand_far_rows = send_far(far_leaves)

    arrived_second, expand_far_rows, reduce_held, reduce_leaves = fence(
        arrived_second, expand_far_rows, reduce_held, far_of(reduce_held)
    )
    reduce_held = reduce_held + send_far(reduce_leaves)
    expand_held = list(zip(wide_held, rest_held)) + [(rows,) for rows in expand_far_rows]
    arrived = [jnp.concatenate([first_blocks[0], second_blocks[0]], axis=1)] + [
        jnp.concatenate([one, two], axis=1) for one, two in zip(arrived_first, arrived_second)
    ]
    own_joined = jnp.concatenate(swapped_if(part_at, arrived[:2]), axis=1)
    other_joined = jnp.concatenate(swapped_if(part_at, arrived[2:]), axis=1)
    mixed_in = jnp.concatenate(swapped_if(clip_at, [own_joined, other_joined]), axis=0)
    mixer_part = product(mixed_in, mixer_full, ROW_BY_ROW).astype(LOW)
    mixer_swapped = swap(mixer_part, "tp", 1)
    mixer_row = mixer_bias[None]
    (second_normed,) = by_rows(
        second_norm_kernel, "second_norm", [LOW], False,
        flat_tokens, mixer_part, mixer_swapped, mixer_row, second_gain[None], second_shift[None],
    )
    valid = clip_mask.astype(FULL)[:, None, None]
    reduce_slope = (cotangent.astype(FULL) * valid).astype(LOW).reshape(tokens_here, width)
    reduce_bias_grad = jnp.sum(reduce_slope.astype(FULL), axis=0)

    second_normed, reduce_slope, reduce_held = fence(second_normed, reduce_slope, reduce_held)
    four = lax.axis_size("fsdp") == 4
    start = jnp.zeros((), jnp.int32)
    if four:
        rows = width // 4
        pieces_at = jnp.stack([shard, shard ^ 1, shard ^ 2, shard ^ 3, shard ^ 3]) * rows
        pieces_at = pieces_at.astype(jnp.int32) + jnp.array([0, 0, 0, 0, rows // 2], jnp.int32)
    else:
        pieces_at = start.reshape(1)
    activated, expand_slope, second_part, expand_bias_grad = feed_forward(
        second_normed, reduce_slope, expand_bias[None], expand_held, early,
        [(piece,) for piece in reduce_held], pieces_at,
    )
    expand_bias_grad = expand_bias_grad[0]

    second_swapped = swap(second_part, "tp", 1)
    place, order = (shard, (3, 2, 1, 0)) if four else (start, (0, 1, 2, 3))
    if four:
        half = width // 8
        far = grad_rows(second_normed, expand_slope, 3)
        far_top, far_low, normed_again, expand_slope = fence(
            far[:half], far[half:], second_normed, expand_slope
        )
        expand_far = (swap(far_top, "fsdp", 1), swap(far_low, "fsdp", 2))
        expand_parts = [grad_rows(normed_again, expand_slope, d) for d in (0, 1, 2)]
        expand_parts, second_swapped = fence(expand_parts, second_swapped)
    else:
        expand_far = ()
        expand_whole = product(second_normed, expand_slope, COLUMN_BY_COLUMN).astype(LOW)
    mixer_slope, first_sum_back, second_sums = by_rows(
        second_norm_back_kernel, "second_norm_back", [LOW, FULL], True,
        flat_tokens, mixer_part, mixer_swapped, mixer_row, second_gain[None],
        second_part, second_swapped, reduce_slope,
    )
    attended_slope = product(mixer_slope, mixer_full, PLAIN).astype(LOW)

    leaving = []
    for distance in range(4):
        to = block ^ distance
        corner = ((to >> 1) * rows_here, (to & 1) * part_width)
        leaving.append(lax.dynamic_slice(attended_slope, corner, (rows_here, part_width)))
    expand_near = add_far(expand_parts[1], expand_parts[2], expand_far) if four else ()
    leaving, mixer_slope, mixed_in, activated, expand_near = fence(
        leaving, mixer_slope, mixed_in, activated, expand_near
    )
    slope_blocks = [leaving[0]] + [swap(leaving[d], "ctx", d) for d in (1, 2, 3)]
    if four:
        expand_near = near_rows_out(expand_near)
    wide = (
        product(reduce_slope, activated, COLUMN_BY_COLUMN).astype(LOW),
        product(mixer_slope, mixed_in, COLUMN_BY_COLUMN).astype(LOW),
    )
    if four:
        wide_far, wide_side, wide_next = (rows_at(wide, distance) for distance in (3, 2, 1))
        far_top, far_low = wide_far[:half], wide_far[half:]
        wide_early = (wide_next[:half], wide_side[half:])
    else:
        far_top, far_low, wide_early = (), (), ()

    slope_blocks, expand_near, far_top, far_low = fence(
        slope_blocks, expand_near, far_top, far_low
    )
    if four:
        expand_sum = expand_parts[0].astype(FULL) + both(expand_near)
    else:
        expand_sum = lax.psum_scatter(
            expand_whole, "fsdp", scatter_dimension=0, tiled=True
        ).astype(FULL)
    expand_keep, expand_send = halves(expand_sum, part_at)
    slope_clip = jnp.concatenate(slope_blocks, axis=0)
    expand_send, slope_clip, far_top, far_low = fence(expand_send, slope_clip, far_top, far_low)
    wide_far = (swap(far_top, "fsdp", 1), swap(far_low, "fsdp", 2)) if four else ()
    expand_rows = (expand_keep, swap(expand_send, "ctx", 1))
    grad_first = attention_backward(joint_out, slope_clip, out_first, log_first, 0)

    grad_first, slope_clip, wide_far, expand_rows = fence(
        grad_first, slope_clip, wide_far, expand_rows
    )
    if four:
        wide_late = (
            both((wide_next[half:], wide_far[1])).astype(LOW),
            both((wide_side[:half], wide_far[0])).astype(LOW),
        )
    else:
        wide_late = ()
    expand_keep, expand_send = halves(both(expand_rows), clip_at)
    expand_send, slope_clip, wide_early, wide_late = fence(
        expand_send, slope_clip, wide_early, wide_late
    )
    if four:
        wide_early = near_rows_out(wide_early)
    expand_rows = (expand_keep, swap(expand_send, "ctx", 2))
    grad_second = attention_backward(joint_out, slope_clip, out_second, log_second, 1)

    grad_second, expand_rows, wide_early, wide_late = fence(
        grad_second, expand_rows, wide_early, wide_late
    )
    if four:
        wide_late = near_rows_out(wide_late)
    expand_rows = join_rows(both(expand_rows).astype(LOW), clip_at, 2)
    joint_slope = jnp.concatenate(
        [grad[kind] for kind in range(3) for grad in (grad_first, grad_second)], axis=1
    )
    first_there = product(joint_slope, joint_full[width_half:], ROW_BY_ROW).astype(LOW)
    first_here = rows_product(joint_slope, joint_full[:width_half], "first_slope")
    first_half = both((first_here, swap(first_there, "tp", 1))).astype(LOW)

    if not four:
        wide_near = lax.psum_scatter(
            jnp.concatenate(wide, axis=1), "fsdp", scatter_dimension=0, tiled=True
        )
    first_half, joint_slope = fence(first_half, joint_slope)
    pieces = first_half.reshape(4, rows_here, width_half)
    passing = jnp.concatenate([pieces[1], pieces[3][:, :quarter], pieces[2][:, quarter:]], axis=1)
    passing = swap(passing, "ctx", 1)
    place = (shard if four else start) ^ (2 * core)
    joint_parts = grad_products([normed_mine, normed_other], joint_slope, place, order, "joint_grad")
    slope_sums = jnp.sum(joint_slope.astype(FULL), axis=0)
    bias_sums = jnp.stack([slope_sums[:part_width], slope_sums[2 * part_width :]])
    joint_bias_grad = lax.dynamic_update_slice(
        jnp.zeros((2, features), FULL), bias_sums, (0, part_at * part_width)
    )

    joint_far = far_halves(joint_parts[0]) if four else ()
    passing, joint_far, wide_late, expand_rows = fence(
        passing, joint_far, wide_late, expand_rows
    )
    if four:
        near_sum = [both((wide_early[0], wide_late[1])), both((wide_late[0], wide_early[1]))]
        wide_sum = rows_at(wide, 0).astype(FULL) + jnp.concatenate(near_sum, axis=0)
    else:
        wide_sum = wide_near.astype(FULL)
    wide_keep, wide_send = halves(wide_sum, part_at)
    own_half = both((pieces[0], passing[:, :width_half])).astype(LOW)
    to_left = both((pieces[2][:, :quarter], passing[:, width_half : width_half + quarter]))
    to_right = both((pieces[3][:, quarter:], passing[:, width_half + quarter :]))
    joint_near = add_far(joint_parts[2], joint_parts[1], joint_far) if four else ()
    to_left, to_right, own_half, wide_send, joint_near, activated = fence(
        to_left.astype(LOW), to_right.astype(LOW), own_half, wide_send, joint_near, activated
    )
    other_half = jnp.concatenate([swap(to_left, "ctx", 2), swap(to_right, "ctx", 3)], axis=1)
    wide_rows = (wide_keep, swap(wide_send, "ctx", 1))
    if four:
        joint_near = near_rows_out(joint_near)
    else:
        joint_near = lax.psum_scatter(
            joint_parts.reshape(width, -1), "fsdp", scatter_dimension=0, tiled=True
        )
    reduce_part = reduce_output(activated, reduce_held, pieces_at)

    other_half, joint_near, wide_rows, reduce_part = fence(
        other_half, joint_near, wide_rows, reduce_part
    )
    slope_half = jnp.concatenate(swapped_if(clip_at, [own_half, other_half]), axis=0)
    slope_other = swap(slope_half, "tp", 1)
    slope_other, expand_rows = fence(slope_other, expand_rows)
    expand_grad = join_rows(expand_rows, part_at, 1).astype(FULL)
    first_slope = jnp.concatenate(swapped_if(core, [slope_half, slope_other]), axis=1)
    wide_rows = split_rows(both(wide_rows), clip_at, 2)
    reduce_swapped = swap(reduce_part, "tp", 1)
    joint_sum = joint_parts[3].astype(FULL) + both(joint_near) if four else joint_near
    joint_sum = joint_sum.astype(LOW)
    joint_sum = (joint_sum, swap(joint_sum, "ctx", 2))
    tokens_grad, first_sums = by_rows(
        first_norm_back_kernel, "first_norm_back", [FULL], True,
        flat_tokens, first_slope, first_gain[None],
        cotangent.reshape(tokens_here, width), first_sum_back,
    )
    first_sums, tokens_grad, reduce_swapped = fence(first_sums, tokens_grad, reduce_swapped)
    vectors = [
        first_sums[0],
        first_sums[1],
        joint_bias_grad[0],
        joint_bias_grad[1],
        second_sums[2],
        second_sums[0],
        second_sums[1],
        expand_bias_grad,
        reduce_bias_grad,
    ]
    packed = jnp.concatenate(vectors).reshape(-1, 128)
    packed_pieces = [packed] + [swap(packed, "ctx", d) for d in (1, 2, 3)]
    reduce_out = both((reduce_part, reduce_swapped)) + reduce_bias
    mixer_out = both((mixer_part, mixer_swapped)) + mixer_bias
    branches = (mixer_out + reduce_out).reshape(clips_here, rows_here, width)
    result = (tokens.astype(FULL) + valid * branches).astype(LOW)

    packed_pieces, joint_sum, wide_rows, result = fence(
        packed_pieces, joint_sum, wide_rows, result
    )
    packed = pairwise(packed_pieces)
    if four:
        packed = pairwise([packed] + [swap(packed, "fsdp", d) for d in (1, 2, 3)])
    else:
        packed = lax.psum(packed, "fsdp")
    joint_sum = both(joint_sum).astype(LOW)
    joint_parts = swapped_if(part_at, [joint_sum, swap(joint_sum, "ctx", 1)])
    joint_grad = jnp.concatenate(
        [piece.reshape(-1, 3, part_width) for piece in joint_parts], axis=2
    ).astype(FULL)
    wide_rows = join_rows(both(wide_rows).astype(LOW), clip_at, 2)
    wide_rows = join_rows(wide_rows, part_at, 1).astype(FULL)
    reduce_grad = wide_rows[:, : activated.shape[1]]
    mixer_grad = wide_rows[:, activated.shape[1] :]
    packed = packed.reshape(-1)
    shares = []
    start = 0
    for vector in vectors:
        share = vector.shape[0] // lax.axis_size("fsdp")
        shares.append(lax.dynamic_slice_in_dim(packed, start + shard * share, share, 0))
        start += vector.shape[0]

    shape = (clips_here, rows_here, width)
    return (
        result,
        tokens_grad.reshape(shape),
        shares[0],
        shares[1],
        joint_grad,
        jnp.stack([shares[2], shares[3]]),
        mixer_grad,
        shares[4],
        shares[5],
        shares[6],
        expand_grad,
        shares[7],
        reduce_grad,
        shares[8],
    )


def solution(mesh):
    return jax.shard_map(
        per_device,
        mesh=mesh,
        in_specs=(
            P("fsdp", "ctx", None),
            P("fsdp"),
            P("fsdp", "ctx", None),
            P(),
            P(),
            P("fsdp", None, "tp"),
            P(None, "tp"),
            P("fsdp", "tp"),
            P(),
            P(),
            P(),
            P("fsdp", "tp"),
            P("tp"),
            P("fsdp", "tp"),
            P(),
        ),
        out_specs=(
            P("fsdp", "ctx", None),
            P("fsdp", "ctx", None),
            P("fsdp"),
            P("fsdp"),
            P("fsdp", None, "tp"),
            P(None, ("tp", "fsdp")),
            P("fsdp", "tp"),
            P("fsdp"),
            P("fsdp"),
            P("fsdp"),
            P("fsdp", "tp"),
            P(("tp", "fsdp")),
            P("fsdp", "tp"),
            P("fsdp"),
        ),
        check_vma=False,
    )
```

```python
import jax
import jax.numpy as jnp
from jax import lax
from jax.experimental import pallas as pl
from jax.experimental.pallas import tpu as pltpu
from jax.sharding import PartitionSpec as P

HEAD_DIM = 64
EPSILON = 1e-06
LOW = jnp.bfloat16
FULL = jnp.float32

ROW_BY_ROW = (((1,), (1,)), ((), ()))
PLAIN = (((1,), (0,)), ((), ()))
COLUMN_BY_COLUMN = (((0,), (0,)), ((), ()))


def product(left, right, dims):
    return lax.dot_general(left, right, dims, preferred_element_type=FULL)


def normalize(value_rows):
    center = value_rows - jnp.mean(value_rows, axis=-1, keepdims=True)
    inverse = lax.rsqrt(jnp.mean(center * center, axis=-1, keepdims=True) + EPSILON)
    return (center * inverse, inverse)


def norm_back(upstream, gain, scaled, inverse):
    weighted = upstream * gain
    return inverse * (
        weighted
        - jnp.mean(weighted, axis=-1, keepdims=True)
        - scaled * jnp.mean(weighted * scaled, axis=-1, keepdims=True)
    )


def row_chunk(count, most):
    for chunk in range(most, 0, -16):
        if count % chunk == 0:
            return chunk
    raise ValueError("rows")


def first_norm_kernel(tokens_ref, gain_ref, shift_ref, out_ref):
    scaled, _ = normalize(tokens_ref[...].astype(FULL))
    out_ref[...] = (scaled * gain_ref[...] + shift_ref[...]).astype(LOW)


def second_norm_kernel(tokens_ref, one_ref, two_ref, bias_ref, gain_ref, shift_ref, out_ref):
    mixed = one_ref[...].astype(FULL) + two_ref[...].astype(FULL) + bias_ref[...]
    scaled, _ = normalize(tokens_ref[...].astype(FULL) + mixed)
    out_ref[...] = (scaled * gain_ref[...] + shift_ref[...]).astype(LOW)


def add_sums(ref, rows):
    sums = jnp.concatenate([jnp.sum(row, axis=0, keepdims=True) for row in rows], axis=0)

    @pl.when(pl.program_id(0) == 0)
    def _():
        ref[: len(rows)] = sums

    @pl.when(pl.program_id(0) > 0)
    def _():
        ref[: len(rows)] += sums


def second_norm_back_kernel(
    tokens_ref, one_ref, two_ref, bias_ref, gain_ref, left_ref, right_ref, outer_ref,
    slope_ref, back_ref, sums_ref,
):
    mixed = one_ref[...].astype(FULL) + two_ref[...].astype(FULL) + bias_ref[...]
    scaled, inverse = normalize(tokens_ref[...].astype(FULL) + mixed)
    upstream = left_ref[...].astype(FULL) + right_ref[...].astype(FULL)
    back = norm_back(upstream, gain_ref[...], scaled, inverse)
    slope = (outer_ref[...].astype(FULL) + back).astype(LOW)
    slope_ref[...] = slope
    back_ref[...] = back
    add_sums(sums_ref, [upstream * scaled, upstream, slope.astype(FULL)])


def first_norm_back_kernel(
    tokens_ref, upstream_ref, gain_ref, outer_ref, back_ref, out_ref, sums_ref
):
    scaled, inverse = normalize(tokens_ref[...].astype(FULL))
    upstream = upstream_ref[...].astype(FULL)
    back = norm_back(upstream, gain_ref[...], scaled, inverse)
    out_ref[...] = outer_ref[...].astype(FULL) + back_ref[...] + back
    add_sums(sums_ref, [upstream * scaled, upstream])


def by_rows(kernel, name, out_types, sums, *values):
    count, width = values[0].shape
    chunk = row_chunk(count, 112)
    part = pl.BlockSpec((chunk, width), lambda i: (i, 0))
    in_specs = [
        part if value.shape[0] == count else pl.BlockSpec((1, width), lambda i: (0, 0))
        for value in values
    ]
    out_specs = [part for _ in out_types]
    out_shape = [jax.ShapeDtypeStruct((count, width), kind) for kind in out_types]
    if sums:
        out_specs.append(pl.BlockSpec((8, width), lambda i: (0, 0)))
        out_shape.append(jax.ShapeDtypeStruct((8, width), FULL))
    return pl.pallas_call(
        kernel,
        grid=(count // chunk,),
        in_specs=in_specs,
        out_specs=out_specs,
        out_shape=out_shape,
        compiler_params=pltpu.CompilerParams(vmem_limit_bytes=16 << 20),
        name=name,
    )(*values)


def joint_kernel(mine_ref, other_ref, weight_ref, bias_ref, out_ref):
    half = mine_ref.shape[1]
    out = product(mine_ref[...], weight_ref[:half], PLAIN)
    out += product(other_ref[...], weight_ref[half:], PLAIN)
    out_ref[...] = (out + bias_ref[...]).astype(LOW)


def joint_projection(mine, other, weight, bias):
    count, half = mine.shape
    columns = weight.shape[1]
    chunk = row_chunk(count, 784)
    part = pl.BlockSpec((chunk, half), lambda i: (i, 0))
    return pl.pallas_call(
        joint_kernel,
        grid=(count // chunk,),
        in_specs=[
            part,
            part,
            pl.BlockSpec(weight.shape, lambda i: (0, 0)),
            pl.BlockSpec((1, columns), lambda i: (0, 0)),
        ],
        out_specs=pl.BlockSpec((chunk, columns), lambda i: (i, 0)),
        out_shape=jax.ShapeDtypeStruct((count, columns), LOW),
        compiler_params=pltpu.CompilerParams(vmem_limit_bytes=40 << 20),
        name="joint_projection",
    )(mine, other, weight, bias)


def rows_kernel(left_ref, right_ref, out_ref):
    out_ref[...] = product(left_ref[...], right_ref[...], ROW_BY_ROW).astype(LOW)


def rows_product(left, right, name):
    count, depth = left.shape
    columns = right.shape[0]
    chunk = row_chunk(count, 400)
    return pl.pallas_call(
        rows_kernel,
        grid=(count // chunk,),
        in_specs=[
            pl.BlockSpec((chunk, depth), lambda i: (i, 0)),
            pl.BlockSpec((columns, depth), lambda i: (0, 0)),
        ],
        out_specs=pl.BlockSpec((chunk, columns), lambda i: (i, 0)),
        out_shape=jax.ShapeDtypeStruct((count, columns), LOW),
        compiler_params=pltpu.CompilerParams(vmem_limit_bytes=48 << 20),
        name=name,
    )(left, right)


def grad_kernel(distances, place_ref, *refs):
    lefts, (right_ref, out_ref) = refs[:-2], refs[-2:]
    left = lefts[0][...]
    if len(lefts) == 2:
        slot = place_ref[0] ^ distance_at(distances, pl.program_id(0))
        left = jnp.where((slot >> 1) == 0, left, lefts[1][...])
    out_ref[0] = product(left, right_ref[...], COLUMN_BY_COLUMN).astype(LOW)


def distance_at(distances, step):
    if len(distances) == 1:
        return distances[0]
    return distances[0] + step * (distances[1] - distances[0])


def grad_products(lefts, right, place, distances, name):
    tokens_here, columns = right.shape
    quarter = sum(left.shape[1] for left in lefts) // 4
    blocks = lefts[0].shape[1] // quarter

    def left_at(i, place):
        return (0, (place[0] ^ distance_at(distances, i)) & (blocks - 1))

    return pl.pallas_call(
        lambda *refs: grad_kernel(distances, *refs),
        grid_spec=pltpu.PrefetchScalarGridSpec(
            num_scalar_prefetch=1,
            grid=(len(distances),),
            in_specs=[pl.BlockSpec((tokens_here, quarter), left_at) for _ in lefts]
            + [pl.BlockSpec((tokens_here, columns), lambda i, place: (0, 0))],
            out_specs=pl.BlockSpec((1, quarter, columns), lambda i, place: (i, 0, 0)),
        ),
        out_shape=jax.ShapeDtypeStruct((len(distances), quarter, columns), LOW),
        compiler_params=pltpu.CompilerParams(vmem_limit_bytes=48 << 20),
        name=name,
    )(place.astype(jnp.int32).reshape(1), *lefts, right)


def attention_forward_kernel(q_ref, k_ref, v_ref, o_ref, lse_ref):
    count, width = q_ref.shape
    rows = row_chunk(count, 256)
    lane = lax.broadcasted_iota(jnp.int32, (rows, width), 1)
    k = k_ref[...]
    v = v_ref[...]
    units = [(start, head) for start in range(0, count, rows) for head in range(width // HEAD_DIM)]

    def scores_of(unit):
        start, head = unit
        q = q_ref[start : start + rows] * jnp.asarray(HEAD_DIM ** (-0.5), LOW)
        return product(jnp.where((lane // HEAD_DIM) == head, q, jnp.zeros_like(q)), k, ROW_BY_ROW)

    logs = []
    ahead = scores_of(units[0])
    for step, (start, head) in enumerate(units):
        scores = ahead
        if step + 1 < len(units):
            ahead = scores_of(units[step + 1])
        top = jnp.max(scores, axis=-1, keepdims=True)
        weights = jnp.exp(scores - top)
        total = jnp.sum(weights, axis=-1, keepdims=True)
        part = product(weights.astype(LOW), v, PLAIN) / total
        if head == 0:
            out = part
            logs.append(jnp.zeros((rows, width), FULL))
        else:
            out = jnp.where((lane // HEAD_DIM) == head, part, out)
            o_ref[start : start + rows] = out.astype(LOW)
        logs[-1] = jnp.where(lane == head, top + jnp.log(total), logs[-1])
    lse_ref[...] = jnp.concatenate(logs, axis=0).T[: lse_ref.shape[0]]


def attention_forward(joint, pair):
    count, columns = joint.shape
    width = 2 * HEAD_DIM
    kind = columns // (3 * width)
    return pl.pallas_call(
        attention_forward_kernel,
        grid=(1,),
        in_specs=[
            pl.BlockSpec((count, width), lambda i: (0, pair)),
            pl.BlockSpec((count, width), lambda i: (0, kind + pair)),
            pl.BlockSpec((count, width), lambda i: (0, 2 * kind + pair)),
        ],
        out_specs=[
            pl.BlockSpec((count, width), lambda i: (0, 0)),
            pl.BlockSpec((8, count), lambda i: (0, 0)),
        ],
        out_shape=[
            jax.ShapeDtypeStruct((count, width), LOW),
            jax.ShapeDtypeStruct((8, count), FULL),
        ],
        compiler_params=pltpu.CompilerParams(vmem_limit_bytes=48 << 20),
        name="attention_forward",
    )(joint, joint, joint)


def attention_backward_kernel(
    q_ref, k_ref, v_ref, da_ref, o_ref, lse_ref, dq_ref, dk_ref, dv_ref,
    q_heads, da_heads, delta_ref, dq_total,
):
    count, width = q_ref.shape
    rows = row_chunk(count, 256)
    heads = width // HEAD_DIM
    scale = jnp.asarray(HEAD_DIM ** (-0.5), LOW)

    lane = lax.broadcasted_iota(jnp.int32, (count, width), 1)
    delta = jnp.zeros((count, width), FULL)
    q = q_ref[...] * scale
    da = da_ref[...]
    both_rows = da.astype(FULL) * o_ref[...].astype(FULL)
    for head in range(heads):
        mask = (lane // HEAD_DIM) == head
        q_heads[head] = jnp.where(mask, q, jnp.zeros_like(q))
        da_heads[head] = jnp.where(mask, da, jnp.zeros_like(da))
        row = jnp.sum(jnp.where(mask, both_rows, 0.0), axis=-1, keepdims=True)
        delta = jnp.where(lane == head, row, delta)
    delta_ref[...] = delta.T[:8]
    dq_total[...] = jnp.zeros_like(dq_total)

    lane = lax.broadcasted_iota(jnp.int32, (rows, width), 1)
    for start in range(0, count, rows):
        k = k_ref[start : start + rows]
        v = v_ref[start : start + rows]
        scaled_k = k * scale
        dk = dv = None
        for head in range(heads):
            q = q_heads[head]
            da = da_heads[head]
            probs = jnp.exp(product(k, q, ROW_BY_ROW) - lse_ref[head : head + 1, :])
            slope = probs * (product(v, da, ROW_BY_ROW) - delta_ref[head : head + 1, :])
            slope = slope.astype(LOW)
            dv_part = product(probs.astype(LOW), da, PLAIN)
            dk_part = product(slope, q, PLAIN)
            dv = dv_part if dv is None else dv + dv_part
            dk = dk_part if dk is None else dk + dk_part
            one_k = jnp.where((lane // HEAD_DIM) == head, scaled_k, jnp.zeros_like(k))
            dq_total[...] += product(slope, one_k, COLUMN_BY_COLUMN)
        dk_ref[start : start + rows] = dk.astype(LOW)
        dv_ref[start : start + rows] = dv.astype(LOW)
    dq_ref[...] = dq_total[...].astype(LOW)


def attention_backward(joint, da, out, lse, pair):
    count, columns = joint.shape
    width = 2 * HEAD_DIM
    kind = columns // (3 * width)
    alone = pl.BlockSpec((count, width), lambda i: (0, 0))
    grad = jax.ShapeDtypeStruct((count, width), LOW)
    return pl.pallas_call(
        attention_backward_kernel,
        grid=(1,),
        in_specs=[
            pl.BlockSpec((count, width), lambda i: (0, pair)),
            pl.BlockSpec((count, width), lambda i: (0, kind + pair)),
            pl.BlockSpec((count, width), lambda i: (0, 2 * kind + pair)),
            pl.BlockSpec((count, width), lambda i: (0, pair)),
            alone,
            pl.BlockSpec((8, count), lambda i: (0, 0)),
        ],
        out_specs=[alone, alone, alone],
        out_shape=[grad, grad, grad],
        scratch_shapes=[
            pltpu.VMEM((2, count, width), LOW),
            pltpu.VMEM((2, count, width), LOW),
            pltpu.VMEM((8, count), FULL),
            pltpu.VMEM((count, width), FULL),
        ],
        compiler_params=pltpu.CompilerParams(vmem_limit_bytes=48 << 20),
        name="attention_backward",
    )(joint, joint, joint, da, out, lse)


def put_together(place_ref, whole_ref, pieces, edge=0):
    for piece, refs in enumerate(pieces):
        rows = refs[0].shape[0]
        place = pl.ds(pl.multiple_of(place_ref[piece], rows), rows)
        if len(refs) == 1:
            whole_ref[place, :] = refs[0][...]
            continue

        @pl.when(pl.program_id(0) < edge)
        def _():
            whole_ref[place, :] = refs[0][...]

        @pl.when(pl.program_id(0) >= edge)
        def _():
            whole_ref[place, :] = refs[1][...]


def nested(refs, like):
    refs = iter(refs)
    return [tuple(next(refs) for _ in piece) for piece in like]


def feed_forward_kernel(
    expand, reduce, edge, place_ref, normed_ref, slope_ref, bias_ref, *refs
):
    active_ref, expand_slope_ref, back_ref, bias_grad_ref, total, expand_ref, reduce_ref = refs[-7:]
    arrays = sum(len(piece) for piece in expand)
    put_together(place_ref, expand_ref, nested(refs[:arrays], expand), edge)
    put_together(place_ref, reduce_ref, nested(refs[arrays:-7], reduce))
    step = pl.program_id(0)
    count = normed_ref.shape[0]
    half = count // 2
    bias_grad = None
    for rows in (slice(0, half), slice(half, count)):
        hidden = product(normed_ref[rows], expand_ref[...], PLAIN) + bias_ref[...]
        upstream = product(slope_ref[rows], reduce_ref[...], PLAIN)
        share = 0.5 * (1.0 + lax.erf(hidden * (0.5**0.5)))
        active_ref[rows] = (hidden * share).astype(LOW)
        density = jnp.exp(-0.5 * hidden * hidden) * 0.3989422804014327
        slope = (upstream * (share + hidden * density)).astype(LOW)
        expand_slope_ref[rows] = slope
        part = jnp.sum(slope.astype(FULL), axis=0, keepdims=True)
        bias_grad = part if bias_grad is None else bias_grad + part
        back = product(slope, expand_ref[...], ROW_BY_ROW)

        @pl.when(step == 0)
        def _():
            total[rows] = back

        @pl.when(step > 0)
        def _():
            total[rows] += back

    bias_grad_ref[...] = bias_grad

    @pl.when(step == pl.num_programs(0) - 1)
    def _():
        back_ref[...] = total[...].astype(LOW)


def feed_forward(normed, slope, bias, expand, early, reduce, place):
    count, width = normed.shape
    hidden = bias.shape[1]
    block = 512
    edge = early // block
    whole = pl.BlockSpec((count, width), lambda i, place: (0, 0))
    out = pl.BlockSpec((count, block), lambda i, place: (0, i))
    row = pl.BlockSpec((1, block), lambda i, place: (0, i))
    specs = []
    arrays = []
    for piece in [*expand, *reduce]:
        shape = (piece[0].shape[0], block)
        arrays += piece
        if len(piece) == 1:
            specs.append(pl.BlockSpec(shape, lambda i, place: (0, i)))
        else:
            specs.append(pl.BlockSpec(shape, lambda i, place: (0, jnp.minimum(i, edge - 1))))
            specs.append(pl.BlockSpec(shape, lambda i, place: (0, jnp.maximum(i - edge, 0))))
    return pl.pallas_call(
        lambda *refs: feed_forward_kernel(expand, reduce, edge, *refs),
        grid_spec=pltpu.PrefetchScalarGridSpec(
            num_scalar_prefetch=1,
            grid=(hidden // block,),
            in_specs=[whole, whole, row] + specs,
            out_specs=[out, out, whole, row],
            scratch_shapes=[
                pltpu.VMEM((count, width), FULL),
                pltpu.VMEM((width, block), LOW),
                pltpu.VMEM((width, block), LOW),
            ],
        ),
        out_shape=[
            jax.ShapeDtypeStruct((count, hidden), LOW),
            jax.ShapeDtypeStruct((count, hidden), LOW),
            jax.ShapeDtypeStruct((count, width), LOW),
            jax.ShapeDtypeStruct((1, hidden), FULL),
        ],
        compiler_params=pltpu.CompilerParams(vmem_limit_bytes=44 << 20),
        name="feed_forward",
    )(place, normed, slope, bias, *arrays)


def reduce_kernel(place_ref, active_ref, *refs):
    out_ref, total, reduce_ref = refs[-3:]
    put_together(place_ref, reduce_ref, [(ref,) for ref in refs[:-3]])
    part = product(active_ref[...], reduce_ref[...], ROW_BY_ROW)

    @pl.when(pl.program_id(0) == 0)
    def _():
        total[...] = part

    @pl.when(pl.program_id(0) > 0)
    def _():
        total[...] += part

    @pl.when(pl.program_id(0) == pl.num_programs(0) - 1)
    def _():
        out_ref[...] = total[...].astype(LOW)


def reduce_output(active, reduce, place):
    count, hidden = active.shape
    width = sum(piece.shape[0] for piece in reduce)
    block = 512 if hidden % 512 == 0 else hidden
    return pl.pallas_call(
        reduce_kernel,
        grid_spec=pltpu.PrefetchScalarGridSpec(
            num_scalar_prefetch=1,
            grid=(hidden // block,),
            in_specs=[pl.BlockSpec((count, block), lambda i, place: (0, i))]
            + [
                pl.BlockSpec((piece.shape[0], block), lambda i, place: (0, i)) for piece in reduce
            ],
            out_specs=pl.BlockSpec((count, width), lambda i, place: (0, 0)),
            scratch_shapes=[pltpu.VMEM((count, width), FULL), pltpu.VMEM((width, block), LOW)],
        ),
        out_shape=jax.ShapeDtypeStruct((count, width), LOW),
        compiler_params=pltpu.CompilerParams(vmem_limit_bytes=32 << 20),
        name="reduce_output",
    )(place, active, *reduce)


def swap(value, axis, distance):
    size = lax.axis_size(axis)
    return lax.ppermute(value, axis, [(i, i ^ distance) for i in range(size)])


def fence(*values):
    return lax.optimization_barrier(values)


def gather_near(rows_here):
    if lax.axis_size("fsdp") != 4:
        return (lax.all_gather(rows_here, "fsdp", axis=0, tiled=True),)
    return (rows_here, swap(rows_here, "fsdp", 1), swap(rows_here, "fsdp", 2))


def far_of(held):
    if len(held) == 1:
        return ()
    half = held[0].shape[0] // 2
    return (held[2][:half], held[1][half:])


def send_far(leaves):
    return (swap(leaves[0], "fsdp", 1), swap(leaves[1], "fsdp", 2)) if leaves else ()


def far_of(held):
    if len(held) == 1:
        return ()
    half = held[0].shape[0] // 2
    return (held[2][:half], held[1][half:])


def send_far(leaves):
    return (swap(leaves[0], "fsdp", 1), swap(leaves[1], "fsdp", 2)) if leaves else ()


def gather_far(held):
    return held + send_far(far_of(held))


def place_near(held):
    if len(held) == 1:
        return held[0]
    rows_here, near, side = held[:3]
    me = lax.axis_index("fsdp")
    count, width = rows_here.shape
    out = jnp.zeros((4 * count, width), rows_here.dtype)
    out = lax.dynamic_update_slice(out, rows_here, (me * count, 0))
    out = lax.dynamic_update_slice(out, near, ((me ^ 1) * count, 0))
    return lax.dynamic_update_slice(out, side, ((me ^ 2) * count, 0))


def place_far(out, held):
    if len(held) == 1:
        return out
    far_top, far_low = held[3:]
    half = far_top.shape[0]
    start = (lax.axis_index("fsdp") ^ 3) * 2 * half
    out = lax.dynamic_update_slice(out, far_top, (start, 0))
    return lax.dynamic_update_slice(out, far_low, (start + half, 0))


def grad_rows(left, right, distance):
    count = left.shape[1] // 4
    start = (lax.axis_index("fsdp") ^ distance) * count
    piece = lax.dynamic_slice_in_dim(left, start, count, 1)
    return product(piece, right, COLUMN_BY_COLUMN).astype(LOW)


def rows_at(matrices, distance):
    parts = []
    for matrix in matrices:
        count = matrix.shape[0] // 4
        start = (lax.axis_index("fsdp") ^ distance) * count
        parts.append(lax.dynamic_slice_in_dim(matrix, start, count, 0))
    return parts[0] if len(parts) == 1 else jnp.concatenate(parts, axis=1)


def far_halves(far):
    half = far.shape[0] // 2
    return (swap(far[:half], "fsdp", 1), swap(far[half:], "fsdp", 2))


def add_far(near, side, far):
    half = near.shape[0] // 2
    near = jnp.concatenate([near[:half], both((near[half:], far[1])).astype(LOW)], axis=0)
    side = jnp.concatenate([both((side[:half], far[0])).astype(LOW), side[half:]], axis=0)
    return (near, side)


def near_rows_out(pair):
    return (swap(pair[0], "fsdp", 1), swap(pair[1], "fsdp", 2))


def halves(value, bit):
    half = value.shape[0] // 2
    keep = lax.dynamic_slice_in_dim(value, bit * half, half, 0)
    send = lax.dynamic_slice_in_dim(value, (1 - bit) * half, half, 0)
    return keep, send.astype(LOW)


def split_rows(value, bit, distance):
    keep, send = halves(value, bit)
    return keep, swap(send, "ctx", distance)


def both(pair):
    return pair[0].astype(FULL) + pair[1].astype(FULL)


def join_rows(value, bit, distance):
    other = swap(value, "ctx", distance)
    return jnp.where(
        bit == 0,
        jnp.concatenate([value, other], axis=0),
        jnp.concatenate([other, value], axis=0),
    )


def pairwise(pieces):
    return (pieces[0] + pieces[1]) + (pieces[2] + pieces[3])


def swapped_if(bit, pair):
    return [jnp.where(bit == 0, pair[0], pair[1]), jnp.where(bit == 0, pair[1], pair[0])]


def per_device(
    tokens,
    clip_mask,
    cotangent,
    first_gain,
    first_shift,
    joint_weight,
    joint_bias,
    mixer_weight,
    mixer_bias,
    second_gain,
    second_shift,
    expand_weight,
    expand_bias,
    reduce_weight,
    reduce_bias,
):
    clips_here, rows_here, width = tokens.shape
    if lax.axis_size("ctx") != 4 or lax.axis_size("tp") != 2 or clips_here != 2:
        raise ValueError("mesh")
    shard = lax.axis_index("fsdp")
    block = lax.axis_index("ctx")
    core = lax.axis_index("tp")
    clip_at = block >> 1
    part_at = block & 1
    width_half = width // 2
    quarter = width_half // 2
    features = joint_weight.shape[2]
    part_width = features // 2
    pair_width = 2 * HEAD_DIM
    tokens_here = clips_here * rows_here

    flat_tokens = tokens.reshape(tokens_here, width)
    (first_normed,) = by_rows(
        first_norm_kernel, "first_norm", [LOW], False,
        flat_tokens, first_gain[None], first_shift[None],
    )
    first_normed = first_normed.reshape(clips_here, rows_here, width)
    mine = lax.dynamic_slice_in_dim(first_normed, core * width_half, width_half, 2)
    other_side = lax.dynamic_slice_in_dim(first_normed, (1 - core) * width_half, width_half, 2)
    own_clip = lax.dynamic_index_in_dim(mine, clip_at, 0, False)
    own_other = lax.dynamic_index_in_dim(other_side, clip_at, 0, False)
    other_clip = lax.dynamic_index_in_dim(mine, 1 - clip_at, 0, False)
    joint_part = lax.dynamic_slice_in_dim(joint_weight, part_at * part_width, part_width, 2)
    early = expand_weight.shape[1] // 2
    wide_part = jnp.concatenate(
        [expand_weight[:, :early]] + [joint_part[:, kind] for kind in range(3)] + [mixer_weight],
        axis=1,
    )

    own_clip, left, right, wide_part = fence(
        own_clip, other_clip[:, :quarter], other_clip[:, quarter:], wide_part
    )
    near_rows = swap(own_clip, "ctx", 1)
    across_left = swap(left, "ctx", 2)
    far_right = swap(right, "ctx", 3)
    wide_held = gather_near(wide_part)

    near_rows, across_left, far_right = fence(near_rows, across_left, far_right)
    passed = swap(jnp.concatenate([across_left, far_right], axis=1), "ctx", 1)
    wide_held, expand_rest = fence(wide_held, expand_weight[:, early:])
    held = gather_far(tuple(piece[:, early:] for piece in wide_held))
    rest_held = gather_near(expand_rest)

    (passed,) = fence(passed)
    cross_rows = jnp.concatenate(
        [
            near_rows,
            jnp.concatenate([across_left, passed[:, quarter:]], axis=1),
            jnp.concatenate([passed[:, :quarter], far_right], axis=1),
        ],
        axis=0,
    )
    cross_other = swap(cross_rows, "tp", 1)
    both_full = place_far(place_near(held), held)
    joint_columns = 3 * part_width
    joint_full = jnp.concatenate(
        [
            lax.dynamic_slice(both_full, (start * width_half, 0), (width_half, joint_columns))
            for start in (core, 1 - core)
        ],
        axis=0,
    )

    cross_other, joint_full, both_full, reduce_weight = fence(
        cross_other, joint_full, both_full, reduce_weight
    )
    mixer_full = both_full[:, joint_columns:]
    reduce_held = gather_near(reduce_weight)
    normed_mine = jnp.concatenate([own_clip, cross_rows], axis=0)
    normed_other = jnp.concatenate([own_other, cross_other], axis=0)
    bias_part = lax.dynamic_slice_in_dim(joint_bias, part_at * part_width, part_width, 1)
    bias_row = jnp.concatenate([bias_part[0], jnp.zeros_like(bias_part[0]), bias_part[1]])
    joint_out = joint_projection(normed_mine, normed_other, joint_full, bias_row[None])
    out_first, log_first = attention_forward(joint_out, 0)

    out_first, joint_out, mixer_full, rest_held = fence(
        out_first, joint_out, mixer_full, rest_held
    )
    first_blocks = out_first.reshape(4, rows_here, pair_width)
    arrived_first = [swap(first_blocks[d], "ctx", d) for d in (1, 2, 3)]
    out_second, log_second = attention_forward(joint_out, 1)

    far_leaves = far_of(
        tuple(
            jnp.concatenate([one[:, :early], two], axis=1)
            for one, two in zip(wide_held, rest_held)
        )
    )
    out_second, arrived_first, reduce_held, far_leaves = fence(
        out_second, arrived_first, reduce_held, far_leaves
    )
    second_blocks = out_second.reshape(4, rows_here, pair_width)
    arrived_second = [swap(second_blocks[d], "ctx", d) for d in (1, 2, 3)]
    expand_far_rows = send_far(far_leaves)

    arrived_second, expand_far_rows, reduce_held, reduce_leaves = fence(
        arrived_second, expand_far_rows, reduce_held, far_of(reduce_held)
    )
    reduce_held = reduce_held + send_far(reduce_leaves)
    expand_held = list(zip(wide_held, rest_held)) + [(rows,) for rows in expand_far_rows]
    arrived = [jnp.concatenate([first_blocks[0], second_blocks[0]], axis=1)] + [
        jnp.concatenate([one, two], axis=1) for one, two in zip(arrived_first, arrived_second)
    ]
    own_joined = jnp.concatenate(swapped_if(part_at, arrived[:2]), axis=1)
    other_joined = jnp.concatenate(swapped_if(part_at, arrived[2:]), axis=1)
    mixed_in = jnp.concatenate(swapped_if(clip_at, [own_joined, other_joined]), axis=0)
    mixer_part = product(mixed_in, mixer_full, ROW_BY_ROW).astype(LOW)
    mixer_swapped = swap(mixer_part, "tp", 1)
    mixer_row = mixer_bias[None]
    (second_normed,) = by_rows(
        second_norm_kernel, "second_norm", [LOW], False,
        flat_tokens, mixer_part, mixer_swapped, mixer_row, second_gain[None], second_shift[None],
    )
    valid = clip_mask.astype(FULL)[:, None, None]
    reduce_slope = (cotangent.astype(FULL) * valid).astype(LOW).reshape(tokens_here, width)
    reduce_bias_grad = jnp.sum(reduce_slope.astype(FULL), axis=0)

    second_normed, reduce_slope, reduce_held = fence(second_normed, reduce_slope, reduce_held)
    four = lax.axis_size("fsdp") == 4
    start = jnp.zeros((), jnp.int32)
    if four:
        rows = width // 4
        pieces_at = jnp.stack([shard, shard ^ 1, shard ^ 2, shard ^ 3, shard ^ 3]) * rows
        pieces_at = pieces_at.astype(jnp.int32) + jnp.array([0, 0, 0, 0, rows // 2], jnp.int32)
    else:
        pieces_at = start.reshape(1)
    activated, expand_slope, second_part, expand_bias_grad = feed_forward(
        second_normed, reduce_slope, expand_bias[None], expand_held, early,
        [(piece,) for piece in reduce_held], pieces_at,
    )
    expand_bias_grad = expand_bias_grad[0]

    second_swapped = swap(second_part, "tp", 1)
    place, order = (shard, (3, 2, 1, 0)) if four else (start, (0, 1, 2, 3))
    if four:
        half = width // 8
        far = grad_rows(second_normed, expand_slope, 3)
        far_top, far_low, normed_again, expand_slope = fence(
            far[:half], far[half:], second_normed, expand_slope
        )
        expand_far = (swap(far_top, "fsdp", 1), swap(far_low, "fsdp", 2))
        expand_parts = [grad_rows(normed_again, expand_slope, d) for d in (0, 1, 2)]
        expand_parts, second_swapped = fence(expand_parts, second_swapped)
    else:
        expand_far = ()
        expand_whole = product(second_normed, expand_slope, COLUMN_BY_COLUMN).astype(LOW)
    mixer_slope, first_sum_back, second_sums = by_rows(
        second_norm_back_kernel, "second_norm_back", [LOW, FULL], True,
        flat_tokens, mixer_part, mixer_swapped, mixer_row, second_gain[None],
        second_part, second_swapped, reduce_slope,
    )
    attended_slope = product(mixer_slope, mixer_full, PLAIN).astype(LOW)

    leaving = []
    for distance in range(4):
        to = block ^ distance
        corner = ((to >> 1) * rows_here, (to & 1) * part_width)
        leaving.append(lax.dynamic_slice(attended_slope, corner, (rows_here, part_width)))
    expand_near = add_far(expand_parts[1], expand_parts[2], expand_far) if four else ()
    leaving, mixer_slope, mixed_in, activated, expand_near = fence(
        leaving, mixer_slope, mixed_in, activated, expand_near
    )
    slope_blocks = [leaving[0]] + [swap(leaving[d], "ctx", d) for d in (1, 2, 3)]
    if four:
        expand_near = near_rows_out(expand_near)
    wide = (
        product(reduce_slope, activated, COLUMN_BY_COLUMN).astype(LOW),
        product(mixer_slope, mixed_in, COLUMN_BY_COLUMN).astype(LOW),
    )
    if four:
        wide_far, wide_side, wide_next = (rows_at(wide, distance) for distance in (3, 2, 1))
        far_top, far_low = wide_far[:half], wide_far[half:]
        wide_early = (wide_next[:half], wide_side[half:])
    else:
        far_top, far_low, wide_early = (), (), ()

    slope_blocks, expand_near, far_top, far_low = fence(
        slope_blocks, expand_near, far_top, far_low
    )
    if four:
        expand_sum = expand_parts[0].astype(FULL) + both(expand_near)
    else:
        expand_sum = lax.psum_scatter(
            expand_whole, "fsdp", scatter_dimension=0, tiled=True
        ).astype(FULL)
    expand_keep, expand_send = halves(expand_sum, part_at)
    slope_clip = jnp.concatenate(slope_blocks, axis=0)
    expand_send, slope_clip, far_top, far_low = fence(expand_send, slope_clip, far_top, far_low)
    wide_far = (swap(far_top, "fsdp", 1), swap(far_low, "fsdp", 2)) if four else ()
    expand_rows = (expand_keep, swap(expand_send, "ctx", 1))
    grad_first = attention_backward(joint_out, slope_clip, out_first, log_first, 0)

    grad_first, slope_clip, wide_far, expand_rows = fence(
        grad_first, slope_clip, wide_far, expand_rows
    )
    if four:
        wide_late = (
            both((wide_next[half:], wide_far[1])).astype(LOW),
            both((wide_side[:half], wide_far[0])).astype(LOW),
        )
    else:
        wide_late = ()
    expand_keep, expand_send = halves(both(expand_rows), clip_at)
    expand_send, slope_clip, wide_early, wide_late = fence(
        expand_send, slope_clip, wide_early, wide_late
    )
    if four:
        wide_early = near_rows_out(wide_early)
    expand_rows = (expand_keep, swap(expand_send, "ctx", 2))
    grad_second = attention_backward(joint_out, slope_clip, out_second, log_second, 1)

    grad_second, expand_rows, wide_early, wide_late = fence(
        grad_second, expand_rows, wide_early, wide_late
    )
    if four:
        wide_late = near_rows_out(wide_late)
    expand_rows = both(expand_rows).astype(LOW)
    joint_slope = jnp.concatenate(
        [grad[kind] for kind in range(3) for grad in (grad_first, grad_second)], axis=1
    )
    first_there = product(joint_slope, joint_full[width_half:], ROW_BY_ROW).astype(LOW)
    first_here = rows_product(joint_slope, joint_full[:width_half], "first_slope")
    first_half = both((first_here, swap(first_there, "tp", 1))).astype(LOW)

    if not four:
        wide_near = lax.psum_scatter(
            jnp.concatenate(wide, axis=1), "fsdp", scatter_dimension=0, tiled=True
        )
    first_half, joint_slope, expand_rows, wide_late = fence(
        first_half, joint_slope, expand_rows, wide_late
    )
    expand_rows = join_rows(expand_rows, clip_at, 2)
    pieces = first_half.reshape(4, rows_here, width_half)
    passing = jnp.concatenate([pieces[1], pieces[3][:, :quarter], pieces[2][:, quarter:]], axis=1)
    passing = swap(passing, "ctx", 1)
    place = (shard if four else start) ^ (2 * core)
    joint_parts = grad_products([normed_mine, normed_other], joint_slope, place, order, "joint_grad")
    slope_sums = jnp.sum(joint_slope.astype(FULL), axis=0)
    bias_sums = jnp.stack([slope_sums[:part_width], slope_sums[2 * part_width :]])
    joint_bias_grad = lax.dynamic_update_slice(
        jnp.zeros((2, features), FULL), bias_sums, (0, part_at * part_width)
    )

    joint_far = far_halves(joint_parts[0]) if four else ()
    passing, joint_far, expand_rows = fence(passing, joint_far, expand_rows)
    if four:
        near_sum = [both((wide_early[0], wide_late[1])), both((wide_late[0], wide_early[1]))]
        wide_sum = rows_at(wide, 0).astype(FULL) + jnp.concatenate(near_sum, axis=0)
    else:
        wide_sum = wide_near.astype(FULL)
    wide_keep, wide_send = halves(wide_sum, part_at)
    own_half = both((pieces[0], passing[:, :width_half])).astype(LOW)
    to_left = both((pieces[2][:, :quarter], passing[:, width_half : width_half + quarter]))
    to_right = both((pieces[3][:, quarter:], passing[:, width_half + quarter :]))
    joint_near = add_far(joint_parts[2], joint_parts[1], joint_far) if four else ()
    to_left, to_right, own_half, wide_send, joint_near, activated = fence(
        to_left.astype(LOW), to_right.astype(LOW), own_half, wide_send, joint_near, activated
    )
    other_half = jnp.concatenate([swap(to_left, "ctx", 2), swap(to_right, "ctx", 3)], axis=1)
    wide_rows = (wide_keep, swap(wide_send, "ctx", 1))
    if four:
        joint_near = near_rows_out(joint_near)
    else:
        joint_near = lax.psum_scatter(
            joint_parts.reshape(width, -1), "fsdp", scatter_dimension=0, tiled=True
        )
    reduce_part = reduce_output(activated, reduce_held, pieces_at)

    other_half, joint_near, wide_rows, reduce_part = fence(
        other_half, joint_near, wide_rows, reduce_part
    )
    slope_half = jnp.concatenate(swapped_if(clip_at, [own_half, other_half]), axis=0)
    slope_other = swap(slope_half, "tp", 1)
    slope_other, expand_rows = fence(slope_other, expand_rows)
    expand_grad = join_rows(expand_rows, part_at, 1).astype(FULL)
    first_slope = jnp.concatenate(swapped_if(core, [slope_half, slope_other]), axis=1)
    wide_rows = split_rows(both(wide_rows), clip_at, 2)
    reduce_swapped = swap(reduce_part, "tp", 1)
    joint_sum = joint_parts[3].astype(FULL) + both(joint_near) if four else joint_near
    joint_sum = joint_sum.astype(LOW)
    joint_sum = (joint_sum, swap(joint_sum, "ctx", 2))
    tokens_grad, first_sums = by_rows(
        first_norm_back_kernel, "first_norm_back", [FULL], True,
        flat_tokens, first_slope, first_gain[None],
        cotangent.reshape(tokens_here, width), first_sum_back,
    )
    first_sums, tokens_grad, reduce_swapped = fence(first_sums, tokens_grad, reduce_swapped)
    vectors = [
        first_sums[0],
        first_sums[1],
        joint_bias_grad[0],
        joint_bias_grad[1],
        second_sums[2],
        second_sums[0],
        second_sums[1],
        expand_bias_grad,
        reduce_bias_grad,
    ]
    packed = jnp.concatenate(vectors).reshape(-1, 128)
    packed_pieces = [packed] + [swap(packed, "ctx", d) for d in (1, 2, 3)]
    reduce_out = both((reduce_part, reduce_swapped)) + reduce_bias
    mixer_out = both((mixer_part, mixer_swapped)) + mixer_bias
    branches = (mixer_out + reduce_out).reshape(clips_here, rows_here, width)
    result = (tokens.astype(FULL) + valid * branches).astype(LOW)

    packed_pieces, joint_sum, wide_rows, result = fence(
        packed_pieces, joint_sum, wide_rows, result
    )
    packed = pairwise(packed_pieces)
    if four:
        packed = pairwise([packed] + [swap(packed, "fsdp", d) for d in (1, 2, 3)])
    else:
        packed = lax.psum(packed, "fsdp")
    joint_sum = both(joint_sum).astype(LOW)
    joint_parts = swapped_if(part_at, [joint_sum, swap(joint_sum, "ctx", 1)])
    joint_grad = jnp.concatenate(
        [piece.reshape(-1, 3, part_width) for piece in joint_parts], axis=2
    ).astype(FULL)
    wide_rows = join_rows(both(wide_rows).astype(LOW), clip_at, 2)
    wide_rows = join_rows(wide_rows, part_at, 1).astype(FULL)
    reduce_grad = wide_rows[:, : activated.shape[1]]
    mixer_grad = wide_rows[:, activated.shape[1] :]
    packed = packed.reshape(-1)
    shares = []
    start = 0
    for vector in vectors:
        share = vector.shape[0] // lax.axis_size("fsdp")
        shares.append(lax.dynamic_slice_in_dim(packed, start + shard * share, share, 0))
        start += vector.shape[0]

    shape = (clips_here, rows_here, width)
    return (
        result,
        tokens_grad.reshape(shape),
        shares[0],
        shares[1],
        joint_grad,
        jnp.stack([shares[2], shares[3]]),
        mixer_grad,
        shares[4],
        shares[5],
        shares[6],
        expand_grad,
        shares[7],
        reduce_grad,
        shares[8],
    )


def solution(mesh):
    return jax.shard_map(
        per_device,
        mesh=mesh,
        in_specs=(
            P("fsdp", "ctx", None),
            P("fsdp"),
            P("fsdp", "ctx", None),
            P(),
            P(),
            P("fsdp", None, "tp"),
            P(None, "tp"),
            P("fsdp", "tp"),
            P(),
            P(),
            P(),
            P("fsdp", "tp"),
            P("tp"),
            P("fsdp", "tp"),
            P(),
        ),
        out_specs=(
            P("fsdp", "ctx", None),
            P("fsdp", "ctx", None),
            P("fsdp"),
            P("fsdp"),
            P("fsdp", None, "tp"),
            P(None, ("tp", "fsdp")),
            P("fsdp", "tp"),
            P("fsdp"),
            P("fsdp"),
            P("fsdp"),
            P("fsdp", "tp"),
            P(("tp", "fsdp")),
            P("fsdp", "tp"),
            P("fsdp"),
        ),
        check_vma=False,
    )
```

```python
import jax
import jax.numpy as jnp
from jax import lax
from jax.experimental import pallas as pl
from jax.experimental.pallas import tpu as pltpu
from jax.sharding import PartitionSpec as P

HEAD_DIM = 64
EPSILON = 1e-06
LOW = jnp.bfloat16
FULL = jnp.float32

ROW_BY_ROW = (((1,), (1,)), ((), ()))
PLAIN = (((1,), (0,)), ((), ()))
COLUMN_BY_COLUMN = (((0,), (0,)), ((), ()))


def product(left, right, dims):
    return lax.dot_general(left, right, dims, preferred_element_type=FULL)


def normalize(value_rows):
    center = value_rows - jnp.mean(value_rows, axis=-1, keepdims=True)
    inverse = lax.rsqrt(jnp.mean(center * center, axis=-1, keepdims=True) + EPSILON)
    return (center * inverse, inverse)


def norm_back(upstream, gain, scaled, inverse):
    weighted = upstream * gain
    return inverse * (
        weighted
        - jnp.mean(weighted, axis=-1, keepdims=True)
        - scaled * jnp.mean(weighted * scaled, axis=-1, keepdims=True)
    )


def row_chunk(count, most):
    for chunk in range(most, 0, -16):
        if count % chunk == 0:
            return chunk
    raise ValueError("rows")


def first_norm_kernel(tokens_ref, gain_ref, shift_ref, out_ref):
    scaled, _ = normalize(tokens_ref[...].astype(FULL))
    out_ref[...] = (scaled * gain_ref[...] + shift_ref[...]).astype(LOW)


def second_norm_kernel(tokens_ref, one_ref, two_ref, bias_ref, gain_ref, shift_ref, out_ref):
    mixed = one_ref[...].astype(FULL) + two_ref[...].astype(FULL) + bias_ref[...]
    scaled, _ = normalize(tokens_ref[...].astype(FULL) + mixed)
    out_ref[...] = (scaled * gain_ref[...] + shift_ref[...]).astype(LOW)


def add_sums(ref, rows):
    sums = jnp.concatenate([jnp.sum(row, axis=0, keepdims=True) for row in rows], axis=0)

    @pl.when(pl.program_id(0) == 0)
    def _():
        ref[: len(rows)] = sums

    @pl.when(pl.program_id(0) > 0)
    def _():
        ref[: len(rows)] += sums


def second_norm_back_kernel(
    tokens_ref, one_ref, two_ref, bias_ref, gain_ref, left_ref, right_ref, outer_ref,
    slope_ref, back_ref, sums_ref,
):
    mixed = one_ref[...].astype(FULL) + two_ref[...].astype(FULL) + bias_ref[...]
    scaled, inverse = normalize(tokens_ref[...].astype(FULL) + mixed)
    upstream = left_ref[...].astype(FULL) + right_ref[...].astype(FULL)
    back = norm_back(upstream, gain_ref[...], scaled, inverse)
    slope = (outer_ref[...].astype(FULL) + back).astype(LOW)
    slope_ref[...] = slope
    back_ref[...] = back
    add_sums(sums_ref, [upstream * scaled, upstream, slope.astype(FULL)])


def first_norm_back_kernel(
    tokens_ref, upstream_ref, gain_ref, outer_ref, back_ref, out_ref, sums_ref
):
    scaled, inverse = normalize(tokens_ref[...].astype(FULL))
    upstream = upstream_ref[...].astype(FULL)
    back = norm_back(upstream, gain_ref[...], scaled, inverse)
    out_ref[...] = outer_ref[...].astype(FULL) + back_ref[...] + back
    add_sums(sums_ref, [upstream * scaled, upstream])


def by_rows(kernel, name, out_types, sums, *values):
    count, width = values[0].shape
    chunk = row_chunk(count, 112)
    part = pl.BlockSpec((chunk, width), lambda i: (i, 0))
    in_specs = [
        part if value.shape[0] == count else pl.BlockSpec((1, width), lambda i: (0, 0))
        for value in values
    ]
    out_specs = [part for _ in out_types]
    out_shape = [jax.ShapeDtypeStruct((count, width), kind) for kind in out_types]
    if sums:
        out_specs.append(pl.BlockSpec((8, width), lambda i: (0, 0)))
        out_shape.append(jax.ShapeDtypeStruct((8, width), FULL))
    return pl.pallas_call(
        kernel,
        grid=(count // chunk,),
        in_specs=in_specs,
        out_specs=out_specs,
        out_shape=out_shape,
        compiler_params=pltpu.CompilerParams(vmem_limit_bytes=16 << 20),
        name=name,
    )(*values)


def joint_kernel(mine_ref, other_ref, weight_ref, bias_ref, out_ref):
    half = mine_ref.shape[1]
    out = product(mine_ref[...], weight_ref[:half], PLAIN)
    out += product(other_ref[...], weight_ref[half:], PLAIN)
    out_ref[...] = (out + bias_ref[...]).astype(LOW)


def joint_projection(mine, other, weight, bias):
    count, half = mine.shape
    columns = weight.shape[1]
    chunk = row_chunk(count, 784)
    part = pl.BlockSpec((chunk, half), lambda i: (i, 0))
    return pl.pallas_call(
        joint_kernel,
        grid=(count // chunk,),
        in_specs=[
            part,
            part,
            pl.BlockSpec(weight.shape, lambda i: (0, 0)),
            pl.BlockSpec((1, columns), lambda i: (0, 0)),
        ],
        out_specs=pl.BlockSpec((chunk, columns), lambda i: (i, 0)),
        out_shape=jax.ShapeDtypeStruct((count, columns), LOW),
        compiler_params=pltpu.CompilerParams(vmem_limit_bytes=40 << 20),
        name="joint_projection",
    )(mine, other, weight, bias)


def rows_kernel(left_ref, right_ref, out_ref):
    out_ref[...] = product(left_ref[...], right_ref[...], ROW_BY_ROW).astype(LOW)


def rows_product(left, right, name):
    count, depth = left.shape
    columns = right.shape[0]
    chunk = row_chunk(count, 400)
    return pl.pallas_call(
        rows_kernel,
        grid=(count // chunk,),
        in_specs=[
            pl.BlockSpec((chunk, depth), lambda i: (i, 0)),
            pl.BlockSpec((columns, depth), lambda i: (0, 0)),
        ],
        out_specs=pl.BlockSpec((chunk, columns), lambda i: (i, 0)),
        out_shape=jax.ShapeDtypeStruct((count, columns), LOW),
        compiler_params=pltpu.CompilerParams(vmem_limit_bytes=48 << 20),
        name=name,
    )(left, right)


def grad_kernel(distances, place_ref, *refs):
    lefts, (right_ref, out_ref) = refs[:-2], refs[-2:]
    left = lefts[0][...]
    if len(lefts) == 2:
        slot = place_ref[0] ^ distance_at(distances, pl.program_id(0))
        left = jnp.where((slot >> 1) == 0, left, lefts[1][...])
    out_ref[0] = product(left, right_ref[...], COLUMN_BY_COLUMN).astype(LOW)


def distance_at(distances, step):
    if len(distances) == 1:
        return distances[0]
    return distances[0] + step * (distances[1] - distances[0])


def grad_products(lefts, right, place, distances, name):
    tokens_here, columns = right.shape
    quarter = sum(left.shape[1] for left in lefts) // 4
    blocks = lefts[0].shape[1] // quarter

    def left_at(i, place):
        return (0, (place[0] ^ distance_at(distances, i)) & (blocks - 1))

    return pl.pallas_call(
        lambda *refs: grad_kernel(distances, *refs),
        grid_spec=pltpu.PrefetchScalarGridSpec(
            num_scalar_prefetch=1,
            grid=(len(distances),),
            in_specs=[pl.BlockSpec((tokens_here, quarter), left_at) for _ in lefts]
            + [pl.BlockSpec((tokens_here, columns), lambda i, place: (0, 0))],
            out_specs=pl.BlockSpec((1, quarter, columns), lambda i, place: (i, 0, 0)),
        ),
        out_shape=jax.ShapeDtypeStruct((len(distances), quarter, columns), LOW),
        compiler_params=pltpu.CompilerParams(vmem_limit_bytes=48 << 20),
        name=name,
    )(place.astype(jnp.int32).reshape(1), *lefts, right)


def attention_forward_kernel(q_ref, k_ref, v_ref, o_ref, lse_ref):
    count, width = q_ref.shape
    rows = row_chunk(count, 256)
    lane = lax.broadcasted_iota(jnp.int32, (rows, width), 1)
    k = k_ref[...]
    v = v_ref[...]
    units = [(start, head) for start in range(0, count, rows) for head in range(width // HEAD_DIM)]

    def scores_of(unit):
        start, head = unit
        q = q_ref[start : start + rows] * jnp.asarray(HEAD_DIM ** (-0.5), LOW)
        return product(jnp.where((lane // HEAD_DIM) == head, q, jnp.zeros_like(q)), k, ROW_BY_ROW)

    logs = []
    ahead = scores_of(units[0])
    for step, (start, head) in enumerate(units):
        scores = ahead
        if step + 1 < len(units):
            ahead = scores_of(units[step + 1])
        top = jnp.max(scores, axis=-1, keepdims=True)
        weights = jnp.exp(scores - top)
        total = jnp.sum(weights, axis=-1, keepdims=True)
        part = product(weights.astype(LOW), v, PLAIN) / total
        if head == 0:
            out = part
            logs.append(jnp.zeros((rows, width), FULL))
        else:
            out = jnp.where((lane // HEAD_DIM) == head, part, out)
            o_ref[start : start + rows] = out.astype(LOW)
        logs[-1] = jnp.where(lane == head, top + jnp.log(total), logs[-1])
    lse_ref[...] = jnp.concatenate(logs, axis=0).T[: lse_ref.shape[0]]


def attention_forward(joint, pair):
    count, columns = joint.shape
    width = 2 * HEAD_DIM
    kind = columns // (3 * width)
    return pl.pallas_call(
        attention_forward_kernel,
        grid=(1,),
        in_specs=[
            pl.BlockSpec((count, width), lambda i: (0, pair)),
            pl.BlockSpec((count, width), lambda i: (0, kind + pair)),
            pl.BlockSpec((count, width), lambda i: (0, 2 * kind + pair)),
        ],
        out_specs=[
            pl.BlockSpec((count, width), lambda i: (0, 0)),
            pl.BlockSpec((8, count), lambda i: (0, 0)),
        ],
        out_shape=[
            jax.ShapeDtypeStruct((count, width), LOW),
            jax.ShapeDtypeStruct((8, count), FULL),
        ],
        compiler_params=pltpu.CompilerParams(vmem_limit_bytes=48 << 20),
        name="attention_forward",
    )(joint, joint, joint)


def attention_backward_kernel(
    q_ref, k_ref, v_ref, da_ref, o_ref, lse_ref, dq_ref, dk_ref, dv_ref,
    q_heads, da_heads, delta_ref, dq_total,
):
    count, width = q_ref.shape
    rows = row_chunk(count, 256)
    heads = width // HEAD_DIM
    scale = jnp.asarray(HEAD_DIM ** (-0.5), LOW)

    lane = lax.broadcasted_iota(jnp.int32, (count, width), 1)
    delta = jnp.zeros((count, width), FULL)
    q = q_ref[...] * scale
    da = da_ref[...]
    both_rows = da.astype(FULL) * o_ref[...].astype(FULL)
    for head in range(heads):
        mask = (lane // HEAD_DIM) == head
        q_heads[head] = jnp.where(mask, q, jnp.zeros_like(q))
        da_heads[head] = jnp.where(mask, da, jnp.zeros_like(da))
        row = jnp.sum(jnp.where(mask, both_rows, 0.0), axis=-1, keepdims=True)
        delta = jnp.where(lane == head, row, delta)
    delta_ref[...] = delta.T[:8]
    dq_total[...] = jnp.zeros_like(dq_total)

    lane = lax.broadcasted_iota(jnp.int32, (rows, width), 1)
    for start in range(0, count, rows):
        k = k_ref[start : start + rows]
        v = v_ref[start : start + rows]
        scaled_k = k * scale
        dk = dv = None
        for head in range(heads):
            q = q_heads[head]
            da = da_heads[head]
            probs = jnp.exp(product(k, q, ROW_BY_ROW) - lse_ref[head : head + 1, :])
            slope = probs * (product(v, da, ROW_BY_ROW) - delta_ref[head : head + 1, :])
            slope = slope.astype(LOW)
            dv_part = product(probs.astype(LOW), da, PLAIN)
            dk_part = product(slope, q, PLAIN)
            dv = dv_part if dv is None else dv + dv_part
            dk = dk_part if dk is None else dk + dk_part
            one_k = jnp.where((lane // HEAD_DIM) == head, scaled_k, jnp.zeros_like(k))
            dq_total[...] += product(slope, one_k, COLUMN_BY_COLUMN)
        dk_ref[start : start + rows] = dk.astype(LOW)
        dv_ref[start : start + rows] = dv.astype(LOW)
    dq_ref[...] = dq_total[...].astype(LOW)


def attention_backward(joint, da, out, lse, pair):
    count, columns = joint.shape
    width = 2 * HEAD_DIM
    kind = columns // (3 * width)
    alone = pl.BlockSpec((count, width), lambda i: (0, 0))
    grad = jax.ShapeDtypeStruct((count, width), LOW)
    return pl.pallas_call(
        attention_backward_kernel,
        grid=(1,),
        in_specs=[
            pl.BlockSpec((count, width), lambda i: (0, pair)),
            pl.BlockSpec((count, width), lambda i: (0, kind + pair)),
            pl.BlockSpec((count, width), lambda i: (0, 2 * kind + pair)),
            pl.BlockSpec((count, width), lambda i: (0, pair)),
            alone,
            pl.BlockSpec((8, count), lambda i: (0, 0)),
        ],
        out_specs=[alone, alone, alone],
        out_shape=[grad, grad, grad],
        scratch_shapes=[
            pltpu.VMEM((2, count, width), LOW),
            pltpu.VMEM((2, count, width), LOW),
            pltpu.VMEM((8, count), FULL),
            pltpu.VMEM((count, width), FULL),
        ],
        compiler_params=pltpu.CompilerParams(vmem_limit_bytes=48 << 20),
        name="attention_backward",
    )(joint, joint, joint, da, out, lse)


def put_together(place_ref, whole_ref, pieces, edge=0):
    for piece, refs in enumerate(pieces):
        rows = refs[0].shape[0]
        place = pl.ds(pl.multiple_of(place_ref[piece], rows), rows)
        if len(refs) == 1:
            whole_ref[place, :] = refs[0][...]
            continue

        @pl.when(pl.program_id(0) < edge)
        def _():
            whole_ref[place, :] = refs[0][...]

        @pl.when(pl.program_id(0) >= edge)
        def _():
            whole_ref[place, :] = refs[1][...]


def nested(refs, like):
    refs = iter(refs)
    return [tuple(next(refs) for _ in piece) for piece in like]


def feed_forward_kernel(
    expand, reduce, edge, place_ref, normed_ref, slope_ref, bias_ref, *refs
):
    active_ref, expand_slope_ref, back_ref, bias_grad_ref, total, expand_ref, reduce_ref = refs[-7:]
    arrays = sum(len(piece) for piece in expand)
    put_together(place_ref, expand_ref, nested(refs[:arrays], expand), edge)
    put_together(place_ref, reduce_ref, nested(refs[arrays:-7], reduce))
    step = pl.program_id(0)
    count = normed_ref.shape[0]
    half = count // 2
    bias_grad = None
    for rows in (slice(0, half), slice(half, count)):
        hidden = product(normed_ref[rows], expand_ref[...], PLAIN) + bias_ref[...]
        upstream = product(slope_ref[rows], reduce_ref[...], PLAIN)
        share = 0.5 * (1.0 + lax.erf(hidden * (0.5**0.5)))
        active_ref[rows] = (hidden * share).astype(LOW)
        density = jnp.exp(-0.5 * hidden * hidden) * 0.3989422804014327
        slope = (upstream * (share + hidden * density)).astype(LOW)
        expand_slope_ref[rows] = slope
        part = jnp.sum(slope.astype(FULL), axis=0, keepdims=True)
        bias_grad = part if bias_grad is None else bias_grad + part
        back = product(slope, expand_ref[...], ROW_BY_ROW)

        @pl.when(step == 0)
        def _():
            total[rows] = back

        @pl.when(step > 0)
        def _():
            total[rows] += back

    bias_grad_ref[...] = bias_grad

    @pl.when(step == pl.num_programs(0) - 1)
    def _():
        back_ref[...] = total[...].astype(LOW)


def feed_forward(normed, slope, bias, expand, early, reduce, place):
    count, width = normed.shape
    hidden = bias.shape[1]
    block = 512
    edge = early // block
    whole = pl.BlockSpec((count, width), lambda i, place: (0, 0))
    out = pl.BlockSpec((count, block), lambda i, place: (0, i))
    row = pl.BlockSpec((1, block), lambda i, place: (0, i))
    specs = []
    arrays = []
    for piece in [*expand, *reduce]:
        shape = (piece[0].shape[0], block)
        arrays += piece
        if len(piece) == 1:
            specs.append(pl.BlockSpec(shape, lambda i, place: (0, i)))
        else:
            specs.append(pl.BlockSpec(shape, lambda i, place: (0, jnp.minimum(i, edge - 1))))
            specs.append(pl.BlockSpec(shape, lambda i, place: (0, jnp.maximum(i - edge, 0))))
    return pl.pallas_call(
        lambda *refs: feed_forward_kernel(expand, reduce, edge, *refs),
        grid_spec=pltpu.PrefetchScalarGridSpec(
            num_scalar_prefetch=1,
            grid=(hidden // block,),
            in_specs=[whole, whole, row] + specs,
            out_specs=[out, out, whole, row],
            scratch_shapes=[
                pltpu.VMEM((count, width), FULL),
                pltpu.VMEM((width, block), LOW),
                pltpu.VMEM((width, block), LOW),
            ],
        ),
        out_shape=[
            jax.ShapeDtypeStruct((count, hidden), LOW),
            jax.ShapeDtypeStruct((count, hidden), LOW),
            jax.ShapeDtypeStruct((count, width), LOW),
            jax.ShapeDtypeStruct((1, hidden), FULL),
        ],
        compiler_params=pltpu.CompilerParams(vmem_limit_bytes=44 << 20),
        name="feed_forward",
    )(place, normed, slope, bias, *arrays)


def reduce_kernel(place_ref, active_ref, *refs):
    out_ref, total, reduce_ref = refs[-3:]
    put_together(place_ref, reduce_ref, [(ref,) for ref in refs[:-3]])
    part = product(active_ref[...], reduce_ref[...], ROW_BY_ROW)

    @pl.when(pl.program_id(0) == 0)
    def _():
        total[...] = part

    @pl.when(pl.program_id(0) > 0)
    def _():
        total[...] += part

    @pl.when(pl.program_id(0) == pl.num_programs(0) - 1)
    def _():
        out_ref[...] = total[...].astype(LOW)


def reduce_output(active, reduce, place):
    count, hidden = active.shape
    width = sum(piece.shape[0] for piece in reduce)
    block = 512 if hidden % 512 == 0 else hidden
    return pl.pallas_call(
        reduce_kernel,
        grid_spec=pltpu.PrefetchScalarGridSpec(
            num_scalar_prefetch=1,
            grid=(hidden // block,),
            in_specs=[pl.BlockSpec((count, block), lambda i, place: (0, i))]
            + [
                pl.BlockSpec((piece.shape[0], block), lambda i, place: (0, i)) for piece in reduce
            ],
            out_specs=pl.BlockSpec((count, width), lambda i, place: (0, 0)),
            scratch_shapes=[pltpu.VMEM((count, width), FULL), pltpu.VMEM((width, block), LOW)],
        ),
        out_shape=jax.ShapeDtypeStruct((count, width), LOW),
        compiler_params=pltpu.CompilerParams(vmem_limit_bytes=32 << 20),
        name="reduce_output",
    )(place, active, *reduce)


def swap(value, axis, distance):
    size = lax.axis_size(axis)
    return lax.ppermute(value, axis, [(i, i ^ distance) for i in range(size)])


def fence(*values):
    return lax.optimization_barrier(values)


def gather_near(rows_here):
    if lax.axis_size("fsdp") != 4:
        return (lax.all_gather(rows_here, "fsdp", axis=0, tiled=True),)
    return (rows_here, swap(rows_here, "fsdp", 1), swap(rows_here, "fsdp", 2))


def far_of(held):
    if len(held) == 1:
        return ()
    half = held[0].shape[0] // 2
    return (held[2][:half], held[1][half:])


def send_far(leaves):
    return (swap(leaves[0], "fsdp", 1), swap(leaves[1], "fsdp", 2)) if leaves else ()


def far_of(held):
    if len(held) == 1:
        return ()
    half = held[0].shape[0] // 2
    return (held[2][:half], held[1][half:])


def send_far(leaves):
    return (swap(leaves[0], "fsdp", 1), swap(leaves[1], "fsdp", 2)) if leaves else ()


def gather_far(held):
    return held + send_far(far_of(held))


def place_near(held):
    if len(held) == 1:
        return held[0]
    rows_here, near, side = held[:3]
    me = lax.axis_index("fsdp")
    count, width = rows_here.shape
    out = jnp.zeros((4 * count, width), rows_here.dtype)
    out = lax.dynamic_update_slice(out, rows_here, (me * count, 0))
    out = lax.dynamic_update_slice(out, near, ((me ^ 1) * count, 0))
    return lax.dynamic_update_slice(out, side, ((me ^ 2) * count, 0))


def place_far(out, held):
    if len(held) == 1:
        return out
    far_top, far_low = held[3:]
    half = far_top.shape[0]
    start = (lax.axis_index("fsdp") ^ 3) * 2 * half
    out = lax.dynamic_update_slice(out, far_top, (start, 0))
    return lax.dynamic_update_slice(out, far_low, (start + half, 0))


def grad_rows(left, right, distance):
    count = left.shape[1] // 4
    start = (lax.axis_index("fsdp") ^ distance) * count
    piece = lax.dynamic_slice_in_dim(left, start, count, 1)
    return product(piece, right, COLUMN_BY_COLUMN).astype(LOW)


def rows_at(matrices, distance):
    parts = []
    for matrix in matrices:
        count = matrix.shape[0] // 4
        start = (lax.axis_index("fsdp") ^ distance) * count
        parts.append(lax.dynamic_slice_in_dim(matrix, start, count, 0))
    return parts[0] if len(parts) == 1 else jnp.concatenate(parts, axis=1)


def far_halves(far):
    half = far.shape[0] // 2
    return (swap(far[:half], "fsdp", 1), swap(far[half:], "fsdp", 2))


def add_far(near, side, far):
    half = near.shape[0] // 2
    near = jnp.concatenate([near[:half], both((near[half:], far[1])).astype(LOW)], axis=0)
    side = jnp.concatenate([both((side[:half], far[0])).astype(LOW), side[half:]], axis=0)
    return (near, side)


def near_rows_out(pair):
    return (swap(pair[0], "fsdp", 1), swap(pair[1], "fsdp", 2))


def halves(value, bit):
    half = value.shape[0] // 2
    keep = lax.dynamic_slice_in_dim(value, bit * half, half, 0)
    send = lax.dynamic_slice_in_dim(value, (1 - bit) * half, half, 0)
    return keep, send.astype(LOW)


def split_rows(value, bit, distance):
    keep, send = halves(value, bit)
    return keep, swap(send, "ctx", distance)


def both(pair):
    return pair[0].astype(FULL) + pair[1].astype(FULL)


def join_rows(value, bit, distance):
    other = swap(value, "ctx", distance)
    return jnp.where(
        bit == 0,
        jnp.concatenate([value, other], axis=0),
        jnp.concatenate([other, value], axis=0),
    )


def pairwise(pieces):
    return (pieces[0] + pieces[1]) + (pieces[2] + pieces[3])


def swapped_if(bit, pair):
    return [jnp.where(bit == 0, pair[0], pair[1]), jnp.where(bit == 0, pair[1], pair[0])]


def per_device(
    tokens,
    clip_mask,
    cotangent,
    first_gain,
    first_shift,
    joint_weight,
    joint_bias,
    mixer_weight,
    mixer_bias,
    second_gain,
    second_shift,
    expand_weight,
    expand_bias,
    reduce_weight,
    reduce_bias,
):
    clips_here, rows_here, width = tokens.shape
    if lax.axis_size("ctx") != 4 or lax.axis_size("tp") != 2 or clips_here != 2:
        raise ValueError("mesh")
    shard = lax.axis_index("fsdp")
    block = lax.axis_index("ctx")
    core = lax.axis_index("tp")
    clip_at = block >> 1
    part_at = block & 1
    width_half = width // 2
    quarter = width_half // 2
    features = joint_weight.shape[2]
    part_width = features // 2
    pair_width = 2 * HEAD_DIM
    tokens_here = clips_here * rows_here

    flat_tokens = tokens.reshape(tokens_here, width)
    (first_normed,) = by_rows(
        first_norm_kernel, "first_norm", [LOW], False,
        flat_tokens, first_gain[None], first_shift[None],
    )
    first_normed = first_normed.reshape(clips_here, rows_here, width)
    mine = lax.dynamic_slice_in_dim(first_normed, core * width_half, width_half, 2)
    other_side = lax.dynamic_slice_in_dim(first_normed, (1 - core) * width_half, width_half, 2)
    own_clip = lax.dynamic_index_in_dim(mine, clip_at, 0, False)
    own_other = lax.dynamic_index_in_dim(other_side, clip_at, 0, False)
    other_clip = lax.dynamic_index_in_dim(mine, 1 - clip_at, 0, False)
    joint_part = lax.dynamic_slice_in_dim(joint_weight, part_at * part_width, part_width, 2)
    early = expand_weight.shape[1] // 2
    wide_part = jnp.concatenate(
        [expand_weight[:, :early]] + [joint_part[:, kind] for kind in range(3)] + [mixer_weight],
        axis=1,
    )

    own_clip, left, right, wide_part = fence(
        own_clip, other_clip[:, :quarter], other_clip[:, quarter:], wide_part
    )
    near_rows = swap(own_clip, "ctx", 1)
    across_left = swap(left, "ctx", 2)
    far_right = swap(right, "ctx", 3)
    wide_held = gather_near(wide_part)

    near_rows, across_left, far_right = fence(near_rows, across_left, far_right)
    passed = swap(jnp.concatenate([across_left, far_right], axis=1), "ctx", 1)
    (wide_held,) = fence(wide_held)
    held = gather_far(tuple(piece[:, early:] for piece in wide_held))

    passed, held, expand_rest = fence(passed, held, expand_weight[:, early:])
    rest_held = gather_near(expand_rest)
    cross_rows = jnp.concatenate(
        [
            near_rows,
            jnp.concatenate([across_left, passed[:, quarter:]], axis=1),
            jnp.concatenate([passed[:, :quarter], far_right], axis=1),
        ],
        axis=0,
    )
    cross_other = swap(cross_rows, "tp", 1)
    both_full = place_far(place_near(held), held)
    joint_columns = 3 * part_width
    joint_full = jnp.concatenate(
        [
            lax.dynamic_slice(both_full, (start * width_half, 0), (width_half, joint_columns))
            for start in (core, 1 - core)
        ],
        axis=0,
    )

    cross_other, joint_full, both_full, reduce_weight = fence(
        cross_other, joint_full, both_full, reduce_weight
    )
    mixer_full = both_full[:, joint_columns:]
    reduce_held = gather_near(reduce_weight)
    normed_mine = jnp.concatenate([own_clip, cross_rows], axis=0)
    normed_other = jnp.concatenate([own_other, cross_other], axis=0)
    bias_part = lax.dynamic_slice_in_dim(joint_bias, part_at * part_width, part_width, 1)
    bias_row = jnp.concatenate([bias_part[0], jnp.zeros_like(bias_part[0]), bias_part[1]])
    joint_out = joint_projection(normed_mine, normed_other, joint_full, bias_row[None])
    out_first, log_first = attention_forward(joint_out, 0)

    out_first, joint_out, mixer_full, rest_held = fence(
        out_first, joint_out, mixer_full, rest_held
    )
    first_blocks = out_first.reshape(4, rows_here, pair_width)
    arrived_first = [swap(first_blocks[d], "ctx", d) for d in (1, 2, 3)]
    out_second, log_second = attention_forward(joint_out, 1)

    far_leaves = far_of(
        tuple(
            jnp.concatenate([one[:, :early], two], axis=1)
            for one, two in zip(wide_held, rest_held)
        )
    )
    out_second, arrived_first, reduce_held, far_leaves = fence(
        out_second, arrived_first, reduce_held, far_leaves
    )
    second_blocks = out_second.reshape(4, rows_here, pair_width)
    arrived_second = [swap(second_blocks[d], "ctx", d) for d in (1, 2, 3)]
    expand_far_rows = send_far(far_leaves)

    arrived_second, expand_far_rows, reduce_held, reduce_leaves = fence(
        arrived_second, expand_far_rows, reduce_held, far_of(reduce_held)
    )
    reduce_held = reduce_held + send_far(reduce_leaves)
    expand_held = list(zip(wide_held, rest_held)) + [(rows,) for rows in expand_far_rows]
    arrived = [jnp.concatenate([first_blocks[0], second_blocks[0]], axis=1)] + [
        jnp.concatenate([one, two], axis=1) for one, two in zip(arrived_first, arrived_second)
    ]
    own_joined = jnp.concatenate(swapped_if(part_at, arrived[:2]), axis=1)
    other_joined = jnp.concatenate(swapped_if(part_at, arrived[2:]), axis=1)
    mixed_in = jnp.concatenate(swapped_if(clip_at, [own_joined, other_joined]), axis=0)
    mixer_part = product(mixed_in, mixer_full, ROW_BY_ROW).astype(LOW)
    mixer_swapped = swap(mixer_part, "tp", 1)
    mixer_row = mixer_bias[None]
    (second_normed,) = by_rows(
        second_norm_kernel, "second_norm", [LOW], False,
        flat_tokens, mixer_part, mixer_swapped, mixer_row, second_gain[None], second_shift[None],
    )
    valid = clip_mask.astype(FULL)[:, None, None]
    reduce_slope = (cotangent.astype(FULL) * valid).astype(LOW).reshape(tokens_here, width)
    reduce_bias_grad = jnp.sum(reduce_slope.astype(FULL), axis=0)

    second_normed, reduce_slope, reduce_held = fence(second_normed, reduce_slope, reduce_held)
    four = lax.axis_size("fsdp") == 4
    start = jnp.zeros((), jnp.int32)
    if four:
        rows = width // 4
        pieces_at = jnp.stack([shard, shard ^ 1, shard ^ 2, shard ^ 3, shard ^ 3]) * rows
        pieces_at = pieces_at.astype(jnp.int32) + jnp.array([0, 0, 0, 0, rows // 2], jnp.int32)
    else:
        pieces_at = start.reshape(1)
    activated, expand_slope, second_part, expand_bias_grad = feed_forward(
        second_normed, reduce_slope, expand_bias[None], expand_held, early,
        [(piece,) for piece in reduce_held], pieces_at,
    )
    expand_bias_grad = expand_bias_grad[0]

    second_swapped = swap(second_part, "tp", 1)
    place, order = (shard, (3, 2, 1, 0)) if four else (start, (0, 1, 2, 3))
    if four:
        half = width // 8
        far = grad_rows(second_normed, expand_slope, 3)
        far_top, far_low, normed_again, expand_slope = fence(
            far[:half], far[half:], second_normed, expand_slope
        )
        expand_far = (swap(far_top, "fsdp", 1), swap(far_low, "fsdp", 2))
        expand_parts = [grad_rows(normed_again, expand_slope, d) for d in (0, 1, 2)]
        expand_parts, second_swapped = fence(expand_parts, second_swapped)
    else:
        expand_far = ()
        expand_whole = product(second_normed, expand_slope, COLUMN_BY_COLUMN).astype(LOW)
    mixer_slope, first_sum_back, second_sums = by_rows(
        second_norm_back_kernel, "second_norm_back", [LOW, FULL], True,
        flat_tokens, mixer_part, mixer_swapped, mixer_row, second_gain[None],
        second_part, second_swapped, reduce_slope,
    )
    attended_slope = product(mixer_slope, mixer_full, PLAIN).astype(LOW)

    leaving = []
    for distance in range(4):
        to = block ^ distance
        corner = ((to >> 1) * rows_here, (to & 1) * part_width)
        leaving.append(lax.dynamic_slice(attended_slope, corner, (rows_here, part_width)))
    expand_near = add_far(expand_parts[1], expand_parts[2], expand_far) if four else ()
    leaving, mixer_slope, mixed_in, activated, expand_near = fence(
        leaving, mixer_slope, mixed_in, activated, expand_near
    )
    slope_blocks = [leaving[0]] + [swap(leaving[d], "ctx", d) for d in (1, 2, 3)]
    if four:
        expand_near = near_rows_out(expand_near)
    wide = (
        product(reduce_slope, activated, COLUMN_BY_COLUMN).astype(LOW),
        product(mixer_slope, mixed_in, COLUMN_BY_COLUMN).astype(LOW),
    )
    if four:
        wide_far, wide_side, wide_next = (rows_at(wide, distance) for distance in (3, 2, 1))
        far_top, far_low = wide_far[:half], wide_far[half:]
        wide_early = (wide_next[:half], wide_side[half:])
    else:
        far_top, far_low, wide_early = (), (), ()

    slope_blocks, expand_near, far_top, far_low = fence(
        slope_blocks, expand_near, far_top, far_low
    )
    if four:
        expand_sum = expand_parts[0].astype(FULL) + both(expand_near)
    else:
        expand_sum = lax.psum_scatter(
            expand_whole, "fsdp", scatter_dimension=0, tiled=True
        ).astype(FULL)
    expand_keep, expand_send = halves(expand_sum, part_at)
    slope_clip = jnp.concatenate(slope_blocks, axis=0)
    expand_send, slope_clip, far_top, far_low = fence(expand_send, slope_clip, far_top, far_low)
    wide_far = (swap(far_top, "fsdp", 1), swap(far_low, "fsdp", 2)) if four else ()
    expand_rows = (expand_keep, swap(expand_send, "ctx", 1))
    grad_first = attention_backward(joint_out, slope_clip, out_first, log_first, 0)

    grad_first, slope_clip, wide_far, expand_rows = fence(
        grad_first, slope_clip, wide_far, expand_rows
    )
    if four:
        wide_late = (
            both((wide_next[half:], wide_far[1])).astype(LOW),
            both((wide_side[:half], wide_far[0])).astype(LOW),
        )
    else:
        wide_late = ()
    expand_keep, expand_send = halves(both(expand_rows), clip_at)
    expand_send, slope_clip, wide_early, wide_late = fence(
        expand_send, slope_clip, wide_early, wide_late
    )
    if four:
        wide_early = near_rows_out(wide_early)
    expand_rows = (expand_keep, swap(expand_send, "ctx", 2))
    grad_second = attention_backward(joint_out, slope_clip, out_second, log_second, 1)

    grad_second, expand_rows, wide_early, wide_late = fence(
        grad_second, expand_rows, wide_early, wide_late
    )
    if four:
        wide_late = near_rows_out(wide_late)
    expand_rows = join_rows(both(expand_rows).astype(LOW), clip_at, 2)
    joint_slope = jnp.concatenate(
        [grad[kind] for kind in range(3) for grad in (grad_first, grad_second)], axis=1
    )
    first_there = product(joint_slope, joint_full[width_half:], ROW_BY_ROW).astype(LOW)
    first_here = rows_product(joint_slope, joint_full[:width_half], "first_slope")
    first_half = both((first_here, swap(first_there, "tp", 1))).astype(LOW)

    if not four:
        wide_near = lax.psum_scatter(
            jnp.concatenate(wide, axis=1), "fsdp", scatter_dimension=0, tiled=True
        )
    first_half, joint_slope = fence(first_half, joint_slope)
    pieces = first_half.reshape(4, rows_here, width_half)
    passing = jnp.concatenate([pieces[1], pieces[3][:, :quarter], pieces[2][:, quarter:]], axis=1)
    passing = swap(passing, "ctx", 1)
    place = (shard if four else start) ^ (2 * core)
    joint_parts = grad_products([normed_mine, normed_other], joint_slope, place, order, "joint_grad")
    slope_sums = jnp.sum(joint_slope.astype(FULL), axis=0)
    bias_sums = jnp.stack([slope_sums[:part_width], slope_sums[2 * part_width :]])
    joint_bias_grad = lax.dynamic_update_slice(
        jnp.zeros((2, features), FULL), bias_sums, (0, part_at * part_width)
    )

    joint_far = far_halves(joint_parts[0]) if four else ()
    passing, joint_far, wide_late, expand_rows = fence(
        passing, joint_far, wide_late, expand_rows
    )
    if four:
        near_sum = [both((wide_early[0], wide_late[1])), both((wide_late[0], wide_early[1]))]
        wide_sum = rows_at(wide, 0).astype(FULL) + jnp.concatenate(near_sum, axis=0)
    else:
        wide_sum = wide_near.astype(FULL)
    wide_keep, wide_send = halves(wide_sum, part_at)
    own_half = both((pieces[0], passing[:, :width_half])).astype(LOW)
    to_left = both((pieces[2][:, :quarter], passing[:, width_half : width_half + quarter]))
    to_right = both((pieces[3][:, quarter:], passing[:, width_half + quarter :]))
    joint_near = add_far(joint_parts[2], joint_parts[1], joint_far) if four else ()
    to_left, to_right, own_half, wide_send, joint_near, activated = fence(
        to_left.astype(LOW), to_right.astype(LOW), own_half, wide_send, joint_near, activated
    )
    other_half = jnp.concatenate([swap(to_left, "ctx", 2), swap(to_right, "ctx", 3)], axis=1)
    wide_rows = (wide_keep, swap(wide_send, "ctx", 1))
    if four:
        joint_near = near_rows_out(joint_near)
    else:
        joint_near = lax.psum_scatter(
            joint_parts.reshape(width, -1), "fsdp", scatter_dimension=0, tiled=True
        )
    reduce_part = reduce_output(activated, reduce_held, pieces_at)

    other_half, joint_near, wide_rows, reduce_part = fence(
        other_half, joint_near, wide_rows, reduce_part
    )
    slope_half = jnp.concatenate(swapped_if(clip_at, [own_half, other_half]), axis=0)
    slope_other = swap(slope_half, "tp", 1)
    slope_other, expand_rows = fence(slope_other, expand_rows)
    expand_grad = join_rows(expand_rows, part_at, 1).astype(FULL)
    first_slope = jnp.concatenate(swapped_if(core, [slope_half, slope_other]), axis=1)
    wide_rows = split_rows(both(wide_rows), clip_at, 2)
    reduce_swapped = swap(reduce_part, "tp", 1)
    joint_sum = joint_parts[3].astype(FULL) + both(joint_near) if four else joint_near
    joint_sum = joint_sum.astype(LOW)
    joint_sum = (joint_sum, swap(joint_sum, "ctx", 2))
    tokens_grad, first_sums = by_rows(
        first_norm_back_kernel, "first_norm_back", [FULL], True,
        flat_tokens, first_slope, first_gain[None],
        cotangent.reshape(tokens_here, width), first_sum_back,
    )
    first_sums, tokens_grad, reduce_swapped = fence(first_sums, tokens_grad, reduce_swapped)
    vectors = [
        first_sums[0],
        first_sums[1],
        joint_bias_grad[0],
        joint_bias_grad[1],
        second_sums[2],
        second_sums[0],
        second_sums[1],
        expand_bias_grad,
        reduce_bias_grad,
    ]
    packed = jnp.concatenate(vectors).reshape(-1, 128)
    packed_pieces = [packed] + [swap(packed, "ctx", d) for d in (1, 2, 3)]
    reduce_out = both((reduce_part, reduce_swapped)) + reduce_bias
    mixer_out = both((mixer_part, mixer_swapped)) + mixer_bias
    branches = (mixer_out + reduce_out).reshape(clips_here, rows_here, width)
    result = (tokens.astype(FULL) + valid * branches).astype(LOW)

    packed_pieces, joint_sum, wide_rows, result = fence(
        packed_pieces, joint_sum, wide_rows, result
    )
    packed = pairwise(packed_pieces)
    if four:
        packed = pairwise([packed] + [swap(packed, "fsdp", d) for d in (1, 2, 3)])
    else:
        packed = lax.psum(packed, "fsdp")
    joint_sum = both(joint_sum).astype(LOW)
    joint_parts = swapped_if(part_at, [joint_sum, swap(joint_sum, "ctx", 1)])
    joint_grad = jnp.concatenate(
        [piece.reshape(-1, 3, part_width) for piece in joint_parts], axis=2
    ).astype(FULL)
    wide_rows = join_rows(both(wide_rows).astype(LOW), clip_at, 2)
    wide_rows = join_rows(wide_rows, part_at, 1).astype(FULL)
    reduce_grad = wide_rows[:, : activated.shape[1]]
    mixer_grad = wide_rows[:, activated.shape[1] :]
    packed = packed.reshape(-1)
    shares = []
    start = 0
    for vector in vectors:
        share = vector.shape[0] // lax.axis_size("fsdp")
        shares.append(lax.dynamic_slice_in_dim(packed, start + shard * share, share, 0))
        start += vector.shape[0]

    shape = (clips_here, rows_here, width)
    return (
        result,
        tokens_grad.reshape(shape),
        shares[0],
        shares[1],
        joint_grad,
        jnp.stack([shares[2], shares[3]]),
        mixer_grad,
        shares[4],
        shares[5],
        shares[6],
        expand_grad,
        shares[7],
        reduce_grad,
        shares[8],
    )


def solution(mesh):
    return jax.shard_map(
        per_device,
        mesh=mesh,
        in_specs=(
            P("fsdp", "ctx", None),
            P("fsdp"),
            P("fsdp", "ctx", None),
            P(),
            P(),
            P("fsdp", None, "tp"),
            P(None, "tp"),
            P("fsdp", "tp"),
            P(),
            P(),
            P(),
            P("fsdp", "tp"),
            P("tp"),
            P("fsdp", "tp"),
            P(),
        ),
        out_specs=(
            P("fsdp", "ctx", None),
            P("fsdp", "ctx", None),
            P("fsdp"),
            P("fsdp"),
            P("fsdp", None, "tp"),
            P(None, ("tp", "fsdp")),
            P("fsdp", "tp"),
            P("fsdp"),
            P("fsdp"),
            P("fsdp"),
            P("fsdp", "tp"),
            P(("tp", "fsdp")),
            P("fsdp", "tp"),
            P("fsdp"),
        ),
        check_vma=False,
    )
```

```python
import jax
import jax.numpy as jnp
from jax import lax
from jax.experimental import pallas as pl
from jax.experimental.pallas import tpu as pltpu
from jax.sharding import PartitionSpec as P

HEAD_DIM = 64
EPSILON = 1e-06
LOW = jnp.bfloat16
FULL = jnp.float32

ROW_BY_ROW = (((1,), (1,)), ((), ()))
PLAIN = (((1,), (0,)), ((), ()))
COLUMN_BY_COLUMN = (((0,), (0,)), ((), ()))


def product(left, right, dims):
    return lax.dot_general(left, right, dims, preferred_element_type=FULL)


def normalize(value_rows):
    center = value_rows - jnp.mean(value_rows, axis=-1, keepdims=True)
    inverse = lax.rsqrt(jnp.mean(center * center, axis=-1, keepdims=True) + EPSILON)
    return (center * inverse, inverse)


def norm_back(upstream, gain, scaled, inverse):
    weighted = upstream * gain
    return inverse * (
        weighted
        - jnp.mean(weighted, axis=-1, keepdims=True)
        - scaled * jnp.mean(weighted * scaled, axis=-1, keepdims=True)
    )


def row_chunk(count, most):
    for chunk in range(most, 0, -16):
        if count % chunk == 0:
            return chunk
    raise ValueError("rows")


def first_norm_kernel(tokens_ref, gain_ref, shift_ref, out_ref):
    scaled, _ = normalize(tokens_ref[...].astype(FULL))
    out_ref[...] = (scaled * gain_ref[...] + shift_ref[...]).astype(LOW)


def second_norm_kernel(tokens_ref, one_ref, two_ref, bias_ref, gain_ref, shift_ref, out_ref):
    mixed = one_ref[...].astype(FULL) + two_ref[...].astype(FULL) + bias_ref[...]
    scaled, _ = normalize(tokens_ref[...].astype(FULL) + mixed)
    out_ref[...] = (scaled * gain_ref[...] + shift_ref[...]).astype(LOW)


def add_sums(ref, rows):
    sums = jnp.concatenate([jnp.sum(row, axis=0, keepdims=True) for row in rows], axis=0)

    @pl.when(pl.program_id(0) == 0)
    def _():
        ref[: len(rows)] = sums

    @pl.when(pl.program_id(0) > 0)
    def _():
        ref[: len(rows)] += sums


def second_norm_back_kernel(
    tokens_ref, one_ref, two_ref, bias_ref, gain_ref, left_ref, right_ref, outer_ref,
    slope_ref, back_ref, sums_ref,
):
    mixed = one_ref[...].astype(FULL) + two_ref[...].astype(FULL) + bias_ref[...]
    scaled, inverse = normalize(tokens_ref[...].astype(FULL) + mixed)
    upstream = left_ref[...].astype(FULL) + right_ref[...].astype(FULL)
    back = norm_back(upstream, gain_ref[...], scaled, inverse)
    slope = (outer_ref[...].astype(FULL) + back).astype(LOW)
    slope_ref[...] = slope
    back_ref[...] = back
    add_sums(sums_ref, [upstream * scaled, upstream, slope.astype(FULL)])


def first_norm_back_kernel(
    tokens_ref, upstream_ref, gain_ref, outer_ref, back_ref, out_ref, sums_ref
):
    scaled, inverse = normalize(tokens_ref[...].astype(FULL))
    upstream = upstream_ref[...].astype(FULL)
    back = norm_back(upstream, gain_ref[...], scaled, inverse)
    out_ref[...] = outer_ref[...].astype(FULL) + back_ref[...] + back
    add_sums(sums_ref, [upstream * scaled, upstream])


def by_rows(kernel, name, out_types, sums, *values):
    count, width = values[0].shape
    chunk = count // 2 if count % 16 == 0 else count
    part = pl.BlockSpec((chunk, width), lambda i: (i, 0))
    in_specs = [
        part if value.shape[0] == count else pl.BlockSpec((1, width), lambda i: (0, 0))
        for value in values
    ]
    out_specs = [part for _ in out_types]
    out_shape = [jax.ShapeDtypeStruct((count, width), kind) for kind in out_types]
    if sums:
        out_specs.append(pl.BlockSpec((8, width), lambda i: (0, 0)))
        out_shape.append(jax.ShapeDtypeStruct((8, width), FULL))
    return pl.pallas_call(
        kernel,
        grid=(count // chunk,),
        in_specs=in_specs,
        out_specs=out_specs,
        out_shape=out_shape,
        compiler_params=pltpu.CompilerParams(vmem_limit_bytes=40 << 20),
        name=name,
    )(*values)


def joint_kernel(mine_ref, other_ref, weight_ref, bias_ref, out_ref):
    half = mine_ref.shape[1]
    out = product(mine_ref[...], weight_ref[:half], PLAIN)
    out += product(other_ref[...], weight_ref[half:], PLAIN)
    out_ref[...] = (out + bias_ref[...]).astype(LOW)


def joint_projection(mine, other, weight, bias):
    count, half = mine.shape
    columns = weight.shape[1]
    chunk = row_chunk(count, 784)
    part = pl.BlockSpec((chunk, half), lambda i: (i, 0))
    return pl.pallas_call(
        joint_kernel,
        grid=(count // chunk,),
        in_specs=[
            part,
            part,
            pl.BlockSpec(weight.shape, lambda i: (0, 0)),
            pl.BlockSpec((1, columns), lambda i: (0, 0)),
        ],
        out_specs=pl.BlockSpec((chunk, columns), lambda i: (i, 0)),
        out_shape=jax.ShapeDtypeStruct((count, columns), LOW),
        compiler_params=pltpu.CompilerParams(vmem_limit_bytes=40 << 20),
        name="joint_projection",
    )(mine, other, weight, bias)


def rows_kernel(left_ref, right_ref, out_ref):
    out_ref[...] = product(left_ref[...], right_ref[...], ROW_BY_ROW).astype(LOW)


def rows_product(left, right, name):
    count, depth = left.shape
    columns = right.shape[0]
    chunk = row_chunk(count, 400)
    return pl.pallas_call(
        rows_kernel,
        grid=(count // chunk,),
        in_specs=[
            pl.BlockSpec((chunk, depth), lambda i: (i, 0)),
            pl.BlockSpec((columns, depth), lambda i: (0, 0)),
        ],
        out_specs=pl.BlockSpec((chunk, columns), lambda i: (i, 0)),
        out_shape=jax.ShapeDtypeStruct((count, columns), LOW),
        compiler_params=pltpu.CompilerParams(vmem_limit_bytes=48 << 20),
        name=name,
    )(left, right)


def grad_kernel(distances, place_ref, *refs):
    lefts, (right_ref, out_ref) = refs[:-2], refs[-2:]
    left = lefts[0][...]
    if len(lefts) == 2:
        slot = place_ref[0] ^ distance_at(distances, pl.program_id(0))
        left = jnp.where((slot >> 1) == 0, left, lefts[1][...])
    out_ref[0] = product(left, right_ref[...], COLUMN_BY_COLUMN).astype(LOW)


def distance_at(distances, step):
    if len(distances) == 1:
        return distances[0]
    return distances[0] + step * (distances[1] - distances[0])


def grad_products(lefts, right, place, distances, name):
    tokens_here, columns = right.shape
    quarter = sum(left.shape[1] for left in lefts) // 4
    blocks = lefts[0].shape[1] // quarter

    def left_at(i, place):
        return (0, (place[0] ^ distance_at(distances, i)) & (blocks - 1))

    return pl.pallas_call(
        lambda *refs: grad_kernel(distances, *refs),
        grid_spec=pltpu.PrefetchScalarGridSpec(
            num_scalar_prefetch=1,
            grid=(len(distances),),
            in_specs=[pl.BlockSpec((tokens_here, quarter), left_at) for _ in lefts]
            + [pl.BlockSpec((tokens_here, columns), lambda i, place: (0, 0))],
            out_specs=pl.BlockSpec((1, quarter, columns), lambda i, place: (i, 0, 0)),
        ),
        out_shape=jax.ShapeDtypeStruct((len(distances), quarter, columns), LOW),
        compiler_params=pltpu.CompilerParams(vmem_limit_bytes=48 << 20),
        name=name,
    )(place.astype(jnp.int32).reshape(1), *lefts, right)


def attention_forward_kernel(q_ref, k_ref, v_ref, o_ref, lse_ref):
    count, width = q_ref.shape
    rows = row_chunk(count, 256)
    lane = lax.broadcasted_iota(jnp.int32, (rows, width), 1)
    k = k_ref[...]
    v = v_ref[...]
    units = [(start, head) for start in range(0, count, rows) for head in range(width // HEAD_DIM)]

    def scores_of(unit):
        start, head = unit
        q = q_ref[start : start + rows] * jnp.asarray(HEAD_DIM ** (-0.5), LOW)
        return product(jnp.where((lane // HEAD_DIM) == head, q, jnp.zeros_like(q)), k, ROW_BY_ROW)

    logs = []
    ahead = scores_of(units[0])
    for step, (start, head) in enumerate(units):
        scores = ahead
        if step + 1 < len(units):
            ahead = scores_of(units[step + 1])
        top = jnp.max(scores, axis=-1, keepdims=True)
        weights = jnp.exp(scores - top)
        total = jnp.sum(weights, axis=-1, keepdims=True)
        part = product(weights.astype(LOW), v, PLAIN) / total
        if head == 0:
            out = part
            logs.append(jnp.zeros((rows, width), FULL))
        else:
            out = jnp.where((lane // HEAD_DIM) == head, part, out)
            o_ref[start : start + rows] = out.astype(LOW)
        logs[-1] = jnp.where(lane == head, top + jnp.log(total), logs[-1])
    lse_ref[...] = jnp.concatenate(logs, axis=0).T[: lse_ref.shape[0]]


def attention_forward(joint, pair):
    count, columns = joint.shape
    width = 2 * HEAD_DIM
    kind = columns // (3 * width)
    return pl.pallas_call(
        attention_forward_kernel,
        grid=(1,),
        in_specs=[
            pl.BlockSpec((count, width), lambda i: (0, pair)),
            pl.BlockSpec((count, width), lambda i: (0, kind + pair)),
            pl.BlockSpec((count, width), lambda i: (0, 2 * kind + pair)),
        ],
        out_specs=[
            pl.BlockSpec((count, width), lambda i: (0, 0)),
            pl.BlockSpec((8, count), lambda i: (0, 0)),
        ],
        out_shape=[
            jax.ShapeDtypeStruct((count, width), LOW),
            jax.ShapeDtypeStruct((8, count), FULL),
        ],
        compiler_params=pltpu.CompilerParams(vmem_limit_bytes=48 << 20),
        name="attention_forward",
    )(joint, joint, joint)


def attention_backward_kernel(
    q_ref, k_ref, v_ref, da_ref, o_ref, lse_ref, dq_ref, dk_ref, dv_ref,
    q_heads, da_heads, delta_ref, dq_total,
):
    count, width = q_ref.shape
    rows = row_chunk(count, 256)
    heads = width // HEAD_DIM
    scale = jnp.asarray(HEAD_DIM ** (-0.5), LOW)

    lane = lax.broadcasted_iota(jnp.int32, (count, width), 1)
    delta = jnp.zeros((count, width), FULL)
    q = q_ref[...] * scale
    da = da_ref[...]
    both_rows = da.astype(FULL) * o_ref[...].astype(FULL)
    for head in range(heads):
        mask = (lane // HEAD_DIM) == head
        q_heads[head] = jnp.where(mask, q, jnp.zeros_like(q))
        da_heads[head] = jnp.where(mask, da, jnp.zeros_like(da))
        row = jnp.sum(jnp.where(mask, both_rows, 0.0), axis=-1, keepdims=True)
        delta = jnp.where(lane == head, row, delta)
    delta_ref[...] = delta.T[:8]
    dq_total[...] = jnp.zeros_like(dq_total)

    lane = lax.broadcasted_iota(jnp.int32, (rows, width), 1)
    for start in range(0, count, rows):
        k = k_ref[start : start + rows]
        v = v_ref[start : start + rows]
        scaled_k = k * scale
        dk = dv = None
        for head in range(heads):
            q = q_heads[head]
            da = da_heads[head]
            probs = jnp.exp(product(k, q, ROW_BY_ROW) - lse_ref[head : head + 1, :])
            slope = probs * (product(v, da, ROW_BY_ROW) - delta_ref[head : head + 1, :])
            slope = slope.astype(LOW)
            dv_part = product(probs.astype(LOW), da, PLAIN)
            dk_part = product(slope, q, PLAIN)
            dv = dv_part if dv is None else dv + dv_part
            dk = dk_part if dk is None else dk + dk_part
            one_k = jnp.where((lane // HEAD_DIM) == head, scaled_k, jnp.zeros_like(k))
            dq_total[...] += product(slope, one_k, COLUMN_BY_COLUMN)
        dk_ref[start : start + rows] = dk.astype(LOW)
        dv_ref[start : start + rows] = dv.astype(LOW)
    dq_ref[...] = dq_total[...].astype(LOW)


def attention_backward(joint, da, out, lse, pair):
    count, columns = joint.shape
    width = 2 * HEAD_DIM
    kind = columns // (3 * width)
    alone = pl.BlockSpec((count, width), lambda i: (0, 0))
    grad = jax.ShapeDtypeStruct((count, width), LOW)
    return pl.pallas_call(
        attention_backward_kernel,
        grid=(1,),
        in_specs=[
            pl.BlockSpec((count, width), lambda i: (0, pair)),
            pl.BlockSpec((count, width), lambda i: (0, kind + pair)),
            pl.BlockSpec((count, width), lambda i: (0, 2 * kind + pair)),
            pl.BlockSpec((count, width), lambda i: (0, pair)),
            alone,
            pl.BlockSpec((8, count), lambda i: (0, 0)),
        ],
        out_specs=[alone, alone, alone],
        out_shape=[grad, grad, grad],
        scratch_shapes=[
            pltpu.VMEM((2, count, width), LOW),
            pltpu.VMEM((2, count, width), LOW),
            pltpu.VMEM((8, count), FULL),
            pltpu.VMEM((count, width), FULL),
        ],
        compiler_params=pltpu.CompilerParams(vmem_limit_bytes=48 << 20),
        name="attention_backward",
    )(joint, joint, joint, da, out, lse)


def put_together(place_ref, whole_ref, pieces, edge=0):
    for piece, refs in enumerate(pieces):
        rows = refs[0].shape[0]
        place = pl.ds(pl.multiple_of(place_ref[piece], rows), rows)
        if len(refs) == 1:
            whole_ref[place, :] = refs[0][...]
            continue

        @pl.when(pl.program_id(0) < edge)
        def _():
            whole_ref[place, :] = refs[0][...]

        @pl.when(pl.program_id(0) >= edge)
        def _():
            whole_ref[place, :] = refs[1][...]


def nested(refs, like):
    refs = iter(refs)
    return [tuple(next(refs) for _ in piece) for piece in like]


def feed_forward_kernel(
    expand, reduce, edge, place_ref, normed_ref, slope_ref, bias_ref, *refs
):
    active_ref, expand_slope_ref, back_ref, bias_grad_ref, total, expand_ref, reduce_ref = refs[-7:]
    arrays = sum(len(piece) for piece in expand)
    put_together(place_ref, expand_ref, nested(refs[:arrays], expand), edge)
    put_together(place_ref, reduce_ref, nested(refs[arrays:-7], reduce))
    step = pl.program_id(0)
    count = normed_ref.shape[0]
    half = count // 2
    bias_grad = None
    for rows in (slice(0, half), slice(half, count)):
        hidden = product(normed_ref[rows], expand_ref[...], PLAIN) + bias_ref[...]
        upstream = product(slope_ref[rows], reduce_ref[...], PLAIN)
        share = 0.5 * (1.0 + lax.erf(hidden * (0.5**0.5)))
        active_ref[rows] = (hidden * share).astype(LOW)
        density = jnp.exp(-0.5 * hidden * hidden) * 0.3989422804014327
        slope = (upstream * (share + hidden * density)).astype(LOW)
        expand_slope_ref[rows] = slope
        part = jnp.sum(slope.astype(FULL), axis=0, keepdims=True)
        bias_grad = part if bias_grad is None else bias_grad + part
        back = product(slope, expand_ref[...], ROW_BY_ROW)

        @pl.when(step == 0)
        def _():
            total[rows] = back

        @pl.when(step > 0)
        def _():
            total[rows] += back

    bias_grad_ref[...] = bias_grad

    @pl.when(step == pl.num_programs(0) - 1)
    def _():
        back_ref[...] = total[...].astype(LOW)


def feed_forward(normed, slope, bias, expand, early, reduce, place):
    count, width = normed.shape
    hidden = bias.shape[1]
    block = 512
    edge = early // block
    whole = pl.BlockSpec((count, width), lambda i, place: (0, 0))
    out = pl.BlockSpec((count, block), lambda i, place: (0, i))
    row = pl.BlockSpec((1, block), lambda i, place: (0, i))
    specs = []
    arrays = []
    for piece in [*expand, *reduce]:
        shape = (piece[0].shape[0], block)
        arrays += piece
        if len(piece) == 1:
            specs.append(pl.BlockSpec(shape, lambda i, place: (0, i)))
        else:
            specs.append(pl.BlockSpec(shape, lambda i, place: (0, jnp.minimum(i, edge - 1))))
            specs.append(pl.BlockSpec(shape, lambda i, place: (0, jnp.maximum(i - edge, 0))))
    return pl.pallas_call(
        lambda *refs: feed_forward_kernel(expand, reduce, edge, *refs),
        grid_spec=pltpu.PrefetchScalarGridSpec(
            num_scalar_prefetch=1,
            grid=(hidden // block,),
            in_specs=[whole, whole, row] + specs,
            out_specs=[out, out, whole, row],
            scratch_shapes=[
                pltpu.VMEM((count, width), FULL),
                pltpu.VMEM((width, block), LOW),
                pltpu.VMEM((width, block), LOW),
            ],
        ),
        out_shape=[
            jax.ShapeDtypeStruct((count, hidden), LOW),
            jax.ShapeDtypeStruct((count, hidden), LOW),
            jax.ShapeDtypeStruct((count, width), LOW),
            jax.ShapeDtypeStruct((1, hidden), FULL),
        ],
        compiler_params=pltpu.CompilerParams(vmem_limit_bytes=44 << 20),
        name="feed_forward",
    )(place, normed, slope, bias, *arrays)


def reduce_kernel(place_ref, active_ref, *refs):
    out_ref, total, reduce_ref = refs[-3:]
    put_together(place_ref, reduce_ref, [(ref,) for ref in refs[:-3]])
    part = product(active_ref[...], reduce_ref[...], ROW_BY_ROW)

    @pl.when(pl.program_id(0) == 0)
    def _():
        total[...] = part

    @pl.when(pl.program_id(0) > 0)
    def _():
        total[...] += part

    @pl.when(pl.program_id(0) == pl.num_programs(0) - 1)
    def _():
        out_ref[...] = total[...].astype(LOW)


def reduce_output(active, reduce, place):
    count, hidden = active.shape
    width = sum(piece.shape[0] for piece in reduce)
    block = 512 if hidden % 512 == 0 else hidden
    return pl.pallas_call(
        reduce_kernel,
        grid_spec=pltpu.PrefetchScalarGridSpec(
            num_scalar_prefetch=1,
            grid=(hidden // block,),
            in_specs=[pl.BlockSpec((count, block), lambda i, place: (0, i))]
            + [
                pl.BlockSpec((piece.shape[0], block), lambda i, place: (0, i)) for piece in reduce
            ],
            out_specs=pl.BlockSpec((count, width), lambda i, place: (0, 0)),
            scratch_shapes=[pltpu.VMEM((count, width), FULL), pltpu.VMEM((width, block), LOW)],
        ),
        out_shape=jax.ShapeDtypeStruct((count, width), LOW),
        compiler_params=pltpu.CompilerParams(vmem_limit_bytes=32 << 20),
        name="reduce_output",
    )(place, active, *reduce)


def swap(value, axis, distance):
    size = lax.axis_size(axis)
    return lax.ppermute(value, axis, [(i, i ^ distance) for i in range(size)])


def fence(*values):
    return lax.optimization_barrier(values)


def gather_near(rows_here):
    if lax.axis_size("fsdp") != 4:
        return (lax.all_gather(rows_here, "fsdp", axis=0, tiled=True),)
    return (rows_here, swap(rows_here, "fsdp", 1), swap(rows_here, "fsdp", 2))


def far_of(held):
    if len(held) == 1:
        return ()
    half = held[0].shape[0] // 2
    return (held[2][:half], held[1][half:])


def send_far(leaves):
    return (swap(leaves[0], "fsdp", 1), swap(leaves[1], "fsdp", 2)) if leaves else ()


def far_of(held):
    if len(held) == 1:
        return ()
    half = held[0].shape[0] // 2
    return (held[2][:half], held[1][half:])


def send_far(leaves):
    return (swap(leaves[0], "fsdp", 1), swap(leaves[1], "fsdp", 2)) if leaves else ()


def gather_far(held):
    return held + send_far(far_of(held))


def place_near(held):
    if len(held) == 1:
        return held[0]
    rows_here, near, side = held[:3]
    me = lax.axis_index("fsdp")
    count, width = rows_here.shape
    out = jnp.zeros((4 * count, width), rows_here.dtype)
    out = lax.dynamic_update_slice(out, rows_here, (me * count, 0))
    out = lax.dynamic_update_slice(out, near, ((me ^ 1) * count, 0))
    return lax.dynamic_update_slice(out, side, ((me ^ 2) * count, 0))


def place_far(out, held):
    if len(held) == 1:
        return out
    far_top, far_low = held[3:]
    half = far_top.shape[0]
    start = (lax.axis_index("fsdp") ^ 3) * 2 * half
    out = lax.dynamic_update_slice(out, far_top, (start, 0))
    return lax.dynamic_update_slice(out, far_low, (start + half, 0))


def grad_rows(left, right, distance):
    count = left.shape[1] // 4
    start = (lax.axis_index("fsdp") ^ distance) * count
    piece = lax.dynamic_slice_in_dim(left, start, count, 1)
    return product(piece, right, COLUMN_BY_COLUMN).astype(LOW)


def rows_at(matrices, distance):
    parts = []
    for matrix in matrices:
        count = matrix.shape[0] // 4
        start = (lax.axis_index("fsdp") ^ distance) * count
        parts.append(lax.dynamic_slice_in_dim(matrix, start, count, 0))
    return parts[0] if len(parts) == 1 else jnp.concatenate(parts, axis=1)


def far_halves(far):
    half = far.shape[0] // 2
    return (swap(far[:half], "fsdp", 1), swap(far[half:], "fsdp", 2))


def add_far(near, side, far):
    half = near.shape[0] // 2
    near = jnp.concatenate([near[:half], both((near[half:], far[1])).astype(LOW)], axis=0)
    side = jnp.concatenate([both((side[:half], far[0])).astype(LOW), side[half:]], axis=0)
    return (near, side)


def near_rows_out(pair):
    return (swap(pair[0], "fsdp", 1), swap(pair[1], "fsdp", 2))


def halves(value, bit):
    half = value.shape[0] // 2
    keep = lax.dynamic_slice_in_dim(value, bit * half, half, 0)
    send = lax.dynamic_slice_in_dim(value, (1 - bit) * half, half, 0)
    return keep, send.astype(LOW)


def split_rows(value, bit, distance):
    keep, send = halves(value, bit)
    return keep, swap(send, "ctx", distance)


def both(pair):
    return pair[0].astype(FULL) + pair[1].astype(FULL)


def join_rows(value, bit, distance):
    other = swap(value, "ctx", distance)
    return jnp.where(
        bit == 0,
        jnp.concatenate([value, other], axis=0),
        jnp.concatenate([other, value], axis=0),
    )


def pairwise(pieces):
    return (pieces[0] + pieces[1]) + (pieces[2] + pieces[3])


def swapped_if(bit, pair):
    return [jnp.where(bit == 0, pair[0], pair[1]), jnp.where(bit == 0, pair[1], pair[0])]


def per_device(
    tokens,
    clip_mask,
    cotangent,
    first_gain,
    first_shift,
    joint_weight,
    joint_bias,
    mixer_weight,
    mixer_bias,
    second_gain,
    second_shift,
    expand_weight,
    expand_bias,
    reduce_weight,
    reduce_bias,
):
    clips_here, rows_here, width = tokens.shape
    if lax.axis_size("ctx") != 4 or lax.axis_size("tp") != 2 or clips_here != 2:
        raise ValueError("mesh")
    shard = lax.axis_index("fsdp")
    block = lax.axis_index("ctx")
    core = lax.axis_index("tp")
    clip_at = block >> 1
    part_at = block & 1
    width_half = width // 2
    quarter = width_half // 2
    features = joint_weight.shape[2]
    part_width = features // 2
    pair_width = 2 * HEAD_DIM
    tokens_here = clips_here * rows_here

    flat_tokens = tokens.reshape(tokens_here, width)
    (first_normed,) = by_rows(
        first_norm_kernel, "first_norm", [LOW], False,
        flat_tokens, first_gain[None], first_shift[None],
    )
    first_normed = first_normed.reshape(clips_here, rows_here, width)
    mine = lax.dynamic_slice_in_dim(first_normed, core * width_half, width_half, 2)
    other_side = lax.dynamic_slice_in_dim(first_normed, (1 - core) * width_half, width_half, 2)
    own_clip = lax.dynamic_index_in_dim(mine, clip_at, 0, False)
    own_other = lax.dynamic_index_in_dim(other_side, clip_at, 0, False)
    other_clip = lax.dynamic_index_in_dim(mine, 1 - clip_at, 0, False)
    joint_part = lax.dynamic_slice_in_dim(joint_weight, part_at * part_width, part_width, 2)
    early = expand_weight.shape[1] // 2
    wide_part = jnp.concatenate(
        [expand_weight[:, :early]] + [joint_part[:, kind] for kind in range(3)] + [mixer_weight],
        axis=1,
    )

    own_clip, left, right, wide_part = fence(
        own_clip, other_clip[:, :quarter], other_clip[:, quarter:], wide_part
    )
    near_rows = swap(own_clip, "ctx", 1)
    across_left = swap(left, "ctx", 2)
    far_right = swap(right, "ctx", 3)
    wide_held = gather_near(wide_part)

    near_rows, across_left, far_right = fence(near_rows, across_left, far_right)
    passed = swap(jnp.concatenate([across_left, far_right], axis=1), "ctx", 1)
    (wide_held,) = fence(wide_held)
    held = gather_far(tuple(piece[:, early:] for piece in wide_held))

    passed, held, expand_rest = fence(passed, held, expand_weight[:, early:])
    rest_held = gather_near(expand_rest)
    cross_rows = jnp.concatenate(
        [
            near_rows,
            jnp.concatenate([across_left, passed[:, quarter:]], axis=1),
            jnp.concatenate([passed[:, :quarter], far_right], axis=1),
        ],
        axis=0,
    )
    cross_other = swap(cross_rows, "tp", 1)
    both_full = place_far(place_near(held), held)
    joint_columns = 3 * part_width
    joint_full = jnp.concatenate(
        [
            lax.dynamic_slice(both_full, (start * width_half, 0), (width_half, joint_columns))
            for start in (core, 1 - core)
        ],
        axis=0,
    )

    cross_other, joint_full, both_full, reduce_weight = fence(
        cross_other, joint_full, both_full, reduce_weight
    )
    mixer_full = both_full[:, joint_columns:]
    reduce_held = gather_near(reduce_weight)
    normed_mine = jnp.concatenate([own_clip, cross_rows], axis=0)
    normed_other = jnp.concatenate([own_other, cross_other], axis=0)
    bias_part = lax.dynamic_slice_in_dim(joint_bias, part_at * part_width, part_width, 1)
    bias_row = jnp.concatenate([bias_part[0], jnp.zeros_like(bias_part[0]), bias_part[1]])
    joint_out = joint_projection(normed_mine, normed_other, joint_full, bias_row[None])
    out_first, log_first = attention_forward(joint_out, 0)

    out_first, joint_out, mixer_full, rest_held = fence(
        out_first, joint_out, mixer_full, rest_held
    )
    first_blocks = out_first.reshape(4, rows_here, pair_width)
    arrived_first = [swap(first_blocks[d], "ctx", d) for d in (1, 2, 3)]
    out_second, log_second = attention_forward(joint_out, 1)

    far_leaves = far_of(
        tuple(
            jnp.concatenate([one[:, :early], two], axis=1)
            for one, two in zip(wide_held, rest_held)
        )
    )
    out_second, arrived_first, reduce_held, far_leaves = fence(
        out_second, arrived_first, reduce_held, far_leaves
    )
    second_blocks = out_second.reshape(4, rows_here, pair_width)
    arrived_second = [swap(second_blocks[d], "ctx", d) for d in (1, 2, 3)]
    expand_far_rows = send_far(far_leaves)

    arrived_second, expand_far_rows, reduce_held, reduce_leaves = fence(
        arrived_second, expand_far_rows, reduce_held, far_of(reduce_held)
    )
    reduce_held = reduce_held + send_far(reduce_leaves)
    expand_held = list(zip(wide_held, rest_held)) + [(rows,) for rows in expand_far_rows]
    arrived = [jnp.concatenate([first_blocks[0], second_blocks[0]], axis=1)] + [
        jnp.concatenate([one, two], axis=1) for one, two in zip(arrived_first, arrived_second)
    ]
    own_joined = jnp.concatenate(swapped_if(part_at, arrived[:2]), axis=1)
    other_joined = jnp.concatenate(swapped_if(part_at, arrived[2:]), axis=1)
    mixed_in = jnp.concatenate(swapped_if(clip_at, [own_joined, other_joined]), axis=0)
    mixer_part = product(mixed_in, mixer_full, ROW_BY_ROW).astype(LOW)
    mixer_swapped = swap(mixer_part, "tp", 1)
    mixer_row = mixer_bias[None]
    (second_normed,) = by_rows(
        second_norm_kernel, "second_norm", [LOW], False,
        flat_tokens, mixer_part, mixer_swapped, mixer_row, second_gain[None], second_shift[None],
    )
    valid = clip_mask.astype(FULL)[:, None, None]
    reduce_slope = (cotangent.astype(FULL) * valid).astype(LOW).reshape(tokens_here, width)
    reduce_bias_grad = jnp.sum(reduce_slope.astype(FULL), axis=0)

    second_normed, reduce_slope, reduce_held = fence(second_normed, reduce_slope, reduce_held)
    four = lax.axis_size("fsdp") == 4
    start = jnp.zeros((), jnp.int32)
    if four:
        rows = width // 4
        pieces_at = jnp.stack([shard, shard ^ 1, shard ^ 2, shard ^ 3, shard ^ 3]) * rows
        pieces_at = pieces_at.astype(jnp.int32) + jnp.array([0, 0, 0, 0, rows // 2], jnp.int32)
    else:
        pieces_at = start.reshape(1)
    activated, expand_slope, second_part, expand_bias_grad = feed_forward(
        second_normed, reduce_slope, expand_bias[None], expand_held, early,
        [(piece,) for piece in reduce_held], pieces_at,
    )
    expand_bias_grad = expand_bias_grad[0]

    second_swapped = swap(second_part, "tp", 1)
    place, order = (shard, (3, 2, 1, 0)) if four else (start, (0, 1, 2, 3))
    if four:
        half = width // 8
        far = grad_rows(second_normed, expand_slope, 3)
        far_top, far_low, normed_again, expand_slope = fence(
            far[:half], far[half:], second_normed, expand_slope
        )
        expand_far = (swap(far_top, "fsdp", 1), swap(far_low, "fsdp", 2))
        expand_parts = [grad_rows(normed_again, expand_slope, d) for d in (0, 1, 2)]
        expand_parts, second_swapped = fence(expand_parts, second_swapped)
    else:
        expand_far = ()
        expand_whole = product(second_normed, expand_slope, COLUMN_BY_COLUMN).astype(LOW)
    mixer_slope, first_sum_back, second_sums = by_rows(
        second_norm_back_kernel, "second_norm_back", [LOW, FULL], True,
        flat_tokens, mixer_part, mixer_swapped, mixer_row, second_gain[None],
        second_part, second_swapped, reduce_slope,
    )
    attended_slope = product(mixer_slope, mixer_full, PLAIN).astype(LOW)

    leaving = []
    for distance in range(4):
        to = block ^ distance
        corner = ((to >> 1) * rows_here, (to & 1) * part_width)
        leaving.append(lax.dynamic_slice(attended_slope, corner, (rows_here, part_width)))
    expand_near = add_far(expand_parts[1], expand_parts[2], expand_far) if four else ()
    leaving, mixer_slope, mixed_in, activated, expand_near = fence(
        leaving, mixer_slope, mixed_in, activated, expand_near
    )
    slope_blocks = [leaving[0]] + [swap(leaving[d], "ctx", d) for d in (1, 2, 3)]
    if four:
        expand_near = near_rows_out(expand_near)
    wide = (
        product(reduce_slope, activated, COLUMN_BY_COLUMN).astype(LOW),
        product(mixer_slope, mixed_in, COLUMN_BY_COLUMN).astype(LOW),
    )
    if four:
        wide_far, wide_side, wide_next = (rows_at(wide, distance) for distance in (3, 2, 1))
        far_top, far_low = wide_far[:half], wide_far[half:]
        wide_early = (wide_next[:half], wide_side[half:])
    else:
        far_top, far_low, wide_early = (), (), ()

    slope_blocks, expand_near, far_top, far_low = fence(
        slope_blocks, expand_near, far_top, far_low
    )
    if four:
        expand_sum = expand_parts[0].astype(FULL) + both(expand_near)
    else:
        expand_sum = lax.psum_scatter(
            expand_whole, "fsdp", scatter_dimension=0, tiled=True
        ).astype(FULL)
    expand_keep, expand_send = halves(expand_sum, part_at)
    slope_clip = jnp.concatenate(slope_blocks, axis=0)
    expand_send, slope_clip, far_top, far_low = fence(expand_send, slope_clip, far_top, far_low)
    wide_far = (swap(far_top, "fsdp", 1), swap(far_low, "fsdp", 2)) if four else ()
    expand_rows = (expand_keep, swap(expand_send, "ctx", 1))
    grad_first = attention_backward(joint_out, slope_clip, out_first, log_first, 0)

    grad_first, slope_clip, wide_far, expand_rows = fence(
        grad_first, slope_clip, wide_far, expand_rows
    )
    if four:
        wide_late = (
            both((wide_next[half:], wide_far[1])).astype(LOW),
            both((wide_side[:half], wide_far[0])).astype(LOW),
        )
    else:
        wide_late = ()
    expand_keep, expand_send = halves(both(expand_rows), clip_at)
    expand_send, slope_clip, wide_early, wide_late = fence(
        expand_send, slope_clip, wide_early, wide_late
    )
    if four:
        wide_early = near_rows_out(wide_early)
    expand_rows = (expand_keep, swap(expand_send, "ctx", 2))
    grad_second = attention_backward(joint_out, slope_clip, out_second, log_second, 1)

    grad_second, expand_rows, wide_early, wide_late = fence(
        grad_second, expand_rows, wide_early, wide_late
    )
    if four:
        wide_late = near_rows_out(wide_late)
    expand_rows = join_rows(both(expand_rows).astype(LOW), clip_at, 2)
    joint_slope = jnp.concatenate(
        [grad[kind] for kind in range(3) for grad in (grad_first, grad_second)], axis=1
    )
    first_there = product(joint_slope, joint_full[width_half:], ROW_BY_ROW).astype(LOW)
    first_here = rows_product(joint_slope, joint_full[:width_half], "first_slope")
    first_half = both((first_here, swap(first_there, "tp", 1))).astype(LOW)

    if not four:
        wide_near = lax.psum_scatter(
            jnp.concatenate(wide, axis=1), "fsdp", scatter_dimension=0, tiled=True
        )
    first_half, joint_slope = fence(first_half, joint_slope)
    pieces = first_half.reshape(4, rows_here, width_half)
    passing = jnp.concatenate([pieces[1], pieces[3][:, :quarter], pieces[2][:, quarter:]], axis=1)
    passing = swap(passing, "ctx", 1)
    place = (shard if four else start) ^ (2 * core)
    joint_parts = grad_products([normed_mine, normed_other], joint_slope, place, order, "joint_grad")
    slope_sums = jnp.sum(joint_slope.astype(FULL), axis=0)
    bias_sums = jnp.stack([slope_sums[:part_width], slope_sums[2 * part_width :]])
    joint_bias_grad = lax.dynamic_update_slice(
        jnp.zeros((2, features), FULL), bias_sums, (0, part_at * part_width)
    )

    joint_far = far_halves(joint_parts[0]) if four else ()
    passing, joint_far, wide_late, expand_rows = fence(
        passing, joint_far, wide_late, expand_rows
    )
    if four:
        near_sum = [both((wide_early[0], wide_late[1])), both((wide_late[0], wide_early[1]))]
        wide_sum = rows_at(wide, 0).astype(FULL) + jnp.concatenate(near_sum, axis=0)
    else:
        wide_sum = wide_near.astype(FULL)
    wide_keep, wide_send = halves(wide_sum, part_at)
    own_half = both((pieces[0], passing[:, :width_half])).astype(LOW)
    to_left = both((pieces[2][:, :quarter], passing[:, width_half : width_half + quarter]))
    to_right = both((pieces[3][:, quarter:], passing[:, width_half + quarter :]))
    joint_near = add_far(joint_parts[2], joint_parts[1], joint_far) if four else ()
    to_left, to_right, own_half, wide_send, joint_near, activated = fence(
        to_left.astype(LOW), to_right.astype(LOW), own_half, wide_send, joint_near, activated
    )
    other_half = jnp.concatenate([swap(to_left, "ctx", 2), swap(to_right, "ctx", 3)], axis=1)
    wide_rows = (wide_keep, swap(wide_send, "ctx", 1))
    if four:
        joint_near = near_rows_out(joint_near)
    else:
        joint_near = lax.psum_scatter(
            joint_parts.reshape(width, -1), "fsdp", scatter_dimension=0, tiled=True
        )
    reduce_part = reduce_output(activated, reduce_held, pieces_at)

    other_half, joint_near, wide_rows, reduce_part = fence(
        other_half, joint_near, wide_rows, reduce_part
    )
    slope_half = jnp.concatenate(swapped_if(clip_at, [own_half, other_half]), axis=0)
    slope_other = swap(slope_half, "tp", 1)
    slope_other, expand_rows = fence(slope_other, expand_rows)
    expand_grad = join_rows(expand_rows, part_at, 1).astype(FULL)
    first_slope = jnp.concatenate(swapped_if(core, [slope_half, slope_other]), axis=1)
    wide_rows = split_rows(both(wide_rows), clip_at, 2)
    reduce_swapped = swap(reduce_part, "tp", 1)
    joint_sum = joint_parts[3].astype(FULL) + both(joint_near) if four else joint_near
    joint_sum = joint_sum.astype(LOW)
    joint_sum = (joint_sum, swap(joint_sum, "ctx", 2))
    tokens_grad, first_sums = by_rows(
        first_norm_back_kernel, "first_norm_back", [FULL], True,
        flat_tokens, first_slope, first_gain[None],
        cotangent.reshape(tokens_here, width), first_sum_back,
    )
    first_sums, tokens_grad, reduce_swapped = fence(first_sums, tokens_grad, reduce_swapped)
    vectors = [
        first_sums[0],
        first_sums[1],
        joint_bias_grad[0],
        joint_bias_grad[1],
        second_sums[2],
        second_sums[0],
        second_sums[1],
        expand_bias_grad,
        reduce_bias_grad,
    ]
    packed = jnp.concatenate(vectors).reshape(-1, 128)
    packed_pieces = [packed] + [swap(packed, "ctx", d) for d in (1, 2, 3)]
    reduce_out = both((reduce_part, reduce_swapped)) + reduce_bias
    mixer_out = both((mixer_part, mixer_swapped)) + mixer_bias
    branches = (mixer_out + reduce_out).reshape(clips_here, rows_here, width)
    result = (tokens.astype(FULL) + valid * branches).astype(LOW)

    packed_pieces, joint_sum, wide_rows, result = fence(
        packed_pieces, joint_sum, wide_rows, result
    )
    packed = pairwise(packed_pieces)
    if four:
        packed = pairwise([packed] + [swap(packed, "fsdp", d) for d in (1, 2, 3)])
    else:
        packed = lax.psum(packed, "fsdp")
    joint_sum = both(joint_sum).astype(LOW)
    joint_parts = swapped_if(part_at, [joint_sum, swap(joint_sum, "ctx", 1)])
    joint_grad = jnp.concatenate(
        [piece.reshape(-1, 3, part_width) for piece in joint_parts], axis=2
    ).astype(FULL)
    wide_rows = join_rows(both(wide_rows).astype(LOW), clip_at, 2)
    wide_other = swap(wide_rows, "ctx", 1)
    reduce_grad, mixer_grad = (
        jnp.concatenate(
            swapped_if(part_at, [wide_rows[:, columns], wide_other[:, columns]]), axis=0
        ).astype(FULL)
        for columns in (slice(None, activated.shape[1]), slice(activated.shape[1], None))
    )
    packed = packed.reshape(-1)
    shares = []
    start = 0
    for vector in vectors:
        share = vector.shape[0] // lax.axis_size("fsdp")
        shares.append(lax.dynamic_slice_in_dim(packed, start + shard * share, share, 0))
        start += vector.shape[0]

    shape = (clips_here, rows_here, width)
    return (
        result,
        tokens_grad.reshape(shape),
        shares[0],
        shares[1],
        joint_grad,
        jnp.stack([shares[2], shares[3]]),
        mixer_grad,
        shares[4],
        shares[5],
        shares[6],
        expand_grad,
        shares[7],
        reduce_grad,
        shares[8],
    )


def solution(mesh):
    return jax.shard_map(
        per_device,
        mesh=mesh,
        in_specs=(
            P("fsdp", "ctx", None),
            P("fsdp"),
            P("fsdp", "ctx", None),
            P(),
            P(),
            P("fsdp", None, "tp"),
            P(None, "tp"),
            P("fsdp", "tp"),
            P(),
            P(),
            P(),
            P("fsdp", "tp"),
            P("tp"),
            P("fsdp", "tp"),
            P(),
        ),
        out_specs=(
            P("fsdp", "ctx", None),
            P("fsdp", "ctx", None),
            P("fsdp"),
            P("fsdp"),
            P("fsdp", None, "tp"),
            P(None, ("tp", "fsdp")),
            P("fsdp", "tp"),
            P("fsdp"),
            P("fsdp"),
            P("fsdp"),
            P("fsdp", "tp"),
            P(("tp", "fsdp")),
            P("fsdp", "tp"),
            P("fsdp"),
        ),
        check_vma=False,
    )
```

```python
import jax
import jax.numpy as jnp
from jax import lax
from jax.experimental import pallas as pl
from jax.experimental.pallas import tpu as pltpu
from jax.sharding import PartitionSpec as P

HEAD_DIM = 64
EPSILON = 1e-06
LOW = jnp.bfloat16
FULL = jnp.float32

ROW_BY_ROW = (((1,), (1,)), ((), ()))
PLAIN = (((1,), (0,)), ((), ()))
COLUMN_BY_COLUMN = (((0,), (0,)), ((), ()))


def product(left, right, dims):
    return lax.dot_general(left, right, dims, preferred_element_type=FULL)


def normalize(value_rows):
    center = value_rows - jnp.mean(value_rows, axis=-1, keepdims=True)
    inverse = lax.rsqrt(jnp.mean(center * center, axis=-1, keepdims=True) + EPSILON)
    return (center * inverse, inverse)


def norm_back(upstream, gain, scaled, inverse):
    weighted = upstream * gain
    return inverse * (
        weighted
        - jnp.mean(weighted, axis=-1, keepdims=True)
        - scaled * jnp.mean(weighted * scaled, axis=-1, keepdims=True)
    )


def row_chunk(count, most):
    for chunk in range(most, 0, -16):
        if count % chunk == 0:
            return chunk
    raise ValueError("rows")


def first_norm_kernel(tokens_ref, gain_ref, shift_ref, out_ref):
    scaled, _ = normalize(tokens_ref[...].astype(FULL))
    out_ref[...] = (scaled * gain_ref[...] + shift_ref[...]).astype(LOW)


def second_norm_kernel(tokens_ref, one_ref, two_ref, bias_ref, gain_ref, shift_ref, out_ref):
    mixed = one_ref[...].astype(FULL) + two_ref[...].astype(FULL) + bias_ref[...]
    scaled, _ = normalize(tokens_ref[...].astype(FULL) + mixed)
    out_ref[...] = (scaled * gain_ref[...] + shift_ref[...]).astype(LOW)


def add_sums(ref, rows):
    sums = jnp.concatenate([jnp.sum(row, axis=0, keepdims=True) for row in rows], axis=0)

    @pl.when(pl.program_id(0) == 0)
    def _():
        ref[: len(rows)] = sums

    @pl.when(pl.program_id(0) > 0)
    def _():
        ref[: len(rows)] += sums


def second_norm_back_kernel(
    tokens_ref, one_ref, two_ref, bias_ref, gain_ref, left_ref, right_ref, outer_ref,
    slope_ref, back_ref, sums_ref,
):
    mixed = one_ref[...].astype(FULL) + two_ref[...].astype(FULL) + bias_ref[...]
    scaled, inverse = normalize(tokens_ref[...].astype(FULL) + mixed)
    upstream = left_ref[...].astype(FULL) + right_ref[...].astype(FULL)
    back = norm_back(upstream, gain_ref[...], scaled, inverse)
    slope = (outer_ref[...].astype(FULL) + back).astype(LOW)
    slope_ref[...] = slope
    back_ref[...] = back
    add_sums(sums_ref, [upstream * scaled, upstream, slope.astype(FULL)])


def first_norm_back_kernel(
    tokens_ref, upstream_ref, gain_ref, outer_ref, back_ref, out_ref, sums_ref
):
    scaled, inverse = normalize(tokens_ref[...].astype(FULL))
    upstream = upstream_ref[...].astype(FULL)
    back = norm_back(upstream, gain_ref[...], scaled, inverse)
    out_ref[...] = outer_ref[...].astype(FULL) + back_ref[...] + back
    add_sums(sums_ref, [upstream * scaled, upstream])


def by_rows(kernel, name, out_types, sums, *values):
    count, width = values[0].shape
    chunk = count // 2 if count % 16 == 0 else count
    part = pl.BlockSpec((chunk, width), lambda i: (i, 0))
    in_specs = [
        part if value.shape[0] == count else pl.BlockSpec((1, width), lambda i: (0, 0))
        for value in values
    ]
    out_specs = [part for _ in out_types]
    out_shape = [jax.ShapeDtypeStruct((count, width), kind) for kind in out_types]
    if sums:
        out_specs.append(pl.BlockSpec((8, width), lambda i: (0, 0)))
        out_shape.append(jax.ShapeDtypeStruct((8, width), FULL))
    return pl.pallas_call(
        kernel,
        grid=(count // chunk,),
        in_specs=in_specs,
        out_specs=out_specs,
        out_shape=out_shape,
        compiler_params=pltpu.CompilerParams(vmem_limit_bytes=40 << 20),
        name=name,
    )(*values)


def joint_kernel(mine_ref, other_ref, weight_ref, bias_ref, out_ref):
    half = mine_ref.shape[1]
    out = product(mine_ref[...], weight_ref[:half], PLAIN)
    out += product(other_ref[...], weight_ref[half:], PLAIN)
    out_ref[...] = (out + bias_ref[...]).astype(LOW)


def joint_projection(mine, other, weight, bias):
    count, half = mine.shape
    columns = weight.shape[1]
    chunk = row_chunk(count, 784)
    part = pl.BlockSpec((chunk, half), lambda i: (i, 0))
    return pl.pallas_call(
        joint_kernel,
        grid=(count // chunk,),
        in_specs=[
            part,
            part,
            pl.BlockSpec(weight.shape, lambda i: (0, 0)),
            pl.BlockSpec((1, columns), lambda i: (0, 0)),
        ],
        out_specs=pl.BlockSpec((chunk, columns), lambda i: (i, 0)),
        out_shape=jax.ShapeDtypeStruct((count, columns), LOW),
        compiler_params=pltpu.CompilerParams(vmem_limit_bytes=40 << 20),
        name="joint_projection",
    )(mine, other, weight, bias)


def rows_kernel(left_ref, right_ref, out_ref):
    out_ref[...] = product(left_ref[...], right_ref[...], ROW_BY_ROW).astype(LOW)


def rows_product(left, right, name):
    count, depth = left.shape
    columns = right.shape[0]
    chunk = row_chunk(count, 400)
    return pl.pallas_call(
        rows_kernel,
        grid=(count // chunk,),
        in_specs=[
            pl.BlockSpec((chunk, depth), lambda i: (i, 0)),
            pl.BlockSpec((columns, depth), lambda i: (0, 0)),
        ],
        out_specs=pl.BlockSpec((chunk, columns), lambda i: (i, 0)),
        out_shape=jax.ShapeDtypeStruct((count, columns), LOW),
        compiler_params=pltpu.CompilerParams(vmem_limit_bytes=48 << 20),
        name=name,
    )(left, right)


def grad_kernel(distances, place_ref, *refs):
    lefts, (right_ref, out_ref) = refs[:-2], refs[-2:]
    left = lefts[0][...]
    if len(lefts) == 2:
        slot = place_ref[0] ^ distance_at(distances, pl.program_id(0))
        left = jnp.where((slot >> 1) == 0, left, lefts[1][...])
    out_ref[0] = product(left, right_ref[...], COLUMN_BY_COLUMN).astype(LOW)


def distance_at(distances, step):
    if len(distances) == 1:
        return distances[0]
    return distances[0] + step * (distances[1] - distances[0])


def grad_products(lefts, right, place, distances, name):
    tokens_here, columns = right.shape
    quarter = sum(left.shape[1] for left in lefts) // 4
    blocks = lefts[0].shape[1] // quarter

    def left_at(i, place):
        return (0, (place[0] ^ distance_at(distances, i)) & (blocks - 1))

    return pl.pallas_call(
        lambda *refs: grad_kernel(distances, *refs),
        grid_spec=pltpu.PrefetchScalarGridSpec(
            num_scalar_prefetch=1,
            grid=(len(distances),),
            in_specs=[pl.BlockSpec((tokens_here, quarter), left_at) for _ in lefts]
            + [pl.BlockSpec((tokens_here, columns), lambda i, place: (0, 0))],
            out_specs=pl.BlockSpec((1, quarter, columns), lambda i, place: (i, 0, 0)),
        ),
        out_shape=jax.ShapeDtypeStruct((len(distances), quarter, columns), LOW),
        compiler_params=pltpu.CompilerParams(vmem_limit_bytes=48 << 20),
        name=name,
    )(place.astype(jnp.int32).reshape(1), *lefts, right)


def attention_forward_kernel(q_ref, k_ref, v_ref, o_ref, lse_ref):
    count, width = q_ref.shape
    rows = row_chunk(count, 256)
    lane = lax.broadcasted_iota(jnp.int32, (rows, width), 1)
    k = k_ref[...]
    v = v_ref[...]
    units = [(start, head) for start in range(0, count, rows) for head in range(width // HEAD_DIM)]

    def scores_of(unit):
        start, head = unit
        q = q_ref[start : start + rows] * jnp.asarray(HEAD_DIM ** (-0.5), LOW)
        return product(jnp.where((lane // HEAD_DIM) == head, q, jnp.zeros_like(q)), k, ROW_BY_ROW)

    logs = []
    ahead = scores_of(units[0])
    for step, (start, head) in enumerate(units):
        scores = ahead
        if step + 1 < len(units):
            ahead = scores_of(units[step + 1])
        top = jnp.max(scores, axis=-1, keepdims=True)
        weights = jnp.exp(scores - top)
        total = jnp.sum(weights, axis=-1, keepdims=True)
        part = product(weights.astype(LOW), v, PLAIN) / total
        if head == 0:
            out = part
            logs.append(jnp.zeros((rows, width), FULL))
        else:
            out = jnp.where((lane // HEAD_DIM) == head, part, out)
            o_ref[start : start + rows] = out.astype(LOW)
        logs[-1] = jnp.where(lane == head, top + jnp.log(total), logs[-1])
    lse_ref[...] = jnp.concatenate(logs, axis=0).T[: lse_ref.shape[0]]


def attention_forward(joint, pair):
    count, columns = joint.shape
    width = 2 * HEAD_DIM
    kind = columns // (3 * width)
    return pl.pallas_call(
        attention_forward_kernel,
        grid=(1,),
        in_specs=[
            pl.BlockSpec((count, width), lambda i: (0, pair)),
            pl.BlockSpec((count, width), lambda i: (0, kind + pair)),
            pl.BlockSpec((count, width), lambda i: (0, 2 * kind + pair)),
        ],
        out_specs=[
            pl.BlockSpec((count, width), lambda i: (0, 0)),
            pl.BlockSpec((8, count), lambda i: (0, 0)),
        ],
        out_shape=[
            jax.ShapeDtypeStruct((count, width), LOW),
            jax.ShapeDtypeStruct((8, count), FULL),
        ],
        compiler_params=pltpu.CompilerParams(vmem_limit_bytes=48 << 20),
        name="attention_forward",
    )(joint, joint, joint)


def attention_backward_kernel(
    q_ref, k_ref, v_ref, da_ref, o_ref, lse_ref, dq_ref, dk_ref, dv_ref,
    q_heads, da_heads, delta_ref, dq_total,
):
    count, width = q_ref.shape
    rows = row_chunk(count, 256)
    heads = width // HEAD_DIM
    scale = jnp.asarray(HEAD_DIM ** (-0.5), LOW)

    lane = lax.broadcasted_iota(jnp.int32, (count, width), 1)
    delta = jnp.zeros((count, width), FULL)
    q = q_ref[...] * scale
    da = da_ref[...]
    both_rows = da.astype(FULL) * o_ref[...].astype(FULL)
    for head in range(heads):
        mask = (lane // HEAD_DIM) == head
        q_heads[head] = jnp.where(mask, q, jnp.zeros_like(q))
        da_heads[head] = jnp.where(mask, da, jnp.zeros_like(da))
        row = jnp.sum(jnp.where(mask, both_rows, 0.0), axis=-1, keepdims=True)
        delta = jnp.where(lane == head, row, delta)
    delta_ref[...] = delta.T[:8]
    dq_total[...] = jnp.zeros_like(dq_total)

    lane = lax.broadcasted_iota(jnp.int32, (rows, width), 1)
    for start in range(0, count, rows):
        k = k_ref[start : start + rows]
        v = v_ref[start : start + rows]
        scaled_k = k * scale
        dk = dv = None
        for head in range(heads):
            q = q_heads[head]
            da = da_heads[head]
            probs = jnp.exp(product(k, q, ROW_BY_ROW) - lse_ref[head : head + 1, :])
            slope = probs * (product(v, da, ROW_BY_ROW) - delta_ref[head : head + 1, :])
            slope = slope.astype(LOW)
            dv_part = product(probs.astype(LOW), da, PLAIN)
            dk_part = product(slope, q, PLAIN)
            dv = dv_part if dv is None else dv + dv_part
            dk = dk_part if dk is None else dk + dk_part
            one_k = jnp.where((lane // HEAD_DIM) == head, scaled_k, jnp.zeros_like(k))
            dq_total[...] += product(slope, one_k, COLUMN_BY_COLUMN)
        dk_ref[start : start + rows] = dk.astype(LOW)
        dv_ref[start : start + rows] = dv.astype(LOW)
    dq_ref[...] = dq_total[...].astype(LOW)


def attention_backward(joint, da, out, lse, pair):
    count, columns = joint.shape
    width = 2 * HEAD_DIM
    kind = columns // (3 * width)
    alone = pl.BlockSpec((count, width), lambda i: (0, 0))
    grad = jax.ShapeDtypeStruct((count, width), LOW)
    return pl.pallas_call(
        attention_backward_kernel,
        grid=(1,),
        in_specs=[
            pl.BlockSpec((count, width), lambda i: (0, pair)),
            pl.BlockSpec((count, width), lambda i: (0, kind + pair)),
            pl.BlockSpec((count, width), lambda i: (0, 2 * kind + pair)),
            pl.BlockSpec((count, width), lambda i: (0, pair)),
            alone,
            pl.BlockSpec((8, count), lambda i: (0, 0)),
        ],
        out_specs=[alone, alone, alone],
        out_shape=[grad, grad, grad],
        scratch_shapes=[
            pltpu.VMEM((2, count, width), LOW),
            pltpu.VMEM((2, count, width), LOW),
            pltpu.VMEM((8, count), FULL),
            pltpu.VMEM((count, width), FULL),
        ],
        compiler_params=pltpu.CompilerParams(vmem_limit_bytes=48 << 20),
        name="attention_backward",
    )(joint, joint, joint, da, out, lse)


def put_together(place_ref, whole_ref, pieces, edge=0):
    for piece, refs in enumerate(pieces):
        rows = refs[0].shape[0]
        place = pl.ds(pl.multiple_of(place_ref[piece], rows), rows)
        if len(refs) == 1:
            whole_ref[place, :] = refs[0][...]
            continue

        @pl.when(pl.program_id(0) < edge)
        def _():
            whole_ref[place, :] = refs[0][...]

        @pl.when(pl.program_id(0) >= edge)
        def _():
            whole_ref[place, :] = refs[1][...]


def nested(refs, like):
    refs = iter(refs)
    return [tuple(next(refs) for _ in piece) for piece in like]


def feed_forward_kernel(
    expand, reduce, edge, place_ref, normed_ref, slope_ref, bias_ref, *refs
):
    active_ref, expand_slope_ref, back_ref, bias_grad_ref, total, expand_ref, reduce_ref = refs[-7:]
    arrays = sum(len(piece) for piece in expand)
    put_together(place_ref, expand_ref, nested(refs[:arrays], expand), edge)
    put_together(place_ref, reduce_ref, nested(refs[arrays:-7], reduce))
    step = pl.program_id(0)
    count = normed_ref.shape[0]
    half = count // 2
    bias_grad = None
    for rows in (slice(0, half), slice(half, count)):
        hidden = product(normed_ref[rows], expand_ref[...], PLAIN) + bias_ref[...]
        upstream = product(slope_ref[rows], reduce_ref[...], PLAIN)
        share = 0.5 * (1.0 + lax.erf(hidden * (0.5**0.5)))
        active_ref[rows] = (hidden * share).astype(LOW)
        density = jnp.exp(-0.5 * hidden * hidden) * 0.3989422804014327
        slope = (upstream * (share + hidden * density)).astype(LOW)
        expand_slope_ref[rows] = slope
        part = jnp.sum(slope.astype(FULL), axis=0, keepdims=True)
        bias_grad = part if bias_grad is None else bias_grad + part
        back = product(slope, expand_ref[...], ROW_BY_ROW)

        @pl.when(step == 0)
        def _():
            total[rows] = back

        @pl.when(step > 0)
        def _():
            total[rows] += back

    bias_grad_ref[...] = bias_grad

    @pl.when(step == pl.num_programs(0) - 1)
    def _():
        back_ref[...] = total[...].astype(LOW)


def feed_forward(normed, slope, bias, expand, early, reduce, place):
    count, width = normed.shape
    hidden = bias.shape[1]
    block = 512
    edge = early // block
    whole = pl.BlockSpec((count, width), lambda i, place: (0, 0))
    out = pl.BlockSpec((count, block), lambda i, place: (0, i))
    row = pl.BlockSpec((1, block), lambda i, place: (0, i))
    specs = []
    arrays = []
    for piece in [*expand, *reduce]:
        shape = (piece[0].shape[0], block)
        arrays += piece
        if len(piece) == 1:
            specs.append(pl.BlockSpec(shape, lambda i, place: (0, i)))
        else:
            specs.append(pl.BlockSpec(shape, lambda i, place: (0, jnp.minimum(i, edge - 1))))
            specs.append(pl.BlockSpec(shape, lambda i, place: (0, jnp.maximum(i - edge, 0))))
    return pl.pallas_call(
        lambda *refs: feed_forward_kernel(expand, reduce, edge, *refs),
        grid_spec=pltpu.PrefetchScalarGridSpec(
            num_scalar_prefetch=1,
            grid=(hidden // block,),
            in_specs=[whole, whole, row] + specs,
            out_specs=[out, out, whole, row],
            scratch_shapes=[
                pltpu.VMEM((count, width), FULL),
                pltpu.VMEM((width, block), LOW),
                pltpu.VMEM((width, block), LOW),
            ],
        ),
        out_shape=[
            jax.ShapeDtypeStruct((count, hidden), LOW),
            jax.ShapeDtypeStruct((count, hidden), LOW),
            jax.ShapeDtypeStruct((count, width), LOW),
            jax.ShapeDtypeStruct((1, hidden), FULL),
        ],
        compiler_params=pltpu.CompilerParams(vmem_limit_bytes=44 << 20),
        name="feed_forward",
    )(place, normed, slope, bias, *arrays)


def reduce_kernel(place_ref, active_ref, *refs):
    out_ref, total, reduce_ref = refs[-3:]
    put_together(place_ref, reduce_ref, [(ref,) for ref in refs[:-3]])
    part = product(active_ref[...], reduce_ref[...], ROW_BY_ROW)

    @pl.when(pl.program_id(0) == 0)
    def _():
        total[...] = part

    @pl.when(pl.program_id(0) > 0)
    def _():
        total[...] += part

    @pl.when(pl.program_id(0) == pl.num_programs(0) - 1)
    def _():
        out_ref[...] = total[...].astype(LOW)


def reduce_output(active, reduce, place):
    count, hidden = active.shape
    width = sum(piece.shape[0] for piece in reduce)
    block = 512 if hidden % 512 == 0 else hidden
    return pl.pallas_call(
        reduce_kernel,
        grid_spec=pltpu.PrefetchScalarGridSpec(
            num_scalar_prefetch=1,
            grid=(hidden // block,),
            in_specs=[pl.BlockSpec((count, block), lambda i, place: (0, i))]
            + [
                pl.BlockSpec((piece.shape[0], block), lambda i, place: (0, i)) for piece in reduce
            ],
            out_specs=pl.BlockSpec((count, width), lambda i, place: (0, 0)),
            scratch_shapes=[pltpu.VMEM((count, width), FULL), pltpu.VMEM((width, block), LOW)],
        ),
        out_shape=jax.ShapeDtypeStruct((count, width), LOW),
        compiler_params=pltpu.CompilerParams(vmem_limit_bytes=32 << 20),
        name="reduce_output",
    )(place, active, *reduce)


def swap(value, axis, distance):
    size = lax.axis_size(axis)
    return lax.ppermute(value, axis, [(i, i ^ distance) for i in range(size)])


def fence(*values):
    return lax.optimization_barrier(values)


def gather_near(rows_here):
    if lax.axis_size("fsdp") != 4:
        return (lax.all_gather(rows_here, "fsdp", axis=0, tiled=True),)
    return (rows_here, swap(rows_here, "fsdp", 1), swap(rows_here, "fsdp", 2))


def far_of(held):
    if len(held) == 1:
        return ()
    half = held[0].shape[0] // 2
    return (held[2][:half], held[1][half:])


def send_far(leaves):
    return (swap(leaves[0], "fsdp", 1), swap(leaves[1], "fsdp", 2)) if leaves else ()


def far_of(held):
    if len(held) == 1:
        return ()
    half = held[0].shape[0] // 2
    return (held[2][:half], held[1][half:])


def send_far(leaves):
    return (swap(leaves[0], "fsdp", 1), swap(leaves[1], "fsdp", 2)) if leaves else ()


def gather_far(held):
    return held + send_far(far_of(held))


def place_near(held):
    if len(held) == 1:
        return held[0]
    rows_here, near, side = held[:3]
    me = lax.axis_index("fsdp")
    count, width = rows_here.shape
    out = jnp.zeros((4 * count, width), rows_here.dtype)
    out = lax.dynamic_update_slice(out, rows_here, (me * count, 0))
    out = lax.dynamic_update_slice(out, near, ((me ^ 1) * count, 0))
    return lax.dynamic_update_slice(out, side, ((me ^ 2) * count, 0))


def place_far(out, held):
    if len(held) == 1:
        return out
    far_top, far_low = held[3:]
    half = far_top.shape[0]
    start = (lax.axis_index("fsdp") ^ 3) * 2 * half
    out = lax.dynamic_update_slice(out, far_top, (start, 0))
    return lax.dynamic_update_slice(out, far_low, (start + half, 0))


def grad_rows(left, right, distance):
    count = left.shape[1] // 4
    start = (lax.axis_index("fsdp") ^ distance) * count
    piece = lax.dynamic_slice_in_dim(left, start, count, 1)
    return product(piece, right, COLUMN_BY_COLUMN).astype(LOW)


def rows_at(matrices, distance):
    parts = []
    for matrix in matrices:
        count = matrix.shape[0] // 4
        start = (lax.axis_index("fsdp") ^ distance) * count
        parts.append(lax.dynamic_slice_in_dim(matrix, start, count, 0))
    return parts[0] if len(parts) == 1 else jnp.concatenate(parts, axis=1)


def far_halves(far):
    half = far.shape[0] // 2
    return (swap(far[:half], "fsdp", 1), swap(far[half:], "fsdp", 2))


def add_far(near, side, far):
    half = near.shape[0] // 2
    near = jnp.concatenate([near[:half], both((near[half:], far[1])).astype(LOW)], axis=0)
    side = jnp.concatenate([both((side[:half], far[0])).astype(LOW), side[half:]], axis=0)
    return (near, side)


def near_rows_out(pair):
    return (swap(pair[0], "fsdp", 1), swap(pair[1], "fsdp", 2))


def halves(value, bit):
    half = value.shape[0] // 2
    keep = lax.dynamic_slice_in_dim(value, bit * half, half, 0)
    send = lax.dynamic_slice_in_dim(value, (1 - bit) * half, half, 0)
    return keep, send.astype(LOW)


def split_rows(value, bit, distance):
    keep, send = halves(value, bit)
    return keep, swap(send, "ctx", distance)


def both(pair):
    return pair[0].astype(FULL) + pair[1].astype(FULL)


def join_rows(value, bit, distance):
    other = swap(value, "ctx", distance)
    return jnp.where(
        bit == 0,
        jnp.concatenate([value, other], axis=0),
        jnp.concatenate([other, value], axis=0),
    )


def pairwise(pieces):
    return (pieces[0] + pieces[1]) + (pieces[2] + pieces[3])


def swapped_if(bit, pair):
    return [jnp.where(bit == 0, pair[0], pair[1]), jnp.where(bit == 0, pair[1], pair[0])]


def per_device(
    tokens,
    clip_mask,
    cotangent,
    first_gain,
    first_shift,
    joint_weight,
    joint_bias,
    mixer_weight,
    mixer_bias,
    second_gain,
    second_shift,
    expand_weight,
    expand_bias,
    reduce_weight,
    reduce_bias,
):
    clips_here, rows_here, width = tokens.shape
    if lax.axis_size("ctx") != 4 or lax.axis_size("tp") != 2 or clips_here != 2:
        raise ValueError("mesh")
    shard = lax.axis_index("fsdp")
    block = lax.axis_index("ctx")
    core = lax.axis_index("tp")
    clip_at = block >> 1
    part_at = block & 1
    width_half = width // 2
    quarter = width_half // 2
    features = joint_weight.shape[2]
    part_width = features // 2
    pair_width = 2 * HEAD_DIM
    tokens_here = clips_here * rows_here

    flat_tokens = tokens.reshape(tokens_here, width)
    (first_normed,) = by_rows(
        first_norm_kernel, "first_norm", [LOW], False,
        flat_tokens, first_gain[None], first_shift[None],
    )
    first_normed = first_normed.reshape(clips_here, rows_here, width)
    mine = lax.dynamic_slice_in_dim(first_normed, core * width_half, width_half, 2)
    other_side = lax.dynamic_slice_in_dim(first_normed, (1 - core) * width_half, width_half, 2)
    own_clip = lax.dynamic_index_in_dim(mine, clip_at, 0, False)
    own_other = lax.dynamic_index_in_dim(other_side, clip_at, 0, False)
    other_clip = lax.dynamic_index_in_dim(mine, 1 - clip_at, 0, False)
    joint_part = lax.dynamic_slice_in_dim(joint_weight, part_at * part_width, part_width, 2)
    early = expand_weight.shape[1] // 2
    wide_part = jnp.concatenate(
        [expand_weight[:, :early]] + [joint_part[:, kind] for kind in range(3)] + [mixer_weight],
        axis=1,
    )

    own_clip, left, right, wide_part = fence(
        own_clip, other_clip[:, :quarter], other_clip[:, quarter:], wide_part
    )
    near_rows = swap(own_clip, "ctx", 1)
    across_left = swap(left, "ctx", 2)
    far_right = swap(right, "ctx", 3)
    wide_held = gather_near(wide_part)

    near_rows, across_left, far_right = fence(near_rows, across_left, far_right)
    passed = swap(jnp.concatenate([across_left, far_right], axis=1), "ctx", 1)
    (wide_held,) = fence(wide_held)
    held = gather_far(tuple(piece[:, early:] for piece in wide_held))

    passed, held, expand_rest = fence(passed, held, expand_weight[:, early:])
    rest_held = gather_near(expand_rest)
    cross_rows = jnp.concatenate(
        [
            near_rows,
            jnp.concatenate([across_left, passed[:, quarter:]], axis=1),
            jnp.concatenate([passed[:, :quarter], far_right], axis=1),
        ],
        axis=0,
    )
    cross_other = swap(cross_rows, "tp", 1)
    both_full = place_far(place_near(held), held)
    joint_columns = 3 * part_width
    joint_full = jnp.concatenate(
        [
            lax.dynamic_slice(both_full, (start * width_half, 0), (width_half, joint_columns))
            for start in (core, 1 - core)
        ],
        axis=0,
    )

    cross_other, joint_full, both_full, reduce_weight = fence(
        cross_other, joint_full, both_full, reduce_weight
    )
    mixer_full = both_full[:, joint_columns:]
    reduce_held = gather_near(reduce_weight)
    normed_mine = jnp.concatenate([own_clip, cross_rows], axis=0)
    normed_other = jnp.concatenate([own_other, cross_other], axis=0)
    bias_part = lax.dynamic_slice_in_dim(joint_bias, part_at * part_width, part_width, 1)
    bias_row = jnp.concatenate([bias_part[0], jnp.zeros_like(bias_part[0]), bias_part[1]])
    joint_out = joint_projection(normed_mine, normed_other, joint_full, bias_row[None])
    out_first, log_first = attention_forward(joint_out, 0)

    out_first, joint_out, mixer_full, rest_held = fence(
        out_first, joint_out, mixer_full, rest_held
    )
    first_blocks = out_first.reshape(4, rows_here, pair_width)
    arrived_first = [swap(first_blocks[d], "ctx", d) for d in (1, 2, 3)]
    out_second, log_second = attention_forward(joint_out, 1)

    far_leaves = far_of(
        tuple(
            jnp.concatenate([one[:, :early], two], axis=1)
            for one, two in zip(wide_held, rest_held)
        )
    )
    out_second, arrived_first, reduce_held, far_leaves = fence(
        out_second, arrived_first, reduce_held, far_leaves
    )
    second_blocks = out_second.reshape(4, rows_here, pair_width)
    arrived_second = [swap(second_blocks[d], "ctx", d) for d in (1, 2, 3)]
    expand_far_rows = send_far(far_leaves)

    arrived_second, expand_far_rows, reduce_held, reduce_leaves = fence(
        arrived_second, expand_far_rows, reduce_held, far_of(reduce_held)
    )
    reduce_held = reduce_held + send_far(reduce_leaves)
    expand_held = list(zip(wide_held, rest_held)) + [(rows,) for rows in expand_far_rows]
    arrived = [jnp.concatenate([first_blocks[0], second_blocks[0]], axis=1)] + [
        jnp.concatenate([one, two], axis=1) for one, two in zip(arrived_first, arrived_second)
    ]
    own_joined = jnp.concatenate(swapped_if(part_at, arrived[:2]), axis=1)
    other_joined = jnp.concatenate(swapped_if(part_at, arrived[2:]), axis=1)
    mixed_in = jnp.concatenate(swapped_if(clip_at, [own_joined, other_joined]), axis=0)
    mixer_part = product(mixed_in, mixer_full, ROW_BY_ROW).astype(LOW)
    mixer_swapped = swap(mixer_part, "tp", 1)
    mixer_row = mixer_bias[None]
    (second_normed,) = by_rows(
        second_norm_kernel, "second_norm", [LOW], False,
        flat_tokens, mixer_part, mixer_swapped, mixer_row, second_gain[None], second_shift[None],
    )
    valid = clip_mask.astype(FULL)[:, None, None]
    reduce_slope = (cotangent.astype(FULL) * valid).astype(LOW).reshape(tokens_here, width)
    reduce_bias_grad = jnp.sum(reduce_slope.astype(FULL), axis=0)

    second_normed, reduce_slope, reduce_held = fence(second_normed, reduce_slope, reduce_held)
    four = lax.axis_size("fsdp") == 4
    start = jnp.zeros((), jnp.int32)
    if four:
        rows = width // 4
        pieces_at = jnp.stack([shard, shard ^ 1, shard ^ 2, shard ^ 3, shard ^ 3]) * rows
        pieces_at = pieces_at.astype(jnp.int32) + jnp.array([0, 0, 0, 0, rows // 2], jnp.int32)
    else:
        pieces_at = start.reshape(1)
    activated, expand_slope, second_part, expand_bias_grad = feed_forward(
        second_normed, reduce_slope, expand_bias[None], expand_held, early,
        [(piece,) for piece in reduce_held], pieces_at,
    )
    expand_bias_grad = expand_bias_grad[0]

    second_swapped = swap(second_part, "tp", 1)
    place, order = (shard, (3, 2, 1, 0)) if four else (start, (0, 1, 2, 3))
    if four:
        half = width // 8
        far = grad_rows(second_normed, expand_slope, 3)
        far_top, far_low, normed_again, expand_slope = fence(
            far[:half], far[half:], second_normed, expand_slope
        )
        expand_far = (swap(far_top, "fsdp", 1), swap(far_low, "fsdp", 2))
        expand_parts = [grad_rows(normed_again, expand_slope, d) for d in (0, 1, 2)]
        expand_parts, second_swapped = fence(expand_parts, second_swapped)
    else:
        expand_far = ()
        expand_whole = product(second_normed, expand_slope, COLUMN_BY_COLUMN).astype(LOW)
    mixer_slope, first_sum_back, second_sums = by_rows(
        second_norm_back_kernel, "second_norm_back", [LOW, FULL], True,
        flat_tokens, mixer_part, mixer_swapped, mixer_row, second_gain[None],
        second_part, second_swapped, reduce_slope,
    )
    attended_slope = product(mixer_slope, mixer_full, PLAIN).astype(LOW)

    leaving = []
    for distance in range(4):
        to = block ^ distance
        corner = ((to >> 1) * rows_here, (to & 1) * part_width)
        leaving.append(lax.dynamic_slice(attended_slope, corner, (rows_here, part_width)))
    expand_near = add_far(expand_parts[1], expand_parts[2], expand_far) if four else ()
    leaving, mixer_slope, mixed_in, activated, expand_near = fence(
        leaving, mixer_slope, mixed_in, activated, expand_near
    )
    slope_blocks = [leaving[0]] + [swap(leaving[d], "ctx", d) for d in (1, 2, 3)]
    if four:
        expand_near = near_rows_out(expand_near)
    wide = (
        product(reduce_slope, activated, COLUMN_BY_COLUMN).astype(LOW),
        product(mixer_slope, mixed_in, COLUMN_BY_COLUMN).astype(LOW),
    )
    if four:
        wide_far, wide_side, wide_next = (rows_at(wide, distance) for distance in (3, 2, 1))
        far_top, far_low = wide_far[:half], wide_far[half:]
        wide_early = (wide_next[:half], wide_side[half:])
    else:
        far_top, far_low, wide_early = (), (), ()

    slope_blocks, expand_near, far_top, far_low = fence(
        slope_blocks, expand_near, far_top, far_low
    )
    if four:
        expand_sum = expand_parts[0].astype(FULL) + both(expand_near)
    else:
        expand_sum = lax.psum_scatter(
            expand_whole, "fsdp", scatter_dimension=0, tiled=True
        ).astype(FULL)
    expand_keep, expand_send = halves(expand_sum, part_at)
    slope_clip = jnp.concatenate(slope_blocks, axis=0)
    expand_send, slope_clip, far_top, far_low = fence(expand_send, slope_clip, far_top, far_low)
    wide_far = (swap(far_top, "fsdp", 1), swap(far_low, "fsdp", 2)) if four else ()
    expand_rows = (expand_keep, swap(expand_send, "ctx", 1))
    grad_first = attention_backward(joint_out, slope_clip, out_first, log_first, 0)

    grad_first, slope_clip, wide_far, expand_rows = fence(
        grad_first, slope_clip, wide_far, expand_rows
    )
    expand_keep, expand_send = halves(both(expand_rows), clip_at)
    expand_send, slope_clip, wide_early = fence(expand_send, slope_clip, wide_early)
    if four:
        wide_early = near_rows_out(wide_early)
    expand_rows = (expand_keep, swap(expand_send, "ctx", 2))
    grad_second = attention_backward(joint_out, slope_clip, out_second, log_second, 1)

    grad_second, expand_rows, wide_early, wide_far = fence(
        grad_second, expand_rows, wide_early, wide_far
    )
    if four:
        wide_late = (
            both((wide_next[half:], wide_far[1])).astype(LOW),
            both((wide_side[:half], wide_far[0])).astype(LOW),
        )
    else:
        wide_late = ()
    if four:
        wide_late = near_rows_out(wide_late)
    expand_rows = join_rows(both(expand_rows).astype(LOW), clip_at, 2)
    joint_slope = jnp.concatenate(
        [grad[kind] for kind in range(3) for grad in (grad_first, grad_second)], axis=1
    )
    first_there = product(joint_slope, joint_full[width_half:], ROW_BY_ROW).astype(LOW)
    first_here = rows_product(joint_slope, joint_full[:width_half], "first_slope")
    first_half = both((first_here, swap(first_there, "tp", 1))).astype(LOW)

    if not four:
        wide_near = lax.psum_scatter(
            jnp.concatenate(wide, axis=1), "fsdp", scatter_dimension=0, tiled=True
        )
    first_half, joint_slope = fence(first_half, joint_slope)
    pieces = first_half.reshape(4, rows_here, width_half)
    passing = jnp.concatenate([pieces[1], pieces[3][:, :quarter], pieces[2][:, quarter:]], axis=1)
    passing = swap(passing, "ctx", 1)
    place = (shard if four else start) ^ (2 * core)
    joint_parts = grad_products([normed_mine, normed_other], joint_slope, place, order, "joint_grad")
    slope_sums = jnp.sum(joint_slope.astype(FULL), axis=0)
    bias_sums = jnp.stack([slope_sums[:part_width], slope_sums[2 * part_width :]])
    joint_bias_grad = lax.dynamic_update_slice(
        jnp.zeros((2, features), FULL), bias_sums, (0, part_at * part_width)
    )

    joint_leaves, wide_late = fence(joint_parts[0], wide_late)
    joint_far = far_halves(joint_leaves) if four else ()
    passing, joint_far, expand_rows = fence(passing, joint_far, expand_rows)
    if four:
        near_sum = [both((wide_early[0], wide_late[1])), both((wide_late[0], wide_early[1]))]
        wide_sum = rows_at(wide, 0).astype(FULL) + jnp.concatenate(near_sum, axis=0)
    else:
        wide_sum = wide_near.astype(FULL)
    wide_keep, wide_send = halves(wide_sum, part_at)
    own_half = both((pieces[0], passing[:, :width_half])).astype(LOW)
    to_left = both((pieces[2][:, :quarter], passing[:, width_half : width_half + quarter]))
    to_right = both((pieces[3][:, quarter:], passing[:, width_half + quarter :]))
    joint_near = add_far(joint_parts[2], joint_parts[1], joint_far) if four else ()
    to_left, to_right, own_half, wide_send, joint_near, activated = fence(
        to_left.astype(LOW), to_right.astype(LOW), own_half, wide_send, joint_near, activated
    )
    other_half = jnp.concatenate([swap(to_left, "ctx", 2), swap(to_right, "ctx", 3)], axis=1)
    wide_rows = (wide_keep, swap(wide_send, "ctx", 1))
    if four:
        joint_near = near_rows_out(joint_near)
    else:
        joint_near = lax.psum_scatter(
            joint_parts.reshape(width, -1), "fsdp", scatter_dimension=0, tiled=True
        )
    reduce_part = reduce_output(activated, reduce_held, pieces_at)

    other_half, joint_near, wide_rows, reduce_part = fence(
        other_half, joint_near, wide_rows, reduce_part
    )
    slope_half = jnp.concatenate(swapped_if(clip_at, [own_half, other_half]), axis=0)
    slope_other = swap(slope_half, "tp", 1)
    slope_other, expand_rows = fence(slope_other, expand_rows)
    expand_grad = join_rows(expand_rows, part_at, 1).astype(FULL)
    first_slope = jnp.concatenate(swapped_if(core, [slope_half, slope_other]), axis=1)
    wide_rows = split_rows(both(wide_rows), clip_at, 2)
    reduce_swapped = swap(reduce_part, "tp", 1)
    joint_sum = joint_parts[3].astype(FULL) + both(joint_near) if four else joint_near
    joint_sum = joint_sum.astype(LOW)
    joint_sum = (joint_sum, swap(joint_sum, "ctx", 2))
    tokens_grad, first_sums = by_rows(
        first_norm_back_kernel, "first_norm_back", [FULL], True,
        flat_tokens, first_slope, first_gain[None],
        cotangent.reshape(tokens_here, width), first_sum_back,
    )
    first_sums, tokens_grad, reduce_swapped = fence(first_sums, tokens_grad, reduce_swapped)
    vectors = [
        first_sums[0],
        first_sums[1],
        joint_bias_grad[0],
        joint_bias_grad[1],
        second_sums[2],
        second_sums[0],
        second_sums[1],
        expand_bias_grad,
        reduce_bias_grad,
    ]
    packed = jnp.concatenate(vectors).reshape(-1, 128)
    packed_pieces = [packed] + [swap(packed, "ctx", d) for d in (1, 2, 3)]
    reduce_out = both((reduce_part, reduce_swapped)) + reduce_bias
    mixer_out = both((mixer_part, mixer_swapped)) + mixer_bias
    branches = (mixer_out + reduce_out).reshape(clips_here, rows_here, width)
    result = (tokens.astype(FULL) + valid * branches).astype(LOW)

    packed_pieces, joint_sum, wide_rows, result = fence(
        packed_pieces, joint_sum, wide_rows, result
    )
    packed = pairwise(packed_pieces)
    if four:
        packed = pairwise([packed] + [swap(packed, "fsdp", d) for d in (1, 2, 3)])
    else:
        packed = lax.psum(packed, "fsdp")
    joint_sum = both(joint_sum).astype(LOW)
    joint_parts = swapped_if(part_at, [joint_sum, swap(joint_sum, "ctx", 1)])
    joint_grad = jnp.concatenate(
        [piece.reshape(-1, 3, part_width) for piece in joint_parts], axis=2
    ).astype(FULL)
    wide_rows = join_rows(both(wide_rows).astype(LOW), clip_at, 2)
    wide_other = swap(wide_rows, "ctx", 1)
    rows = wide_rows.shape[0]

    def placed(columns):
        mine, other = wide_rows[:, columns], wide_other[:, columns]
        out = jnp.zeros((2 * rows, mine.shape[1]), FULL)
        out = lax.dynamic_update_slice(out, mine.astype(FULL), (part_at * rows, 0))
        return lax.dynamic_update_slice(out, other.astype(FULL), ((1 - part_at) * rows, 0))

    reduce_grad = placed(slice(None, activated.shape[1]))
    mixer_grad = placed(slice(activated.shape[1], None))
    packed = packed.reshape(-1)
    shares = []
    start = 0
    for vector in vectors:
        share = vector.shape[0] // lax.axis_size("fsdp")
        shares.append(lax.dynamic_slice_in_dim(packed, start + shard * share, share, 0))
        start += vector.shape[0]

    shape = (clips_here, rows_here, width)
    return (
        result,
        tokens_grad.reshape(shape),
        shares[0],
        shares[1],
        joint_grad,
        jnp.stack([shares[2], shares[3]]),
        mixer_grad,
        shares[4],
        shares[5],
        shares[6],
        expand_grad,
        shares[7],
        reduce_grad,
        shares[8],
    )


def solution(mesh):
    return jax.shard_map(
        per_device,
        mesh=mesh,
        in_specs=(
            P("fsdp", "ctx", None),
            P("fsdp"),
            P("fsdp", "ctx", None),
            P(),
            P(),
            P("fsdp", None, "tp"),
            P(None, "tp"),
            P("fsdp", "tp"),
            P(),
            P(),
            P(),
            P("fsdp", "tp"),
            P("tp"),
            P("fsdp", "tp"),
            P(),
        ),
        out_specs=(
            P("fsdp", "ctx", None),
            P("fsdp", "ctx", None),
            P("fsdp"),
            P("fsdp"),
            P("fsdp", None, "tp"),
            P(None, ("tp", "fsdp")),
            P("fsdp", "tp"),
            P("fsdp"),
            P("fsdp"),
            P("fsdp"),
            P("fsdp", "tp"),
            P(("tp", "fsdp")),
            P("fsdp", "tp"),
            P("fsdp"),
        ),
        check_vma=False,
    )
```

```python
import jax
import jax.numpy as jnp
from jax import lax
from jax.experimental import pallas as pl
from jax.experimental.pallas import tpu as pltpu
from jax.sharding import PartitionSpec as P

HEAD_DIM = 64
EPSILON = 1e-06
LOW = jnp.bfloat16
FULL = jnp.float32

ROW_BY_ROW = (((1,), (1,)), ((), ()))
PLAIN = (((1,), (0,)), ((), ()))
COLUMN_BY_COLUMN = (((0,), (0,)), ((), ()))


def product(left, right, dims):
    return lax.dot_general(left, right, dims, preferred_element_type=FULL)


def normalize(value_rows):
    center = value_rows - jnp.mean(value_rows, axis=-1, keepdims=True)
    inverse = lax.rsqrt(jnp.mean(center * center, axis=-1, keepdims=True) + EPSILON)
    return (center * inverse, inverse)


def norm_back(upstream, gain, scaled, inverse):
    weighted = upstream * gain
    return inverse * (
        weighted
        - jnp.mean(weighted, axis=-1, keepdims=True)
        - scaled * jnp.mean(weighted * scaled, axis=-1, keepdims=True)
    )


def row_chunk(count, most):
    for chunk in range(most, 0, -16):
        if count % chunk == 0:
            return chunk
    raise ValueError("rows")


def first_norm_kernel(tokens_ref, gain_ref, shift_ref, out_ref):
    scaled, _ = normalize(tokens_ref[...].astype(FULL))
    out_ref[...] = (scaled * gain_ref[...] + shift_ref[...]).astype(LOW)


def second_norm_kernel(tokens_ref, one_ref, two_ref, bias_ref, gain_ref, shift_ref, out_ref):
    mixed = one_ref[...].astype(FULL) + two_ref[...].astype(FULL) + bias_ref[...]
    scaled, _ = normalize(tokens_ref[...].astype(FULL) + mixed)
    out_ref[...] = (scaled * gain_ref[...] + shift_ref[...]).astype(LOW)


def add_sums(ref, rows):
    sums = jnp.concatenate([jnp.sum(row, axis=0, keepdims=True) for row in rows], axis=0)

    @pl.when(pl.program_id(0) == 0)
    def _():
        ref[: len(rows)] = sums

    @pl.when(pl.program_id(0) > 0)
    def _():
        ref[: len(rows)] += sums


def second_norm_back_kernel(
    tokens_ref, one_ref, two_ref, bias_ref, gain_ref, left_ref, right_ref, outer_ref,
    slope_ref, back_ref, sums_ref,
):
    mixed = one_ref[...].astype(FULL) + two_ref[...].astype(FULL) + bias_ref[...]
    scaled, inverse = normalize(tokens_ref[...].astype(FULL) + mixed)
    upstream = left_ref[...].astype(FULL) + right_ref[...].astype(FULL)
    back = norm_back(upstream, gain_ref[...], scaled, inverse)
    slope = (outer_ref[...].astype(FULL) + back).astype(LOW)
    slope_ref[...] = slope
    back_ref[...] = back
    add_sums(sums_ref, [upstream * scaled, upstream, slope.astype(FULL)])


def first_norm_back_kernel(
    tokens_ref, upstream_ref, gain_ref, outer_ref, back_ref, out_ref, sums_ref
):
    scaled, inverse = normalize(tokens_ref[...].astype(FULL))
    upstream = upstream_ref[...].astype(FULL)
    back = norm_back(upstream, gain_ref[...], scaled, inverse)
    out_ref[...] = outer_ref[...].astype(FULL) + back_ref[...] + back
    add_sums(sums_ref, [upstream * scaled, upstream])


def by_rows(kernel, name, out_types, sums, *values):
    count, width = values[0].shape
    chunk = count // 2 if count % 16 == 0 else count
    part = pl.BlockSpec((chunk, width), lambda i: (i, 0))
    in_specs = [
        part if value.shape[0] == count else pl.BlockSpec((1, width), lambda i: (0, 0))
        for value in values
    ]
    out_specs = [part for _ in out_types]
    out_shape = [jax.ShapeDtypeStruct((count, width), kind) for kind in out_types]
    if sums:
        out_specs.append(pl.BlockSpec((8, width), lambda i: (0, 0)))
        out_shape.append(jax.ShapeDtypeStruct((8, width), FULL))
    return pl.pallas_call(
        kernel,
        grid=(count // chunk,),
        in_specs=in_specs,
        out_specs=out_specs,
        out_shape=out_shape,
        compiler_params=pltpu.CompilerParams(vmem_limit_bytes=40 << 20),
        name=name,
    )(*values)


def joint_kernel(mine_ref, other_ref, weight_ref, bias_ref, out_ref):
    half = mine_ref.shape[1]
    out = product(mine_ref[...], weight_ref[:half], PLAIN)
    out += product(other_ref[...], weight_ref[half:], PLAIN)
    out_ref[...] = (out + bias_ref[...]).astype(LOW)


def joint_projection(mine, other, weight, bias):
    count, half = mine.shape
    columns = weight.shape[1]
    chunk = row_chunk(count, 784)
    part = pl.BlockSpec((chunk, half), lambda i: (i, 0))
    return pl.pallas_call(
        joint_kernel,
        grid=(count // chunk,),
        in_specs=[
            part,
            part,
            pl.BlockSpec(weight.shape, lambda i: (0, 0)),
            pl.BlockSpec((1, columns), lambda i: (0, 0)),
        ],
        out_specs=pl.BlockSpec((chunk, columns), lambda i: (i, 0)),
        out_shape=jax.ShapeDtypeStruct((count, columns), LOW),
        compiler_params=pltpu.CompilerParams(vmem_limit_bytes=40 << 20),
        name="joint_projection",
    )(mine, other, weight, bias)


def rows_kernel(left_ref, right_ref, out_ref):
    out_ref[...] = product(left_ref[...], right_ref[...], ROW_BY_ROW).astype(LOW)


def rows_product(left, right, columns, name):
    count, depth = left.shape
    chunk = row_chunk(count, 400)
    return pl.pallas_call(
        rows_kernel,
        grid=(count // chunk,),
        in_specs=[
            pl.BlockSpec((chunk, depth), lambda i: (i, 0)),
            pl.BlockSpec((columns, depth), lambda i: (0, 0)),
        ],
        out_specs=pl.BlockSpec((chunk, columns), lambda i: (i, 0)),
        out_shape=jax.ShapeDtypeStruct((count, columns), LOW),
        compiler_params=pltpu.CompilerParams(vmem_limit_bytes=48 << 20),
        name=name,
    )(left, right)


def grad_kernel(distances, place_ref, *refs):
    lefts, (right_ref, out_ref) = refs[:-2], refs[-2:]
    left = lefts[0][...]
    if len(lefts) == 2:
        slot = place_ref[0] ^ distance_at(distances, pl.program_id(0))
        left = jnp.where((slot >> 1) == 0, left, lefts[1][...])
    out_ref[0] = product(left, right_ref[...], COLUMN_BY_COLUMN).astype(LOW)


def distance_at(distances, step):
    if len(distances) == 1:
        return distances[0]
    return distances[0] + step * (distances[1] - distances[0])


def grad_products(lefts, right, place, distances, name):
    tokens_here, columns = right.shape
    quarter = sum(left.shape[1] for left in lefts) // 4
    blocks = lefts[0].shape[1] // quarter

    def left_at(i, place):
        return (0, (place[0] ^ distance_at(distances, i)) & (blocks - 1))

    return pl.pallas_call(
        lambda *refs: grad_kernel(distances, *refs),
        grid_spec=pltpu.PrefetchScalarGridSpec(
            num_scalar_prefetch=1,
            grid=(len(distances),),
            in_specs=[pl.BlockSpec((tokens_here, quarter), left_at) for _ in lefts]
            + [pl.BlockSpec((tokens_here, columns), lambda i, place: (0, 0))],
            out_specs=pl.BlockSpec((1, quarter, columns), lambda i, place: (i, 0, 0)),
        ),
        out_shape=jax.ShapeDtypeStruct((len(distances), quarter, columns), LOW),
        compiler_params=pltpu.CompilerParams(vmem_limit_bytes=48 << 20),
        name=name,
    )(place.astype(jnp.int32).reshape(1), *lefts, right)


def attention_forward_kernel(q_ref, k_ref, v_ref, o_ref, lse_ref):
    count, width = q_ref.shape
    rows = row_chunk(count, 256)
    lane = lax.broadcasted_iota(jnp.int32, (rows, width), 1)
    k = k_ref[...]
    v = v_ref[...]
    units = [(start, head) for start in range(0, count, rows) for head in range(width // HEAD_DIM)]

    def scores_of(unit):
        start, head = unit
        q = q_ref[start : start + rows] * jnp.asarray(HEAD_DIM ** (-0.5), LOW)
        return product(jnp.where((lane // HEAD_DIM) == head, q, jnp.zeros_like(q)), k, ROW_BY_ROW)

    logs = []
    ahead = scores_of(units[0])
    for step, (start, head) in enumerate(units):
        scores = ahead
        if step + 1 < len(units):
            ahead = scores_of(units[step + 1])
        top = jnp.max(scores, axis=-1, keepdims=True)
        weights = jnp.exp(scores - top)
        total = jnp.sum(weights, axis=-1, keepdims=True)
        part = product(weights.astype(LOW), v, PLAIN) / total
        if head == 0:
            out = part
            logs.append(jnp.zeros((rows, width), FULL))
        else:
            out = jnp.where((lane // HEAD_DIM) == head, part, out)
            o_ref[start : start + rows] = out.astype(LOW)
        logs[-1] = jnp.where(lane == head, top + jnp.log(total), logs[-1])
    lse_ref[...] = jnp.concatenate(logs, axis=0).T[: lse_ref.shape[0]]


def attention_forward(joint, pair):
    count, columns = joint.shape
    width = 2 * HEAD_DIM
    kind = columns // (3 * width)
    return pl.pallas_call(
        attention_forward_kernel,
        grid=(1,),
        in_specs=[
            pl.BlockSpec((count, width), lambda i: (0, pair)),
            pl.BlockSpec((count, width), lambda i: (0, kind + pair)),
            pl.BlockSpec((count, width), lambda i: (0, 2 * kind + pair)),
        ],
        out_specs=[
            pl.BlockSpec((count, width), lambda i: (0, 0)),
            pl.BlockSpec((8, count), lambda i: (0, 0)),
        ],
        out_shape=[
            jax.ShapeDtypeStruct((count, width), LOW),
            jax.ShapeDtypeStruct((8, count), FULL),
        ],
        compiler_params=pltpu.CompilerParams(vmem_limit_bytes=48 << 20),
        name="attention_forward",
    )(joint, joint, joint)


def attention_backward_kernel(
    q_ref, k_ref, v_ref, da_ref, o_ref, lse_ref, dq_ref, dk_ref, dv_ref,
    q_heads, da_heads, delta_ref, dq_total,
):
    count, width = q_ref.shape
    rows = row_chunk(count, 256)
    heads = width // HEAD_DIM
    scale = jnp.asarray(HEAD_DIM ** (-0.5), LOW)

    lane = lax.broadcasted_iota(jnp.int32, (count, width), 1)
    delta = jnp.zeros((count, width), FULL)
    q = q_ref[...] * scale
    da = da_ref[...]
    both_rows = da.astype(FULL) * o_ref[...].astype(FULL)
    for head in range(heads):
        mask = (lane // HEAD_DIM) == head
        q_heads[head] = jnp.where(mask, q, jnp.zeros_like(q))
        da_heads[head] = jnp.where(mask, da, jnp.zeros_like(da))
        row = jnp.sum(jnp.where(mask, both_rows, 0.0), axis=-1, keepdims=True)
        delta = jnp.where(lane == head, row, delta)
    delta_ref[...] = delta.T[:8]
    dq_total[...] = jnp.zeros_like(dq_total)

    lane = lax.broadcasted_iota(jnp.int32, (rows, width), 1)
    for start in range(0, count, rows):
        k = k_ref[start : start + rows]
        v = v_ref[start : start + rows]
        scaled_k = k * scale
        dk = dv = None
        for head in range(heads):
            q = q_heads[head]
            da = da_heads[head]
            probs = jnp.exp(product(k, q, ROW_BY_ROW) - lse_ref[head : head + 1, :])
            slope = probs * (product(v, da, ROW_BY_ROW) - delta_ref[head : head + 1, :])
            slope = slope.astype(LOW)
            dv_part = product(probs.astype(LOW), da, PLAIN)
            dk_part = product(slope, q, PLAIN)
            dv = dv_part if dv is None else dv + dv_part
            dk = dk_part if dk is None else dk + dk_part
            one_k = jnp.where((lane // HEAD_DIM) == head, scaled_k, jnp.zeros_like(k))
            dq_total[...] += product(slope, one_k, COLUMN_BY_COLUMN)
        dk_ref[start : start + rows] = dk.astype(LOW)
        dv_ref[start : start + rows] = dv.astype(LOW)
    dq_ref[...] = dq_total[...].astype(LOW)


def attention_backward(joint, da, out, lse, pair):
    count, columns = joint.shape
    width = 2 * HEAD_DIM
    kind = columns // (3 * width)
    alone = pl.BlockSpec((count, width), lambda i: (0, 0))
    grad = jax.ShapeDtypeStruct((count, width), LOW)
    return pl.pallas_call(
        attention_backward_kernel,
        grid=(1,),
        in_specs=[
            pl.BlockSpec((count, width), lambda i: (0, pair)),
            pl.BlockSpec((count, width), lambda i: (0, kind + pair)),
            pl.BlockSpec((count, width), lambda i: (0, 2 * kind + pair)),
            pl.BlockSpec((count, width), lambda i: (0, pair)),
            alone,
            pl.BlockSpec((8, count), lambda i: (0, 0)),
        ],
        out_specs=[alone, alone, alone],
        out_shape=[grad, grad, grad],
        scratch_shapes=[
            pltpu.VMEM((2, count, width), LOW),
            pltpu.VMEM((2, count, width), LOW),
            pltpu.VMEM((8, count), FULL),
            pltpu.VMEM((count, width), FULL),
        ],
        compiler_params=pltpu.CompilerParams(vmem_limit_bytes=48 << 20),
        name="attention_backward",
    )(joint, joint, joint, da, out, lse)


def put_together(place_ref, whole_ref, pieces, edge=0):
    for piece, refs in enumerate(pieces):
        rows = refs[0].shape[0]
        place = pl.ds(pl.multiple_of(place_ref[piece], rows), rows)
        if len(refs) == 1:
            whole_ref[place, :] = refs[0][...]
            continue

        @pl.when(pl.program_id(0) < edge)
        def _():
            whole_ref[place, :] = refs[0][...]

        @pl.when(pl.program_id(0) >= edge)
        def _():
            whole_ref[place, :] = refs[1][...]


def nested(refs, like):
    refs = iter(refs)
    return [tuple(next(refs) for _ in piece) for piece in like]


def feed_forward_kernel(
    expand, reduce, edge, place_ref, normed_ref, slope_ref, bias_ref, *refs
):
    active_ref, expand_slope_ref, back_ref, bias_grad_ref, total, expand_ref, reduce_ref = refs[-7:]
    arrays = sum(len(piece) for piece in expand)
    put_together(place_ref, expand_ref, nested(refs[:arrays], expand), edge)
    put_together(place_ref, reduce_ref, nested(refs[arrays:-7], reduce))
    step = pl.program_id(0)
    hidden = product(normed_ref[...], expand_ref[...], PLAIN) + bias_ref[...]
    upstream = product(slope_ref[...], reduce_ref[...], PLAIN)
    share = 0.5 * (1.0 + lax.erf(hidden * (0.5**0.5)))
    active_ref[...] = (hidden * share).astype(LOW)
    density = jnp.exp(-0.5 * hidden * hidden) * 0.3989422804014327
    slope = (upstream * (share + hidden * density)).astype(LOW)
    expand_slope_ref[...] = slope
    bias_grad_ref[...] = jnp.sum(slope.astype(FULL), axis=0, keepdims=True)
    back = product(slope, expand_ref[...], ROW_BY_ROW)

    @pl.when(step == 0)
    def _():
        total[...] = back

    @pl.when(step > 0)
    def _():
        total[...] += back

    @pl.when(step == pl.num_programs(0) - 1)
    def _():
        back_ref[...] = total[...].astype(LOW)


def feed_forward(normed, slope, bias, expand, early, reduce, place):
    count, width = normed.shape
    hidden = bias.shape[1]
    block = 512
    edge = early // block
    whole = pl.BlockSpec((count, width), lambda i, place: (0, 0))
    out = pl.BlockSpec((count, block), lambda i, place: (0, i))
    row = pl.BlockSpec((1, block), lambda i, place: (0, i))
    specs = []
    arrays = []
    for piece in [*expand, *reduce]:
        shape = (piece[0].shape[0], block)
        arrays += piece
        if len(piece) == 1:
            specs.append(pl.BlockSpec(shape, lambda i, place: (0, i)))
        else:
            specs.append(pl.BlockSpec(shape, lambda i, place: (0, jnp.minimum(i, edge - 1))))
            specs.append(pl.BlockSpec(shape, lambda i, place: (0, jnp.maximum(i - edge, 0))))
    return pl.pallas_call(
        lambda *refs: feed_forward_kernel(expand, reduce, edge, *refs),
        grid_spec=pltpu.PrefetchScalarGridSpec(
            num_scalar_prefetch=1,
            grid=(hidden // block,),
            in_specs=[whole, whole, row] + specs,
            out_specs=[out, out, whole, row],
            scratch_shapes=[
                pltpu.VMEM((count, width), FULL),
                pltpu.VMEM((width, block), LOW),
                pltpu.VMEM((width, block), LOW),
            ],
        ),
        out_shape=[
            jax.ShapeDtypeStruct((count, hidden), LOW),
            jax.ShapeDtypeStruct((count, hidden), LOW),
            jax.ShapeDtypeStruct((count, width), LOW),
            jax.ShapeDtypeStruct((1, hidden), FULL),
        ],
        compiler_params=pltpu.CompilerParams(vmem_limit_bytes=44 << 20),
        name="feed_forward",
    )(place, normed, slope, bias, *arrays)


def reduce_kernel(place_ref, active_ref, *refs):
    out_ref, total, reduce_ref = refs[-3:]
    put_together(place_ref, reduce_ref, [(ref,) for ref in refs[:-3]])
    part = product(active_ref[...], reduce_ref[...], ROW_BY_ROW)

    @pl.when(pl.program_id(0) == 0)
    def _():
        total[...] = part

    @pl.when(pl.program_id(0) > 0)
    def _():
        total[...] += part

    @pl.when(pl.program_id(0) == pl.num_programs(0) - 1)
    def _():
        out_ref[...] = total[...].astype(LOW)


def reduce_output(active, reduce, place):
    count, hidden = active.shape
    width = sum(piece.shape[0] for piece in reduce)
    block = 512 if hidden % 512 == 0 else hidden
    return pl.pallas_call(
        reduce_kernel,
        grid_spec=pltpu.PrefetchScalarGridSpec(
            num_scalar_prefetch=1,
            grid=(hidden // block,),
            in_specs=[pl.BlockSpec((count, block), lambda i, place: (0, i))]
            + [
                pl.BlockSpec((piece.shape[0], block), lambda i, place: (0, i)) for piece in reduce
            ],
            out_specs=pl.BlockSpec((count, width), lambda i, place: (0, 0)),
            scratch_shapes=[pltpu.VMEM((count, width), FULL), pltpu.VMEM((width, block), LOW)],
        ),
        out_shape=jax.ShapeDtypeStruct((count, width), LOW),
        compiler_params=pltpu.CompilerParams(vmem_limit_bytes=32 << 20),
        name="reduce_output",
    )(place, active, *reduce)


def swap(value, axis, distance):
    size = lax.axis_size(axis)
    return lax.ppermute(value, axis, [(i, i ^ distance) for i in range(size)])


def fence(*values):
    return lax.optimization_barrier(values)


def gather_near(rows_here):
    if lax.axis_size("fsdp") != 4:
        return (lax.all_gather(rows_here, "fsdp", axis=0, tiled=True),)
    return (rows_here, swap(rows_here, "fsdp", 1), swap(rows_here, "fsdp", 2))


def far_of(held):
    if len(held) == 1:
        return ()
    half = held[0].shape[0] // 2
    return (held[2][:half], held[1][half:])


def send_far(leaves):
    return (swap(leaves[0], "fsdp", 1), swap(leaves[1], "fsdp", 2)) if leaves else ()


def far_of(held):
    if len(held) == 1:
        return ()
    half = held[0].shape[0] // 2
    return (held[2][:half], held[1][half:])


def send_far(leaves):
    return (swap(leaves[0], "fsdp", 1), swap(leaves[1], "fsdp", 2)) if leaves else ()


def gather_far(held):
    return held + send_far(far_of(held))


def place_near(held):
    if len(held) == 1:
        return held[0]
    rows_here, near, side = held[:3]
    me = lax.axis_index("fsdp")
    count, width = rows_here.shape
    out = jnp.zeros((4 * count, width), rows_here.dtype)
    out = lax.dynamic_update_slice(out, rows_here, (me * count, 0))
    out = lax.dynamic_update_slice(out, near, ((me ^ 1) * count, 0))
    return lax.dynamic_update_slice(out, side, ((me ^ 2) * count, 0))


def place_far(out, held):
    if len(held) == 1:
        return out
    far_top, far_low = held[3:]
    half = far_top.shape[0]
    start = (lax.axis_index("fsdp") ^ 3) * 2 * half
    out = lax.dynamic_update_slice(out, far_top, (start, 0))
    return lax.dynamic_update_slice(out, far_low, (start + half, 0))


def grad_rows(left, right, distance):
    count = left.shape[1] // 4
    start = (lax.axis_index("fsdp") ^ distance) * count
    piece = lax.dynamic_slice_in_dim(left, start, count, 1)
    return product(piece, right, COLUMN_BY_COLUMN).astype(LOW)


def rows_at(matrices, distance):
    parts = []
    for matrix in matrices:
        count = matrix.shape[0] // 4
        start = (lax.axis_index("fsdp") ^ distance) * count
        parts.append(lax.dynamic_slice_in_dim(matrix, start, count, 0))
    return parts[0] if len(parts) == 1 else jnp.concatenate(parts, axis=1)


def far_halves(far):
    half = far.shape[0] // 2
    return (swap(far[:half], "fsdp", 1), swap(far[half:], "fsdp", 2))


def add_far(near, side, far):
    half = near.shape[0] // 2
    near = jnp.concatenate([near[:half], both((near[half:], far[1])).astype(LOW)], axis=0)
    side = jnp.concatenate([both((side[:half], far[0])).astype(LOW), side[half:]], axis=0)
    return (near, side)


def near_rows_out(pair):
    return (swap(pair[0], "fsdp", 1), swap(pair[1], "fsdp", 2))


def halves(value, bit):
    half = value.shape[0] // 2
    keep = lax.dynamic_slice_in_dim(value, bit * half, half, 0)
    send = lax.dynamic_slice_in_dim(value, (1 - bit) * half, half, 0)
    return keep, send.astype(LOW)


def split_rows(value, bit, distance):
    keep, send = halves(value, bit)
    return keep, swap(send, "ctx", distance)


def both(pair):
    return pair[0].astype(FULL) + pair[1].astype(FULL)


def join_rows(value, bit, distance):
    other = swap(value, "ctx", distance)
    return jnp.where(
        bit == 0,
        jnp.concatenate([value, other], axis=0),
        jnp.concatenate([other, value], axis=0),
    )


def pairwise(pieces):
    return (pieces[0] + pieces[1]) + (pieces[2] + pieces[3])


def swapped_if(bit, pair):
    return [jnp.where(bit == 0, pair[0], pair[1]), jnp.where(bit == 0, pair[1], pair[0])]


def per_device(
    tokens,
    clip_mask,
    cotangent,
    first_gain,
    first_shift,
    joint_weight,
    joint_bias,
    mixer_weight,
    mixer_bias,
    second_gain,
    second_shift,
    expand_weight,
    expand_bias,
    reduce_weight,
    reduce_bias,
):
    clips_here, rows_here, width = tokens.shape
    if lax.axis_size("ctx") != 4 or lax.axis_size("tp") != 2 or clips_here != 2:
        raise ValueError("mesh")
    shard = lax.axis_index("fsdp")
    block = lax.axis_index("ctx")
    core = lax.axis_index("tp")
    clip_at = block >> 1
    part_at = block & 1
    width_half = width // 2
    quarter = width_half // 2
    features = joint_weight.shape[2]
    part_width = features // 2
    pair_width = 2 * HEAD_DIM
    tokens_here = clips_here * rows_here

    flat_tokens = tokens.reshape(tokens_here, width)
    (first_normed,) = by_rows(
        first_norm_kernel, "first_norm", [LOW], False,
        flat_tokens, first_gain[None], first_shift[None],
    )
    first_normed = first_normed.reshape(clips_here, rows_here, width)
    mine = lax.dynamic_slice_in_dim(first_normed, core * width_half, width_half, 2)
    other_side = lax.dynamic_slice_in_dim(first_normed, (1 - core) * width_half, width_half, 2)
    own_clip = lax.dynamic_index_in_dim(mine, clip_at, 0, False)
    own_other = lax.dynamic_index_in_dim(other_side, clip_at, 0, False)
    other_clip = lax.dynamic_index_in_dim(mine, 1 - clip_at, 0, False)
    joint_part = lax.dynamic_slice_in_dim(joint_weight, part_at * part_width, part_width, 2)
    early = expand_weight.shape[1] // 2
    wide_part = jnp.concatenate(
        [expand_weight[:, :early]] + [joint_part[:, kind] for kind in range(3)] + [mixer_weight],
        axis=1,
    )

    own_clip, left, right, wide_part = fence(
        own_clip, other_clip[:, :quarter], other_clip[:, quarter:], wide_part
    )
    near_rows = swap(own_clip, "ctx", 1)
    across_left = swap(left, "ctx", 2)
    far_right = swap(right, "ctx", 3)
    wide_held = gather_near(wide_part)

    near_rows, across_left, far_right = fence(near_rows, across_left, far_right)
    passed = swap(jnp.concatenate([across_left, far_right], axis=1), "ctx", 1)
    (wide_held,) = fence(wide_held)
    held = gather_far(tuple(piece[:, early:] for piece in wide_held))

    passed, held, expand_rest = fence(passed, held, expand_weight[:, early:])
    rest_held = gather_near(expand_rest)
    cross_rows = jnp.concatenate(
        [
            near_rows,
            jnp.concatenate([across_left, passed[:, quarter:]], axis=1),
            jnp.concatenate([passed[:, :quarter], far_right], axis=1),
        ],
        axis=0,
    )
    cross_other = swap(cross_rows, "tp", 1)
    both_full = place_far(place_near(held), held)
    joint_columns = 3 * part_width
    joint_full = jnp.concatenate(
        [
            lax.dynamic_slice(both_full, (start * width_half, 0), (width_half, joint_columns))
            for start in (core, 1 - core)
        ],
        axis=0,
    )

    cross_other, joint_full, both_full, reduce_weight = fence(
        cross_other, joint_full, both_full, reduce_weight
    )
    mixer_full = both_full[:, joint_columns:]
    reduce_held = gather_near(reduce_weight)
    normed_mine = jnp.concatenate([own_clip, cross_rows], axis=0)
    normed_other = jnp.concatenate([own_other, cross_other], axis=0)
    bias_part = lax.dynamic_slice_in_dim(joint_bias, part_at * part_width, part_width, 1)
    bias_row = jnp.concatenate([bias_part[0], jnp.zeros_like(bias_part[0]), bias_part[1]])
    joint_out = joint_projection(normed_mine, normed_other, joint_full, bias_row[None])
    out_first, log_first = attention_forward(joint_out, 0)

    out_first, joint_out, mixer_full, rest_held = fence(
        out_first, joint_out, mixer_full, rest_held
    )
    first_blocks = out_first.reshape(4, rows_here, pair_width)
    arrived_first = [swap(first_blocks[d], "ctx", d) for d in (1, 2, 3)]
    out_second, log_second = attention_forward(joint_out, 1)

    far_leaves = far_of(
        tuple(
            jnp.concatenate([one[:, :early], two], axis=1)
            for one, two in zip(wide_held, rest_held)
        )
    )
    out_second, arrived_first, reduce_held, far_leaves = fence(
        out_second, arrived_first, reduce_held, far_leaves
    )
    second_blocks = out_second.reshape(4, rows_here, pair_width)
    arrived_second = [swap(second_blocks[d], "ctx", d) for d in (1, 2, 3)]
    expand_far_rows = send_far(far_leaves)

    arrived_second, expand_far_rows, reduce_held, reduce_leaves = fence(
        arrived_second, expand_far_rows, reduce_held, far_of(reduce_held)
    )
    reduce_held = reduce_held + send_far(reduce_leaves)
    expand_held = list(zip(wide_held, rest_held)) + [(rows,) for rows in expand_far_rows]
    arrived = [jnp.concatenate([first_blocks[0], second_blocks[0]], axis=1)] + [
        jnp.concatenate([one, two], axis=1) for one, two in zip(arrived_first, arrived_second)
    ]
    own_joined = jnp.concatenate(swapped_if(part_at, arrived[:2]), axis=1)
    other_joined = jnp.concatenate(swapped_if(part_at, arrived[2:]), axis=1)
    mixed_in = jnp.concatenate(swapped_if(clip_at, [own_joined, other_joined]), axis=0)
    mixer_part = product(mixed_in, mixer_full, ROW_BY_ROW).astype(LOW)
    mixer_swapped = swap(mixer_part, "tp", 1)
    mixer_row = mixer_bias[None]
    (second_normed,) = by_rows(
        second_norm_kernel, "second_norm", [LOW], False,
        flat_tokens, mixer_part, mixer_swapped, mixer_row, second_gain[None], second_shift[None],
    )
    valid = clip_mask.astype(FULL)[:, None, None]
    reduce_slope = (cotangent.astype(FULL) * valid).astype(LOW).reshape(tokens_here, width)
    reduce_bias_grad = jnp.sum(reduce_slope.astype(FULL), axis=0)

    second_normed, reduce_slope, reduce_held = fence(second_normed, reduce_slope, reduce_held)
    four = lax.axis_size("fsdp") == 4
    start = jnp.zeros((), jnp.int32)
    if four:
        rows = width // 4
        pieces_at = jnp.stack([shard, shard ^ 1, shard ^ 2, shard ^ 3, shard ^ 3]) * rows
        pieces_at = pieces_at.astype(jnp.int32) + jnp.array([0, 0, 0, 0, rows // 2], jnp.int32)
    else:
        pieces_at = start.reshape(1)
    activated, expand_slope, second_part, expand_bias_grad = feed_forward(
        second_normed, reduce_slope, expand_bias[None], expand_held, early,
        [(piece,) for piece in reduce_held], pieces_at,
    )
    expand_bias_grad = expand_bias_grad[0]

    second_swapped = swap(second_part, "tp", 1)
    place, order = (shard, (3, 2, 1, 0)) if four else (start, (0, 1, 2, 3))
    if four:
        half = width // 8
        far = grad_rows(second_normed, expand_slope, 3)
        far_top, far_low, normed_again, expand_slope = fence(
            far[:half], far[half:], second_normed, expand_slope
        )
        expand_far = (swap(far_top, "fsdp", 1), swap(far_low, "fsdp", 2))
        expand_parts = [grad_rows(normed_again, expand_slope, d) for d in (0, 1, 2)]
        expand_parts, second_swapped = fence(expand_parts, second_swapped)
    else:
        expand_far = ()
        expand_whole = product(second_normed, expand_slope, COLUMN_BY_COLUMN).astype(LOW)
    mixer_slope, first_sum_back, second_sums = by_rows(
        second_norm_back_kernel, "second_norm_back", [LOW, FULL], True,
        flat_tokens, mixer_part, mixer_swapped, mixer_row, second_gain[None],
        second_part, second_swapped, reduce_slope,
    )
    attended_slope = product(mixer_slope, mixer_full, PLAIN).astype(LOW)

    leaving = []
    for distance in range(4):
        to = block ^ distance
        corner = ((to >> 1) * rows_here, (to & 1) * part_width)
        leaving.append(lax.dynamic_slice(attended_slope, corner, (rows_here, part_width)))
    expand_near = add_far(expand_parts[1], expand_parts[2], expand_far) if four else ()
    leaving, mixer_slope, mixed_in, activated, expand_near = fence(
        leaving, mixer_slope, mixed_in, activated, expand_near
    )
    slope_blocks = [leaving[0]] + [swap(leaving[d], "ctx", d) for d in (1, 2, 3)]
    if four:
        expand_near = near_rows_out(expand_near)
    wide = (
        product(reduce_slope, activated, COLUMN_BY_COLUMN).astype(LOW),
        product(mixer_slope, mixed_in, COLUMN_BY_COLUMN).astype(LOW),
    )
    if four:
        wide_far, wide_side, wide_next = (rows_at(wide, distance) for distance in (3, 2, 1))
        far_top, far_low = wide_far[:half], wide_far[half:]
        wide_early = (wide_next[:half], wide_side[half:])
    else:
        far_top, far_low, wide_early = (), (), ()

    slope_blocks, expand_near, far_top, far_low = fence(
        slope_blocks, expand_near, far_top, far_low
    )
    if four:
        expand_sum = expand_parts[0].astype(FULL) + both(expand_near)
    else:
        expand_sum = lax.psum_scatter(
            expand_whole, "fsdp", scatter_dimension=0, tiled=True
        ).astype(FULL)
    expand_keep, expand_send = halves(expand_sum, part_at)
    slope_clip = jnp.concatenate(slope_blocks, axis=0)
    expand_send, slope_clip, far_top, far_low = fence(expand_send, slope_clip, far_top, far_low)
    wide_far = (swap(far_top, "fsdp", 1), swap(far_low, "fsdp", 2)) if four else ()
    expand_rows = (expand_keep, swap(expand_send, "ctx", 1))
    grad_first = attention_backward(joint_out, slope_clip, out_first, log_first, 0)

    grad_first, slope_clip, wide_far, expand_rows = fence(
        grad_first, slope_clip, wide_far, expand_rows
    )
    if four:
        wide_late = (
            both((wide_next[half:], wide_far[1])).astype(LOW),
            both((wide_side[:half], wide_far[0])).astype(LOW),
        )
    else:
        wide_late = ()
    expand_keep, expand_send = halves(both(expand_rows), clip_at)
    expand_send, slope_clip, wide_early, wide_late = fence(
        expand_send, slope_clip, wide_early, wide_late
    )
    if four:
        wide_early = near_rows_out(wide_early)
    expand_rows = (expand_keep, swap(expand_send, "ctx", 2))
    grad_second = attention_backward(joint_out, slope_clip, out_second, log_second, 1)

    grad_second, expand_rows, wide_early, wide_late = fence(
        grad_second, expand_rows, wide_early, wide_late
    )
    if four:
        wide_late = near_rows_out(wide_late)
    expand_rows = join_rows(both(expand_rows).astype(LOW), clip_at, 2)
    joint_slope = jnp.concatenate(
        [grad[kind] for kind in range(3) for grad in (grad_first, grad_second)], axis=1
    )
    first_there = product(joint_slope, joint_full[width_half:], ROW_BY_ROW).astype(LOW)
    first_here = rows_product(joint_slope, joint_full, width_half, "first_slope")
    first_half = both((first_here, swap(first_there, "tp", 1))).astype(LOW)

    if not four:
        wide_near = lax.psum_scatter(
            jnp.concatenate(wide, axis=1), "fsdp", scatter_dimension=0, tiled=True
        )
    first_half, joint_slope = fence(first_half, joint_slope)
    pieces = first_half.reshape(4, rows_here, width_half)
    passing = jnp.concatenate([pieces[1], pieces[3][:, :quarter], pieces[2][:, quarter:]], axis=1)
    passing = swap(passing, "ctx", 1)
    place = (shard if four else start) ^ (2 * core)
    joint_parts = grad_products([normed_mine, normed_other], joint_slope, place, order, "joint_grad")
    slope_sums = jnp.sum(joint_slope.astype(FULL), axis=0)
    bias_sums = jnp.stack([slope_sums[:part_width], slope_sums[2 * part_width :]])
    joint_bias_grad = lax.dynamic_update_slice(
        jnp.zeros((2, features), FULL), bias_sums, (0, part_at * part_width)
    )

    joint_far = far_halves(joint_parts[0]) if four else ()
    passing, joint_far, wide_late, expand_rows = fence(
        passing, joint_far, wide_late, expand_rows
    )
    if four:
        near_sum = [both((wide_early[0], wide_late[1])), both((wide_late[0], wide_early[1]))]
        wide_sum = rows_at(wide, 0).astype(FULL) + jnp.concatenate(near_sum, axis=0)
    else:
        wide_sum = wide_near.astype(FULL)
    wide_keep, wide_send = halves(wide_sum, part_at)
    own_half = both((pieces[0], passing[:, :width_half])).astype(LOW)
    to_left = both((pieces[2][:, :quarter], passing[:, width_half : width_half + quarter]))
    to_right = both((pieces[3][:, quarter:], passing[:, width_half + quarter :]))
    joint_near = add_far(joint_parts[2], joint_parts[1], joint_far) if four else ()
    to_left, to_right, own_half, wide_send, joint_near, activated = fence(
        to_left.astype(LOW), to_right.astype(LOW), own_half, wide_send, joint_near, activated
    )
    other_half = jnp.concatenate([swap(to_left, "ctx", 2), swap(to_right, "ctx", 3)], axis=1)
    wide_rows = (wide_keep, swap(wide_send, "ctx", 1))
    if four:
        joint_near = near_rows_out(joint_near)
    else:
        joint_near = lax.psum_scatter(
            joint_parts.reshape(width, -1), "fsdp", scatter_dimension=0, tiled=True
        )
    reduce_part = reduce_output(activated, reduce_held, pieces_at)

    other_half, joint_near, wide_rows, reduce_part = fence(
        other_half, joint_near, wide_rows, reduce_part
    )
    slope_half = jnp.concatenate(swapped_if(clip_at, [own_half, other_half]), axis=0)
    slope_other = swap(slope_half, "tp", 1)
    slope_other, expand_rows = fence(slope_other, expand_rows)
    expand_grad = join_rows(expand_rows, part_at, 1).astype(FULL)
    first_slope = jnp.concatenate(swapped_if(core, [slope_half, slope_other]), axis=1)
    wide_rows = split_rows(both(wide_rows), clip_at, 2)
    reduce_swapped = swap(reduce_part, "tp", 1)
    joint_sum = joint_parts[3].astype(FULL) + both(joint_near) if four else joint_near
    joint_sum = joint_sum.astype(LOW)
    joint_sum = (joint_sum, swap(joint_sum, "ctx", 2))
    tokens_grad, first_sums = by_rows(
        first_norm_back_kernel, "first_norm_back", [FULL], True,
        flat_tokens, first_slope, first_gain[None],
        cotangent.reshape(tokens_here, width), first_sum_back,
    )
    first_sums, tokens_grad, reduce_swapped = fence(first_sums, tokens_grad, reduce_swapped)
    vectors = [
        first_sums[0],
        first_sums[1],
        joint_bias_grad[0],
        joint_bias_grad[1],
        second_sums[2],
        second_sums[0],
        second_sums[1],
        expand_bias_grad,
        reduce_bias_grad,
    ]
    packed = jnp.concatenate(vectors).reshape(-1, 128)
    packed_pieces = [packed] + [swap(packed, "ctx", d) for d in (1, 2, 3)]
    reduce_out = both((reduce_part, reduce_swapped)) + reduce_bias
    mixer_out = both((mixer_part, mixer_swapped)) + mixer_bias
    branches = (mixer_out + reduce_out).reshape(clips_here, rows_here, width)
    result = (tokens.astype(FULL) + valid * branches).astype(LOW)

    packed_pieces, joint_sum, wide_rows, result = fence(
        packed_pieces, joint_sum, wide_rows, result
    )
    packed = pairwise(packed_pieces)
    if four:
        packed = pairwise([packed] + [swap(packed, "fsdp", d) for d in (1, 2, 3)])
    else:
        packed = lax.psum(packed, "fsdp")
    joint_sum = both(joint_sum).astype(LOW)
    joint_parts = swapped_if(part_at, [joint_sum, swap(joint_sum, "ctx", 1)])
    joint_grad = jnp.concatenate(
        [piece.reshape(-1, 3, part_width) for piece in joint_parts], axis=2
    ).astype(FULL)
    wide_rows = join_rows(both(wide_rows).astype(LOW), clip_at, 2)
    wide_other = swap(wide_rows, "ctx", 1)
    rows = wide_rows.shape[0]

    def placed(columns):
        mine, other = wide_rows[:, columns], wide_other[:, columns]
        out = jnp.zeros((2 * rows, mine.shape[1]), FULL)
        out = lax.dynamic_update_slice(out, mine.astype(FULL), (part_at * rows, 0))
        return lax.dynamic_update_slice(out, other.astype(FULL), ((1 - part_at) * rows, 0))

    reduce_grad = placed(slice(None, activated.shape[1]))
    mixer_grad = placed(slice(activated.shape[1], None))
    packed = packed.reshape(-1)
    shares = []
    start = 0
    for vector in vectors:
        share = vector.shape[0] // lax.axis_size("fsdp")
        shares.append(lax.dynamic_slice_in_dim(packed, start + shard * share, share, 0))
        start += vector.shape[0]

    shape = (clips_here, rows_here, width)
    return (
        result,
        tokens_grad.reshape(shape),
        shares[0],
        shares[1],
        joint_grad,
        jnp.stack([shares[2], shares[3]]),
        mixer_grad,
        shares[4],
        shares[5],
        shares[6],
        expand_grad,
        shares[7],
        reduce_grad,
        shares[8],
    )


def solution(mesh):
    return jax.shard_map(
        per_device,
        mesh=mesh,
        in_specs=(
            P("fsdp", "ctx", None),
            P("fsdp"),
            P("fsdp", "ctx", None),
            P(),
            P(),
            P("fsdp", None, "tp"),
            P(None, "tp"),
            P("fsdp", "tp"),
            P(),
            P(),
            P(),
            P("fsdp", "tp"),
            P("tp"),
            P("fsdp", "tp"),
            P(),
        ),
        out_specs=(
            P("fsdp", "ctx", None),
            P("fsdp", "ctx", None),
            P("fsdp"),
            P("fsdp"),
            P("fsdp", None, "tp"),
            P(None, ("tp", "fsdp")),
            P("fsdp", "tp"),
            P("fsdp"),
            P("fsdp"),
            P("fsdp"),
            P("fsdp", "tp"),
            P(("tp", "fsdp")),
            P("fsdp", "tp"),
            P("fsdp"),
        ),
        check_vma=False,
    )
```

```python
import jax
import jax.numpy as jnp
from jax import lax
from jax.experimental import pallas as pl
from jax.experimental.pallas import tpu as pltpu
from jax.sharding import PartitionSpec as P

HEAD_DIM = 64
EPSILON = 1e-06
LOW = jnp.bfloat16
FULL = jnp.float32

ROW_BY_ROW = (((1,), (1,)), ((), ()))
PLAIN = (((1,), (0,)), ((), ()))
COLUMN_BY_COLUMN = (((0,), (0,)), ((), ()))


def product(left, right, dims):
    return lax.dot_general(left, right, dims, preferred_element_type=FULL)


def normalize(value_rows):
    center = value_rows - jnp.mean(value_rows, axis=-1, keepdims=True)
    inverse = lax.rsqrt(jnp.mean(center * center, axis=-1, keepdims=True) + EPSILON)
    return (center * inverse, inverse)


def norm_back(upstream, gain, scaled, inverse):
    weighted = upstream * gain
    return inverse * (
        weighted
        - jnp.mean(weighted, axis=-1, keepdims=True)
        - scaled * jnp.mean(weighted * scaled, axis=-1, keepdims=True)
    )


def row_chunk(count, most):
    for chunk in range(most, 0, -16):
        if count % chunk == 0:
            return chunk
    raise ValueError("rows")


def first_norm_kernel(tokens_ref, gain_ref, shift_ref, out_ref):
    scaled, _ = normalize(tokens_ref[...].astype(FULL))
    out_ref[...] = (scaled * gain_ref[...] + shift_ref[...]).astype(LOW)


def second_norm_kernel(tokens_ref, one_ref, two_ref, bias_ref, gain_ref, shift_ref, out_ref):
    mixed = one_ref[...].astype(FULL) + two_ref[...].astype(FULL) + bias_ref[...]
    scaled, _ = normalize(tokens_ref[...].astype(FULL) + mixed)
    out_ref[...] = (scaled * gain_ref[...] + shift_ref[...]).astype(LOW)


def add_sums(ref, rows):
    sums = jnp.concatenate([jnp.sum(row, axis=0, keepdims=True) for row in rows], axis=0)

    @pl.when(pl.program_id(0) == 0)
    def _():
        ref[: len(rows)] = sums

    @pl.when(pl.program_id(0) > 0)
    def _():
        ref[: len(rows)] += sums


def second_norm_back_kernel(
    tokens_ref, one_ref, two_ref, bias_ref, gain_ref, left_ref, right_ref, outer_ref,
    slope_ref, back_ref, sums_ref,
):
    mixed = one_ref[...].astype(FULL) + two_ref[...].astype(FULL) + bias_ref[...]
    scaled, inverse = normalize(tokens_ref[...].astype(FULL) + mixed)
    upstream = left_ref[...].astype(FULL) + right_ref[...].astype(FULL)
    back = norm_back(upstream, gain_ref[...], scaled, inverse)
    slope = (outer_ref[...].astype(FULL) + back).astype(LOW)
    slope_ref[...] = slope
    back_ref[...] = back
    add_sums(sums_ref, [upstream * scaled, upstream, slope.astype(FULL)])


def first_norm_back_kernel(
    tokens_ref, upstream_ref, gain_ref, outer_ref, back_ref, out_ref, sums_ref
):
    scaled, inverse = normalize(tokens_ref[...].astype(FULL))
    upstream = upstream_ref[...].astype(FULL)
    back = norm_back(upstream, gain_ref[...], scaled, inverse)
    out_ref[...] = outer_ref[...].astype(FULL) + back_ref[...] + back
    add_sums(sums_ref, [upstream * scaled, upstream])


def by_rows(kernel, name, out_types, sums, *values):
    count, width = values[0].shape
    chunk = count // 2 if count % 16 == 0 else count
    part = pl.BlockSpec((chunk, width), lambda i: (i, 0))
    in_specs = [
        part if value.shape[0] == count else pl.BlockSpec((1, width), lambda i: (0, 0))
        for value in values
    ]
    out_specs = [part for _ in out_types]
    out_shape = [jax.ShapeDtypeStruct((count, width), kind) for kind in out_types]
    if sums:
        out_specs.append(pl.BlockSpec((8, width), lambda i: (0, 0)))
        out_shape.append(jax.ShapeDtypeStruct((8, width), FULL))
    return pl.pallas_call(
        kernel,
        grid=(count // chunk,),
        in_specs=in_specs,
        out_specs=out_specs,
        out_shape=out_shape,
        compiler_params=pltpu.CompilerParams(vmem_limit_bytes=40 << 20),
        name=name,
    )(*values)


def joint_kernel(mine_ref, other_ref, weight_ref, bias_ref, out_ref):
    half = mine_ref.shape[1]
    out = product(mine_ref[...], weight_ref[:half], PLAIN)
    out += product(other_ref[...], weight_ref[half:], PLAIN)
    out_ref[...] = (out + bias_ref[...]).astype(LOW)


def joint_projection(mine, other, weight, bias):
    count, half = mine.shape
    columns = weight.shape[1]
    chunk = row_chunk(count, 784)
    part = pl.BlockSpec((chunk, half), lambda i: (i, 0))
    return pl.pallas_call(
        joint_kernel,
        grid=(count // chunk,),
        in_specs=[
            part,
            part,
            pl.BlockSpec(weight.shape, lambda i: (0, 0)),
            pl.BlockSpec((1, columns), lambda i: (0, 0)),
        ],
        out_specs=pl.BlockSpec((chunk, columns), lambda i: (i, 0)),
        out_shape=jax.ShapeDtypeStruct((count, columns), LOW),
        compiler_params=pltpu.CompilerParams(vmem_limit_bytes=40 << 20),
        name="joint_projection",
    )(mine, other, weight, bias)


def rows_kernel(left_ref, right_ref, out_ref):
    out_ref[...] = product(left_ref[...], right_ref[...], ROW_BY_ROW).astype(LOW)


def rows_product(left, right, columns, name):
    count, depth = left.shape
    chunk = row_chunk(count, 400)
    return pl.pallas_call(
        rows_kernel,
        grid=(count // chunk,),
        in_specs=[
            pl.BlockSpec((chunk, depth), lambda i: (i, 0)),
            pl.BlockSpec((columns, depth), lambda i: (0, 0)),
        ],
        out_specs=pl.BlockSpec((chunk, columns), lambda i: (i, 0)),
        out_shape=jax.ShapeDtypeStruct((count, columns), LOW),
        compiler_params=pltpu.CompilerParams(vmem_limit_bytes=48 << 20),
        name=name,
    )(left, right)


def grad_kernel(distances, place_ref, *refs):
    lefts, (right_ref, out_ref) = refs[:-2], refs[-2:]
    left = lefts[0][...]
    if len(lefts) == 2:
        slot = place_ref[0] ^ distance_at(distances, pl.program_id(0))
        left = jnp.where((slot >> 1) == 0, left, lefts[1][...])
    out_ref[0] = product(left, right_ref[...], COLUMN_BY_COLUMN).astype(LOW)


def distance_at(distances, step):
    if len(distances) == 1:
        return distances[0]
    return distances[0] + step * (distances[1] - distances[0])


def grad_products(lefts, right, place, distances, name):
    tokens_here, columns = right.shape
    quarter = sum(left.shape[1] for left in lefts) // 4
    blocks = lefts[0].shape[1] // quarter

    def left_at(i, place):
        return (0, (place[0] ^ distance_at(distances, i)) & (blocks - 1))

    return pl.pallas_call(
        lambda *refs: grad_kernel(distances, *refs),
        grid_spec=pltpu.PrefetchScalarGridSpec(
            num_scalar_prefetch=1,
            grid=(len(distances),),
            in_specs=[pl.BlockSpec((tokens_here, quarter), left_at) for _ in lefts]
            + [pl.BlockSpec((tokens_here, columns), lambda i, place: (0, 0))],
            out_specs=pl.BlockSpec((1, quarter, columns), lambda i, place: (i, 0, 0)),
        ),
        out_shape=jax.ShapeDtypeStruct((len(distances), quarter, columns), LOW),
        compiler_params=pltpu.CompilerParams(vmem_limit_bytes=48 << 20),
        name=name,
    )(place.astype(jnp.int32).reshape(1), *lefts, right)


def attention_forward_kernel(q_ref, k_ref, v_ref, o_ref, lse_ref):
    count, width = q_ref.shape
    rows = row_chunk(count, 256)
    lane = lax.broadcasted_iota(jnp.int32, (rows, width), 1)
    k = k_ref[...]
    v = v_ref[...]
    units = [(start, head) for start in range(0, count, rows) for head in range(width // HEAD_DIM)]

    def scores_of(unit):
        start, head = unit
        q = q_ref[start : start + rows] * jnp.asarray(HEAD_DIM ** (-0.5), LOW)
        return product(jnp.where((lane // HEAD_DIM) == head, q, jnp.zeros_like(q)), k, ROW_BY_ROW)

    logs = []
    ahead = scores_of(units[0])
    for step, (start, head) in enumerate(units):
        scores = ahead
        if step + 1 < len(units):
            ahead = scores_of(units[step + 1])
        top = jnp.max(scores, axis=-1, keepdims=True)
        weights = jnp.exp(scores - top)
        total = jnp.sum(weights, axis=-1, keepdims=True)
        part = product(weights.astype(LOW), v, PLAIN) / total
        if head == 0:
            out = part
            logs.append(jnp.zeros((rows, width), FULL))
        else:
            out = jnp.where((lane // HEAD_DIM) == head, part, out)
            o_ref[start : start + rows] = out.astype(LOW)
        logs[-1] = jnp.where(lane == head, top + jnp.log(total), logs[-1])
    lse_ref[...] = jnp.concatenate(logs, axis=0).T[: lse_ref.shape[0]]


def attention_forward(joint, pair):
    count, columns = joint.shape
    width = 2 * HEAD_DIM
    kind = columns // (3 * width)
    return pl.pallas_call(
        attention_forward_kernel,
        grid=(1,),
        in_specs=[
            pl.BlockSpec((count, width), lambda i: (0, pair)),
            pl.BlockSpec((count, width), lambda i: (0, kind + pair)),
            pl.BlockSpec((count, width), lambda i: (0, 2 * kind + pair)),
        ],
        out_specs=[
            pl.BlockSpec((count, width), lambda i: (0, 0)),
            pl.BlockSpec((8, count), lambda i: (0, 0)),
        ],
        out_shape=[
            jax.ShapeDtypeStruct((count, width), LOW),
            jax.ShapeDtypeStruct((8, count), FULL),
        ],
        compiler_params=pltpu.CompilerParams(vmem_limit_bytes=48 << 20),
        name="attention_forward",
    )(joint, joint, joint)


def attention_backward_kernel(
    q_ref, k_ref, v_ref, da_ref, o_ref, lse_ref, dq_ref, dk_ref, dv_ref,
    q_heads, da_heads, delta_ref, dq_total,
):
    count, width = q_ref.shape
    rows = row_chunk(count, 256)
    heads = width // HEAD_DIM
    scale = jnp.asarray(HEAD_DIM ** (-0.5), LOW)

    lane = lax.broadcasted_iota(jnp.int32, (count, width), 1)
    delta = jnp.zeros((count, width), FULL)
    q = q_ref[...] * scale
    da = da_ref[...]
    both_rows = da.astype(FULL) * o_ref[...].astype(FULL)
    for head in range(heads):
        mask = (lane // HEAD_DIM) == head
        q_heads[head] = jnp.where(mask, q, jnp.zeros_like(q))
        da_heads[head] = jnp.where(mask, da, jnp.zeros_like(da))
        row = jnp.sum(jnp.where(mask, both_rows, 0.0), axis=-1, keepdims=True)
        delta = jnp.where(lane == head, row, delta)
    delta_ref[...] = delta.T[:8]
    dq_total[...] = jnp.zeros_like(dq_total)

    lane = lax.broadcasted_iota(jnp.int32, (rows, width), 1)
    for start in range(0, count, rows):
        k = k_ref[start : start + rows]
        v = v_ref[start : start + rows]
        scaled_k = k * scale
        dk = dv = None
        for head in range(heads):
            q = q_heads[head]
            da = da_heads[head]
            probs = jnp.exp(product(k, q, ROW_BY_ROW) - lse_ref[head : head + 1, :])
            slope = probs * (product(v, da, ROW_BY_ROW) - delta_ref[head : head + 1, :])
            slope = slope.astype(LOW)
            dv_part = product(probs.astype(LOW), da, PLAIN)
            dk_part = product(slope, q, PLAIN)
            dv = dv_part if dv is None else dv + dv_part
            dk = dk_part if dk is None else dk + dk_part
            one_k = jnp.where((lane // HEAD_DIM) == head, scaled_k, jnp.zeros_like(k))
            dq_total[...] += product(slope, one_k, COLUMN_BY_COLUMN)
        dk_ref[start : start + rows] = dk.astype(LOW)
        dv_ref[start : start + rows] = dv.astype(LOW)
    dq_ref[...] = dq_total[...].astype(LOW)


def attention_backward(joint, da, out, lse, pair):
    count, columns = joint.shape
    width = 2 * HEAD_DIM
    kind = columns // (3 * width)
    alone = pl.BlockSpec((count, width), lambda i: (0, 0))
    grad = jax.ShapeDtypeStruct((count, width), LOW)
    return pl.pallas_call(
        attention_backward_kernel,
        grid=(1,),
        in_specs=[
            pl.BlockSpec((count, width), lambda i: (0, pair)),
            pl.BlockSpec((count, width), lambda i: (0, kind + pair)),
            pl.BlockSpec((count, width), lambda i: (0, 2 * kind + pair)),
            pl.BlockSpec((count, width), lambda i: (0, pair)),
            alone,
            pl.BlockSpec((8, count), lambda i: (0, 0)),
        ],
        out_specs=[alone, alone, alone],
        out_shape=[grad, grad, grad],
        scratch_shapes=[
            pltpu.VMEM((2, count, width), LOW),
            pltpu.VMEM((2, count, width), LOW),
            pltpu.VMEM((8, count), FULL),
            pltpu.VMEM((count, width), FULL),
        ],
        compiler_params=pltpu.CompilerParams(vmem_limit_bytes=48 << 20),
        name="attention_backward",
    )(joint, joint, joint, da, out, lse)


def put_together(place_ref, whole_ref, pieces, edge=0):
    for piece, refs in enumerate(pieces):
        rows = refs[0].shape[0]
        place = pl.ds(pl.multiple_of(place_ref[piece], rows), rows)
        if len(refs) == 1:
            whole_ref[place, :] = refs[0][...]
            continue

        @pl.when(pl.program_id(0) < edge)
        def _():
            whole_ref[place, :] = refs[0][...]

        @pl.when(pl.program_id(0) >= edge)
        def _():
            whole_ref[place, :] = refs[1][...]


def nested(refs, like):
    refs = iter(refs)
    return [tuple(next(refs) for _ in piece) for piece in like]


def feed_forward_kernel(
    expand, reduce, edge, place_ref, normed_ref, slope_ref, bias_ref, *refs
):
    active_ref, expand_slope_ref, back_ref, bias_grad_ref, total, expand_ref, reduce_ref = refs[-7:]
    arrays = sum(len(piece) for piece in expand)
    put_together(place_ref, expand_ref, nested(refs[:arrays], expand), edge)
    put_together(place_ref, reduce_ref, nested(refs[arrays:-7], reduce))
    step = pl.program_id(0)
    hidden = product(normed_ref[...], expand_ref[...], PLAIN) + bias_ref[...]
    upstream = product(slope_ref[...], reduce_ref[...], PLAIN)
    share = 0.5 * (1.0 + lax.erf(hidden * (0.5**0.5)))
    active_ref[...] = (hidden * share).astype(LOW)
    density = jnp.exp(-0.5 * hidden * hidden) * 0.3989422804014327
    slope = (upstream * (share + hidden * density)).astype(LOW)
    expand_slope_ref[...] = slope
    bias_grad_ref[...] = jnp.sum(slope.astype(FULL), axis=0, keepdims=True)
    back = product(slope, expand_ref[...], ROW_BY_ROW)

    @pl.when(step == 0)
    def _():
        total[...] = back

    @pl.when(step > 0)
    def _():
        total[...] += back

    @pl.when(step == pl.num_programs(0) - 1)
    def _():
        back_ref[...] = total[...].astype(LOW)


def feed_forward(normed, slope, bias, expand, early, reduce, place):
    count, width = normed.shape
    hidden = bias.shape[1]
    block = 512
    edge = early // block
    whole = pl.BlockSpec((count, width), lambda i, place: (0, 0))
    out = pl.BlockSpec((count, block), lambda i, place: (0, i))
    row = pl.BlockSpec((1, block), lambda i, place: (0, i))
    specs = []
    arrays = []
    for piece in [*expand, *reduce]:
        shape = (piece[0].shape[0], block)
        arrays += piece
        if len(piece) == 1:
            specs.append(pl.BlockSpec(shape, lambda i, place: (0, i)))
        else:
            specs.append(pl.BlockSpec(shape, lambda i, place: (0, jnp.minimum(i, edge - 1))))
            specs.append(pl.BlockSpec(shape, lambda i, place: (0, jnp.maximum(i - edge, 0))))
    return pl.pallas_call(
        lambda *refs: feed_forward_kernel(expand, reduce, edge, *refs),
        grid_spec=pltpu.PrefetchScalarGridSpec(
            num_scalar_prefetch=1,
            grid=(hidden // block,),
            in_specs=[whole, whole, row] + specs,
            out_specs=[out, out, whole, row],
            scratch_shapes=[
                pltpu.VMEM((count, width), FULL),
                pltpu.VMEM((width, block), LOW),
                pltpu.VMEM((width, block), LOW),
            ],
        ),
        out_shape=[
            jax.ShapeDtypeStruct((count, hidden), LOW),
            jax.ShapeDtypeStruct((count, hidden), LOW),
            jax.ShapeDtypeStruct((count, width), LOW),
            jax.ShapeDtypeStruct((1, hidden), FULL),
        ],
        compiler_params=pltpu.CompilerParams(vmem_limit_bytes=44 << 20),
        name="feed_forward",
    )(place, normed, slope, bias, *arrays)


def reduce_kernel(place_ref, active_ref, *refs):
    out_ref, total, reduce_ref = refs[-3:]
    put_together(place_ref, reduce_ref, [(ref,) for ref in refs[:-3]])
    part = product(active_ref[...], reduce_ref[...], ROW_BY_ROW)

    @pl.when(pl.program_id(0) == 0)
    def _():
        total[...] = part

    @pl.when(pl.program_id(0) > 0)
    def _():
        total[...] += part

    @pl.when(pl.program_id(0) == pl.num_programs(0) - 1)
    def _():
        out_ref[...] = total[...].astype(LOW)


def reduce_output(active, reduce, place):
    count, hidden = active.shape
    width = sum(piece.shape[0] for piece in reduce)
    block = 512 if hidden % 512 == 0 else hidden
    return pl.pallas_call(
        reduce_kernel,
        grid_spec=pltpu.PrefetchScalarGridSpec(
            num_scalar_prefetch=1,
            grid=(hidden // block,),
            in_specs=[pl.BlockSpec((count, block), lambda i, place: (0, i))]
            + [
                pl.BlockSpec((piece.shape[0], block), lambda i, place: (0, i)) for piece in reduce
            ],
            out_specs=pl.BlockSpec((count, width), lambda i, place: (0, 0)),
            scratch_shapes=[pltpu.VMEM((count, width), FULL), pltpu.VMEM((width, block), LOW)],
        ),
        out_shape=jax.ShapeDtypeStruct((count, width), LOW),
        compiler_params=pltpu.CompilerParams(vmem_limit_bytes=32 << 20),
        name="reduce_output",
    )(place, active, *reduce)


def swap(value, axis, distance):
    size = lax.axis_size(axis)
    return lax.ppermute(value, axis, [(i, i ^ distance) for i in range(size)])


def fence(*values):
    return lax.optimization_barrier(values)


def gather_near(rows_here):
    if lax.axis_size("fsdp") != 4:
        return (lax.all_gather(rows_here, "fsdp", axis=0, tiled=True),)
    return (rows_here, swap(rows_here, "fsdp", 1), swap(rows_here, "fsdp", 2))


def far_of(held):
    if len(held) == 1:
        return ()
    half = held[0].shape[0] // 2
    return (held[2][:half], held[1][half:])


def send_far(leaves):
    return (swap(leaves[0], "fsdp", 1), swap(leaves[1], "fsdp", 2)) if leaves else ()


def far_of(held):
    if len(held) == 1:
        return ()
    half = held[0].shape[0] // 2
    return (held[2][:half], held[1][half:])


def send_far(leaves):
    return (swap(leaves[0], "fsdp", 1), swap(leaves[1], "fsdp", 2)) if leaves else ()


def gather_far(held):
    return held + send_far(far_of(held))


def place_near(held):
    if len(held) == 1:
        return held[0]
    rows_here, near, side = held[:3]
    me = lax.axis_index("fsdp")
    count, width = rows_here.shape
    out = jnp.zeros((4 * count, width), rows_here.dtype)
    out = lax.dynamic_update_slice(out, rows_here, (me * count, 0))
    out = lax.dynamic_update_slice(out, near, ((me ^ 1) * count, 0))
    return lax.dynamic_update_slice(out, side, ((me ^ 2) * count, 0))


def place_far(out, held):
    if len(held) == 1:
        return out
    far_top, far_low = held[3:]
    half = far_top.shape[0]
    start = (lax.axis_index("fsdp") ^ 3) * 2 * half
    out = lax.dynamic_update_slice(out, far_top, (start, 0))
    return lax.dynamic_update_slice(out, far_low, (start + half, 0))


def grad_rows(left, right, distance):
    count = left.shape[1] // 4
    start = (lax.axis_index("fsdp") ^ distance) * count
    piece = lax.dynamic_slice_in_dim(left, start, count, 1)
    return product(piece, right, COLUMN_BY_COLUMN).astype(LOW)


def rows_at(matrices, distance):
    parts = []
    for matrix in matrices:
        count = matrix.shape[0] // 4
        start = (lax.axis_index("fsdp") ^ distance) * count
        parts.append(lax.dynamic_slice_in_dim(matrix, start, count, 0))
    return parts[0] if len(parts) == 1 else jnp.concatenate(parts, axis=1)


def far_halves(far):
    half = far.shape[0] // 2
    return (swap(far[:half], "fsdp", 1), swap(far[half:], "fsdp", 2))


def add_far(near, side, far):
    half = near.shape[0] // 2
    near = jnp.concatenate([near[:half], both((near[half:], far[1])).astype(LOW)], axis=0)
    side = jnp.concatenate([both((side[:half], far[0])).astype(LOW), side[half:]], axis=0)
    return (near, side)


def near_rows_out(pair):
    return (swap(pair[0], "fsdp", 1), swap(pair[1], "fsdp", 2))


def halves(value, bit):
    half = value.shape[0] // 2
    keep = lax.dynamic_slice_in_dim(value, bit * half, half, 0)
    send = lax.dynamic_slice_in_dim(value, (1 - bit) * half, half, 0)
    return keep, send.astype(LOW)


def split_rows(value, bit, distance):
    keep, send = halves(value, bit)
    return keep, swap(send, "ctx", distance)


def both(pair):
    return pair[0].astype(FULL) + pair[1].astype(FULL)


def joined(pair, bit):
    value, other = pair
    return jnp.where(
        bit == 0,
        jnp.concatenate([value, other], axis=0),
        jnp.concatenate([other, value], axis=0),
    )


def join_rows(value, bit, distance):
    return joined((value, swap(value, "ctx", distance)), bit)


def pairwise(pieces):
    return (pieces[0] + pieces[1]) + (pieces[2] + pieces[3])


def swapped_if(bit, pair):
    return [jnp.where(bit == 0, pair[0], pair[1]), jnp.where(bit == 0, pair[1], pair[0])]


def per_device(
    tokens,
    clip_mask,
    cotangent,
    first_gain,
    first_shift,
    joint_weight,
    joint_bias,
    mixer_weight,
    mixer_bias,
    second_gain,
    second_shift,
    expand_weight,
    expand_bias,
    reduce_weight,
    reduce_bias,
):
    clips_here, rows_here, width = tokens.shape
    if lax.axis_size("ctx") != 4 or lax.axis_size("tp") != 2 or clips_here != 2:
        raise ValueError("mesh")
    shard = lax.axis_index("fsdp")
    block = lax.axis_index("ctx")
    core = lax.axis_index("tp")
    clip_at = block >> 1
    part_at = block & 1
    width_half = width // 2
    quarter = width_half // 2
    features = joint_weight.shape[2]
    part_width = features // 2
    pair_width = 2 * HEAD_DIM
    tokens_here = clips_here * rows_here

    flat_tokens = tokens.reshape(tokens_here, width)
    (first_normed,) = by_rows(
        first_norm_kernel, "first_norm", [LOW], False,
        flat_tokens, first_gain[None], first_shift[None],
    )
    first_normed = first_normed.reshape(clips_here, rows_here, width)
    mine = lax.dynamic_slice_in_dim(first_normed, core * width_half, width_half, 2)
    other_side = lax.dynamic_slice_in_dim(first_normed, (1 - core) * width_half, width_half, 2)
    own_clip = lax.dynamic_index_in_dim(mine, clip_at, 0, False)
    own_other = lax.dynamic_index_in_dim(other_side, clip_at, 0, False)
    other_clip = lax.dynamic_index_in_dim(mine, 1 - clip_at, 0, False)
    joint_part = lax.dynamic_slice_in_dim(joint_weight, part_at * part_width, part_width, 2)
    early = expand_weight.shape[1] // 2
    wide_part = jnp.concatenate(
        [expand_weight[:, :early]] + [joint_part[:, kind] for kind in range(3)] + [mixer_weight],
        axis=1,
    )

    own_clip, left, right, wide_part = fence(
        own_clip, other_clip[:, :quarter], other_clip[:, quarter:], wide_part
    )
    near_rows = swap(own_clip, "ctx", 1)
    across_left = swap(left, "ctx", 2)
    far_right = swap(right, "ctx", 3)
    wide_held = gather_near(wide_part)

    near_rows, across_left, far_right = fence(near_rows, across_left, far_right)
    passed = swap(jnp.concatenate([across_left, far_right], axis=1), "ctx", 1)
    (wide_held,) = fence(wide_held)
    held = gather_far(tuple(piece[:, early:] for piece in wide_held))

    passed, held, expand_rest = fence(passed, held, expand_weight[:, early:])
    rest_held = gather_near(expand_rest)
    cross_rows = jnp.concatenate(
        [
            near_rows,
            jnp.concatenate([across_left, passed[:, quarter:]], axis=1),
            jnp.concatenate([passed[:, :quarter], far_right], axis=1),
        ],
        axis=0,
    )
    cross_other = swap(cross_rows, "tp", 1)
    both_full = place_far(place_near(held), held)
    joint_columns = 3 * part_width
    joint_full = jnp.concatenate(
        [
            lax.dynamic_slice(both_full, (start * width_half, 0), (width_half, joint_columns))
            for start in (core, 1 - core)
        ],
        axis=0,
    )

    cross_other, joint_full, both_full, reduce_weight = fence(
        cross_other, joint_full, both_full, reduce_weight
    )
    mixer_full = both_full[:, joint_columns:]
    reduce_held = gather_near(reduce_weight)
    normed_mine = jnp.concatenate([own_clip, cross_rows], axis=0)
    normed_other = jnp.concatenate([own_other, cross_other], axis=0)
    bias_part = lax.dynamic_slice_in_dim(joint_bias, part_at * part_width, part_width, 1)
    bias_row = jnp.concatenate([bias_part[0], jnp.zeros_like(bias_part[0]), bias_part[1]])
    joint_out = joint_projection(normed_mine, normed_other, joint_full, bias_row[None])
    out_first, log_first = attention_forward(joint_out, 0)

    out_first, joint_out, mixer_full, rest_held = fence(
        out_first, joint_out, mixer_full, rest_held
    )
    first_blocks = out_first.reshape(4, rows_here, pair_width)
    arrived_first = [swap(first_blocks[d], "ctx", d) for d in (1, 2, 3)]
    out_second, log_second = attention_forward(joint_out, 1)

    far_leaves = far_of(
        tuple(
            jnp.concatenate([one[:, :early], two], axis=1)
            for one, two in zip(wide_held, rest_held)
        )
    )
    out_second, arrived_first, reduce_held, far_leaves = fence(
        out_second, arrived_first, reduce_held, far_leaves
    )
    second_blocks = out_second.reshape(4, rows_here, pair_width)
    arrived_second = [swap(second_blocks[d], "ctx", d) for d in (1, 2, 3)]
    expand_far_rows = send_far(far_leaves)

    arrived_second, expand_far_rows, reduce_held, reduce_leaves = fence(
        arrived_second, expand_far_rows, reduce_held, far_of(reduce_held)
    )
    reduce_held = reduce_held + send_far(reduce_leaves)
    expand_held = list(zip(wide_held, rest_held)) + [(rows,) for rows in expand_far_rows]
    arrived = [jnp.concatenate([first_blocks[0], second_blocks[0]], axis=1)] + [
        jnp.concatenate([one, two], axis=1) for one, two in zip(arrived_first, arrived_second)
    ]
    own_joined = jnp.concatenate(swapped_if(part_at, arrived[:2]), axis=1)
    other_joined = jnp.concatenate(swapped_if(part_at, arrived[2:]), axis=1)
    mixed_in = jnp.concatenate(swapped_if(clip_at, [own_joined, other_joined]), axis=0)
    mixer_part = product(mixed_in, mixer_full, ROW_BY_ROW).astype(LOW)
    mixer_swapped = swap(mixer_part, "tp", 1)
    mixer_row = mixer_bias[None]
    (second_normed,) = by_rows(
        second_norm_kernel, "second_norm", [LOW], False,
        flat_tokens, mixer_part, mixer_swapped, mixer_row, second_gain[None], second_shift[None],
    )
    valid = clip_mask.astype(FULL)[:, None, None]
    reduce_slope = (cotangent.astype(FULL) * valid).astype(LOW).reshape(tokens_here, width)
    reduce_bias_grad = jnp.sum(reduce_slope.astype(FULL), axis=0)

    second_normed, reduce_slope, reduce_held = fence(second_normed, reduce_slope, reduce_held)
    four = lax.axis_size("fsdp") == 4
    start = jnp.zeros((), jnp.int32)
    if four:
        rows = width // 4
        pieces_at = jnp.stack([shard, shard ^ 1, shard ^ 2, shard ^ 3, shard ^ 3]) * rows
        pieces_at = pieces_at.astype(jnp.int32) + jnp.array([0, 0, 0, 0, rows // 2], jnp.int32)
    else:
        pieces_at = start.reshape(1)
    activated, expand_slope, second_part, expand_bias_grad = feed_forward(
        second_normed, reduce_slope, expand_bias[None], expand_held, early,
        [(piece,) for piece in reduce_held], pieces_at,
    )
    expand_bias_grad = expand_bias_grad[0]

    second_swapped = swap(second_part, "tp", 1)
    place, order = (shard, (3, 2, 1, 0)) if four else (start, (0, 1, 2, 3))
    if four:
        half = width // 8
        far = grad_rows(second_normed, expand_slope, 3)
        far_top, far_low, normed_again, expand_slope = fence(
            far[:half], far[half:], second_normed, expand_slope
        )
        expand_far = (swap(far_top, "fsdp", 1), swap(far_low, "fsdp", 2))
        expand_parts = [grad_rows(normed_again, expand_slope, d) for d in (0, 1, 2)]
        expand_parts, second_swapped = fence(expand_parts, second_swapped)
    else:
        expand_far = ()
        expand_whole = product(second_normed, expand_slope, COLUMN_BY_COLUMN).astype(LOW)
    mixer_slope, first_sum_back, second_sums = by_rows(
        second_norm_back_kernel, "second_norm_back", [LOW, FULL], True,
        flat_tokens, mixer_part, mixer_swapped, mixer_row, second_gain[None],
        second_part, second_swapped, reduce_slope,
    )
    attended_slope = product(mixer_slope, mixer_full, PLAIN).astype(LOW)

    leaving = []
    for distance in range(4):
        to = block ^ distance
        corner = ((to >> 1) * rows_here, (to & 1) * part_width)
        leaving.append(lax.dynamic_slice(attended_slope, corner, (rows_here, part_width)))
    expand_near = add_far(expand_parts[1], expand_parts[2], expand_far) if four else ()
    leaving, mixer_slope, mixed_in, activated, expand_near = fence(
        leaving, mixer_slope, mixed_in, activated, expand_near
    )
    slope_blocks = [leaving[0]] + [swap(leaving[d], "ctx", d) for d in (1, 2, 3)]
    if four:
        expand_near = near_rows_out(expand_near)
    wide = (
        product(reduce_slope, activated, COLUMN_BY_COLUMN).astype(LOW),
        product(mixer_slope, mixed_in, COLUMN_BY_COLUMN).astype(LOW),
    )
    if four:
        wide_far, wide_side, wide_next = (rows_at(wide, distance) for distance in (3, 2, 1))
        far_top, far_low = wide_far[:half], wide_far[half:]
        wide_early = (wide_next[:half], wide_side[half:])
    else:
        far_top, far_low, wide_early = (), (), ()

    slope_blocks, expand_near, far_top, far_low = fence(
        slope_blocks, expand_near, far_top, far_low
    )
    if four:
        expand_sum = expand_parts[0].astype(FULL) + both(expand_near)
    else:
        expand_sum = lax.psum_scatter(
            expand_whole, "fsdp", scatter_dimension=0, tiled=True
        ).astype(FULL)
    expand_keep, expand_send = halves(expand_sum, part_at)
    slope_clip = jnp.concatenate(slope_blocks, axis=0)
    expand_send, slope_clip, far_top, far_low = fence(expand_send, slope_clip, far_top, far_low)
    wide_far = (swap(far_top, "fsdp", 1), swap(far_low, "fsdp", 2)) if four else ()
    expand_rows = (expand_keep, swap(expand_send, "ctx", 1))
    grad_first = attention_backward(joint_out, slope_clip, out_first, log_first, 0)

    grad_first, slope_clip, wide_far, expand_rows = fence(
        grad_first, slope_clip, wide_far, expand_rows
    )
    if four:
        wide_late = (
            both((wide_next[half:], wide_far[1])).astype(LOW),
            both((wide_side[:half], wide_far[0])).astype(LOW),
        )
    else:
        wide_late = ()
    expand_keep, expand_send = halves(both(expand_rows), clip_at)
    expand_send, slope_clip, wide_early, wide_late = fence(
        expand_send, slope_clip, wide_early, wide_late
    )
    if four:
        wide_early = near_rows_out(wide_early)
    expand_rows = (expand_keep, swap(expand_send, "ctx", 2))
    grad_second = attention_backward(joint_out, slope_clip, out_second, log_second, 1)

    grad_second, expand_rows, wide_early, wide_late = fence(
        grad_second, expand_rows, wide_early, wide_late
    )
    if four:
        wide_late = near_rows_out(wide_late)
    expand_rows = both(expand_rows).astype(LOW)
    expand_rows = (expand_rows, swap(expand_rows, "ctx", 2))
    joint_slope = jnp.concatenate(
        [grad[kind] for kind in range(3) for grad in (grad_first, grad_second)], axis=1
    )
    first_there = product(joint_slope, joint_full[width_half:], ROW_BY_ROW).astype(LOW)
    first_here = rows_product(joint_slope, joint_full, width_half, "first_slope")
    first_half = both((first_here, swap(first_there, "tp", 1))).astype(LOW)

    if not four:
        wide_near = lax.psum_scatter(
            jnp.concatenate(wide, axis=1), "fsdp", scatter_dimension=0, tiled=True
        )
    first_half, joint_slope = fence(first_half, joint_slope)
    pieces = first_half.reshape(4, rows_here, width_half)
    passing = jnp.concatenate([pieces[1], pieces[3][:, :quarter], pieces[2][:, quarter:]], axis=1)
    passing = swap(passing, "ctx", 1)
    place = (shard if four else start) ^ (2 * core)
    joint_parts = grad_products([normed_mine, normed_other], joint_slope, place, order, "joint_grad")
    slope_sums = jnp.sum(joint_slope.astype(FULL), axis=0)
    bias_sums = jnp.stack([slope_sums[:part_width], slope_sums[2 * part_width :]])
    joint_bias_grad = lax.dynamic_update_slice(
        jnp.zeros((2, features), FULL), bias_sums, (0, part_at * part_width)
    )

    joint_far = far_halves(joint_parts[0]) if four else ()
    passing, joint_far, wide_late, expand_rows = fence(
        passing, joint_far, wide_late, expand_rows
    )
    expand_rows = joined(expand_rows, clip_at)
    if four:
        near_sum = [both((wide_early[0], wide_late[1])), both((wide_late[0], wide_early[1]))]
        wide_sum = rows_at(wide, 0).astype(FULL) + jnp.concatenate(near_sum, axis=0)
    else:
        wide_sum = wide_near.astype(FULL)
    wide_keep, wide_send = halves(wide_sum, part_at)
    own_half = both((pieces[0], passing[:, :width_half])).astype(LOW)
    to_left = both((pieces[2][:, :quarter], passing[:, width_half : width_half + quarter]))
    to_right = both((pieces[3][:, quarter:], passing[:, width_half + quarter :]))
    joint_near = add_far(joint_parts[2], joint_parts[1], joint_far) if four else ()
    to_left, to_right, own_half, wide_send, joint_near, activated = fence(
        to_left.astype(LOW), to_right.astype(LOW), own_half, wide_send, joint_near, activated
    )
    other_half = jnp.concatenate([swap(to_left, "ctx", 2), swap(to_right, "ctx", 3)], axis=1)
    wide_rows = (wide_keep, swap(wide_send, "ctx", 1))
    if four:
        joint_near = near_rows_out(joint_near)
    else:
        joint_near = lax.psum_scatter(
            joint_parts.reshape(width, -1), "fsdp", scatter_dimension=0, tiled=True
        )
    reduce_part = reduce_output(activated, reduce_held, pieces_at)

    other_half, joint_near, wide_rows, reduce_part = fence(
        other_half, joint_near, wide_rows, reduce_part
    )
    slope_half = jnp.concatenate(swapped_if(clip_at, [own_half, other_half]), axis=0)
    slope_other = swap(slope_half, "tp", 1)
    slope_other, expand_rows = fence(slope_other, expand_rows)
    expand_grad = join_rows(expand_rows, part_at, 1).astype(FULL)
    first_slope = jnp.concatenate(swapped_if(core, [slope_half, slope_other]), axis=1)
    wide_rows = split_rows(both(wide_rows), clip_at, 2)
    reduce_swapped = swap(reduce_part, "tp", 1)
    joint_sum = joint_parts[3].astype(FULL) + both(joint_near) if four else joint_near
    joint_sum = joint_sum.astype(LOW)
    joint_sum = (joint_sum, swap(joint_sum, "ctx", 2))
    tokens_grad, first_sums = by_rows(
        first_norm_back_kernel, "first_norm_back", [FULL], True,
        flat_tokens, first_slope, first_gain[None],
        cotangent.reshape(tokens_here, width), first_sum_back,
    )
    first_sums, tokens_grad, reduce_swapped = fence(first_sums, tokens_grad, reduce_swapped)
    vectors = [
        first_sums[0],
        first_sums[1],
        joint_bias_grad[0],
        joint_bias_grad[1],
        second_sums[2],
        second_sums[0],
        second_sums[1],
        expand_bias_grad,
        reduce_bias_grad,
    ]
    packed = jnp.concatenate(vectors).reshape(-1, 128)
    packed_pieces = [packed] + [swap(packed, "ctx", d) for d in (1, 2, 3)]
    reduce_out = both((reduce_part, reduce_swapped)) + reduce_bias
    mixer_out = both((mixer_part, mixer_swapped)) + mixer_bias
    branches = (mixer_out + reduce_out).reshape(clips_here, rows_here, width)
    result = (tokens.astype(FULL) + valid * branches).astype(LOW)

    packed_pieces, joint_sum, wide_rows, result = fence(
        packed_pieces, joint_sum, wide_rows, result
    )
    packed = pairwise(packed_pieces)
    if four:
        packed = pairwise([packed] + [swap(packed, "fsdp", d) for d in (1, 2, 3)])
    else:
        packed = lax.psum(packed, "fsdp")
    joint_sum = both(joint_sum).astype(LOW)
    joint_parts = swapped_if(part_at, [joint_sum, swap(joint_sum, "ctx", 1)])
    joint_grad = jnp.concatenate(
        [piece.reshape(-1, 3, part_width) for piece in joint_parts], axis=2
    ).astype(FULL)
    wide_rows = join_rows(both(wide_rows).astype(LOW), clip_at, 2)
    wide_other = swap(wide_rows, "ctx", 1)
    rows = wide_rows.shape[0]

    def placed(columns):
        mine, other = wide_rows[:, columns], wide_other[:, columns]
        out = jnp.zeros((2 * rows, mine.shape[1]), FULL)
        out = lax.dynamic_update_slice(out, mine.astype(FULL), (part_at * rows, 0))
        return lax.dynamic_update_slice(out, other.astype(FULL), ((1 - part_at) * rows, 0))

    reduce_grad = placed(slice(None, activated.shape[1]))
    mixer_grad = placed(slice(activated.shape[1], None))
    packed = packed.reshape(-1)
    shares = []
    start = 0
    for vector in vectors:
        share = vector.shape[0] // lax.axis_size("fsdp")
        shares.append(lax.dynamic_slice_in_dim(packed, start + shard * share, share, 0))
        start += vector.shape[0]

    shape = (clips_here, rows_here, width)
    return (
        result,
        tokens_grad.reshape(shape),
        shares[0],
        shares[1],
        joint_grad,
        jnp.stack([shares[2], shares[3]]),
        mixer_grad,
        shares[4],
        shares[5],
        shares[6],
        expand_grad,
        shares[7],
        reduce_grad,
        shares[8],
    )


def solution(mesh):
    return jax.shard_map(
        per_device,
        mesh=mesh,
        in_specs=(
            P("fsdp", "ctx", None),
            P("fsdp"),
            P("fsdp", "ctx", None),
            P(),
            P(),
            P("fsdp", None, "tp"),
            P(None, "tp"),
            P("fsdp", "tp"),
            P(),
            P(),
            P(),
            P("fsdp", "tp"),
            P("tp"),
            P("fsdp", "tp"),
            P(),
        ),
        out_specs=(
            P("fsdp", "ctx", None),
            P("fsdp", "ctx", None),
            P("fsdp"),
            P("fsdp"),
            P("fsdp", None, "tp"),
            P(None, ("tp", "fsdp")),
            P("fsdp", "tp"),
            P("fsdp"),
            P("fsdp"),
            P("fsdp"),
            P("fsdp", "tp"),
            P(("tp", "fsdp")),
            P("fsdp", "tp"),
            P("fsdp"),
        ),
        check_vma=False,
    )
```
